32 devices in a mesh: rep: 2 (over y), shard: 8 (over z, x), mp: 2 (over core).
Axes of the slice: x: 2, y: 2, z: 4, core: 2. Of those that a mesh axis runs over, the one named last changes fastest.
Arguments:
- inputs: bfloat16 [32, 512, 1024], P(('rep', 'shard'), None, 'mp'), may hold values from -6 to 6
- encoded: bfloat16 [32, 128, 1024], P(('rep', 'shard'), None, 'mp'), may hold values from -6 to 6
- cotangent: bfloat16 [32, 512, 1024], P(('rep', 'shard'), None, 'mp'), may hold values from -6 to 6
- lengths: int32 [32], replicated, may hold values from 64 to 512, as said below
- seq_slots: int32 [32], replicated, may hold values from 0 to 31, each once
- block_slots: int32 [128], replicated, may hold values from 0 to 127, as said below
- weights: float32 [2, 128, 256, 256], P('mp', 'shard')
- left_stat: float32 [2, 128, 256, 256], P('mp', 'shard')
- right_stat: float32 [2, 128, 256, 256], P('mp', 'shard')
- left_root: float32 [2, 128, 256, 256], P('mp', 'shard')
- right_root: float32 [2, 128, 256, 256], P('mp', 'shard')
- vectors: float32 [2, 8704], P('mp', 'shard')
- vec_stat: float32 [2, 8704], P('mp', 'shard'), may hold values from 819 to 16384
Outputs:
- outputs: bfloat16 [32, 512, 1024], P(('rep', 'shard'), None, 'mp')
- input_grad: bfloat16 [32, 512, 1024], P(('rep', 'shard'), None, 'mp')
- encoded_grad: bfloat16 [32, 128, 1024], P(('rep', 'shard'), None, 'mp')
- block_grad: float32 [2, 128, 256, 256], P('mp', 'shard')
- left_new: float32 [2, 128, 256, 256], P('mp', 'shard')
- right_new: float32 [2, 128, 256, 256], P('mp', 'shard')
- weights_new: float32 [2, 128, 256, 256], P('mp', 'shard')
- vector_grad: float32 [2, 8704], P('mp', 'shard')
- vec_stat_new: float32 [2, 8704], P('mp', 'shard')
- vectors_new: float32 [2, 8704], P('mp', 'shard')
The draws below stay inside these ranges and needn't reach their ends.
Inputs may be any that keep to these rules, and one draw needn't show every extreme that they name: Rows from lengths[i] on are padding; some sequence has exactly 512 valid tokens. `seq_slots`: slot s lies on the data device s // 2 of the joined rep and shard axes; each slot holds one sequence. `block_slots`: A permutation of the 128 natural blocks.
All inputs are finite; a program needn't handle non-finite values.
Results may differ from the reference program's by a relative error of at most 0.029.
Values may be sent and summed in bfloat16 or wider, within the bound.
No kernel may reach another device: no remote copies, remote signals or barrier semaphores. Data moves between devices by JAX's collectives and lax.ppermute only.
A program may use at most 168 MiB of HBM per device.

```python
import math
import jax
import jax.numpy as jnp
from jax import lax

D = 1024
FF = 4096
HEADS = 16
HEAD_DIM = 64
SEQ = 512
ENC = 128
BS = 256
NSEQ = 32
TOKENS = 16384
NB = 128
VEC_HALF = 8704
N_MP = 2


def dealing(key):
    return jax.random.permutation(jax.random.fold_in(key, 11), NB).astype(jnp.int32)


def draw_block_slots(key, part):
    return dealing(key)


def draw_weights(key, part):
    half_d = D // N_MP
    half_f = FF // N_MP
    entries = D ** (-0.5)
    table = ((D, half_d, entries), (D, half_d, entries), (D, half_d, entries), (half_d, D, entries * math.sqrt(SEQ) / 4.0), (D, half_d, entries), (D, half_d, entries), (D, half_d, entries), (half_d, D, entries * math.sqrt(ENC) / 4.0), (D, half_f, entries), (half_f, D, FF ** (-0.5)))
    scales = jnp.concatenate([jnp.full((row_count // BS * (col_count // BS),), factor, jnp.float32) for row_count, col_count, factor in table])
    slot_scale = jnp.take(scales, dealing(key))
    base = jax.random.normal(jax.random.fold_in(key, 3), (N_MP, NB, BS, BS), jnp.float32)
    return base * slot_scale[None, :, None, None]


def symmetric(key):
    noise = jax.random.normal(key, (N_MP, NB, BS, BS), jnp.float32)
    return (noise + jnp.swapaxes(noise, 2, 3)) * (0.3 / math.sqrt(2.0 * BS))


def statistic(key):
    level = jnp.exp(jax.random.uniform(jax.random.fold_in(key, 5), (N_MP, NB, 1, 1), jnp.float32, 0.0, math.log(4.0)))
    level = level * (BS * TOKENS * 0.02)
    return level * (jnp.eye(BS, dtype=jnp.float32) + symmetric(jax.random.fold_in(key, 6)))


def draw_left_stat(key, part):
    return statistic(jax.random.fold_in(key, 21))


def draw_right_stat(key, part):
    return statistic(jax.random.fold_in(key, 22))


def draw_left_root(key, part):
    return jnp.eye(BS, dtype=jnp.float32) + symmetric(jax.random.fold_in(key, 23))


def draw_right_root(key, part):
    return jnp.eye(BS, dtype=jnp.float32) + symmetric(jax.random.fold_in(key, 24))


def draw_vectors(key, part):
    half_d = D // N_MP
    position = jnp.arange(VEC_HALF)
    segment = position // half_d
    is_gain = (segment == 3) | (segment == 8) | (segment == 11)
    gains = 1.0 + 0.3 * jax.random.uniform(jax.random.fold_in(key, 41), (N_MP, VEC_HALF), jnp.float32, -1.0, 1.0)
    biases = 0.3 * jax.random.normal(jax.random.fold_in(key, 42), (N_MP, VEC_HALF), jnp.float32)
    return jnp.where(is_gain[None, :], gains, biases)


def draw_lengths(key, part):
    drawn = jax.random.randint(jax.random.fold_in(key, 31), (NSEQ,), SEQ // 8, SEQ + 1)
    chosen = jax.random.randint(jax.random.fold_in(key, 32), (), 0, NSEQ)
    return jnp.where(jnp.arange(NSEQ) == chosen, SEQ, drawn).astype(jnp.int32)


def steps_of(own_key, extent, cuts, smallest, top_value):
    level, own = 1.0, jax.random.fold_in(own_key, 6)
    for dim, shards_of in cuts:
        draws = jnp.exp(jax.random.uniform(jax.random.fold_in(own, dim), (shards_of,), jnp.float32, smallest / len(cuts), top_value / len(cuts)))
        level = level * jnp.repeat(draws, extent[dim] // shards_of).reshape([-1 if axis == dim else 1 for axis in range(len(extent))])
    return level


def bell_draw(stream_key, shape, width, reach, shards=(), kind=jnp.bfloat16):
    array = jax.random.normal(stream_key, shape, jnp.float32) * width
    if len(shards) > 0:
        array = steps_of(stream_key, shape, shards, -0.22, 0.18) * array
    return jnp.clip(array, min=-reach, max=reach).astype(kind)


def setup_inputs(seed: int = 0) -> dict:
    seeds = jax.random.split(jax.random.key(seed), 14)
    inputs = bell_draw(seeds[0], (NSEQ, SEQ, D), 1.0, 6.0, ((0, 16), (2, 2)))
    encoded = bell_draw(seeds[1], (NSEQ, ENC, D), 1.0, 6.0, ((0, 16), (2, 2)))
    cotangent = bell_draw(seeds[2], (NSEQ, SEQ, D), 1.0, 6.0, ((0, 16), (2, 2)))
    lengths = draw_lengths(jax.random.fold_in(seeds[13], 71), 0)
    seq_slots = jax.random.permutation(seeds[4], NSEQ).astype(jnp.int32)
    block_slots = draw_block_slots(jax.random.fold_in(seeds[13], 71), 0)
    weights = draw_weights(jax.random.fold_in(seeds[13], 71), 0)
    left_stat = draw_left_stat(jax.random.fold_in(seeds[13], 71), 0)
    right_stat = draw_right_stat(jax.random.fold_in(seeds[13], 71), 0)
    left_root = draw_left_root(jax.random.fold_in(seeds[13], 71), 0)
    right_root = draw_right_root(jax.random.fold_in(seeds[13], 71), 0)
    vectors = draw_vectors(jax.random.fold_in(seeds[13], 71), 0)
    vec_stat = jnp.clip(jnp.exp(math.log(16384.0) - 2.9959764 * jax.random.uniform(seeds[12], (N_MP, VEC_HALF), jnp.float32) ** steps_of(seeds[12], (N_MP, VEC_HALF), ((0, 2), (1, 8)), -0.2, 0.2)), 819.0, 16384.0)
    return {"inputs": inputs, "encoded": encoded, "cotangent": cotangent, "lengths": lengths, "seq_slots": seq_slots, "block_slots": block_slots, "weights": weights, "left_stat": left_stat, "right_stat": right_stat, "left_root": left_root, "right_root": right_root, "vectors": vectors, "vec_stat": vec_stat}


@jax.custom_vjp
def low(v):
    return lax.optimization_barrier(v.astype(jnp.bfloat16)).astype(jnp.float32)

@jax.custom_vjp
def low_back(v):
    return v

def low_keep(v):
    return (low(v), None)

def low_pass(kept, grad):
    return (grad,)

def back_keep(v):
    return (v, None)

def back_low(kept, grad):
    return (low(grad),)
low.defvjp(low_keep, low_pass)
low_back.defvjp(back_keep, back_low)
highest = lax.Precision.HIGHEST
join_axes = (1, 1, 1, 0, 1, 1, 1, 0, 1, 0)

def layouts(model_width, half_d, half_f):
    return ((model_width, half_d), (model_width, half_d), (model_width, half_d), (half_d, model_width), (model_width, half_d), (model_width, half_d), (model_width, half_d), (half_d, model_width), (model_width, half_f), (half_f, model_width))

def to_blocks(matrix):
    row_count, col_count = matrix.shape
    tiles = matrix.reshape(row_count // BS, BS, col_count // BS, BS)
    return jnp.transpose(tiles, (0, 2, 1, 3)).reshape(-1, BS, BS)

def from_blocks(blocks, row_count, col_count):
    tiles = blocks.reshape(row_count // BS, col_count // BS, BS, BS)
    return jnp.transpose(tiles, (0, 2, 1, 3)).reshape(row_count, col_count)

def split_blocks(natural, shapes):
    matrices = []
    offset = 0
    for row_count, col_count in shapes:
        amount = row_count // BS * (col_count // BS)
        matrices.append(from_blocks(natural[offset:offset + amount], row_count, col_count))
        offset = offset + amount
    return matrices

def split_vector(vector, half_d, half_f):
    pieces = [vector[which * half_d:(which + 1) * half_d] for which in range(13)]
    pieces.append(vector[13 * half_d:13 * half_d + half_f])
    return pieces

def both(value):
    return low(low_back(value))

def product(former, latter):
    return jnp.dot(former, latter, precision=highest, preferred_element_type=jnp.float32)

def layer_norm(value, gain, shift):
    center = value - lax.optimization_barrier(jnp.mean(value, axis=1, keepdims=True))
    spread = lax.optimization_barrier(jnp.mean(center * center, axis=1, keepdims=True))
    return center * lax.rsqrt(spread + 1e-05) * gain + shift

def attend(query, key_rows, value_rows, allowed):
    seq_len = query.shape[0]
    q_heads = query.reshape(seq_len, HEADS, HEAD_DIM)
    k_heads = key_rows.reshape(key_rows.shape[0], HEADS, HEAD_DIM)
    v_heads = value_rows.reshape(value_rows.shape[0], HEADS, HEAD_DIM)
    scores = jnp.einsum('qhd,khd->hqk', q_heads, k_heads, precision=highest) * HEAD_DIM ** (-0.5)
    scores = low_back(jnp.where(allowed[None], scores, -1e+30))
    probs = low(jax.nn.softmax(scores, axis=-1))
    return jnp.einsum('hqk,khd->qhd', probs, v_heads, precision=highest).reshape(seq_len, -1)

def sequence(matrices, vector_parts, tokens, states, length):
    w_sq, w_sk, w_sv, w_so, w_cq, w_ck, w_cv, w_co, w_fi, w_fo = matrices
    b_sq, b_sv, b_so, g_one, b_one, b_cq, b_cv, b_co, g_two, b_two, b_fo, g_three, b_three, b_fi = vector_parts
    position = jnp.arange(SEQ)
    live_rows = position < length
    causal = (position[None, :] <= position[:, None]) & live_rows[None, :]
    q_self = both(product(tokens, w_sq) + b_sq)
    k_self = both(product(tokens, w_sk))
    v_self = both(product(tokens, w_sv) + b_sv)
    o_self = both(attend(q_self, k_self, v_self, causal))
    z_one = tokens + low_back(product(o_self, w_so)) + b_so
    h_one = layer_norm(z_one, g_one, b_one)
    q_cross = both(product(low(h_one), w_cq) + b_cq)
    k_cross = both(product(states, w_ck))
    v_cross = both(product(states, w_cv) + b_cv)
    every = jnp.ones((SEQ, ENC), dtype=jnp.bool_)
    o_cross = both(attend(q_cross, k_cross, v_cross, every))
    z_two = h_one + low_back(product(o_cross, w_co)) + b_co
    h_two = layer_norm(z_two, g_two, b_two)
    hidden = low_back(product(low(h_two), w_fi) + b_fi)
    active = low(jax.nn.gelu(hidden, approximate=False))
    z_three = h_two + low_back(product(active, w_fo)) + b_fo
    return layer_norm(z_three, g_three, b_three) * live_rows[:, None].astype(jnp.float32)

def reference(inputs, encoded, cotangent, lengths, seq_slots, block_slots, weights, left_stat, right_stat, left_root, right_root, vectors, vec_stat):
    half_d = D // N_MP
    half_f = FF // N_MP
    shapes = layouts(D, half_d, half_f)
    inverse = jnp.zeros((NB,), jnp.int32).at[block_slots].set(jnp.arange(NB, dtype=jnp.int32))
    natural = jnp.take(weights, inverse, axis=1)
    halves = [split_blocks(natural[half_index], shapes) for half_index in range(N_MP)]
    matrices = [jnp.concatenate([halves[half_index][which] for half_index in range(N_MP)], axis=join_axes[which]) for which in range(10)]
    vec_halves = [split_vector(vectors[half_index], half_d, half_f) for half_index in range(N_MP)]
    vector_parts = [jnp.concatenate([vec_halves[half_index][which] for half_index in range(N_MP)]) for which in range(14)]
    source = jnp.zeros((NSEQ,), jnp.int32).at[seq_slots].set(jnp.arange(NSEQ, dtype=jnp.int32))
    token_rows = inputs.astype(jnp.float32)
    state_rows = encoded.astype(jnp.float32)

    def forward(mat_list, vec_list, token_all, state_all):
        low_mats = [low(matrix) for matrix in mat_list]
        low_vecs = [low(vector) for vector in vec_list]

        def one_sequence(sequence_item):
            return sequence(low_mats, low_vecs, sequence_item[0], sequence_item[1], sequence_item[2])
        return lax.map(jax.checkpoint(one_sequence), (token_all, state_all, lengths))
    layer_out, pull_back = jax.vjp(forward, matrices, vector_parts, token_rows, state_rows)
    mat_grads, vec_grads, token_grad, state_grad = pull_back(jnp.take(cotangent.astype(jnp.float32), seq_slots, axis=0))
    grad_halves = []
    vector_halves = []
    for half_index in range(N_MP):
        pieces = [to_blocks(jnp.split(mat_grads[which], N_MP, axis=join_axes[which])[half_index]) for which in range(10)]
        grad_halves.append(jnp.take(jnp.concatenate(pieces), block_slots, axis=0))
        vector_halves.append(jnp.concatenate([jnp.split(vec_grads[which], N_MP)[half_index] for which in range(14)]))
    block_grad = jnp.stack(grad_halves)
    vector_grad = jnp.stack(vector_halves)
    left_new = 0.5 * left_stat + 0.5 * jnp.einsum('pnij,pnkj->pnik', block_grad, block_grad, precision=highest)
    right_new = 0.5 * right_stat + 0.5 * jnp.einsum('pnji,pnjk->pnik', block_grad, block_grad, precision=highest)
    inner = jnp.einsum('pnij,pnjk->pnik', block_grad, right_root, precision=highest)
    direction = jnp.einsum('pnij,pnjk->pnik', left_root, inner, precision=highest)
    spread = jnp.sqrt(lax.optimization_barrier(jnp.mean(direction * direction, axis=(2, 3), keepdims=True)) + 1e-06)
    weights_new = weights - D ** (-0.5) * direction / spread
    vec_stat_new = 0.5 * vec_stat + 0.5 * vector_grad * vector_grad
    vectors_new = vectors - 0.1 * vector_grad * lax.rsqrt(vec_stat_new)
    outputs = jnp.take(layer_out, source, axis=0).astype(jnp.bfloat16)
    return (outputs, token_grad.astype(jnp.bfloat16), state_grad.astype(jnp.bfloat16), block_grad, left_new, right_new, weights_new, vector_grad, vec_stat_new, vectors_new)
```

```python
import functools

import jax
import jax.numpy as jnp
from jax import lax
from jax.experimental import pallas as pl
from jax.experimental.pallas import tpu as pltpu
from jax.sharding import PartitionSpec as P

D = 1024
FF = 4096
HEAD_DIM = 64
BS = 256
LANES = 128

eps_norm = 1e-05
masked_score = -1e30
scale = HEAD_DIM**-0.5
bf16 = jnp.bfloat16
f32 = jnp.float32

NT = (((1,), (1,)), ((), ()))
TN = (((0,), (0,)), ((), ()))

VMEM_LIMIT = 60 * 1024 * 1024

ERFC_SLOPE = 0.3
ERFC_POLY = (
    0.1691880090604902,
    0.17071516163759975,
    0.14833963774537734,
    0.21492421686136995,
    -0.09464635292673967,
    0.5477136065073498,
    -0.5122723795383668,
    0.4855603950654946,
    -0.1295223139805042,
)


def dot_nn(a, b):
    return jnp.dot(a, b, preferred_element_type=f32)


def dot_nt(a, b):
    return lax.dot_general(a, b, NT, preferred_element_type=f32)


def dot_tn(a, b):
    return lax.dot_general(a, b, TN, preferred_element_type=f32)


def params(**kw):
    return pltpu.CompilerParams(vmem_limit_bytes=VMEM_LIMIT, **kw)


class Net:
    def __init__(self, n_rep, n_shard, n_mp):
        self.n_rep, self.n_shard, self.n_mp = n_rep, n_shard, n_mp
        bits = []
        b = 1
        while b < n_shard:
            bits.append(b)
            b *= 2
        down = tuple(reversed(bits))
        if len(bits) == 3:
            x, z1, z2 = bits
            self.near_order = ((z2, x, z1), (z2, z1, x))
            self.mid_order = ((z1, z2, x), (z2, x, z1))
        else:
            self.near_order = (down, down)
            self.mid_order = (down[1:] + down[:1], down)
        self.depth = len(bits)

    def swap_core(self, value):
        return lax.ppermute(value, "mp", [(i, i ^ 1) for i in range(self.n_mp)])

    def swap_rep(self, value):
        return lax.ppermute(value, "rep", [(i, i ^ 1) for i in range(self.n_rep)])

    def swap_shard(self, value, order, step):
        pairs = []
        for r in range(self.n_rep):
            for s in range(self.n_shard):
                for m in range(self.n_mp):
                    here = (r * self.n_shard + s) * self.n_mp + m
                    there = (r * self.n_shard + (s ^ order[m][step])) * self.n_mp + m
                    pairs.append((here, there))
        return lax.ppermute(value, ("rep", "shard", "mp"), pairs)


def together(*values):
    return lax.optimization_barrier(values)


def start_of(part, plane, counts):
    nblk, na, _ = counts
    return {
        "own": 0,
        "mid": na,
        "near": plane * (nblk - na),
        "far": (1 - plane) * (nblk - na),
    }[part]


def relative(q, which, order):
    rel = 0
    for s in range(len(order[0])):
        bit = jnp.where(which == 0, order[0][s], order[1][s])
        rel = rel + ((q >> s) & 1) * bit
    return rel


def place_body(scal, tab, *refs, pieces, first, counts):
    nblk, na, total = counts
    many = len(pieces)
    srcs = refs[: 2 * many]
    refs = refs[2 * many :]
    if not first:
        refs = refs[3:]
    sq, fi, fo, buf, s_in, s_out = refs
    me, plane, core = scal[0], scal[1], scal[2]

    base = 0
    for k, (order, position, part) in enumerate(pieces):
        n = srcs[2 * k].shape[0]
        for h in range(2):

            def incoming(i, src=srcs[2 * k + h], at=base + h * n):
                pltpu.make_async_copy(src.at[i], buf.at[at + i], s_in.at[at + i]).start()

            pl.loop(0, n)(incoming)
        base += 2 * n

    base = 0
    for k, (order, position, part) in enumerate(pieces):
        n = srcs[2 * k].shape[0]
        per = n // position[1]
        for h in range(2):

            def outgoing(
                i, src=srcs[2 * k + h], at=base + h * n, which=core if h == 0 else 1 - core
            ):
                pltpu.make_async_copy(src.at[i], buf.at[at + i], s_in.at[at + i]).wait()
                shard = me ^ relative(position[0] + i // per, which, order)
                slot = shard * nblk + start_of(part, plane, counts) + i % per
                row_of = (which * total + slot) * 3
                kind = tab[row_of]
                row = pl.multiple_of(tab[row_of + 1], BS)
                col = pl.multiple_of(tab[row_of + 2], BS)
                for c, dst in enumerate((sq, fi, fo)):

                    @pl.when(kind == c)
                    def _():
                        pltpu.make_async_copy(
                            buf.at[at + i],
                            dst.at[pl.ds(row, BS), pl.ds(col, BS)],
                            s_out.at[at + i],
                        ).start()

            pl.loop(0, n)(outgoing)
        base += 2 * n

    def finish(i):
        pltpu.make_async_copy(
            buf.at[i], sq.at[pl.ds(0, BS), pl.ds(0, BS)], s_out.at[i]
        ).wait()

    pl.loop(0, base)(finish)


def place(scal, tab, todo, held, counts):
    first = held is None
    shapes = (
        jax.ShapeDtypeStruct((8 * D, D), bf16),
        jax.ShapeDtypeStruct((D, FF), bf16),
        jax.ShapeDtypeStruct((FF, D), bf16),
    )
    anyspec = pl.BlockSpec(memory_space=pl.ANY)
    smem = pl.BlockSpec(memory_space=pltpu.SMEM)
    values = [v for item in todo for v in item[:2]]
    pieces = [item[2:] for item in todo]
    n = sum(v.shape[0] for v in values)
    ins = [scal, tab] + values + ([] if first else list(held))
    at = 2 + len(values)
    return pl.pallas_call(
        functools.partial(place_body, pieces=pieces, first=first, counts=counts),
        out_shape=shapes,
        in_specs=[smem, smem] + [anyspec] * (len(ins) - 2),
        out_specs=(anyspec,) * 3,
        scratch_shapes=[
            pltpu.VMEM((n, BS, BS), bf16),
            pltpu.SemaphoreType.DMA((n,)),
            pltpu.SemaphoreType.DMA((n,)),
        ],
        input_output_aliases={} if first else {at: 0, at + 1: 1, at + 2: 2},
        compiler_params=pltpu.CompilerParams(vmem_limit_bytes=n * BS * BS * 2 + (2 << 20)),
        cost_estimate=pl.CostEstimate(
            flops=0, bytes_accessed=4 * n * BS * BS, transcendentals=0
        ),
        name="place",
    )(*ins)


def place_table(block_slots, half_d, half_f):
    j = block_slots
    rows_d = D // BS
    cols_h = half_d // BS
    per = rows_d * cols_h
    mid = jnp.minimum(j // per, 7)
    t = j - mid * per
    tall = (mid == 3) | (mid == 7)
    f0 = 8 * per
    cols_f = half_f // BS
    per_f = rows_d * cols_f
    tf = j - f0
    to = tf - per_f
    is_sq, is_fi = j < f0, (j >= f0) & (j < f0 + per_f)
    out = []
    for p in range(D // half_d):
        row_sq = mid * D + jnp.where(tall, p * half_d + (t // rows_d) * BS, (t // cols_h) * BS)
        col_sq = jnp.where(tall, (t % rows_d) * BS, p * half_d + (t % cols_h) * BS)
        row_fi, col_fi = (tf // cols_f) * BS, p * half_f + (tf % cols_f) * BS
        row_fo, col_fo = p * half_f + (to // rows_d) * BS, (to % rows_d) * BS
        kind = jnp.where(is_sq, 0, jnp.where(is_fi, 1, 2))
        row = jnp.where(is_sq, row_sq, jnp.where(is_fi, row_fi, row_fo))
        col = jnp.where(is_sq, col_sq, jnp.where(is_fi, col_fi, col_fo))
        out.append(jnp.stack([kind, row, col], axis=1))
    return jnp.stack(out).astype(jnp.int32).reshape(-1)


def gather_weights(net, scal, tab, low, plane, counts):
    nblk, na, _ = counts
    depth = net.depth
    lag = 1 if na else 0
    cur = {}
    if na:
        cur["near"] = lax.dynamic_slice_in_dim(low, plane * (nblk - na), na, axis=0)
    cur["mid"] = low[na : nblk - na]
    kept = []
    fresh = [(low, net.near_order, (0, 1), "own")]
    waiting = []
    held = None
    last = depth + lag
    for r in range(last):
        todo = []
        moved = []
        if na and r < depth:
            got = net.swap_shard(cur["near"], net.near_order, r)
            moved.append((got, net.near_order, (1 << r, 1 << r), "near"))
        if 0 <= r - lag < depth:
            s = r - lag
            got = net.swap_shard(cur["mid"], net.mid_order, s)
            moved.append((got, net.mid_order, (1 << s, 1 << s), "mid"))
        if na and r == depth - 1:
            across = net.swap_rep(jnp.concatenate(kept) if len(kept) > 1 else kept[0])
            moved.append((across, net.near_order, (1, (1 << (depth - 1)) - 1), "far"))
        if na and r == depth:
            across = net.swap_rep(kept[-1])
            moved.append((across, net.near_order, (1 << (depth - 1), 1 << (depth - 1)), "far"))
        others = [net.swap_core(item[0]) for item in fresh]
        if waiting:
            held = place(scal, tab, waiting, held, counts)
        values = together(*[m[0] for m in moved], *others, *(held or ()))
        moved = [(v,) + m[1:] for v, m in zip(values, moved)]
        others = values[len(moved) : len(moved) + len(fresh)]
        held = values[len(moved) + len(fresh) :] or None
        waiting = [(f[0], o) + f[1:] for f, o in zip(fresh, others)]
        for v, _, position, part in moved:
            if part == "near":
                kept.append(v)
                cur[part] = jnp.concatenate([cur[part], v])
            elif part == "mid":
                cur[part] = jnp.concatenate([cur[part], v])
        fresh = moved
    others = [net.swap_core(item[0]) for item in fresh]
    held = place(scal, tab, waiting, held, counts)
    waiting = [(f[0], o) + f[1:] for f, o in zip(fresh, others)]
    return place(scal, tab, waiting, held, counts)


def deal_body(scal, slots, grads, *refs, pieces, counts):
    nblk, na, _ = counts
    outs = refs[: len(pieces)]
    buf, s_in, s_out = refs[len(pieces) :]
    me, plane, core = scal[0], scal[1], scal[2]
    base = 0
    for out, (order, first, part) in zip(outs, pieces):
        n = out.shape[0]
        per = na if part != "mid" else nblk - 2 * na

        def incoming(i, at=base, order=order, first=first, part=part, per=per):
            shard = me ^ relative(first + i // per, core, order)
            slot = shard * nblk + start_of(part, plane, counts) + i % per
            pltpu.make_async_copy(
                grads.at[slots[slot]], buf.at[at + i], s_in.at[at + i]
            ).start()

        pl.loop(0, n)(incoming)
        base += n
    base = 0
    for out in outs:

        def outgoing(i, at=base, out=out):
            pltpu.make_async_copy(grads.at[0], buf.at[at + i], s_in.at[at + i]).wait()
            pltpu.make_async_copy(buf.at[at + i], out.at[i], s_out.at[at + i]).start()

        pl.loop(0, out.shape[0])(outgoing)
        base += out.shape[0]

    def finish(i):
        pltpu.make_async_copy(buf.at[i], outs[0].at[0], s_out.at[i]).wait()

    pl.loop(0, base)(finish)


def deal(scal, block_slots, grads, pieces, sizes, counts):
    anyspec = pl.BlockSpec(memory_space=pl.ANY)
    smem = pl.BlockSpec(memory_space=pltpu.SMEM)
    n = sum(sizes)
    return pl.pallas_call(
        functools.partial(deal_body, pieces=pieces, counts=counts),
        out_shape=tuple(jax.ShapeDtypeStruct((k, BS, BS), bf16) for k in sizes),
        in_specs=[smem, smem, anyspec],
        out_specs=(anyspec,) * len(sizes),
        scratch_shapes=[
            pltpu.VMEM((n, BS, BS), bf16),
            pltpu.SemaphoreType.DMA((n,)),
            pltpu.SemaphoreType.DMA((n,)),
        ],
        compiler_params=pltpu.CompilerParams(vmem_limit_bytes=n * BS * BS * 2 + (2 << 20)),
        cost_estimate=pl.CostEstimate(
            flops=0, bytes_accessed=4 * n * BS * BS, transcendentals=0
        ),
        name="deal",
    )(scal, block_slots, grads)


def total_of(*terms):
    acc = terms[0].astype(f32)
    for t in terms[1:]:
        acc = acc + t.astype(f32)
    return acc.astype(bf16)


def reduce_gradients(net, scal, grads, plane, block_slots, counts):
    nblk, na, _ = counts
    n = net.n_shard
    depth = net.depth
    cm = nblk - 2 * na
    half = n // 2
    near, mid = net.near_order, net.mid_order
    if na:
        far_send, mid_send = deal(
            scal, block_slots, grads, [(near, half, "far"), (mid, half, "mid")],
            [half * na, half * cm], counts,
        )
        got_far = net.swap_rep(far_send)
        got_mid = net.swap_shard(mid_send, mid, depth - 1)
        far_keep, near_send, near_keep, mid_keep = deal(
            scal, block_slots, grads,
            [(near, 0, "far"), (near, half, "near"), (near, 0, "near"), (mid, 0, "mid")],
            [half * na] * 3 + [half * cm], counts,
        )
        got_far, got_mid, far_keep, near_send, near_keep, mid_keep = together(
            got_far, got_mid, far_keep, near_send, near_keep, mid_keep
        )
        next_near = total_of(near_send, got_far)
        parts_n = [near_keep]
    else:
        mid_send, mid_keep = deal(
            scal, block_slots, grads, [(mid, half, "mid"), (mid, 0, "mid")],
            [half * cm] * 2, counts,
        )
        got_mid = net.swap_shard(mid_send, mid, depth - 1)
    parts_m = [mid_keep, got_mid]
    step_n = depth - 1
    for s in range(depth - 2, -1, -1):
        width = 1 << s
        send_m = total_of(*[p[width * cm :] for p in parts_m])
        keep_m = total_of(*[p[: width * cm] for p in parts_m])
        got = [net.swap_shard(send_m, mid, s)]
        if na:
            got.append(net.swap_shard(next_near, near, step_n))
            if step_n == depth - 1:
                got.append(net.swap_rep(far_keep))
            got = together(*got)
            parts_n = parts_n + list(got[1:])
            low_n = 1 << (step_n - 1)
            next_near = total_of(*[p[low_n * na :] for p in parts_n])
            parts_n = [total_of(*[p[: low_n * na] for p in parts_n])]
            step_n -= 1
        parts_m = [keep_m, got[0]]
    mine = total_of(*parts_m)
    got_m = net.swap_rep(mine)
    if not na:
        return total_of(mine, got_m)
    got_n = net.swap_shard(next_near, near, 0)
    got_m, got_n = together(got_m, got_n)
    summed = total_of(*parts_n, got_n)
    far = net.swap_rep(summed)
    mine = total_of(mine, got_m)
    low_part = jnp.where(plane == 0, summed, far)
    high_part = jnp.where(plane == 0, far, summed)
    return jnp.concatenate([low_part, mine, high_part])


def attend_forward_body(lim, q_ref, k_ref, v_ref, o_ref, lse_ref, *, causal, rows):
    pair = pl.program_id(0)
    seq, keys = q_ref.shape[0], k_ref.shape[0]
    lane = lax.broadcasted_iota(jnp.int32, (1, LANES), 1)
    top = lim[0] - 1

    @pl.when(pair == 0)
    def _():
        lse_ref[...] = jnp.zeros_like(lse_ref)

    for blk in range(seq // rows):
        here = pl.ds(blk * rows, rows)
        width = (blk + 1) * rows if causal else keys
        q = q_ref[here, :] * bf16(scale)
        k = k_ref[pl.ds(0, width), :]
        v = v_ref[pl.ds(0, width), :]
        outs = []
        kept = lse_ref[here, :]
        if causal:
            row = lax.broadcasted_iota(jnp.int32, (rows, 1), 0) + blk * rows
            col = lax.broadcasted_iota(jnp.int32, (1, width), 1)
            allowed = col <= jnp.minimum(row, top)
        for h in range(2):
            mine = (lane // HEAD_DIM) == h
            s = dot_nt(jnp.where(mine, q, bf16(0)), k)
            if causal:
                s = jnp.where(allowed, s, masked_score)
            peak = jnp.max(s, axis=1, keepdims=True)
            e = jnp.exp(s - peak)
            mass = jnp.sum(e, axis=1, keepdims=True)
            outs.append(dot_nn(e.astype(bf16), v) * (1.0 / mass))
            kept = jnp.where(lane == 2 * pair + h, peak + jnp.log(mass), kept)
        o_ref[here, :] = jnp.where(lane < HEAD_DIM, outs[0], outs[1]).astype(bf16)
        lse_ref[here, :] = kept


def attend_forward(limit, q, k, v, causal):
    seq, width = q.shape
    keys = k.shape[0]
    pairs = width // LANES
    rows = min(128 if causal else 256, seq)
    o, lse = pl.pallas_call(
        functools.partial(attend_forward_body, causal=causal, rows=rows),
        grid=(pairs,),
        out_shape=(
            jax.ShapeDtypeStruct((seq, width), bf16),
            jax.ShapeDtypeStruct((seq, LANES), f32),
        ),
        in_specs=[
            pl.BlockSpec(memory_space=pltpu.SMEM),
            pl.BlockSpec((seq, LANES), lambda i: (0, i)),
            pl.BlockSpec((keys, LANES), lambda i: (0, i)),
            pl.BlockSpec((keys, LANES), lambda i: (0, i)),
        ],
        out_specs=(
            pl.BlockSpec((seq, LANES), lambda i: (0, i)),
            pl.BlockSpec((seq, LANES), lambda i: (0, 0)),
        ),
        compiler_params=params(),
        cost_estimate=pl.CostEstimate(
            flops=4 * seq * keys * width, bytes_accessed=8 * seq * width, transcendentals=0
        ),
        name="attend_forward",
    )(limit, q, k, v)
    return o, lse[:, : 2 * pairs].T.reshape(pairs, 2, seq)


def attend_backward_body(
    lim, q_ref, k_ref, v_ref, o_ref, do_ref, lse_ref, dq_ref, dk_ref, dv_ref, dk_acc, dv_acc, *, causal, rows
):
    seq, keys = q_ref.shape[0], k_ref.shape[0]
    lane = lax.broadcasted_iota(jnp.int32, (1, LANES), 1)
    top = lim[0] - 1
    dk_acc[...] = jnp.zeros_like(dk_acc)
    dv_acc[...] = jnp.zeros_like(dv_acc)
    head_row = lax.broadcasted_iota(jnp.int32, (8, LANES), 0)
    head_lane = lax.broadcasted_iota(jnp.int32, (8, LANES), 1) // HEAD_DIM
    pick = (head_row == head_lane).astype(bf16)
    for blk in range(seq // rows):
        here = pl.ds(blk * rows, rows)
        width = (blk + 1) * rows if causal else keys
        span = pl.ds(0, width)
        q = q_ref[here, :] * bf16(scale)
        do = do_ref[here, :]
        k = k_ref[span, :]
        v = v_ref[span, :]
        prod = do.astype(f32) * o_ref[here, :].astype(f32)
        hi = prod.astype(bf16)
        lo = (prod - hi.astype(f32)).astype(bf16)
        delta = dot_nt(pick, hi) + dot_nt(pick, lo)
        lse = lse_ref[0][:, blk * rows : (blk + 1) * rows]
        if causal:
            key = lax.broadcasted_iota(jnp.int32, (width, 1), 0)
            row = lax.broadcasted_iota(jnp.int32, (1, rows), 1) + blk * rows
            allowed = key <= jnp.minimum(row, top)
        dq = jnp.zeros((rows, LANES), f32)
        dk = jnp.zeros((width, LANES), f32)
        dv = jnp.zeros((width, LANES), f32)
        for h in range(2):
            mine = (lane // HEAD_DIM) == h
            qm = jnp.where(mine, q, bf16(0))
            dom = jnp.where(mine, do, bf16(0))
            km = jnp.where(mine, k, bf16(0))
            s = dot_nt(k, qm)
            if causal:
                s = jnp.where(allowed, s, masked_score)
            p = jnp.exp(s - lse[h : h + 1, :])
            dp = dot_nt(v, dom)
            ds = (p * (dp - delta[h : h + 1, :])).astype(bf16)
            dv = dv + dot_nn(p.astype(bf16), dom)
            dk = dk + dot_nn(ds, qm)
            dq = dq + dot_tn(ds, km)
        dq_ref[here, :] = (dq * scale).astype(bf16)
        dk_acc[span, :] += dk
        dv_acc[span, :] += dv
    dk_ref[...] = dk_acc[...].astype(bf16)
    dv_ref[...] = dv_acc[...].astype(bf16)


def attend_backward(limit, q, k, v, o, do, lse, causal):
    seq, width = q.shape
    keys = k.shape[0]
    pairs = width // LANES
    rows = min(128 if causal else 256, seq)
    q_spec = pl.BlockSpec((seq, LANES), lambda i: (0, i))
    k_spec = pl.BlockSpec((keys, LANES), lambda i: (0, i))
    return pl.pallas_call(
        functools.partial(attend_backward_body, causal=causal, rows=rows),
        grid=(pairs,),
        out_shape=(
            jax.ShapeDtypeStruct((seq, width), bf16),
            jax.ShapeDtypeStruct((keys, width), bf16),
            jax.ShapeDtypeStruct((keys, width), bf16),
        ),
        in_specs=[
            pl.BlockSpec(memory_space=pltpu.SMEM),
            q_spec,
            k_spec,
            k_spec,
            q_spec,
            q_spec,
            pl.BlockSpec((1, 2, seq), lambda i: (i, 0, 0)),
        ],
        out_specs=(q_spec, k_spec, k_spec),
        scratch_shapes=[pltpu.VMEM((keys, LANES), f32), pltpu.VMEM((keys, LANES), f32)],
        compiler_params=params(),
        cost_estimate=pl.CostEstimate(
            flops=10 * seq * keys * width, bytes_accessed=16 * seq * width, transcendentals=0
        ),
        name="attend_backward",
    )(limit, q, k, v, o, do, lse)


def gelu_body(h_ref, w_ref, b_ref, act_ref, slope_ref, u_ref, *, chunk):
    u_ref[...] = dot_nn(h_ref[...], w_ref[...]) + b_ref[...]

    def part(i):
        here = pl.ds(pl.multiple_of(i * chunk, chunk), chunk)
        u = u_ref[here, :]
        x = jnp.abs(u) * (0.5**0.5)
        t = 1.0 / (1.0 + ERFC_SLOPE * x)
        poly = jnp.full_like(t, ERFC_POLY[-1])
        for c in ERFC_POLY[-2::-1]:
            poly = poly * t + c
        bell = jnp.exp(-0.5 * (u * u))
        tail = 0.5 * (bell * (t * poly))
        cdf = jnp.where(u < 0, tail, 1.0 - tail)
        act_ref[here, :] = (u * cdf).astype(bf16)
        slope_ref[here, :] = (cdf + u * (bell * 0.3989422804014327)).astype(bf16)

    pl.loop(0, u_ref.shape[0] // chunk)(part)


def gelu_forward(h, w, b):
    seq, width = h.shape
    hidden = w.shape[1]
    tile = 512
    spec = pl.BlockSpec((seq, tile), lambda i: (0, i))
    return pl.pallas_call(
        functools.partial(gelu_body, chunk=32),
        grid=(hidden // tile,),
        out_shape=(jax.ShapeDtypeStruct((seq, hidden), bf16),) * 2,
        in_specs=[
            pl.BlockSpec((seq, width), lambda i: (0, 0)),
            pl.BlockSpec((width, tile), lambda i: (0, i)),
            pl.BlockSpec((1, tile), lambda i: (0, i)),
        ],
        out_specs=(spec, spec),
        scratch_shapes=[pltpu.VMEM((seq, tile), f32)],
        compiler_params=params(),
        cost_estimate=pl.CostEstimate(
            flops=2 * seq * width * hidden + 60 * seq * hidden,
            bytes_accessed=4 * seq * hidden + 2 * width * hidden,
            transcendentals=0,
        ),
        name="gelu_forward",
    )(h, w, b)


def weight_grad_body(scal, x_own, x_sib, y_own, y_sib, *refs):
    out = refs[-1]
    acc = dot_tn(x_own[...], y_own[...]) + dot_tn(x_sib[...], y_sib[...])
    for c in range(out.shape[0]):
        out[c] = acc[:, c * BS : (c + 1) * BS].astype(bf16)


def weight_grad(scal, x_own, x_sib, y_own, y_sib, held, first_block, total, tall, halves):
    seq = x_own.shape[0]
    if tall:
        steps = x_own.shape[1] // halves // BS
        y_width = y_own.shape[1]
        x_spec = pl.BlockSpec((seq, BS), lambda i, s: (0, s[2] * steps + i))
        y_spec = pl.BlockSpec((seq, y_width), lambda i, s: (0, 0))
    else:
        steps = x_own.shape[1] // BS
        y_width = y_own.shape[1] // halves
        x_spec = pl.BlockSpec((seq, BS), lambda i, s: (0, i))
        y_spec = pl.BlockSpec((seq, y_width), lambda i, s: (0, s[2]))
    nb = y_width // BS
    at = first_block // nb
    anyspec = pl.BlockSpec(memory_space=pl.ANY)
    first = held is None
    return pl.pallas_call(
        weight_grad_body,
        grid_spec=pltpu.PrefetchScalarGridSpec(
            num_scalar_prefetch=1,
            grid=(steps,),
            in_specs=[x_spec, x_spec, y_spec, y_spec] + ([] if first else [anyspec]),
            out_specs=pl.BlockSpec((nb, BS, BS), lambda i, s: (at + i, 0, 0)),
        ),
        out_shape=jax.ShapeDtypeStruct((total, BS, BS), bf16),
        input_output_aliases={} if first else {5: 0},
        compiler_params=params(),
        cost_estimate=pl.CostEstimate(
            flops=4 * seq * steps * BS * y_width,
            bytes_accessed=4 * seq * (steps * BS + y_width) + 2 * steps * BS * y_width,
            transcendentals=0,
        ),
        name="weight_grad",
    )(scal, x_own, x_sib, y_own, y_sib, *([] if first else [held]))


def split_low(a):
    hi = a.astype(bf16)
    return hi, (a - hi.astype(f32)).astype(bf16)


def shampoo_body(g_ref, w_ref, ls_ref, rs_ref, lr_ref, rr_ref, og, ol, orr, ow):
    g = g_ref[0]
    og[0, 0] = g.astype(f32)
    ol[0, 0] = 0.5 * ls_ref[0, 0] + 0.5 * dot_nt(g, g)
    orr[0, 0] = 0.5 * rs_ref[0, 0] + 0.5 * dot_tn(g, g)
    r_hi, r_lo = split_low(rr_ref[0, 0])
    i_hi, i_lo = split_low(dot_nn(g, r_hi) + dot_nn(g, r_lo))
    l_hi, l_lo = split_low(lr_ref[0, 0])
    d = dot_nn(l_hi, i_hi) + (dot_nn(l_hi, i_lo) + dot_nn(l_lo, i_hi))
    mean = jnp.mean(jnp.mean(d * d, axis=1, keepdims=True), axis=0, keepdims=True)
    ow[0, 0] = w_ref[0, 0] - (D**-0.5) * d / jnp.sqrt(mean + 1e-06)


def shampoo(owned, weights, left_stat, right_stat, left_root, right_root):
    n = owned.shape[0]
    spec = pl.BlockSpec((1, 1, BS, BS), lambda i: (0, i, 0, 0))
    return pl.pallas_call(
        shampoo_body,
        grid=(n,),
        out_shape=(jax.ShapeDtypeStruct((1, n, BS, BS), f32),) * 4,
        in_specs=[pl.BlockSpec((1, BS, BS), lambda i: (i, 0, 0))] + [spec] * 5,
        out_specs=(spec,) * 4,
        compiler_params=params(),
        cost_estimate=pl.CostEstimate(
            flops=14 * n * BS**3, bytes_accessed=38 * n * BS * BS, transcendentals=0
        ),
        name="shampoo",
    )(owned, weights, left_stat, right_stat, left_root, right_root)


def norm_forward(z, gain, shift):
    center = z - jnp.mean(z, axis=1, keepdims=True)
    inv = lax.rsqrt(jnp.mean(center * center, axis=1, keepdims=True) + eps_norm)
    normed = center * inv
    return normed * gain + shift, normed, inv


def norm_backward(grad, normed, inv, gain):
    scaled = grad * gain
    mean_plain = jnp.mean(scaled, axis=1, keepdims=True)
    mean_cross = jnp.mean(scaled * normed, axis=1, keepdims=True)
    back = inv * (scaled - mean_plain - normed * mean_cross)
    return back, jnp.sum(grad * normed, axis=0), jnp.sum(grad, axis=0)


def route_out(value):
    axes = ("rep", "shard")
    count = lax.axis_size(axes)
    cut = value.reshape(value.shape[0], count, value.shape[1] // count, value.shape[2])
    return lax.all_to_all(cut, axes, split_axis=1, concat_axis=0, tiled=True)


def route_home(pieces, ordering):
    moved = pieces.at[ordering].get(mode="promise_in_bounds")
    back = lax.all_to_all(moved, ("rep", "shard"), split_axis=0, concat_axis=1, tiled=True)
    return back.reshape(back.shape[0], -1, back.shape[3])


def per_device(
    net,
    inputs,
    encoded,
    cotangent,
    lengths,
    seq_slots,
    block_slots,
    weights,
    left_stat,
    right_stat,
    left_root,
    right_root,
    vectors,
    vec_stat,
):
    half_d = inputs.shape[2]
    halves = D // half_d
    half_f = FF // halves
    nblk = weights.shape[1]
    total = block_slots.shape[0]
    counts = (nblk, nblk // 4, total)
    core = lax.axis_index("mp")
    me = lax.axis_index("shard")
    plane = lax.axis_index("rep")
    seq_index = lax.axis_index(("rep", "shard")) * inputs.shape[0] + core
    limit = lax.dynamic_slice_in_dim(lengths, seq_index, 1)
    scal = jnp.stack([me, plane, core]).astype(jnp.int32)
    tab = place_table(block_slots, half_d, half_f)
    is_first = core == 0

    def pick(pair, which):
        return lax.dynamic_index_in_dim(pair, which, axis=0, keepdims=False)

    def joined(low_half, high_half):
        return jnp.concatenate(
            [
                jnp.where(is_first, low_half, high_half),
                jnp.where(is_first, high_half, low_half),
            ],
            axis=1,
        )

    def whole(value):
        other = net.swap_core(value)
        own = joined(pick(value, core), pick(other, core))
        sib = joined(pick(value, 1 - core), pick(other, 1 - core))
        return own, sib

    def halved(full):
        mine = lax.dynamic_slice_in_dim(full, core * half_d, half_d, axis=1)
        away = lax.dynamic_slice_in_dim(full, (1 - core) * half_d, half_d, axis=1)
        got = net.swap_core(away)
        return jnp.stack([jnp.where(is_first, mine, got), jnp.where(is_first, got, mine)])

    x, x_sib = whole(inputs)
    e, e_sib = whole(encoded)

    low = weights[0].astype(bf16)
    sq, w_fi, w_fo = gather_weights(net, scal, tab, low, plane, counts)
    w_sq, w_sk, w_sv, w_so, w_cq, w_ck, w_cv, w_co = [
        lax.slice_in_dim(sq, i * D, (i + 1) * D, axis=0) for i in range(8)
    ]

    vec_low = vectors.astype(bf16)
    vec_mine = lax.all_to_all(
        jnp.broadcast_to(vec_low, (net.n_shard, vec_low.shape[1])),
        "shard",
        split_axis=0,
        concat_axis=0,
        tiled=True,
    ).reshape(1, -1)
    vec_other = net.swap_core(vec_mine)
    vec_both = jnp.concatenate(
        [jnp.where(is_first, vec_mine, vec_other), jnp.where(is_first, vec_other, vec_mine)]
    ).astype(f32)
    vecs = [vec_both[:, i * half_d : (i + 1) * half_d].reshape(1, D) for i in range(13)]
    vecs.append(vec_both[:, 13 * half_d :].reshape(1, FF))
    b_sq, b_sv, b_so, g_one, b_one, b_cq, b_cv, b_co, g_two, b_two, b_fo, g_three, b_three, b_fi = vecs

    q_s = (dot_nn(x, w_sq) + b_sq).astype(bf16)
    k_s = dot_nn(x, w_sk).astype(bf16)
    v_s = (dot_nn(x, w_sv) + b_sv).astype(bf16)
    cot_in, q_s = lax.optimization_barrier((cotangent, q_s))
    o_s, lse_s = attend_forward(limit, q_s, k_s, v_s, True)
    cot_pieces, o_s = together(route_out(cot_in), o_s)
    cot_home = route_home(cot_pieces, seq_slots)
    z_one = x.astype(f32) + dot_nn(o_s, w_so) + b_so
    h_one, n_one, r_one = norm_forward(z_one, g_one, b_one)
    h_one_low = h_one.astype(bf16)
    q_c = (dot_nn(h_one_low, w_cq) + b_cq).astype(bf16)
    k_c = dot_nn(e, w_ck).astype(bf16)
    v_c = (dot_nn(e, w_cv) + b_cv).astype(bf16)
    o_c, lse_c = attend_forward(limit, q_c, k_c, v_c, False)
    z_two = h_one + dot_nn(o_c, w_co) + b_co
    h_two, n_two, r_two = norm_forward(z_two, g_two, b_two)
    h_two_low = h_two.astype(bf16)
    act, slope = gelu_forward(h_two_low, w_fi, b_fi)
    z_three = h_two + dot_nn(act, w_fo) + b_fo
    h_three, n_three, r_three = norm_forward(z_three, g_three, b_three)
    live = (jnp.arange(x.shape[0]) < limit).astype(f32)[:, None]
    source = jnp.sum(
        jnp.where(
            seq_slots[:, None] == jnp.arange(seq_slots.shape[0], dtype=jnp.int32)[None, :],
            jnp.arange(seq_slots.shape[0], dtype=jnp.int32)[:, None],
            0,
        ),
        axis=0,
    )
    finished = halved((h_three * live).astype(bf16))

    cot, _ = whole(cot_home)
    grad_y = cot.astype(f32) * live
    d_three, dg_three, db_three = norm_backward(grad_y, n_three, r_three, g_three)
    a_three = d_three.astype(bf16)
    d_hidden = (dot_nt(a_three, w_fo) * slope.astype(f32)).astype(bf16)
    pieces, d_hidden = together(route_out(finished), d_hidden)
    d_h_two = d_three + dot_nt(d_hidden, w_fi)
    d_two, dg_two, db_two = norm_backward(d_h_two, n_two, r_two, g_two)
    a_two = d_two.astype(bf16)
    d_oc = dot_nt(a_two, w_co).astype(bf16)
    outputs = route_home(pieces, source)
    dq_c, dk_c, dv_c = attend_backward(limit, q_c, k_c, v_c, o_c, d_oc, lse_c, False)
    d_h_one = d_two + dot_nt(dq_c, w_cq)
    d_one, dg_one, db_one = norm_backward(d_h_one, n_one, r_one, g_one)
    a_one = d_one.astype(bf16)
    d_os = dot_nt(a_one, w_so).astype(bf16)
    outputs, d_os = together(outputs, d_os)
    dq_s, dk_s, dv_s = attend_backward(limit, q_s, k_s, v_s, o_s, d_os, lse_s, True)

    per = (D // BS) * (half_d // BS)
    per_f = (D // BS) * (half_f // BS)
    grads = None
    for xo, yo, at, tall, xs in (
        (act, a_three, 8 * per + per_f, True, None),
        (h_two_low, d_hidden, 8 * per, False, None),
        (o_c, a_two, 7 * per, True, None),
        (h_one_low, dq_c, 4 * per, False, None),
        (e, dk_c, 5 * per, False, e_sib),
        (e, dv_c, 6 * per, False, e_sib),
        (o_s, a_one, 3 * per, True, None),
        (x, dq_s, 0, False, x_sib),
        (x, dk_s, per, False, x_sib),
        (x, dv_s, 2 * per, False, x_sib),
    ):
        if xs is None:
            xs = net.swap_core(xo)
        ys = net.swap_core(yo)
        grads = weight_grad(scal, xo, xs, yo, ys, grads, at, total, tall, halves)
    owned = reduce_gradients(net, scal, grads, plane, block_slots, counts)

    back = d_one + dot_nt(dq_s, w_sq) + dot_nt(dk_s, w_sk) + dot_nt(dv_s, w_sv)
    input_grad = halved(back.astype(bf16))
    encoded_grad = halved((dot_nt(dk_c, w_ck) + dot_nt(dv_c, w_cv)).astype(bf16))

    sums = (
        jnp.sum(dq_s.astype(f32), axis=0),
        jnp.sum(dv_s.astype(f32), axis=0),
        jnp.sum(d_one, axis=0),
        dg_one,
        db_one,
        jnp.sum(dq_c.astype(f32), axis=0),
        jnp.sum(dv_c.astype(f32), axis=0),
        jnp.sum(d_two, axis=0),
        dg_two,
        db_two,
        jnp.sum(d_three, axis=0),
        dg_three,
        db_three,
        jnp.sum(d_hidden.astype(f32), axis=0),
    )
    vec_pair = jnp.concatenate([s.reshape(halves, -1) for s in sums], axis=1)
    vec_sum = pick(vec_pair, core) + net.swap_core(pick(vec_pair, 1 - core))
    vec_parts = lax.all_to_all(
        vec_sum.reshape(net.n_shard, -1), "shard", split_axis=0, concat_axis=0, tiled=True
    )
    vec_owned = jnp.sum(vec_parts, axis=0, keepdims=True)
    vec_owned = vec_owned + net.swap_rep(vec_owned)

    block_grad, left_new, right_new, weights_new = shampoo(
        owned, weights, left_stat, right_stat, left_root, right_root
    )
    vec_stat_new = 0.5 * vec_stat + 0.5 * vec_owned * vec_owned
    vectors_new = vectors - 0.1 * vec_owned * lax.rsqrt(vec_stat_new)
    return (
        outputs,
        input_grad,
        encoded_grad,
        block_grad,
        left_new,
        right_new,
        weights_new,
        vec_owned,
        vec_stat_new,
        vectors_new,
    )


def solution(mesh):
    net = Net(mesh.shape["rep"], mesh.shape["shard"], mesh.shape["mp"])
    rows = P(("rep", "shard"), None, "mp")
    blocks = P("mp", "shard", None, None)
    vector = P("mp", "shard")
    in_specs = (rows, rows, rows, P(), P(), P()) + (blocks,) * 5 + (vector, vector)
    out_specs = (rows, rows, rows) + (blocks,) * 4 + (vector,) * 3
    return jax.shard_map(
        functools.partial(per_device, net),
        mesh=mesh,
        in_specs=in_specs,
        out_specs=out_specs,
        check_vma=False,
    )
```

```python
import functools

import jax
import jax.numpy as jnp
import numpy as np
from jax import lax
from jax.experimental import pallas as pl
from jax.experimental.pallas import tpu as pltpu
from jax.sharding import PartitionSpec as P

D = 1024
FF = 4096
HEAD_DIM = 64
BS = 256
LANES = 128

eps_norm = 1e-05
masked_score = -1e30
scale = HEAD_DIM**-0.5
bf16 = jnp.bfloat16
f32 = jnp.float32

NT = (((1,), (1,)), ((), ()))
TN = (((0,), (0,)), ((), ()))

VMEM_LIMIT = 60 * 1024 * 1024

ERFC_SLOPE = 0.3
ERFC_POLY = (
    0.1691880090604902,
    0.17071516163759975,
    0.14833963774537734,
    0.21492421686136995,
    -0.09464635292673967,
    0.5477136065073498,
    -0.5122723795383668,
    0.4855603950654946,
    -0.1295223139805042,
)


def dot_nn(a, b):
    return jnp.dot(a, b, preferred_element_type=f32)


def dot_nt(a, b):
    return lax.dot_general(a, b, NT, preferred_element_type=f32)


def dot_tn(a, b):
    return lax.dot_general(a, b, TN, preferred_element_type=f32)


def params(**kw):
    return pltpu.CompilerParams(vmem_limit_bytes=VMEM_LIMIT, **kw)


GROUPS = (
    (("sq", True), ("sk", True), ("sv", True)),
    (("so", False), ("cq", True), ("ck", True), ("cv", True), ("co", False)),
    (("fi", True),),
    (("fo", False),),
)
SHAPES = {name: (D, D) for name in ("sq", "sk", "sv", "so", "cq", "ck", "cv", "co")}
SHAPES["fi"], SHAPES["fo"] = (D, FF), (FF, D)


class Net:
    def __init__(self, n_rep, n_shard, n_mp):
        self.n_rep, self.n_shard, self.n_mp = n_rep, n_shard, n_mp
        self.n_data = n_rep * n_shard
        power = self.n_data & (self.n_data - 1) == 0
        self.pieces = self.n_data if power and BS % (16 * self.n_data) == 0 else 1
        self.rows = BS // self.pieces
        self.depth = self.pieces.bit_length() - 1
        if self.pieces == 16:
            x, z1, z2, y = 1, 2, 4, 8
            self.orders = (
                ((z2, y, z1, x), (z2, z1, x, y)),
                ((z2, y, z1, x), (z2, x, z1, y)),
                ((z2, z1, x, y), (z2, x, y, z1)),
                ((z2, y, z1, x), (z2, x, y, z1)),
            )
        else:
            down = tuple(1 << s for s in range(self.depth - 1, -1, -1))
            self.orders = ((down,) * n_mp,) * len(GROUPS)

    def swap_core(self, value):
        return lax.ppermute(value, "mp", [(i, i ^ 1) for i in range(self.n_mp)])

    def swap_rep(self, value):
        return lax.ppermute(value, "rep", [(i, i ^ 1) for i in range(self.n_rep)])

    def swap_data(self, value, group, step):
        pairs = []
        for i in range(self.n_data):
            for m in range(self.n_mp):
                there = i ^ self.orders[group][m][step]
                pairs.append((i * self.n_mp + m, there * self.n_mp + m))
        return lax.ppermute(value, ("rep", "shard", "mp"), pairs)

    def table(self, group, core, data_index):
        many = self.pieces
        half = max(many // 2, 1)
        rel = []
        for order in self.orders[group]:
            rel.append([sum(b for s, b in enumerate(order) if q >> s & 1) for q in range(many)])
        rows = []
        for m in range(self.n_mp):
            place = [rel[self.n_mp - 1 - m].index(r) for r in rel[m]]
            low = [p for p in place if p < half][0]
            high = ([p - half for p in place if p >= half] or [0])[0]
            lows, highs = [], []
            for p in place:
                low, high = (p, high) if p < half else (low, p - half)
                lows.append(low)
                highs.append(high)
            rows.append([rel[m], lows, highs, [int(p >= half) for p in place]])
        mine = jnp.asarray(np.array(rows, np.int32))[core]
        mine = mine.at[0].set(mine[0] ^ data_index)
        return jnp.concatenate([mine.reshape(-1), core.reshape(1)]).astype(jnp.int32)


def together(*values):
    return lax.optimization_barrier(values)


class Flow:
    def __init__(self, rounds):
        self.rounds = rounds
        self.flying = next(rounds)

    def advance(self, values):
        try:
            self.flying = self.rounds.send(values)
        except StopIteration as stop:
            self.flying = None
            self.result = stop.value

    def finish(self):
        while self.flying is not None:
            self.advance(self.flying)
        return self.result


def step(main, *flows):
    flows = [f for f in flows if f.flying is not None]
    values = list(together(*main, *[v for f in flows for v in f.flying]))
    main, values = values[: len(main)], values[len(main) :]
    for f in flows:
        many = len(f.flying)
        f.advance(tuple(values[:many]))
        values = values[many:]
    return main


def blocks_of(name, n_mp):
    rows, cols = SHAPES[name]
    return rows * cols // n_mp // (BS * BS)


def group_blocks(group, n_mp):
    return sum(blocks_of(name, n_mp) for name, _ in GROUPS[group])


def place_body(s, *refs, dests, many, half, two):
    q = pl.program_id(0)
    if two:
        own_lo, own_hi, sib_lo, sib_hi = refs[:4]
        outs = refs[4:]
    else:
        own_lo, sib_lo = refs[:2]
        outs = refs[2:]
    core = s[4 * many]
    for b in range(own_lo.shape[1]):
        own, sib = own_lo[0, b], sib_lo[0, b]
        if two:
            own = jnp.where(q < half, own, own_hi[0, b])
            sib = jnp.where(s[3 * many + q] == 0, sib, sib_hi[0, b])
        for h in range(2):
            which, row, col = dests[h][b]
            outs[which][row, :, col : col + BS] = jnp.where(core == h, own, sib)


def place(net, group, table, own, sib):
    many, rows, n_mp = net.pieces, net.rows, net.n_mp
    two = many > 1
    half = max(many // 2, 1)
    dests = ([], [])
    shapes, specs = [], []
    for which, (name, wide) in enumerate(GROUPS[group]):
        height, width = SHAPES[name]
        tall = height if wide else height // n_mp
        flat = width // n_mp if wide else width
        for h in range(n_mp):
            for r in range(tall // BS):
                for c in range(flat // BS):
                    if wide:
                        dests[h].append((which, r, h * flat + c * BS))
                    else:
                        dests[h].append((which, h * (tall // BS) + r, c * BS))
        shapes.append(jax.ShapeDtypeStruct((height // BS, BS, width), bf16))
        specs.append(pl.BlockSpec((height // BS, rows, width), lambda q, s: (0, s[q], 0)))
    nb = own[0].shape[1]
    block = (1, nb, rows, BS)
    lo = pl.BlockSpec(block, lambda q, s: (jnp.minimum(q, half - 1), 0, 0, 0))
    hi = pl.BlockSpec(block, lambda q, s: (jnp.maximum(q - half, 0), 0, 0, 0))
    sib_lo = pl.BlockSpec(block, lambda q, s: (s[many + q], 0, 0, 0))
    sib_hi = pl.BlockSpec(block, lambda q, s: (s[2 * many + q], 0, 0, 0))
    out = pl.pallas_call(
        functools.partial(place_body, dests=dests, many=many, half=half, two=two),
        grid_spec=pltpu.PrefetchScalarGridSpec(
            num_scalar_prefetch=1,
            grid=(many,),
            in_specs=[lo, hi, sib_lo, sib_hi] if two else [lo, sib_lo],
            out_specs=tuple(specs),
        ),
        out_shape=tuple(shapes),
        compiler_params=params(),
        cost_estimate=pl.CostEstimate(
            flops=0, bytes_accessed=8 * many * nb * rows * BS, transcendentals=0
        ),
        name="place",
    )(table, *own, *sib)
    return [o.reshape(-1, o.shape[2]) for o in out]


def gather_rounds(net, group, piece):
    (piece,) = yield (piece,)
    cur = piece[None]
    if net.pieces == 1:
        (sib,) = yield (net.swap_core(cur),)
        return (cur,), (sib,)
    for k in range(net.depth - 1):
        (got,) = yield (net.swap_data(cur, group, k),)
        cur = jnp.concatenate([cur, got])
    got, sib_lo = yield (net.swap_data(cur, group, net.depth - 1), net.swap_core(cur))
    (sib_hi,) = yield (net.swap_core(got),)
    return (cur, got), (sib_lo, sib_hi)


def first_pieces(net, weights, inverse):
    low = weights[0].astype(bf16)
    if net.pieces == 1:
        every = lax.all_gather(low, "shard", axis=0, tiled=True)
    else:
        plane = lax.axis_index("rep")
        nblk = low.shape[0]
        cut = low.reshape(nblk, net.n_rep, net.n_shard, net.rows, BS)
        cut = lax.dynamic_index_in_dim(cut, plane, axis=1, keepdims=False)
        cut = jnp.swapaxes(cut, 0, 1).reshape(-1, net.rows, BS)
        every = lax.all_to_all(cut, "shard", split_axis=0, concat_axis=0, tiled=True)
    return every.at[inverse].get(mode="promise_in_bounds")


def total_of(*terms):
    acc = terms[0].astype(f32)
    for t in terms[1:]:
        acc = acc + t.astype(f32)
    return acc.astype(bf16)


def reduce_rounds(net, group, parts):
    parts = yield parts
    if net.pieces == 1:
        return parts[0][0]
    lo, hi = parts
    (got,) = yield (net.swap_data(hi, group, net.depth - 1),)
    terms = [lo, got]
    for k in range(net.depth - 2, -1, -1):
        width = 1 << k
        send = total_of(*[t[width:] for t in terms])
        keep = total_of(*[t[:width] for t in terms])
        (got,) = yield (net.swap_data(send, group, k),)
        terms = [keep, got]
    return total_of(*terms)[0]


def last_pieces(net, natural, block_slots):
    dealt = natural.at[block_slots].get(mode="promise_in_bounds")
    if net.pieces == 1:
        owned = lax.psum_scatter(dealt, "shard", scatter_dimension=0, tiled=True)
        owned = total_of(owned, net.swap_rep(owned))
        cut = owned.reshape(-1, 2, BS // 32, 16, BS).transpose(1, 2, 0, 3, 4)
        return cut[0], cut[1], jnp.zeros((1,), jnp.int32)
    mine = lax.all_to_all(dealt, "shard", split_axis=0, concat_axis=0, tiled=True)
    mine = mine.reshape(net.n_shard, -1, net.rows, BS)
    return mine, net.swap_rep(mine), lax.axis_index("rep").astype(jnp.int32).reshape(1)


def attend_forward_body(lim, q_ref, k_ref, v_ref, o_ref, lse_ref, *, causal, rows):
    pair = pl.program_id(0)
    seq, keys = q_ref.shape[0], k_ref.shape[0]
    lane = lax.broadcasted_iota(jnp.int32, (1, LANES), 1)
    top = lim[0] - 1

    @pl.when(pair == 0)
    def _():
        lse_ref[...] = jnp.zeros_like(lse_ref)

    for blk in range(seq // rows):
        here = pl.ds(blk * rows, rows)
        width = (blk + 1) * rows if causal else keys
        q = q_ref[here, :] * bf16(scale)
        k = k_ref[pl.ds(0, width), :]
        v = v_ref[pl.ds(0, width), :]
        outs = []
        kept = lse_ref[here, :]
        if causal:
            row = lax.broadcasted_iota(jnp.int32, (rows, 1), 0) + blk * rows
            col = lax.broadcasted_iota(jnp.int32, (1, width), 1)
            allowed = col <= jnp.minimum(row, top)
        for h in range(2):
            mine = (lane // HEAD_DIM) == h
            s = dot_nt(jnp.where(mine, q, bf16(0)), k)
            if causal:
                s = jnp.where(allowed, s, masked_score)
            peak = jnp.max(s, axis=1, keepdims=True)
            e = jnp.exp(s - peak)
            mass = jnp.sum(e, axis=1, keepdims=True)
            outs.append(dot_nn(e.astype(bf16), v) * (1.0 / mass))
            kept = jnp.where(lane == 2 * pair + h, peak + jnp.log(mass), kept)
        o_ref[here, :] = jnp.where(lane < HEAD_DIM, outs[0], outs[1]).astype(bf16)
        lse_ref[here, :] = kept


def attend_forward(limit, q, k, v, causal):
    seq, width = q.shape
    keys = k.shape[0]
    pairs = width // LANES
    rows = min(128 if causal else 256, seq)
    o, lse = pl.pallas_call(
        functools.partial(attend_forward_body, causal=causal, rows=rows),
        grid=(pairs,),
        out_shape=(
            jax.ShapeDtypeStruct((seq, width), bf16),
            jax.ShapeDtypeStruct((seq, LANES), f32),
        ),
        in_specs=[
            pl.BlockSpec(memory_space=pltpu.SMEM),
            pl.BlockSpec((seq, LANES), lambda i: (0, i)),
            pl.BlockSpec((keys, LANES), lambda i: (0, i)),
            pl.BlockSpec((keys, LANES), lambda i: (0, i)),
        ],
        out_specs=(
            pl.BlockSpec((seq, LANES), lambda i: (0, i)),
            pl.BlockSpec((seq, LANES), lambda i: (0, 0)),
        ),
        compiler_params=params(),
        cost_estimate=pl.CostEstimate(
            flops=4 * seq * keys * width, bytes_accessed=8 * seq * width, transcendentals=0
        ),
        name="attend_forward",
    )(limit, q, k, v)
    return o, lse[:, : 2 * pairs].T.reshape(pairs, 2, seq)


def attend_backward_body(
    lim, q_ref, k_ref, v_ref, o_ref, do_ref, lse_ref, dq_ref, dk_ref, dv_ref, dk_acc, dv_acc, *, causal, rows
):
    seq, keys = q_ref.shape[0], k_ref.shape[0]
    lane = lax.broadcasted_iota(jnp.int32, (1, LANES), 1)
    top = lim[0] - 1
    dk_acc[...] = jnp.zeros_like(dk_acc)
    dv_acc[...] = jnp.zeros_like(dv_acc)
    head_row = lax.broadcasted_iota(jnp.int32, (8, LANES), 0)
    head_lane = lax.broadcasted_iota(jnp.int32, (8, LANES), 1) // HEAD_DIM
    pick = (head_row == head_lane).astype(bf16)
    for blk in range(seq // rows):
        here = pl.ds(blk * rows, rows)
        width = (blk + 1) * rows if causal else keys
        span = pl.ds(0, width)
        q = q_ref[here, :] * bf16(scale)
        do = do_ref[here, :]
        k = k_ref[span, :]
        v = v_ref[span, :]
        prod = do.astype(f32) * o_ref[here, :].astype(f32)
        hi = prod.astype(bf16)
        lo = (prod - hi.astype(f32)).astype(bf16)
        delta = dot_nt(pick, hi) + dot_nt(pick, lo)
        lse = lse_ref[0][:, blk * rows : (blk + 1) * rows]
        if causal:
            key = lax.broadcasted_iota(jnp.int32, (width, 1), 0)
            row = lax.broadcasted_iota(jnp.int32, (1, rows), 1) + blk * rows
            allowed = key <= jnp.minimum(row, top)
        dq = jnp.zeros((rows, LANES), f32)
        dk = jnp.zeros((width, LANES), f32)
        dv = jnp.zeros((width, LANES), f32)
        for h in range(2):
            mine = (lane // HEAD_DIM) == h
            qm = jnp.where(mine, q, bf16(0))
            dom = jnp.where(mine, do, bf16(0))
            km = jnp.where(mine, k, bf16(0))
            s = dot_nt(k, qm)
            if causal:
                s = jnp.where(allowed, s, masked_score)
            p = jnp.exp(s - lse[h : h + 1, :])
            dp = dot_nt(v, dom)
            ds = (p * (dp - delta[h : h + 1, :])).astype(bf16)
            dv = dv + dot_nn(p.astype(bf16), dom)
            dk = dk + dot_nn(ds, qm)
            dq = dq + dot_tn(ds, km)
        dq_ref[here, :] = (dq * scale).astype(bf16)
        dk_acc[span, :] += dk
        dv_acc[span, :] += dv
    dk_ref[...] = dk_acc[...].astype(bf16)
    dv_ref[...] = dv_acc[...].astype(bf16)


def attend_backward(limit, q, k, v, o, do, lse, causal):
    seq, width = q.shape
    keys = k.shape[0]
    pairs = width // LANES
    rows = min(128 if causal else 256, seq)
    q_spec = pl.BlockSpec((seq, LANES), lambda i: (0, i))
    k_spec = pl.BlockSpec((keys, LANES), lambda i: (0, i))
    return pl.pallas_call(
        functools.partial(attend_backward_body, causal=causal, rows=rows),
        grid=(pairs,),
        out_shape=(
            jax.ShapeDtypeStruct((seq, width), bf16),
            jax.ShapeDtypeStruct((keys, width), bf16),
            jax.ShapeDtypeStruct((keys, width), bf16),
        ),
        in_specs=[
            pl.BlockSpec(memory_space=pltpu.SMEM),
            q_spec,
            k_spec,
            k_spec,
            q_spec,
            q_spec,
            pl.BlockSpec((1, 2, seq), lambda i: (i, 0, 0)),
        ],
        out_specs=(q_spec, k_spec, k_spec),
        scratch_shapes=[pltpu.VMEM((keys, LANES), f32), pltpu.VMEM((keys, LANES), f32)],
        compiler_params=params(),
        cost_estimate=pl.CostEstimate(
            flops=10 * seq * keys * width, bytes_accessed=16 * seq * width, transcendentals=0
        ),
        name="attend_backward",
    )(limit, q, k, v, o, do, lse)


def gelu_body(h_ref, w_ref, b_ref, act_ref, slope_ref, u_ref, *, chunk):
    u_ref[...] = dot_nn(h_ref[...], w_ref[...]) + b_ref[...]

    def part(i):
        here = pl.ds(pl.multiple_of(i * chunk, chunk), chunk)
        u = u_ref[here, :]
        x = jnp.abs(u) * (0.5**0.5)
        t = 1.0 / (1.0 + ERFC_SLOPE * x)
        poly = jnp.full_like(t, ERFC_POLY[-1])
        for c in ERFC_POLY[-2::-1]:
            poly = poly * t + c
        bell = jnp.exp(-0.5 * (u * u))
        tail = 0.5 * (bell * (t * poly))
        cdf = jnp.where(u < 0, tail, 1.0 - tail)
        act_ref[here, :] = (u * cdf).astype(bf16)
        slope_ref[here, :] = (cdf + u * (bell * 0.3989422804014327)).astype(bf16)

    pl.loop(0, u_ref.shape[0] // chunk)(part)


def gelu_forward(h, w, b):
    seq, width = h.shape
    hidden = w.shape[1]
    tile = 512
    spec = pl.BlockSpec((seq, tile), lambda i: (0, i))
    return pl.pallas_call(
        functools.partial(gelu_body, chunk=32),
        grid=(hidden // tile,),
        out_shape=(jax.ShapeDtypeStruct((seq, hidden), bf16),) * 2,
        in_specs=[
            pl.BlockSpec((seq, width), lambda i: (0, 0)),
            pl.BlockSpec((width, tile), lambda i: (0, i)),
            pl.BlockSpec((1, tile), lambda i: (0, i)),
        ],
        out_specs=(spec, spec),
        scratch_shapes=[pltpu.VMEM((seq, tile), f32)],
        compiler_params=params(),
        cost_estimate=pl.CostEstimate(
            flops=2 * seq * width * hidden + 60 * seq * hidden,
            bytes_accessed=4 * seq * hidden + 2 * width * hidden,
            transcendentals=0,
        ),
        name="gelu_forward",
    )(h, w, b)


def weight_grad_body(s, x_own, x_sib, y_own, y_sib, *refs, outs, many, rows):
    targets, buf = refs[-1 - outs : -1], refs[-1]
    acc = dot_tn(x_own[...], y_own[...]) + dot_tn(x_sib[...], y_sib[...])
    buf[...] = acc.astype(bf16)
    per = many // outs
    for q in range(many):
        here = pl.ds(pl.multiple_of(s[q] * rows, rows), rows)
        for c in range(targets[0].shape[1]):
            targets[q // per][q % per, c] = buf[here, c * BS : (c + 1) * BS]


def weight_grad(net, group, table, x_own, x_sib, y_own, y_sib, held, first_block, wide):
    seq = x_own.shape[0]
    many, rows, halves = net.pieces, net.rows, net.n_mp
    at_core = 4 * many
    if wide:
        steps = x_own.shape[1] // BS
        y_width = y_own.shape[1] // halves
        x_spec = pl.BlockSpec((seq, BS), lambda i, s: (0, i))
        y_spec = pl.BlockSpec((seq, y_width), lambda i, s: (0, s[at_core]))
    else:
        steps = x_own.shape[1] // halves // BS
        y_width = y_own.shape[1]
        x_spec = pl.BlockSpec((seq, BS), lambda i, s: (0, s[at_core] * steps + i))
        y_spec = pl.BlockSpec((seq, y_width), lambda i, s: (0, 0))
    nb = y_width // BS
    at = first_block // nb
    total = group_blocks(group, halves)
    outs = 2 if many > 1 else 1
    anyspec = pl.BlockSpec(memory_space=pl.ANY)
    held = held or ()
    return pl.pallas_call(
        functools.partial(weight_grad_body, outs=outs, many=many, rows=rows),
        grid_spec=pltpu.PrefetchScalarGridSpec(
            num_scalar_prefetch=1,
            grid=(steps,),
            in_specs=[x_spec, x_spec, y_spec, y_spec] + [anyspec] * len(held),
            out_specs=(pl.BlockSpec((many // outs, nb, rows, BS), lambda i, s: (0, at + i, 0, 0)),)
            * outs,
            scratch_shapes=[pltpu.VMEM((BS, y_width), bf16)],
        ),
        out_shape=(jax.ShapeDtypeStruct((many // outs, total, rows, BS), bf16),) * outs,
        input_output_aliases={5 + k: k for k in range(len(held))},
        compiler_params=params(),
        cost_estimate=pl.CostEstimate(
            flops=4 * seq * steps * BS * y_width,
            bytes_accessed=4 * seq * (steps * BS + y_width) + 2 * steps * BS * y_width,
            transcendentals=0,
        ),
        name="weight_grad",
    )(table, x_own, x_sib, y_own, y_sib, *held)


def split_low(a):
    hi = a.astype(bf16)
    return hi, (a - hi.astype(f32)).astype(bf16)


def shampoo_body(flag, mine_ref, other_ref, w_ref, ls_ref, rs_ref, lr_ref, rr_ref, og, ol, orr, ow, g_ref):
    size = mine_ref.shape[0] * mine_ref.shape[2]
    g_ref[pl.ds(pl.multiple_of(flag[0] * size, size), size), :] = mine_ref[:, 0].reshape(size, BS)
    g_ref[pl.ds(pl.multiple_of((1 - flag[0]) * size, size), size), :] = other_ref[:, 0].reshape(size, BS)
    g = g_ref[...]
    og[0, 0] = g.astype(f32)
    ol[0, 0] = 0.5 * ls_ref[0, 0] + 0.5 * dot_nt(g, g)
    orr[0, 0] = 0.5 * rs_ref[0, 0] + 0.5 * dot_tn(g, g)
    r_hi, r_lo = split_low(rr_ref[0, 0])
    i_hi, i_lo = split_low(dot_nn(g, r_hi) + dot_nn(g, r_lo))
    l_hi, l_lo = split_low(lr_ref[0, 0])
    d = dot_nn(l_hi, i_hi) + (dot_nn(l_hi, i_lo) + dot_nn(l_lo, i_hi))
    mean = jnp.mean(jnp.mean(d * d, axis=1, keepdims=True), axis=0, keepdims=True)
    ow[0, 0] = w_ref[0, 0] - (D**-0.5) * d / jnp.sqrt(mean + 1e-06)


def shampoo(flag, mine, other, weights, left_stat, right_stat, left_root, right_root):
    n = mine.shape[1]
    spec = pl.BlockSpec((1, 1, BS, BS), lambda i: (0, i, 0, 0))
    g_spec = pl.BlockSpec((mine.shape[0], 1, mine.shape[2], BS), lambda i: (0, i, 0, 0))
    return pl.pallas_call(
        shampoo_body,
        grid=(n,),
        out_shape=(jax.ShapeDtypeStruct((1, n, BS, BS), f32),) * 4,
        in_specs=[pl.BlockSpec(memory_space=pltpu.SMEM), g_spec, g_spec] + [spec] * 5,
        out_specs=(spec,) * 4,
        scratch_shapes=[pltpu.VMEM((BS, BS), bf16)],
        compiler_params=params(),
        cost_estimate=pl.CostEstimate(
            flops=14 * n * BS**3, bytes_accessed=38 * n * BS * BS, transcendentals=0
        ),
        name="shampoo",
    )(flag, mine, other, weights, left_stat, right_stat, left_root, right_root)


def norm_forward(z, gain, shift):
    center = z - jnp.mean(z, axis=1, keepdims=True)
    inv = lax.rsqrt(jnp.mean(center * center, axis=1, keepdims=True) + eps_norm)
    normed = center * inv
    return normed * gain + shift, normed, inv


def norm_backward(grad, normed, inv, gain):
    scaled = grad * gain
    mean_plain = jnp.mean(scaled, axis=1, keepdims=True)
    mean_cross = jnp.mean(scaled * normed, axis=1, keepdims=True)
    back = inv * (scaled - mean_plain - normed * mean_cross)
    return back, jnp.sum(grad * normed, axis=0), jnp.sum(grad, axis=0)


def inverse_of(order):
    many = jnp.arange(order.shape[0], dtype=jnp.int32)
    return jnp.sum(jnp.where(order[:, None] == many[None, :], many[:, None], 0), axis=0)


def route_out(value):
    axes = ("rep", "shard")
    count = lax.axis_size(axes)
    cut = value.reshape(value.shape[0], count, value.shape[1] // count, value.shape[2])
    return lax.all_to_all(cut, axes, split_axis=1, concat_axis=0, tiled=True)


def route_home(pieces, ordering):
    moved = pieces.at[ordering].get(mode="promise_in_bounds")
    back = lax.all_to_all(moved, ("rep", "shard"), split_axis=0, concat_axis=1, tiled=True)
    return back.reshape(back.shape[0], -1, back.shape[3])


def per_device(
    net,
    inputs,
    encoded,
    cotangent,
    lengths,
    seq_slots,
    block_slots,
    weights,
    left_stat,
    right_stat,
    left_root,
    right_root,
    vectors,
    vec_stat,
):
    half_d = inputs.shape[2]
    halves = D // half_d
    core = lax.axis_index("mp")
    data_index = lax.axis_index(("rep", "shard"))
    seq_index = data_index * inputs.shape[0] + core
    limit = lax.dynamic_slice_in_dim(lengths, seq_index, 1)
    tables = [net.table(k, core, data_index) for k in range(len(GROUPS))]
    is_first = core == 0

    def pick(pair, which):
        return lax.dynamic_index_in_dim(pair, which, axis=0, keepdims=False)

    def joined(low_half, high_half):
        return jnp.concatenate(
            [
                jnp.where(is_first, low_half, high_half),
                jnp.where(is_first, high_half, low_half),
            ],
            axis=1,
        )

    def whole(value):
        other = net.swap_core(value)
        own = joined(pick(value, core), pick(other, core))
        sib = joined(pick(value, 1 - core), pick(other, 1 - core))
        return own, sib

    def halved(full):
        mine = lax.dynamic_slice_in_dim(full, core * half_d, half_d, axis=1)
        away = lax.dynamic_slice_in_dim(full, (1 - core) * half_d, half_d, axis=1)
        got = net.swap_core(away)
        return jnp.stack([jnp.where(is_first, mine, got), jnp.where(is_first, got, mine)])

    x, x_sib = whole(inputs)
    e, e_sib = whole(encoded)

    pieces = first_pieces(net, weights, inverse_of(block_slots))
    flows, base = [], 0
    for k in range(len(GROUPS)):
        size = group_blocks(k, halves)
        flows.append(Flow(gather_rounds(net, k, pieces[base : base + size])))
        base += size
    attn, cross, up, down = flows

    def placed(k):
        return place(net, k, tables[k], *flows[k].finish())

    step((), attn)
    step((), attn, cross)
    step((), attn, cross)
    step((), attn, cross)
    step((), attn, up)
    w_sq, w_sk, w_sv = step(placed(0), cross, up)

    vec_low = vectors.astype(bf16)
    vec_mine = lax.all_to_all(
        jnp.broadcast_to(vec_low, (net.n_shard, vec_low.shape[1])),
        "shard",
        split_axis=0,
        concat_axis=0,
        tiled=True,
    ).reshape(1, -1)
    vec_other = net.swap_core(vec_mine)
    vec_both = jnp.concatenate(
        [jnp.where(is_first, vec_mine, vec_other), jnp.where(is_first, vec_other, vec_mine)]
    ).astype(f32)
    vecs = [vec_both[:, i * half_d : (i + 1) * half_d].reshape(1, D) for i in range(13)]
    vecs.append(vec_both[:, 13 * half_d :].reshape(1, FF))
    b_sq, b_sv, b_so, g_one, b_one, b_cq, b_cv, b_co, g_two, b_two, b_fo, g_three, b_three, b_fi = vecs

    q_s = (dot_nn(x, w_sq) + b_sq).astype(bf16)
    k_s = dot_nn(x, w_sk).astype(bf16)
    v_s = (dot_nn(x, w_sv) + b_sv).astype(bf16)
    cot_in, q_s, k_s, v_s = step((cotangent, q_s, k_s, v_s), up, down)
    cot_pieces = route_out(cot_in)
    o_s, lse_s = attend_forward(limit, q_s, k_s, v_s, True)
    o_s, lse_s = step((o_s, lse_s), cross, up, down)
    w_so, w_cq, w_ck, w_cv, w_co = placed(1)
    z_one = x.astype(f32) + dot_nn(o_s, w_so) + b_so
    h_one, n_one, r_one = norm_forward(z_one, g_one, b_one)
    h_one_low = h_one.astype(bf16)
    q_c = (dot_nn(h_one_low, w_cq) + b_cq).astype(bf16)
    k_c = dot_nn(e, w_ck).astype(bf16)
    v_c = (dot_nn(e, w_cv) + b_cv).astype(bf16)
    cot_pieces, q_c, k_c, v_c = step((cot_pieces, q_c, k_c, v_c), down)
    cot_home = route_home(cot_pieces, seq_slots)
    o_c, lse_c = attend_forward(limit, q_c, k_c, v_c, False)
    z_two = h_one + dot_nn(o_c, w_co) + b_co
    h_two, n_two, r_two = norm_forward(z_two, g_two, b_two)
    h_two, h_two_low = step((h_two, h_two.astype(bf16)), up, down)
    (w_fi,) = placed(2)
    act, slope = gelu_forward(h_two_low, w_fi, b_fi)
    act_sib = net.swap_core(act)
    act, slope = step((act, slope), down)
    (w_fo,) = placed(3)
    z_three = h_two + dot_nn(act, w_fo) + b_fo
    h_three, n_three, r_three = norm_forward(z_three, g_three, b_three)
    live = (jnp.arange(x.shape[0]) < limit).astype(f32)[:, None]
    source = inverse_of(seq_slots)
    finished = halved((h_three * live).astype(bf16))

    def gradient(k, *operands):
        held, base = None, 0
        for (name, wide), ops in zip(GROUPS[k], operands):
            held = weight_grad(net, k, tables[k], *ops, held, base, wide)
            base += blocks_of(name, halves)
        return Flow(reduce_rounds(net, k, held))

    cot, _ = whole(cot_home)
    grad_y = cot.astype(f32) * live
    d_three, dg_three, db_three = norm_backward(grad_y, n_three, r_three, g_three)
    a_three = d_three.astype(bf16)
    d_hidden = (dot_nt(a_three, w_fo) * slope.astype(f32)).astype(bf16)
    d_hidden_sib = net.swap_core(d_hidden)
    down = gradient(3, (act, act_sib, a_three, net.swap_core(a_three)))
    finished, d_hidden, d_hidden_sib = step((finished, d_hidden, d_hidden_sib), down)
    out_pieces = route_out(finished)
    up = gradient(2, (h_two_low, net.swap_core(h_two_low), d_hidden, d_hidden_sib))
    (d_hidden,) = step((d_hidden,), up)
    d_h_two = d_three + dot_nt(d_hidden, w_fi)
    d_two, dg_two, db_two = norm_backward(d_h_two, n_two, r_two, g_two)
    a_two = d_two.astype(bf16)
    d_oc = dot_nt(a_two, w_co).astype(bf16)
    out_pieces, d_oc = step((out_pieces, d_oc), down)
    outputs = route_home(out_pieces, source)
    dq_c, dk_c, dv_c = attend_backward(limit, q_c, k_c, v_c, o_c, d_oc, lse_c, False)
    dq_c_sib, dk_c_sib, dv_c_sib = [net.swap_core(v) for v in (dq_c, dk_c, dv_c)]
    dq_c, dk_c, dv_c = step((dq_c, dk_c, dv_c), up)
    d_h_one = d_two + dot_nt(dq_c, w_cq)
    d_one, dg_one, db_one = norm_backward(d_h_one, n_one, r_one, g_one)
    a_one = d_one.astype(bf16)
    a_one_sib = net.swap_core(a_one)
    d_os = dot_nt(a_one, w_so).astype(bf16)
    a_one, a_one_sib, d_os = step((a_one, a_one_sib, d_os), down)
    cross = gradient(
        1,
        (o_s, net.swap_core(o_s), a_one, a_one_sib),
        (h_one_low, net.swap_core(h_one_low), dq_c, dq_c_sib),
        (e, e_sib, dk_c, dk_c_sib),
        (e, e_sib, dv_c, dv_c_sib),
        (o_c, net.swap_core(o_c), a_two, net.swap_core(a_two)),
    )
    (d_os,) = step((d_os,), cross, up, down)
    dq_s, dk_s, dv_s = attend_backward(limit, q_s, k_s, v_s, o_s, d_os, lse_s, True)
    sibs = [net.swap_core(v) for v in (dq_s, dk_s, dv_s)]
    outputs, dq_s, dk_s, dv_s = step((outputs, dq_s, dk_s, dv_s), up, down)
    state_back = dot_nt(dk_c, w_ck) + dot_nt(dv_c, w_cv)
    attn = gradient(0, *[(x, x_sib, v, w) for v, w in zip((dq_s, dk_s, dv_s), sibs)])
    dq_s, dk_s, dv_s = step((dq_s, dk_s, dv_s), attn, cross, up)
    back = d_one + dot_nt(dq_s, w_sq) + dot_nt(dk_s, w_sk) + dot_nt(dv_s, w_sv)
    (back,) = step((back,), attn, cross)
    input_grad = halved(back.astype(bf16))
    encoded_grad = halved(state_back.astype(bf16))
    step((), attn, cross)
    step((), attn, cross)
    natural = [f.finish() for f in (attn, cross, up, down)]
    mine, other, flag = last_pieces(net, jnp.concatenate(natural), block_slots)

    sums = (
        jnp.sum(dq_s.astype(f32), axis=0),
        jnp.sum(dv_s.astype(f32), axis=0),
        jnp.sum(d_one, axis=0),
        dg_one,
        db_one,
        jnp.sum(dq_c.astype(f32), axis=0),
        jnp.sum(dv_c.astype(f32), axis=0),
        jnp.sum(d_two, axis=0),
        dg_two,
        db_two,
        jnp.sum(d_three, axis=0),
        dg_three,
        db_three,
        jnp.sum(d_hidden.astype(f32), axis=0),
    )
    vec_pair = jnp.concatenate([s.reshape(halves, -1) for s in sums], axis=1)
    vec_sum = pick(vec_pair, core) + net.swap_core(pick(vec_pair, 1 - core))
    vec_parts = lax.all_to_all(
        vec_sum.reshape(net.n_shard, -1), "shard", split_axis=0, concat_axis=0, tiled=True
    )
    vec_owned = jnp.sum(vec_parts, axis=0, keepdims=True)
    vec_owned = vec_owned + net.swap_rep(vec_owned)

    block_grad, left_new, right_new, weights_new = shampoo(
        flag, mine, other, weights, left_stat, right_stat, left_root, right_root
    )
    vec_stat_new = 0.5 * vec_stat + 0.5 * vec_owned * vec_owned
    vectors_new = vectors - 0.1 * vec_owned * lax.rsqrt(vec_stat_new)
    return (
        outputs,
        input_grad,
        encoded_grad,
        block_grad,
        left_new,
        right_new,
        weights_new,
        vec_owned,
        vec_stat_new,
        vectors_new,
    )


def solution(mesh):
    net = Net(mesh.shape["rep"], mesh.shape["shard"], mesh.shape["mp"])
    rows = P(("rep", "shard"), None, "mp")
    blocks = P("mp", "shard", None, None)
    vector = P("mp", "shard")
    in_specs = (rows, rows, rows, P(), P(), P()) + (blocks,) * 5 + (vector, vector)
    out_specs = (rows, rows, rows) + (blocks,) * 4 + (vector,) * 3
    return jax.shard_map(
        functools.partial(per_device, net),
        mesh=mesh,
        in_specs=in_specs,
        out_specs=out_specs,
        check_vma=False,
    )
```

```python
import functools

import jax
import jax.numpy as jnp
import numpy as np
from jax import lax
from jax.experimental import pallas as pl
from jax.experimental.pallas import tpu as pltpu
from jax.sharding import PartitionSpec as P

D = 1024
FF = 4096
HEAD_DIM = 64
BS = 256
LANES = 128

eps_norm = 1e-05
masked_score = -1e30
scale = HEAD_DIM**-0.5
bf16 = jnp.bfloat16
f32 = jnp.float32

NT = (((1,), (1,)), ((), ()))
TN = (((0,), (0,)), ((), ()))

VMEM_LIMIT = 60 * 1024 * 1024

ERFC_SLOPE = 0.3
ERFC_POLY = (
    0.1691880090604902,
    0.17071516163759975,
    0.14833963774537734,
    0.21492421686136995,
    -0.09464635292673967,
    0.5477136065073498,
    -0.5122723795383668,
    0.4855603950654946,
    -0.1295223139805042,
)


def dot_nn(a, b):
    return jnp.dot(a, b, preferred_element_type=f32)


def dot_nt(a, b):
    return lax.dot_general(a, b, NT, preferred_element_type=f32)


def dot_tn(a, b):
    return lax.dot_general(a, b, TN, preferred_element_type=f32)


def small():
    return pl.CostEstimate(flops=1 << 20, bytes_accessed=1 << 20, transcendentals=0)


def params(**kw):
    return pltpu.CompilerParams(vmem_limit_bytes=VMEM_LIMIT, **kw)


GROUPS = (
    (("sq", True), ("sk", True), ("sv", True)),
    (("so", False), ("cq", True), ("ck", True), ("cv", True), ("co", False)),
    (("fi", True),),
    (("fo", False),),
)
SHAPES = {name: (D, D) for name in ("sq", "sk", "sv", "so", "cq", "ck", "cv", "co")}
SHAPES["fi"], SHAPES["fo"] = (D, FF), (FF, D)


def chunk_of(i):
    return (i & 8) | ((i & 2) << 1) | ((i & 1) << 1) | ((i & 4) >> 2)


class Net:
    def __init__(self, n_rep, n_shard, n_mp):
        self.n_rep, self.n_shard, self.n_mp = n_rep, n_shard, n_mp
        self.n_data = n_rep * n_shard
        self.pieces = 16 if (n_rep, n_shard, n_mp) == (2, 8, 2) else 1
        self.rows = BS // self.pieces
        self.depth = self.pieces.bit_length() - 1
        x, z1, z2, y = 1, 2, 4, 8
        self.orders = (
            ((z2, y, z1, x), (z2, z1, x, y)),
            ((z2, z1, y, x), (z2, z1, x, y)),
            ((z2, x, z1, y), (z2, y, z1, x)),
            ((z2, x, y, z1), (z2, y, z1, x)),
        )

    def swap_core(self, value):
        return lax.ppermute(value, "mp", [(i, i ^ 1) for i in range(self.n_mp)])

    def swap_rep(self, value):
        return lax.ppermute(value, "rep", [(i, i ^ 1) for i in range(self.n_rep)])

    def swap_data(self, value, group, step):
        pairs = []
        for i in range(self.n_data):
            for m in range(self.n_mp):
                there = i ^ self.orders[group][m][step]
                pairs.append((i * self.n_mp + m, there * self.n_mp + m))
        return lax.ppermute(value, ("rep", "shard", "mp"), pairs)

    def table(self, group, core, data_index):
        many = self.pieces
        if many == 1:
            return jnp.stack([0, 0, 0, 0, core]).astype(jnp.int32)
        half = many // 4
        rel = []
        for order in self.orders[group]:
            rel.append([sum(b for s, b in enumerate(order) if q >> s & 1) for q in range(many)])
        rows = []
        for m in range(self.n_mp):
            place = [rel[1 - m].index(r) // 2 for r in rel[m][::2]]
            low = [p for p in place if p < half][0]
            high = [p - half for p in place if p >= half][0]
            lows, highs = [], []
            for p in place:
                low, high = (p, high) if p < half else (low, p - half)
                lows.append(low)
                highs.append(high)
            rows.append([chunk_of(r) for r in rel[m]] + lows + highs + [int(p >= half) for p in place])
        mine = jnp.asarray(np.array(rows, np.int32))[core]
        chunks = mine[:many] ^ chunk_of(data_index)
        return jnp.concatenate([chunks, mine[many:], core.reshape(1)]).astype(jnp.int32)


def together(*values):
    return lax.optimization_barrier(values)


class Flow:
    def __init__(self, rounds):
        self.rounds = rounds
        self.flying = next(rounds)

    def advance(self, values):
        try:
            self.flying = self.rounds.send(values)
        except StopIteration as stop:
            self.flying = None
            self.result = stop.value

    def finish(self):
        while self.flying is not None:
            self.advance(self.flying)
        return self.result


def step(main, *flows):
    flows = [f for f in flows if f.flying is not None]
    values = list(together(*main, *[v for f in flows for v in f.flying]))
    main, values = values[: len(main)], values[len(main) :]
    for f in flows:
        many = len(f.flying)
        f.advance(tuple(values[:many]))
        values = values[many:]
    return main


def blocks_of(name, n_mp):
    rows, cols = SHAPES[name]
    return rows * cols // n_mp // (BS * BS)


def group_blocks(group, n_mp):
    return sum(blocks_of(name, n_mp) for name, _ in GROUPS[group])


def place_body(s, *refs, dests, many, two):
    q = pl.program_id(0)
    steps = many // 2 if two else 1
    if two:
        own_lo, own_hi, sib_lo, sib_hi = refs[:4]
        outs = refs[4:]
    else:
        own_lo, sib_lo = refs[:2]
        outs = refs[2:]
    core = s[many + 3 * steps]
    rows = own_lo.shape[2]
    for t in range(own_lo.shape[0]):
        here = pl.ds(0, rows)
        if two:
            here = pl.ds(pl.multiple_of((s[2 * q + t] & 1) * rows, rows), rows)
        for b in range(own_lo.shape[1]):
            own, sib = own_lo[t, b], sib_lo[t, b]
            if two:
                own = jnp.where(q < steps // 2, own, own_hi[t, b])
                sib = jnp.where(s[many + 2 * steps + q] == 0, sib, sib_hi[t, b])
            for h in range(2):
                which, row, col = dests[h][b]
                outs[which][row, here, col : col + BS] = jnp.where(core == h, own, sib)


def place(net, group, table, own, sib):
    many, rows, n_mp = net.pieces, net.rows, net.n_mp
    two = many > 1
    per = 2 if two else 1
    steps = many // per
    half = max(steps // 2, 1)
    dests = ([], [])
    shapes, specs = [], []
    for which, (name, wide) in enumerate(GROUPS[group]):
        height, width = SHAPES[name]
        tall = height if wide else height // n_mp
        flat = width // n_mp if wide else width
        for h in range(n_mp):
            for r in range(tall // BS):
                for c in range(flat // BS):
                    if wide:
                        dests[h].append((which, r, h * flat + c * BS))
                    else:
                        dests[h].append((which, h * (tall // BS) + r, c * BS))
        shapes.append(jax.ShapeDtypeStruct((height // BS, BS, width), bf16))
        specs.append(
            pl.BlockSpec((height // BS, per * rows, width), lambda q, s: (0, s[per * q] // per, 0))
        )
    nb = own[0].shape[1]
    block = (per, nb, rows, BS)
    lo = pl.BlockSpec(block, lambda q, s: (jnp.minimum(q, half - 1), 0, 0, 0))
    hi = pl.BlockSpec(block, lambda q, s: (jnp.maximum(q - half, 0), 0, 0, 0))
    sib_lo = pl.BlockSpec(block, lambda q, s: (s[many + q], 0, 0, 0))
    sib_hi = pl.BlockSpec(block, lambda q, s: (s[many + steps + q], 0, 0, 0))
    out = pl.pallas_call(
        functools.partial(place_body, dests=dests, many=many, two=two),
        grid_spec=pltpu.PrefetchScalarGridSpec(
            num_scalar_prefetch=1,
            grid=(steps,),
            in_specs=[lo, hi, sib_lo, sib_hi] if two else [lo, sib_lo],
            out_specs=tuple(specs),
        ),
        out_shape=tuple(shapes),
        compiler_params=params(),
        cost_estimate=small(),
        name="place",
    )(table, *own, *sib)
    return [o.reshape(-1, o.shape[2]) for o in out]


def gather_rounds(net, group, piece):
    (piece,) = yield (piece,)
    cur = piece[None]
    if net.pieces == 1:
        (sib,) = yield (net.swap_core(cur),)
        return (cur,), (sib,)
    for k in range(net.depth - 1):
        (got,) = yield (net.swap_data(cur, group, k),)
        cur = jnp.concatenate([cur, got])
    got, sib_lo = yield (net.swap_data(cur, group, net.depth - 1), net.swap_core(cur))
    (sib_hi,) = yield (net.swap_core(got),)
    return (cur, got), (sib_lo, sib_hi)


def first_pieces(net, weights, vectors, inverse):
    low = weights[0].astype(bf16)
    vec = vectors.astype(bf16)
    if net.pieces == 1:
        every = lax.all_gather(low, "shard", axis=0, tiled=True)
        vec_every = lax.all_gather(vec, "shard", axis=1, tiled=True)
        return every.at[inverse].get(mode="promise_in_bounds"), vec_every
    nblk = low.shape[0]
    cut = low.reshape(nblk, 2, 2, 2, 2, net.rows, BS)
    cut = lax.dynamic_index_in_dim(cut, lax.axis_index("rep"), axis=1, keepdims=False)
    cut = cut.transpose(3, 1, 2, 0, 4, 5).reshape(net.n_shard, nblk, net.rows, BS)
    room = net.rows * BS
    vec_cut = jnp.pad(vec.reshape(-1), (0, room - vec.shape[1])).reshape(1, 1, net.rows, BS)
    cut = jnp.concatenate([cut, jnp.broadcast_to(vec_cut, (net.n_shard,) + vec_cut.shape[1:])], axis=1)
    every = lax.all_to_all(
        cut.reshape(-1, net.rows, BS), "shard", split_axis=0, concat_axis=0, tiled=True
    )
    pieces = every.at[inverse + inverse // nblk].get(mode="promise_in_bounds")
    vec_every = every.reshape(net.n_shard, nblk + 1, room)[:, nblk, : vec.shape[1]]
    return pieces, vec_every.reshape(1, -1)


def total_of(*terms):
    acc = terms[0].astype(f32)
    for t in terms[1:]:
        acc = acc + t.astype(f32)
    return acc.astype(bf16)


def reduce_rounds(net, group, parts):
    parts = yield parts
    if net.pieces == 1:
        return parts[0][0]
    lo, hi = parts
    (got,) = yield (net.swap_data(hi, group, net.depth - 1),)
    terms = [lo, got]
    for k in range(net.depth - 2, -1, -1):
        width = 1 << k
        send = total_of(*[t[width:] for t in terms])
        keep = total_of(*[t[:width] for t in terms])
        (got,) = yield (net.swap_data(send, group, k),)
        terms = [keep, got]
    return total_of(*terms)[0]


def last_pieces(net, natural, block_slots):
    dealt = natural.at[block_slots].get(mode="promise_in_bounds")
    if net.pieces == 1:
        owned = lax.psum_scatter(dealt, "shard", scatter_dimension=0, tiled=True)
        owned = total_of(owned, net.swap_rep(owned))
        cut = owned.reshape(-1, 2, 8, 16, BS).transpose(1, 2, 0, 3, 4)
        cut = cut[:, np.array([chunk_of(k) for k in range(8)])]
        return cut[0], cut[1], jnp.zeros((1,), jnp.int32)
    mine = lax.all_to_all(dealt, "shard", split_axis=0, concat_axis=0, tiled=True)
    mine = mine.reshape(net.n_shard, -1, net.rows, BS)
    return mine, net.swap_rep(mine), lax.axis_index("rep").astype(jnp.int32).reshape(1)


def attend_forward_body(lim, q_ref, k_ref, v_ref, o_ref, lse_ref, *, causal, rows):
    pair = pl.program_id(0)
    seq, keys = q_ref.shape[0], k_ref.shape[0]
    lane = lax.broadcasted_iota(jnp.int32, (1, LANES), 1)
    top = lim[0] - 1

    @pl.when(pair == 0)
    def _():
        lse_ref[...] = jnp.zeros_like(lse_ref)

    for blk in range(seq // rows):
        here = pl.ds(blk * rows, rows)
        width = (blk + 1) * rows if causal else keys
        q = q_ref[here, :] * bf16(scale)
        k = k_ref[pl.ds(0, width), :]
        v = v_ref[pl.ds(0, width), :]
        outs = []
        kept = lse_ref[here, :]
        if causal:
            row = lax.broadcasted_iota(jnp.int32, (rows, 1), 0) + blk * rows
            col = lax.broadcasted_iota(jnp.int32, (1, width), 1)
            allowed = col <= jnp.minimum(row, top)
        for h in range(2):
            mine = (lane // HEAD_DIM) == h
            s = dot_nt(jnp.where(mine, q, bf16(0)), k)
            if causal:
                s = jnp.where(allowed, s, masked_score)
            peak = jnp.max(s, axis=1, keepdims=True)
            e = jnp.exp(s - peak)
            mass = jnp.sum(e, axis=1, keepdims=True)
            outs.append(dot_nn(e.astype(bf16), v) * (1.0 / mass))
            kept = jnp.where(lane == 2 * pair + h, peak + jnp.log(mass), kept)
        o_ref[here, :] = jnp.where(lane < HEAD_DIM, outs[0], outs[1]).astype(bf16)
        lse_ref[here, :] = kept


def attend_forward(limit, q, k, v, causal):
    seq, width = q.shape
    keys = k.shape[0]
    pairs = width // LANES
    rows = min(128 if causal else 256, seq)
    o, lse = pl.pallas_call(
        functools.partial(attend_forward_body, causal=causal, rows=rows),
        grid=(pairs,),
        out_shape=(
            jax.ShapeDtypeStruct((seq, width), bf16),
            jax.ShapeDtypeStruct((seq, LANES), f32),
        ),
        in_specs=[
            pl.BlockSpec(memory_space=pltpu.SMEM),
            pl.BlockSpec((seq, LANES), lambda i: (0, i)),
            pl.BlockSpec((keys, LANES), lambda i: (0, i)),
            pl.BlockSpec((keys, LANES), lambda i: (0, i)),
        ],
        out_specs=(
            pl.BlockSpec((seq, LANES), lambda i: (0, i)),
            pl.BlockSpec((seq, LANES), lambda i: (0, 0)),
        ),
        compiler_params=params(),
        cost_estimate=small(),
        name="attend_forward",
    )(limit, q, k, v)
    return o, lse[:, : 2 * pairs].T.reshape(pairs, 2, seq)


def attend_backward_body(
    lim, q_ref, k_ref, v_ref, o_ref, do_ref, lse_ref, dq_ref, dk_ref, dv_ref, dk_acc, dv_acc, *, causal, rows
):
    seq, keys = q_ref.shape[0], k_ref.shape[0]
    lane = lax.broadcasted_iota(jnp.int32, (1, LANES), 1)
    top = lim[0] - 1
    dk_acc[...] = jnp.zeros_like(dk_acc)
    dv_acc[...] = jnp.zeros_like(dv_acc)
    head_row = lax.broadcasted_iota(jnp.int32, (8, LANES), 0)
    head_lane = lax.broadcasted_iota(jnp.int32, (8, LANES), 1) // HEAD_DIM
    pick = (head_row == head_lane).astype(bf16)
    for blk in range(seq // rows):
        here = pl.ds(blk * rows, rows)
        width = (blk + 1) * rows if causal else keys
        span = pl.ds(0, width)
        q = q_ref[here, :] * bf16(scale)
        do = do_ref[here, :]
        k = k_ref[span, :]
        v = v_ref[span, :]
        prod = do.astype(f32) * o_ref[here, :].astype(f32)
        hi = prod.astype(bf16)
        lo = (prod - hi.astype(f32)).astype(bf16)
        delta = dot_nt(pick, hi) + dot_nt(pick, lo)
        lse = lse_ref[0][:, blk * rows : (blk + 1) * rows]
        if causal:
            key = lax.broadcasted_iota(jnp.int32, (width, 1), 0)
            row = lax.broadcasted_iota(jnp.int32, (1, rows), 1) + blk * rows
            allowed = key <= jnp.minimum(row, top)
        dq = jnp.zeros((rows, LANES), f32)
        dk = jnp.zeros((width, LANES), f32)
        dv = jnp.zeros((width, LANES), f32)
        for h in range(2):
            mine = (lane // HEAD_DIM) == h
            qm = jnp.where(mine, q, bf16(0))
            dom = jnp.where(mine, do, bf16(0))
            km = jnp.where(mine, k, bf16(0))
            s = dot_nt(k, qm)
            if causal:
                s = jnp.where(allowed, s, masked_score)
            p = jnp.exp(s - lse[h : h + 1, :])
            dp = dot_nt(v, dom)
            ds = (p * (dp - delta[h : h + 1, :])).astype(bf16)
            dv = dv + dot_nn(p.astype(bf16), dom)
            dk = dk + dot_nn(ds, qm)
            dq = dq + dot_tn(ds, km)
        dq_ref[here, :] = (dq * scale).astype(bf16)
        dk_acc[span, :] += dk
        dv_acc[span, :] += dv
    dk_ref[...] = dk_acc[...].astype(bf16)
    dv_ref[...] = dv_acc[...].astype(bf16)


def attend_backward(limit, q, k, v, o, do, lse, causal):
    seq, width = q.shape
    keys = k.shape[0]
    pairs = width // LANES
    rows = min(128 if causal else 256, seq)
    q_spec = pl.BlockSpec((seq, LANES), lambda i: (0, i))
    k_spec = pl.BlockSpec((keys, LANES), lambda i: (0, i))
    return pl.pallas_call(
        functools.partial(attend_backward_body, causal=causal, rows=rows),
        grid=(pairs,),
        out_shape=(
            jax.ShapeDtypeStruct((seq, width), bf16),
            jax.ShapeDtypeStruct((keys, width), bf16),
            jax.ShapeDtypeStruct((keys, width), bf16),
        ),
        in_specs=[
            pl.BlockSpec(memory_space=pltpu.SMEM),
            q_spec,
            k_spec,
            k_spec,
            q_spec,
            q_spec,
            pl.BlockSpec((1, 2, seq), lambda i: (i, 0, 0)),
        ],
        out_specs=(q_spec, k_spec, k_spec),
        scratch_shapes=[pltpu.VMEM((keys, LANES), f32), pltpu.VMEM((keys, LANES), f32)],
        compiler_params=params(),
        cost_estimate=small(),
        name="attend_backward",
    )(limit, q, k, v, o, do, lse)


def gelu_body(h_ref, w_ref, b_ref, act_ref, slope_ref, u_ref, *, chunk):
    u_ref[...] = dot_nn(h_ref[...], w_ref[...]) + b_ref[...]

    def part(i):
        here = pl.ds(pl.multiple_of(i * chunk, chunk), chunk)
        u = u_ref[here, :]
        x = jnp.abs(u) * (0.5**0.5)
        t = 1.0 / (1.0 + ERFC_SLOPE * x)
        poly = jnp.full_like(t, ERFC_POLY[-1])
        for c in ERFC_POLY[-2::-1]:
            poly = poly * t + c
        bell = jnp.exp(-0.5 * (u * u))
        tail = 0.5 * (bell * (t * poly))
        cdf = jnp.where(u < 0, tail, 1.0 - tail)
        act_ref[here, :] = (u * cdf).astype(bf16)
        slope_ref[here, :] = (cdf + u * (bell * 0.3989422804014327)).astype(bf16)

    pl.loop(0, u_ref.shape[0] // chunk)(part)


def gelu_forward(h, w, b):
    seq, width = h.shape
    hidden = w.shape[1]
    tile = 512
    spec = pl.BlockSpec((seq, tile), lambda i: (0, i))
    return pl.pallas_call(
        functools.partial(gelu_body, chunk=32),
        grid=(hidden // tile,),
        out_shape=(jax.ShapeDtypeStruct((seq, hidden), bf16),) * 2,
        in_specs=[
            pl.BlockSpec((seq, width), lambda i: (0, 0)),
            pl.BlockSpec((width, tile), lambda i: (0, i)),
            pl.BlockSpec((1, tile), lambda i: (0, i)),
        ],
        out_specs=(spec, spec),
        scratch_shapes=[pltpu.VMEM((seq, tile), f32)],
        compiler_params=params(),
        cost_estimate=small(),
        name="gelu_forward",
    )(h, w, b)


def weight_grad_body(s, x_own, x_sib, *refs, count, outs, many, rows):
    y_own, y_sib = refs[:count], refs[count : 2 * count]
    targets = refs[-3 - outs : -3]
    t_own, t_sib, buf = refs[-3:]
    t_own[...] = x_own[...].T
    t_sib[...] = x_sib[...].T
    per = many // outs
    for k in range(count):
        acc = dot_nn(t_own[...], y_own[k][...]) + dot_nn(t_sib[...], y_sib[k][...])
        buf[k] = acc.astype(bf16)
    for q in range(many):
        here = pl.ds(pl.multiple_of(s[q] * rows, rows), rows)
        for k in range(count):
            for c in range(targets[0].shape[2]):
                targets[q // per][q % per, k, c] = buf[k, here, c * BS : (c + 1) * BS]


def weight_grad(net, group, table, xs, ys, held, first, wide):
    seq = xs[0].shape[0]
    many, rows, halves = net.pieces, net.rows, net.n_mp
    at_core = table.shape[0] - 1
    count = len(ys)
    width = ys[0][0].shape[1]
    if wide:
        steps = xs[0].shape[1] // BS
        y_width = width // halves
        x_spec = pl.BlockSpec((seq, BS), lambda i, s: (0, i))
        y_spec = pl.BlockSpec((seq, y_width), lambda i, s: (0, s[at_core]))
    else:
        steps = xs[0].shape[1] // halves // BS
        y_width = width
        x_spec = pl.BlockSpec((seq, BS), lambda i, s: (0, s[at_core] * steps + i))
        y_spec = pl.BlockSpec((seq, y_width), lambda i, s: (0, 0))
    nb = y_width // BS
    at = first // count
    outs = 2 if many > 1 else 1
    shape = (many // outs, len(GROUPS[group]), steps * nb, rows, BS)
    anyspec = pl.BlockSpec(memory_space=pl.ANY)
    held = held or ()
    before = 3 + 2 * count
    return pl.pallas_call(
        functools.partial(weight_grad_body, count=count, outs=outs, many=many, rows=rows),
        grid_spec=pltpu.PrefetchScalarGridSpec(
            num_scalar_prefetch=1,
            grid=(steps,),
            in_specs=[x_spec] * 2 + [y_spec] * (2 * count) + [anyspec] * len(held),
            out_specs=(
                pl.BlockSpec((many // outs, count, nb, rows, BS), lambda i, s: (0, at, i, 0, 0)),
            )
            * outs,
            scratch_shapes=[
                pltpu.VMEM((BS, seq), bf16),
                pltpu.VMEM((BS, seq), bf16),
                pltpu.VMEM((count, BS, y_width), bf16),
            ],
        ),
        out_shape=(jax.ShapeDtypeStruct(shape, bf16),) * outs,
        input_output_aliases={before + k: k for k in range(len(held))},
        compiler_params=params(),
        cost_estimate=small(),
        name="weight_grad",
    )(table, *xs, *[y[0] for y in ys], *[y[1] for y in ys], *held)


def split_low(a):
    hi = a.astype(bf16)
    return hi, (a - hi.astype(f32)).astype(bf16)


def shampoo_body(flag, mine_ref, other_ref, w_ref, ls_ref, rs_ref, lr_ref, rr_ref, og, ol, orr, ow, g_ref):
    for k in range(mine_ref.shape[0]):
        for plane, src in ((flag[0], mine_ref), (1 - flag[0], other_ref)):
            row = pl.multiple_of(plane * 128 + chunk_of(k) * 16, 16)
            g_ref[pl.ds(row, 16), :] = src[k, 0]
    g = g_ref[...]
    og[0, 0] = g.astype(f32)
    ol[0, 0] = 0.5 * ls_ref[0, 0] + 0.5 * dot_nt(g, g)
    orr[0, 0] = 0.5 * rs_ref[0, 0] + 0.5 * dot_tn(g, g)
    r_hi, r_lo = split_low(rr_ref[0, 0])
    i_hi, i_lo = split_low(dot_nn(g, r_hi) + dot_nn(g, r_lo))
    l_hi, l_lo = split_low(lr_ref[0, 0])
    d = dot_nn(l_hi, i_hi) + (dot_nn(l_hi, i_lo) + dot_nn(l_lo, i_hi))
    mean = jnp.mean(jnp.mean(d * d, axis=1, keepdims=True), axis=0, keepdims=True)
    ow[0, 0] = w_ref[0, 0] - (D**-0.5) * d / jnp.sqrt(mean + 1e-06)


def shampoo(flag, mine, other, weights, left_stat, right_stat, left_root, right_root):
    n = mine.shape[1]
    spec = pl.BlockSpec((1, 1, BS, BS), lambda i: (0, i, 0, 0))
    g_spec = pl.BlockSpec((mine.shape[0], 1, mine.shape[2], BS), lambda i: (0, i, 0, 0))
    return pl.pallas_call(
        shampoo_body,
        grid=(n,),
        out_shape=(jax.ShapeDtypeStruct((1, n, BS, BS), f32),) * 4,
        in_specs=[pl.BlockSpec(memory_space=pltpu.SMEM), g_spec, g_spec] + [spec] * 5,
        out_specs=(spec,) * 4,
        scratch_shapes=[pltpu.VMEM((BS, BS), bf16)],
        compiler_params=params(),
        cost_estimate=small(),
        name="shampoo",
    )(flag, mine, other, weights, left_stat, right_stat, left_root, right_root)


def norm_forward(z, gain, shift):
    center = z - jnp.mean(z, axis=1, keepdims=True)
    inv = lax.rsqrt(jnp.mean(center * center, axis=1, keepdims=True) + eps_norm)
    normed = center * inv
    return normed * gain + shift, normed, inv


def norm_backward(grad, normed, inv, gain):
    scaled = grad * gain
    mean_plain = jnp.mean(scaled, axis=1, keepdims=True)
    mean_cross = jnp.mean(scaled * normed, axis=1, keepdims=True)
    back = inv * (scaled - mean_plain - normed * mean_cross)
    return back, jnp.sum(grad * normed, axis=0), jnp.sum(grad, axis=0)


def inverse_of(order):
    many = jnp.arange(order.shape[0], dtype=jnp.int32)
    return jnp.sum(jnp.where(order[:, None] == many[None, :], many[:, None], 0), axis=0)


def route_out(value):
    axes = ("rep", "shard")
    count = lax.axis_size(axes)
    cut = value.reshape(value.shape[0], count, value.shape[1] // count, value.shape[2])
    return lax.all_to_all(cut, axes, split_axis=1, concat_axis=0, tiled=True)


def route_home(pieces, ordering):
    moved = pieces.at[ordering].get(mode="promise_in_bounds")
    back = lax.all_to_all(moved, ("rep", "shard"), split_axis=0, concat_axis=1, tiled=True)
    return back.reshape(back.shape[0], -1, back.shape[3])


def per_device(
    net,
    inputs,
    encoded,
    cotangent,
    lengths,
    seq_slots,
    block_slots,
    weights,
    left_stat,
    right_stat,
    left_root,
    right_root,
    vectors,
    vec_stat,
):
    half_d = inputs.shape[2]
    halves = D // half_d
    core = lax.axis_index("mp")
    data_index = lax.axis_index(("rep", "shard"))
    seq_index = data_index * inputs.shape[0] + core
    limit = lax.dynamic_slice_in_dim(lengths, seq_index, 1)
    tables = [net.table(k, core, data_index) for k in range(len(GROUPS))]
    is_first = core == 0

    def pick(pair, which):
        return lax.dynamic_index_in_dim(pair, which, axis=0, keepdims=False)

    def joined(low_half, high_half):
        return jnp.concatenate(
            [
                jnp.where(is_first, low_half, high_half),
                jnp.where(is_first, high_half, low_half),
            ],
            axis=1,
        )

    def whole(value):
        other = net.swap_core(value)
        own = joined(pick(value, core), pick(other, core))
        sib = joined(pick(value, 1 - core), pick(other, 1 - core))
        return own, sib

    def halved(full):
        mine = lax.dynamic_slice_in_dim(full, core * half_d, half_d, axis=1)
        away = lax.dynamic_slice_in_dim(full, (1 - core) * half_d, half_d, axis=1)
        got = net.swap_core(away)
        return jnp.stack([jnp.where(is_first, mine, got), jnp.where(is_first, got, mine)])

    x, x_sib = whole(inputs)
    e, e_sib = whole(encoded)

    pieces, vec_mine = first_pieces(net, weights, vectors, inverse_of(block_slots))
    flows, base = [], 0
    for k in range(len(GROUPS)):
        size = group_blocks(k, halves)
        flows.append(Flow(gather_rounds(net, k, pieces[base : base + size])))
        base += size
    attn, cross, up, down = flows

    def placed(k):
        return place(net, k, tables[k], *flows[k].finish())

    step((), attn)
    step((), attn, cross)
    step((), attn)
    step((), attn, cross)
    vec_mine, x, x_sib, e, e_sib = step((vec_mine, x, x_sib, e, e_sib), attn, cross, up)
    w_sq, w_sk, w_sv = step(placed(0), up)

    vec_other = net.swap_core(vec_mine)
    vec_both = jnp.concatenate(
        [jnp.where(is_first, vec_mine, vec_other), jnp.where(is_first, vec_other, vec_mine)]
    ).astype(f32)
    vecs = [vec_both[:, i * half_d : (i + 1) * half_d].reshape(1, D) for i in range(13)]
    vecs.append(vec_both[:, 13 * half_d :].reshape(1, FF))
    b_sq, b_sv, b_so, g_one, b_one, b_cq, b_cv, b_co, g_two, b_two, b_fo, g_three, b_three, b_fi = vecs

    q_s = (dot_nn(x, w_sq) + b_sq).astype(bf16)
    k_s = dot_nn(x, w_sk).astype(bf16)
    v_s = (dot_nn(x, w_sv) + b_sv).astype(bf16)
    q_s, k_s, v_s = step((q_s, k_s, v_s), cross, up, down)
    o_s, lse_s = attend_forward(limit, q_s, k_s, v_s, True)
    cotangent, o_s, lse_s = step((cotangent, o_s, lse_s), cross, up, down)
    cot_pieces = route_out(cotangent)
    w_so, w_cq, w_ck, w_cv, w_co = placed(1)
    z_one = x.astype(f32) + dot_nn(o_s, w_so) + b_so
    h_one, n_one, r_one = norm_forward(z_one, g_one, b_one)
    h_one_low = h_one.astype(bf16)
    q_c = (dot_nn(h_one_low, w_cq) + b_cq).astype(bf16)
    k_c = dot_nn(e, w_ck).astype(bf16)
    v_c = (dot_nn(e, w_cv) + b_cv).astype(bf16)
    q_c, k_c, v_c = step((q_c, k_c, v_c), down)
    o_c, lse_c = attend_forward(limit, q_c, k_c, v_c, False)
    z_two = h_one + dot_nn(o_c, w_co) + b_co
    h_two, n_two, r_two = norm_forward(z_two, g_two, b_two)
    cot_pieces, h_two, h_two_low = step((cot_pieces, h_two, h_two.astype(bf16)), up, down)
    cot_home = route_home(cot_pieces, seq_slots)
    (w_fi,) = placed(2)
    act, slope = gelu_forward(h_two_low, w_fi, b_fi)
    act_sib = net.swap_core(act)
    act, slope = step((act, slope), down)
    (w_fo,) = placed(3)
    z_three = h_two + dot_nn(act, w_fo) + b_fo
    h_three, n_three, r_three = norm_forward(z_three, g_three, b_three)
    live = (jnp.arange(x.shape[0]) < limit).astype(f32)[:, None]
    source = inverse_of(seq_slots)
    finished = halved((h_three * live).astype(bf16))

    def gradient(k, *calls):
        held, first = None, 0
        for xs, *ys in calls:
            held = weight_grad(net, k, tables[k], xs, ys, held, first, GROUPS[k][first][1])
            first += len(ys)
        parts = tuple(h.reshape(h.shape[0], -1, net.rows, BS) for h in held)
        return Flow(reduce_rounds(net, k, parts))

    cot, _ = whole(cot_home)
    grad_y = cot.astype(f32) * live
    d_three, dg_three, db_three = norm_backward(grad_y, n_three, r_three, g_three)
    a_three = d_three.astype(bf16)
    d_hidden = (dot_nt(a_three, w_fo) * slope.astype(f32)).astype(bf16)
    d_hidden_sib = net.swap_core(d_hidden)
    down = gradient(3, ((act, act_sib), (a_three, net.swap_core(a_three))))
    finished, d_hidden, d_hidden_sib = step((finished, d_hidden, d_hidden_sib), down)
    out_pieces = route_out(finished)
    up = gradient(2, ((h_two_low, net.swap_core(h_two_low)), (d_hidden, d_hidden_sib)))
    (d_hidden,) = step((d_hidden,), up)
    d_h_two = d_three + dot_nt(d_hidden, w_fi)
    d_two, dg_two, db_two = norm_backward(d_h_two, n_two, r_two, g_two)
    a_two = d_two.astype(bf16)
    d_oc = dot_nt(a_two, w_co).astype(bf16)
    out_pieces, d_oc = step((out_pieces, d_oc), down)
    outputs = route_home(out_pieces, source)
    dq_c, dk_c, dv_c = attend_backward(limit, q_c, k_c, v_c, o_c, d_oc, lse_c, False)
    dq_c_sib, dk_c_sib, dv_c_sib = [net.swap_core(v) for v in (dq_c, dk_c, dv_c)]
    dq_c, dk_c, dv_c = step((dq_c, dk_c, dv_c), up)
    d_h_one = d_two + dot_nt(dq_c, w_cq)
    d_one, dg_one, db_one = norm_backward(d_h_one, n_one, r_one, g_one)
    a_one = d_one.astype(bf16)
    a_one_sib = net.swap_core(a_one)
    d_os = dot_nt(a_one, w_so).astype(bf16)
    a_one, a_one_sib, d_os = step((a_one, a_one_sib, d_os), down)
    cross = gradient(
        1,
        ((o_s, net.swap_core(o_s)), (a_one, a_one_sib)),
        ((h_one_low, net.swap_core(h_one_low)), (dq_c, dq_c_sib)),
        ((e, e_sib), (dk_c, dk_c_sib), (dv_c, dv_c_sib)),
        ((o_c, net.swap_core(o_c)), (a_two, net.swap_core(a_two))),
    )
    (d_os,) = step((d_os,), cross, up, down)
    dq_s, dk_s, dv_s = attend_backward(limit, q_s, k_s, v_s, o_s, d_os, lse_s, True)
    sibs = [net.swap_core(v) for v in (dq_s, dk_s, dv_s)]
    outputs, dq_s, dk_s, dv_s = step((outputs, dq_s, dk_s, dv_s), cross, up, down)
    state_back = dot_nt(dk_c, w_ck) + dot_nt(dv_c, w_cv)
    attn = gradient(0, ((x, x_sib), *zip((dq_s, dk_s, dv_s), sibs)))
    dq_s, dk_s, dv_s = step((dq_s, dk_s, dv_s), attn, cross, up)
    back = d_one + dot_nt(dq_s, w_sq) + dot_nt(dk_s, w_sk) + dot_nt(dv_s, w_sv)
    (back,) = step((back,), attn)
    step((), cross)
    input_grad = halved(back.astype(bf16))
    encoded_grad = halved(state_back.astype(bf16))
    step((), attn)
    step((), attn, cross)
    natural = [f.finish() for f in (attn, cross, up, down)]
    mine, other, flag = last_pieces(net, jnp.concatenate(natural), block_slots)

    sums = (
        jnp.sum(dq_s.astype(f32), axis=0),
        jnp.sum(dv_s.astype(f32), axis=0),
        jnp.sum(d_one, axis=0),
        dg_one,
        db_one,
        jnp.sum(dq_c.astype(f32), axis=0),
        jnp.sum(dv_c.astype(f32), axis=0),
        jnp.sum(d_two, axis=0),
        dg_two,
        db_two,
        jnp.sum(d_three, axis=0),
        dg_three,
        db_three,
        jnp.sum(d_hidden.astype(f32), axis=0),
    )
    vec_pair = jnp.concatenate([s.reshape(halves, -1) for s in sums], axis=1)
    vec_sum = pick(vec_pair, core) + net.swap_core(pick(vec_pair, 1 - core))
    vec_parts = lax.all_to_all(
        vec_sum.reshape(net.n_shard, -1), "shard", split_axis=0, concat_axis=0, tiled=True
    )
    vec_owned = jnp.sum(vec_parts, axis=0, keepdims=True)
    vec_owned = vec_owned + net.swap_rep(vec_owned)

    block_grad, left_new, right_new, weights_new = shampoo(
        flag, mine, other, weights, left_stat, right_stat, left_root, right_root
    )
    vec_stat_new = 0.5 * vec_stat + 0.5 * vec_owned * vec_owned
    vectors_new = vectors - 0.1 * vec_owned * lax.rsqrt(vec_stat_new)
    return (
        outputs,
        input_grad,
        encoded_grad,
        block_grad,
        left_new,
        right_new,
        weights_new,
        vec_owned,
        vec_stat_new,
        vectors_new,
    )


def solution(mesh):
    net = Net(mesh.shape["rep"], mesh.shape["shard"], mesh.shape["mp"])
    rows = P(("rep", "shard"), None, "mp")
    blocks = P("mp", "shard", None, None)
    vector = P("mp", "shard")
    in_specs = (rows, rows, rows, P(), P(), P()) + (blocks,) * 5 + (vector, vector)
    out_specs = (rows, rows, rows) + (blocks,) * 4 + (vector,) * 3
    return jax.shard_map(
        functools.partial(per_device, net),
        mesh=mesh,
        in_specs=in_specs,
        out_specs=out_specs,
        check_vma=False,
    )
```

```python
import functools

import jax
import jax.numpy as jnp
import numpy as np
from jax import lax
from jax.experimental import pallas as pl
from jax.experimental.pallas import tpu as pltpu
from jax.sharding import PartitionSpec as P

D = 1024
FF = 4096
HEAD_DIM = 64
BS = 256
LANES = 128

eps_norm = 1e-05
masked_score = -1e30
scale = HEAD_DIM**-0.5
bf16 = jnp.bfloat16
f32 = jnp.float32

NT = (((1,), (1,)), ((), ()))
TN = (((0,), (0,)), ((), ()))

VMEM_LIMIT = 60 * 1024 * 1024

ERFC_SLOPE = 0.3
ERFC_POLY = (
    0.1691880090604902,
    0.17071516163759975,
    0.14833963774537734,
    0.21492421686136995,
    -0.09464635292673967,
    0.5477136065073498,
    -0.5122723795383668,
    0.4855603950654946,
    -0.1295223139805042,
)


def dot_nn(a, b):
    return jnp.dot(a, b, preferred_element_type=f32)


def dot_nt(a, b):
    return lax.dot_general(a, b, NT, preferred_element_type=f32)


def dot_tn(a, b):
    return lax.dot_general(a, b, TN, preferred_element_type=f32)


def small():
    return pl.CostEstimate(flops=1 << 20, bytes_accessed=1 << 20, transcendentals=0)


def params(**kw):
    return pltpu.CompilerParams(vmem_limit_bytes=VMEM_LIMIT, **kw)


GROUPS = (
    (("sq", True), ("sk", True), ("sv", True)),
    (("so", False), ("cq", True), ("ck", True), ("cv", True), ("co", False)),
    (("fi", True),),
    (("fo", False),),
)
SHAPES = {name: (D, D) for name in ("sq", "sk", "sv", "so", "cq", "ck", "cv", "co")}
SHAPES["fi"], SHAPES["fo"] = (D, FF), (FF, D)


def chunk_of(i):
    return (i & 8) | ((i & 2) << 1) | ((i & 1) << 1) | ((i & 4) >> 2)


class Net:
    def __init__(self, n_rep, n_shard, n_mp):
        self.n_rep, self.n_shard, self.n_mp = n_rep, n_shard, n_mp
        self.n_data = n_rep * n_shard
        self.pieces = 16 if (n_rep, n_shard, n_mp) == (2, 8, 2) else 1
        self.rows = BS // self.pieces
        self.depth = self.pieces.bit_length() - 1
        x, z1, z2, y = 1, 2, 4, 8
        gathering = (
            ((z2, y, z1, x), (z2, z1, x, y)),
            ((z2, z1, y, x), (z2, z1, x, y)),
            ((z2, x, z1, y), (z2, y, z1, x)),
            ((z2, x, y, z1), (z2, y, z1, x)),
        )
        reducing = (((z2, y, z1, x), (z2, x, z1, y)),) + gathering[1:]
        self.orders = gathering + reducing

    def swap_core(self, value):
        return lax.ppermute(value, "mp", [(i, i ^ 1) for i in range(self.n_mp)])

    def swap_rep(self, value):
        return lax.ppermute(value, "rep", [(i, i ^ 1) for i in range(self.n_rep)])

    def swap_data(self, value, group, step):
        pairs = []
        for i in range(self.n_data):
            for m in range(self.n_mp):
                there = i ^ self.orders[group][m][step]
                pairs.append((i * self.n_mp + m, there * self.n_mp + m))
        return lax.ppermute(value, ("rep", "shard", "mp"), pairs)

    def table(self, group, core, data_index):
        many = self.pieces
        if many == 1:
            return jnp.stack([0, 0, 0, 0, core]).astype(jnp.int32)
        half = many // 4
        rel = []
        for order in self.orders[group]:
            rel.append([sum(b for s, b in enumerate(order) if q >> s & 1) for q in range(many)])
        rows = []
        for m in range(self.n_mp):
            place = [rel[1 - m].index(r) // 2 for r in rel[m][::2]]
            low = [p for p in place if p < half][0]
            high = [p - half for p in place if p >= half][0]
            lows, highs = [], []
            for p in place:
                low, high = (p, high) if p < half else (low, p - half)
                lows.append(low)
                highs.append(high)
            rows.append([chunk_of(r) for r in rel[m]] + lows + highs + [int(p >= half) for p in place])
        mine = jnp.asarray(np.array(rows, np.int32))[core]
        chunks = mine[:many] ^ chunk_of(data_index)
        return jnp.concatenate([chunks, mine[many:], core.reshape(1)]).astype(jnp.int32)


def together(*values):
    return lax.optimization_barrier(values)


class Flow:
    def __init__(self, rounds):
        self.rounds = rounds
        self.flying = next(rounds)

    def advance(self, values):
        try:
            self.flying = self.rounds.send(values)
        except StopIteration as stop:
            self.flying = None
            self.result = stop.value

    def finish(self):
        while self.flying is not None:
            self.advance(self.flying)
        return self.result


def step(main, *flows):
    flows = [f for f in flows if f.flying is not None]
    values = list(together(*main, *[v for f in flows for v in f.flying]))
    main, values = values[: len(main)], values[len(main) :]
    for f in flows:
        many = len(f.flying)
        f.advance(tuple(values[:many]))
        values = values[many:]
    return main


def blocks_of(name, n_mp):
    rows, cols = SHAPES[name]
    return rows * cols // n_mp // (BS * BS)


def group_blocks(group, n_mp):
    return sum(blocks_of(name, n_mp) for name, _ in GROUPS[group])


def place_body(s, *refs, dests, many, two):
    q = pl.program_id(0)
    steps = many // 2 if two else 1
    if two:
        own_lo, own_hi, sib_lo, sib_hi = refs[:4]
        outs = refs[4:]
    else:
        own_lo, sib_lo = refs[:2]
        outs = refs[2:]
    core = s[many + 3 * steps]
    rows = own_lo.shape[2]
    for t in range(own_lo.shape[0]):
        here = pl.ds(0, rows)
        if two:
            here = pl.ds(pl.multiple_of((s[2 * q + t] & 1) * rows, rows), rows)
        for b in range(own_lo.shape[1]):
            own, sib = own_lo[t, b], sib_lo[t, b]
            if two:
                own = jnp.where(q < steps // 2, own, own_hi[t, b])
                sib = jnp.where(s[many + 2 * steps + q] == 0, sib, sib_hi[t, b])
            for h in range(2):
                which, row, col = dests[h][b]
                outs[which][row, here, col : col + BS] = jnp.where(core == h, own, sib)


def place(net, group, table, own, sib):
    many, rows, n_mp = net.pieces, net.rows, net.n_mp
    two = many > 1
    per = 2 if two else 1
    steps = many // per
    half = max(steps // 2, 1)
    dests = ([], [])
    shapes, specs = [], []
    for which, (name, wide) in enumerate(GROUPS[group]):
        height, width = SHAPES[name]
        tall = height if wide else height // n_mp
        flat = width // n_mp if wide else width
        for h in range(n_mp):
            for r in range(tall // BS):
                for c in range(flat // BS):
                    if wide:
                        dests[h].append((which, r, h * flat + c * BS))
                    else:
                        dests[h].append((which, h * (tall // BS) + r, c * BS))
        shapes.append(jax.ShapeDtypeStruct((height // BS, BS, width), bf16))
        specs.append(
            pl.BlockSpec((height // BS, per * rows, width), lambda q, s: (0, s[per * q] // per, 0))
        )
    nb = own[0].shape[1]
    block = (per, nb, rows, BS)
    lo = pl.BlockSpec(block, lambda q, s: (jnp.minimum(q, half - 1), 0, 0, 0))
    hi = pl.BlockSpec(block, lambda q, s: (jnp.maximum(q - half, 0), 0, 0, 0))
    sib_lo = pl.BlockSpec(block, lambda q, s: (s[many + q], 0, 0, 0))
    sib_hi = pl.BlockSpec(block, lambda q, s: (s[many + steps + q], 0, 0, 0))
    out = pl.pallas_call(
        functools.partial(place_body, dests=dests, many=many, two=two),
        grid_spec=pltpu.PrefetchScalarGridSpec(
            num_scalar_prefetch=1,
            grid=(steps,),
            in_specs=[lo, hi, sib_lo, sib_hi] if two else [lo, sib_lo],
            out_specs=tuple(specs),
        ),
        out_shape=tuple(shapes),
        compiler_params=params(),
        cost_estimate=small(),
        name="place",
    )(table, *own, *sib)
    return [o.reshape(-1, o.shape[2]) for o in out]


def gather_rounds(net, group, piece):
    (piece,) = yield (piece,)
    cur = piece[None]
    if net.pieces == 1:
        (sib,) = yield (net.swap_core(cur),)
        return (cur,), (sib,)
    for k in range(net.depth - 1):
        (got,) = yield (net.swap_data(cur, group, k),)
        cur = jnp.concatenate([cur, got])
    got, sib_lo = yield (net.swap_data(cur, group, net.depth - 1), net.swap_core(cur))
    (sib_hi,) = yield (net.swap_core(got),)
    return (cur, got), (sib_lo, sib_hi)


def first_pieces(net, weights, vectors, inverse):
    low = weights[0].astype(bf16)
    vec = vectors.astype(bf16)
    if net.pieces == 1:
        every = lax.all_gather(low, "shard", axis=0, tiled=True)
        vec_every = lax.all_gather(vec, "shard", axis=1, tiled=True)
        return every.at[inverse].get(mode="promise_in_bounds"), vec_every
    nblk = low.shape[0]
    cut = low.reshape(nblk, 2, 2, 2, 2, net.rows, BS)
    cut = lax.dynamic_index_in_dim(cut, lax.axis_index("rep"), axis=1, keepdims=False)
    cut = cut.transpose(3, 1, 2, 0, 4, 5).reshape(net.n_shard, nblk, net.rows, BS)
    room = net.rows * BS
    vec_cut = jnp.pad(vec.reshape(-1), (0, room - vec.shape[1])).reshape(1, 1, net.rows, BS)
    cut = jnp.concatenate([cut, jnp.broadcast_to(vec_cut, (net.n_shard,) + vec_cut.shape[1:])], axis=1)
    every = lax.all_to_all(
        cut.reshape(-1, net.rows, BS), "shard", split_axis=0, concat_axis=0, tiled=True
    )
    pieces = every.at[inverse + inverse // nblk].get(mode="promise_in_bounds")
    vec_every = every.reshape(net.n_shard, nblk + 1, room)[:, nblk, : vec.shape[1]]
    return pieces, vec_every.reshape(1, -1)


def total_of(*terms):
    acc = terms[0].astype(f32)
    for t in terms[1:]:
        acc = acc + t.astype(f32)
    return acc.astype(bf16)


def reduce_rounds(net, group, parts):
    parts = yield parts
    if net.pieces == 1:
        return parts[0][0]
    lo, hi = parts
    (got,) = yield (net.swap_data(hi, group, net.depth - 1),)
    terms = [lo, got]
    for k in range(net.depth - 2, -1, -1):
        width = 1 << k
        send = total_of(*[t[width:] for t in terms])
        keep = total_of(*[t[:width] for t in terms])
        (got,) = yield (net.swap_data(send, group, k),)
        terms = [keep, got]
    return total_of(*terms)[0]


def last_pieces(net, natural, block_slots, vec_sum):
    if net.pieces == 1:
        dealt = natural.at[block_slots].get(mode="promise_in_bounds")
        owned = lax.psum_scatter(dealt, "shard", scatter_dimension=0, tiled=True)
        owned = total_of(owned, net.swap_rep(owned))
        cut = owned.reshape(-1, 2, 8, 16, BS).transpose(1, 2, 0, 3, 4)
        cut = cut[:, np.array([chunk_of(k) for k in range(8)])]
        vec = lax.psum_scatter(vec_sum, "shard", scatter_dimension=0, tiled=True)[None]
        parts = [(cut[0], cut[1], owned.shape[0])]
        return parts, jnp.zeros((1,), jnp.int32), vec + net.swap_rep(vec)
    n = net.n_shard
    slots = block_slots.reshape(n, -1)
    half = slots.shape[1] // 2
    room = net.rows * BS
    vec_cut = vec_sum.reshape(n, -1)
    width = vec_cut.shape[1]
    vec_cut = jnp.pad(vec_cut.astype(bf16), ((0, 0), (0, room - width)))
    vec_cut = vec_cut.reshape(n, 1, net.rows, BS)
    parts = []
    for k in range(2):
        index = slots[:, k * half : (k + 1) * half].reshape(-1)
        cut = natural.at[index].get(mode="promise_in_bounds")
        if k == 1:
            cut = jnp.concatenate([cut.reshape(n, half, net.rows, BS), vec_cut], axis=1)
            cut = cut.reshape(-1, net.rows, BS)
        mine = lax.all_to_all(cut, "shard", split_axis=0, concat_axis=0, tiled=True)
        mine = mine.reshape(n, -1, net.rows, BS)
        parts.append((mine, net.swap_rep(mine), half))
    terms = [v[:, half].reshape(n, room)[:, :width].astype(f32) for v in parts[1][:2]]
    flag = lax.axis_index("rep").astype(jnp.int32).reshape(1)
    return parts, flag, jnp.sum(terms[0] + terms[1], axis=0, keepdims=True)


def attend_forward_body(lim, q_ref, k_ref, v_ref, o_ref, lse_ref, *, causal, rows):
    pair = pl.program_id(0)
    seq, keys = q_ref.shape[0], k_ref.shape[0]
    lane = lax.broadcasted_iota(jnp.int32, (1, LANES), 1)
    top = lim[0] - 1

    @pl.when(pair == 0)
    def _():
        lse_ref[...] = jnp.zeros_like(lse_ref)

    for blk in range(seq // rows):
        here = pl.ds(blk * rows, rows)
        width = (blk + 1) * rows if causal else keys
        q = q_ref[here, :] * bf16(scale)
        k = k_ref[pl.ds(0, width), :]
        v = v_ref[pl.ds(0, width), :]
        outs = []
        kept = lse_ref[here, :]
        if causal:
            row = lax.broadcasted_iota(jnp.int32, (rows, 1), 0) + blk * rows
            col = lax.broadcasted_iota(jnp.int32, (1, width), 1)
            allowed = col <= jnp.minimum(row, top)
        for h in range(2):
            mine = (lane // HEAD_DIM) == h
            s = dot_nt(jnp.where(mine, q, bf16(0)), k)
            if causal:
                s = jnp.where(allowed, s, masked_score)
            peak = jnp.max(s, axis=1, keepdims=True)
            e = jnp.exp(s - peak)
            mass = jnp.sum(e, axis=1, keepdims=True)
            outs.append(dot_nn(e.astype(bf16), v) * (1.0 / mass))
            kept = jnp.where(lane == 2 * pair + h, peak + jnp.log(mass), kept)
        o_ref[here, :] = jnp.where(lane < HEAD_DIM, outs[0], outs[1]).astype(bf16)
        lse_ref[here, :] = kept


def attend_forward(limit, q, k, v, causal):
    seq, width = q.shape
    keys = k.shape[0]
    pairs = width // LANES
    rows = min(128 if causal else 256, seq)
    o, lse = pl.pallas_call(
        functools.partial(attend_forward_body, causal=causal, rows=rows),
        grid=(pairs,),
        out_shape=(
            jax.ShapeDtypeStruct((seq, width), bf16),
            jax.ShapeDtypeStruct((seq, LANES), f32),
        ),
        in_specs=[
            pl.BlockSpec(memory_space=pltpu.SMEM),
            pl.BlockSpec((seq, LANES), lambda i: (0, i)),
            pl.BlockSpec((keys, LANES), lambda i: (0, i)),
            pl.BlockSpec((keys, LANES), lambda i: (0, i)),
        ],
        out_specs=(
            pl.BlockSpec((seq, LANES), lambda i: (0, i)),
            pl.BlockSpec((seq, LANES), lambda i: (0, 0)),
        ),
        compiler_params=params(),
        cost_estimate=small(),
        name="attend_forward",
    )(limit, q, k, v)
    return o, lse[:, : 2 * pairs].T.reshape(pairs, 2, seq)


def attend_backward_body(
    lim, q_ref, k_ref, v_ref, o_ref, do_ref, lse_ref, dq_ref, dk_ref, dv_ref, dk_acc, dv_acc, *, causal, rows
):
    seq, keys = q_ref.shape[0], k_ref.shape[0]
    lane = lax.broadcasted_iota(jnp.int32, (1, LANES), 1)
    top = lim[0] - 1
    dk_acc[...] = jnp.zeros_like(dk_acc)
    dv_acc[...] = jnp.zeros_like(dv_acc)
    head_row = lax.broadcasted_iota(jnp.int32, (8, LANES), 0)
    head_lane = lax.broadcasted_iota(jnp.int32, (8, LANES), 1) // HEAD_DIM
    pick = (head_row == head_lane).astype(bf16)
    for blk in range(seq // rows):
        here = pl.ds(blk * rows, rows)
        width = (blk + 1) * rows if causal else keys
        span = pl.ds(0, width)
        q = q_ref[here, :] * bf16(scale)
        do = do_ref[here, :]
        k = k_ref[span, :]
        v = v_ref[span, :]
        prod = do.astype(f32) * o_ref[here, :].astype(f32)
        hi = prod.astype(bf16)
        lo = (prod - hi.astype(f32)).astype(bf16)
        delta = dot_nt(pick, hi) + dot_nt(pick, lo)
        lse = lse_ref[0][:, blk * rows : (blk + 1) * rows]
        if causal:
            key = lax.broadcasted_iota(jnp.int32, (width, 1), 0)
            row = lax.broadcasted_iota(jnp.int32, (1, rows), 1) + blk * rows
            allowed = key <= jnp.minimum(row, top)
        dq = jnp.zeros((rows, LANES), f32)
        dk = jnp.zeros((width, LANES), f32)
        dv = jnp.zeros((width, LANES), f32)
        for h in range(2):
            mine = (lane // HEAD_DIM) == h
            qm = jnp.where(mine, q, bf16(0))
            dom = jnp.where(mine, do, bf16(0))
            km = jnp.where(mine, k, bf16(0))
            s = dot_nt(k, qm)
            if causal:
                s = jnp.where(allowed, s, masked_score)
            p = jnp.exp(s - lse[h : h + 1, :])
            dp = dot_nt(v, dom)
            ds = (p * (dp - delta[h : h + 1, :])).astype(bf16)
            dv = dv + dot_nn(p.astype(bf16), dom)
            dk = dk + dot_nn(ds, qm)
            dq = dq + dot_tn(ds, km)
        dq_ref[here, :] = (dq * scale).astype(bf16)
        dk_acc[span, :] += dk
        dv_acc[span, :] += dv
    dk_ref[...] = dk_acc[...].astype(bf16)
    dv_ref[...] = dv_acc[...].astype(bf16)


def attend_backward(limit, q, k, v, o, do, lse, causal):
    seq, width = q.shape
    keys = k.shape[0]
    pairs = width // LANES
    rows = min(128 if causal else 256, seq)
    q_spec = pl.BlockSpec((seq, LANES), lambda i: (0, i))
    k_spec = pl.BlockSpec((keys, LANES), lambda i: (0, i))
    return pl.pallas_call(
        functools.partial(attend_backward_body, causal=causal, rows=rows),
        grid=(pairs,),
        out_shape=(
            jax.ShapeDtypeStruct((seq, width), bf16),
            jax.ShapeDtypeStruct((keys, width), bf16),
            jax.ShapeDtypeStruct((keys, width), bf16),
        ),
        in_specs=[
            pl.BlockSpec(memory_space=pltpu.SMEM),
            q_spec,
            k_spec,
            k_spec,
            q_spec,
            q_spec,
            pl.BlockSpec((1, 2, seq), lambda i: (i, 0, 0)),
        ],
        out_specs=(q_spec, k_spec, k_spec),
        scratch_shapes=[pltpu.VMEM((keys, LANES), f32), pltpu.VMEM((keys, LANES), f32)],
        compiler_params=params(),
        cost_estimate=small(),
        name="attend_backward",
    )(limit, q, k, v, o, do, lse)


def gelu_body(h_ref, w_ref, b_ref, act_ref, slope_ref, u_ref, *, chunk):
    u_ref[...] = dot_nn(h_ref[...], w_ref[...]) + b_ref[...]

    def part(i):
        here = pl.ds(pl.multiple_of(i * chunk, chunk), chunk)
        u = u_ref[here, :]
        x = jnp.abs(u) * (0.5**0.5)
        t = 1.0 / (1.0 + ERFC_SLOPE * x)
        poly = jnp.full_like(t, ERFC_POLY[-1])
        for c in ERFC_POLY[-2::-1]:
            poly = poly * t + c
        bell = jnp.exp(-0.5 * (u * u))
        tail = 0.5 * (bell * (t * poly))
        cdf = jnp.where(u < 0, tail, 1.0 - tail)
        act_ref[here, :] = (u * cdf).astype(bf16)
        slope_ref[here, :] = (cdf + u * (bell * 0.3989422804014327)).astype(bf16)

    pl.loop(0, u_ref.shape[0] // chunk)(part)


def gelu_forward(h, w, b):
    seq, width = h.shape
    hidden = w.shape[1]
    tile = 512
    spec = pl.BlockSpec((seq, tile), lambda i: (0, i))
    return pl.pallas_call(
        functools.partial(gelu_body, chunk=32),
        grid=(hidden // tile,),
        out_shape=(jax.ShapeDtypeStruct((seq, hidden), bf16),) * 2,
        in_specs=[
            pl.BlockSpec((seq, width), lambda i: (0, 0)),
            pl.BlockSpec((width, tile), lambda i: (0, i)),
            pl.BlockSpec((1, tile), lambda i: (0, i)),
        ],
        out_specs=(spec, spec),
        scratch_shapes=[pltpu.VMEM((seq, tile), f32)],
        compiler_params=params(),
        cost_estimate=small(),
        name="gelu_forward",
    )(h, w, b)


def weight_grad_body(s, x_own, x_sib, *refs, count, outs, many, rows):
    y_own, y_sib = refs[:count], refs[count : 2 * count]
    targets = refs[-3 - outs : -3]
    t_own, t_sib, buf = refs[-3:]
    t_own[...] = x_own[...].T
    t_sib[...] = x_sib[...].T
    per = many // outs
    for k in range(count):
        acc = dot_nn(t_own[...], y_own[k][...]) + dot_nn(t_sib[...], y_sib[k][...])
        buf[k] = acc.astype(bf16)
    for q in range(many):
        here = pl.ds(pl.multiple_of(s[q] * rows, rows), rows)
        for k in range(count):
            for c in range(targets[0].shape[2]):
                targets[q // per][q % per, k, c] = buf[k, here, c * BS : (c + 1) * BS]


def weight_grad(net, group, table, xs, ys, held, first, wide):
    seq = xs[0].shape[0]
    many, rows, halves = net.pieces, net.rows, net.n_mp
    at_core = table.shape[0] - 1
    count = len(ys)
    width = ys[0][0].shape[1]
    if wide:
        steps = xs[0].shape[1] // BS
        y_width = width // halves
        x_spec = pl.BlockSpec((seq, BS), lambda i, s: (0, i))
        y_spec = pl.BlockSpec((seq, y_width), lambda i, s: (0, s[at_core]))
    else:
        steps = xs[0].shape[1] // halves // BS
        y_width = width
        x_spec = pl.BlockSpec((seq, BS), lambda i, s: (0, s[at_core] * steps + i))
        y_spec = pl.BlockSpec((seq, y_width), lambda i, s: (0, 0))
    nb = y_width // BS
    at = first // count
    outs = 2 if many > 1 else 1
    shape = (many // outs, len(GROUPS[group]), steps * nb, rows, BS)
    anyspec = pl.BlockSpec(memory_space=pl.ANY)
    held = held or ()
    before = 3 + 2 * count
    return pl.pallas_call(
        functools.partial(weight_grad_body, count=count, outs=outs, many=many, rows=rows),
        grid_spec=pltpu.PrefetchScalarGridSpec(
            num_scalar_prefetch=1,
            grid=(steps,),
            in_specs=[x_spec] * 2 + [y_spec] * (2 * count) + [anyspec] * len(held),
            out_specs=(
                pl.BlockSpec((many // outs, count, nb, rows, BS), lambda i, s: (0, at, i, 0, 0)),
            )
            * outs,
            scratch_shapes=[
                pltpu.VMEM((BS, seq), bf16),
                pltpu.VMEM((BS, seq), bf16),
                pltpu.VMEM((count, BS, y_width), bf16),
            ],
        ),
        out_shape=(jax.ShapeDtypeStruct(shape, bf16),) * outs,
        input_output_aliases={before + k: k for k in range(len(held))},
        compiler_params=params(),
        cost_estimate=small(),
        name="weight_grad",
    )(table, *xs, *[y[0] for y in ys], *[y[1] for y in ys], *held)


def split_low(a):
    hi = a.astype(bf16)
    return hi, (a - hi.astype(f32)).astype(bf16)


def shampoo_body(flag, mine_ref, other_ref, w_ref, ls_ref, rs_ref, lr_ref, rr_ref, *refs):
    og, ol, orr, ow, g_ref = refs[-5:]
    for k in range(mine_ref.shape[0]):
        for plane, src in ((flag[0], mine_ref), (1 - flag[0], other_ref)):
            row = pl.multiple_of(plane * 128 + chunk_of(k) * 16, 16)
            g_ref[pl.ds(row, 16), :] = src[k, 0]
    g = g_ref[...]
    og[0, 0] = g.astype(f32)
    ol[0, 0] = 0.5 * ls_ref[0, 0] + 0.5 * dot_nt(g, g)
    orr[0, 0] = 0.5 * rs_ref[0, 0] + 0.5 * dot_tn(g, g)
    r_hi, r_lo = split_low(rr_ref[0, 0])
    i_hi, i_lo = split_low(dot_nn(g, r_hi) + dot_nn(g, r_lo))
    l_hi, l_lo = split_low(lr_ref[0, 0])
    d = dot_nn(l_hi, i_hi) + (dot_nn(l_hi, i_lo) + dot_nn(l_lo, i_hi))
    mean = jnp.mean(jnp.mean(d * d, axis=1, keepdims=True), axis=0, keepdims=True)
    ow[0, 0] = w_ref[0, 0] - (D**-0.5) * d / jnp.sqrt(mean + 1e-06)


def shampoo(flag, parts, *states):
    total = states[0].shape[1]
    out, first = (), 0
    for mine, other, n in parts:
        at = first // n
        spec = pl.BlockSpec((1, 1, BS, BS), lambda i, at=at, n=n: (0, at * n + i, 0, 0))
        g_spec = pl.BlockSpec((mine.shape[0], 1, mine.shape[2], BS), lambda i: (0, i, 0, 0))
        anyspec = pl.BlockSpec(memory_space=pl.ANY)
        out = pl.pallas_call(
            shampoo_body,
            grid=(n,),
            out_shape=(jax.ShapeDtypeStruct((1, total, BS, BS), f32),) * 4,
            in_specs=[pl.BlockSpec(memory_space=pltpu.SMEM), g_spec, g_spec]
            + [spec] * 5
            + [anyspec] * len(out),
            out_specs=(spec,) * 4,
            scratch_shapes=[pltpu.VMEM((BS, BS), bf16)],
            input_output_aliases={8 + k: k for k in range(len(out))},
            compiler_params=params(),
            cost_estimate=small(),
            name="shampoo",
        )(flag, mine, other, *states, *out)
        first += n
    return out


def norm_forward(z, gain, shift):
    center = z - jnp.mean(z, axis=1, keepdims=True)
    inv = lax.rsqrt(jnp.mean(center * center, axis=1, keepdims=True) + eps_norm)
    normed = center * inv
    return normed * gain + shift, normed, inv


def norm_backward(grad, normed, inv, gain):
    scaled = grad * gain
    mean_plain = jnp.mean(scaled, axis=1, keepdims=True)
    mean_cross = jnp.mean(scaled * normed, axis=1, keepdims=True)
    back = inv * (scaled - mean_plain - normed * mean_cross)
    return back, jnp.sum(grad * normed, axis=0), jnp.sum(grad, axis=0)


def inverse_of(order):
    many = jnp.arange(order.shape[0], dtype=jnp.int32)
    return jnp.sum(jnp.where(order[:, None] == many[None, :], many[:, None], 0), axis=0)


def route_out(value):
    axes = ("rep", "shard")
    count = lax.axis_size(axes)
    cut = value.reshape(value.shape[0], count, value.shape[1] // count, value.shape[2])
    return lax.all_to_all(cut, axes, split_axis=1, concat_axis=0, tiled=True)


def route_home(pieces, ordering):
    moved = pieces.at[ordering].get(mode="promise_in_bounds")
    back = lax.all_to_all(moved, ("rep", "shard"), split_axis=0, concat_axis=1, tiled=True)
    return back.reshape(back.shape[0], -1, back.shape[3])


def per_device(
    net,
    inputs,
    encoded,
    cotangent,
    lengths,
    seq_slots,
    block_slots,
    weights,
    left_stat,
    right_stat,
    left_root,
    right_root,
    vectors,
    vec_stat,
):
    half_d = inputs.shape[2]
    halves = D // half_d
    core = lax.axis_index("mp")
    data_index = lax.axis_index(("rep", "shard"))
    seq_index = data_index * inputs.shape[0] + core
    limit = lax.dynamic_slice_in_dim(lengths, seq_index, 1)
    tables = [net.table(k, core, data_index) for k in range(2 * len(GROUPS))]
    is_first = core == 0

    def pick(pair, which):
        return lax.dynamic_index_in_dim(pair, which, axis=0, keepdims=False)

    def joined(low_half, high_half):
        return jnp.concatenate(
            [
                jnp.where(is_first, low_half, high_half),
                jnp.where(is_first, high_half, low_half),
            ],
            axis=1,
        )

    def whole(value):
        other = net.swap_core(value)
        own = joined(pick(value, core), pick(other, core))
        sib = joined(pick(value, 1 - core), pick(other, 1 - core))
        return own, sib

    def halved(full):
        mine = lax.dynamic_slice_in_dim(full, core * half_d, half_d, axis=1)
        away = lax.dynamic_slice_in_dim(full, (1 - core) * half_d, half_d, axis=1)
        got = net.swap_core(away)
        return jnp.stack([jnp.where(is_first, mine, got), jnp.where(is_first, got, mine)])

    x, x_sib = whole(inputs)
    e, e_sib = whole(encoded)

    pieces, vec_mine = first_pieces(net, weights, vectors, inverse_of(block_slots))
    flows, base = [], 0
    for k in range(len(GROUPS)):
        size = group_blocks(k, halves)
        flows.append(Flow(gather_rounds(net, k, pieces[base : base + size])))
        base += size
    attn, cross, up, down = flows

    def placed(k):
        return place(net, k, tables[k], *flows[k].finish())

    step((), attn)
    step((), attn, cross)
    step((), attn)
    step((), attn, cross)
    vec_mine, x, x_sib, e, e_sib = step((vec_mine, x, x_sib, e, e_sib), attn, cross, up)
    w_sq, w_sk, w_sv = step(placed(0), up)

    vec_other = net.swap_core(vec_mine)
    vec_both = jnp.concatenate(
        [jnp.where(is_first, vec_mine, vec_other), jnp.where(is_first, vec_other, vec_mine)]
    ).astype(f32)
    vecs = [vec_both[:, i * half_d : (i + 1) * half_d].reshape(1, D) for i in range(13)]
    vecs.append(vec_both[:, 13 * half_d :].reshape(1, FF))
    b_sq, b_sv, b_so, g_one, b_one, b_cq, b_cv, b_co, g_two, b_two, b_fo, g_three, b_three, b_fi = vecs

    q_s = (dot_nn(x, w_sq) + b_sq).astype(bf16)
    k_s = dot_nn(x, w_sk).astype(bf16)
    v_s = (dot_nn(x, w_sv) + b_sv).astype(bf16)
    q_s, k_s, v_s = step((q_s, k_s, v_s), cross, up, down)
    o_s, lse_s = attend_forward(limit, q_s, k_s, v_s, True)
    cotangent, o_s, lse_s = step((cotangent, o_s, lse_s), cross, up, down)
    cot_pieces = route_out(cotangent)
    w_so, w_cq, w_ck, w_cv, w_co = placed(1)
    z_one = x.astype(f32) + dot_nn(o_s, w_so) + b_so
    h_one, n_one, r_one = norm_forward(z_one, g_one, b_one)
    h_one_low = h_one.astype(bf16)
    q_c = (dot_nn(h_one_low, w_cq) + b_cq).astype(bf16)
    k_c = dot_nn(e, w_ck).astype(bf16)
    v_c = (dot_nn(e, w_cv) + b_cv).astype(bf16)
    q_c, k_c, v_c = step((q_c, k_c, v_c), down)
    o_c, lse_c = attend_forward(limit, q_c, k_c, v_c, False)
    cot_pieces, o_c, lse_c = step((cot_pieces, o_c, lse_c))
    cot_home = route_home(cot_pieces, seq_slots)
    z_two = h_one + dot_nn(o_c, w_co) + b_co
    h_two, n_two, r_two = norm_forward(z_two, g_two, b_two)
    h_two, h_two_low = step((h_two, h_two.astype(bf16)), up, down)
    (w_fi,) = placed(2)
    act, slope = gelu_forward(h_two_low, w_fi, b_fi)
    act_sib = net.swap_core(act)
    act, slope = step((act, slope), down)
    (w_fo,) = placed(3)
    z_three = h_two + dot_nn(act, w_fo) + b_fo
    h_three, n_three, r_three = norm_forward(z_three, g_three, b_three)
    live = (jnp.arange(x.shape[0]) < limit).astype(f32)[:, None]
    source = inverse_of(seq_slots)
    finished = halved((h_three * live).astype(bf16))

    def gradient(k, *calls):
        held, first = None, 0
        for xs, *ys in calls:
            held = weight_grad(net, k, tables[len(GROUPS) + k], xs, ys, held, first, GROUPS[k][first][1])
            first += len(ys)
        parts = tuple(h.reshape(h.shape[0], -1, net.rows, BS) for h in held)
        return Flow(reduce_rounds(net, len(GROUPS) + k, parts))

    cot, _ = whole(cot_home)
    grad_y = cot.astype(f32) * live
    d_three, dg_three, db_three = norm_backward(grad_y, n_three, r_three, g_three)
    a_three = d_three.astype(bf16)
    d_hidden = (dot_nt(a_three, w_fo) * slope.astype(f32)).astype(bf16)
    d_hidden_sib = net.swap_core(d_hidden)
    down = gradient(3, ((act, act_sib), (a_three, net.swap_core(a_three))))
    d_hidden, d_hidden_sib = step((d_hidden, d_hidden_sib), down)
    up = gradient(2, ((h_two_low, net.swap_core(h_two_low)), (d_hidden, d_hidden_sib)))
    finished, d_hidden = step((finished, d_hidden), up)
    out_pieces = route_out(finished)
    d_h_two = d_three + dot_nt(d_hidden, w_fi)
    d_two, dg_two, db_two = norm_backward(d_h_two, n_two, r_two, g_two)
    a_two = d_two.astype(bf16)
    d_oc = dot_nt(a_two, w_co).astype(bf16)
    dq_c, dk_c, dv_c = attend_backward(limit, q_c, k_c, v_c, o_c, d_oc, lse_c, False)
    dq_c_sib, dk_c_sib, dv_c_sib = [net.swap_core(v) for v in (dq_c, dk_c, dv_c)]
    dq_c, dk_c, dv_c = step((dq_c, dk_c, dv_c), up, down)
    d_h_one = d_two + dot_nt(dq_c, w_cq)
    d_one, dg_one, db_one = norm_backward(d_h_one, n_one, r_one, g_one)
    a_one = d_one.astype(bf16)
    a_one_sib = net.swap_core(a_one)
    d_os = dot_nt(a_one, w_so).astype(bf16)
    out_pieces, a_one, a_one_sib, d_os = step((out_pieces, a_one, a_one_sib, d_os), down)
    outputs = route_home(out_pieces, source)
    cross = gradient(
        1,
        ((o_s, net.swap_core(o_s)), (a_one, a_one_sib)),
        ((h_one_low, net.swap_core(h_one_low)), (dq_c, dq_c_sib)),
        ((e, e_sib), (dk_c, dk_c_sib), (dv_c, dv_c_sib)),
        ((o_c, net.swap_core(o_c)), (a_two, net.swap_core(a_two))),
    )
    (d_os,) = step((d_os,), cross, up, down)
    dq_s, dk_s, dv_s = attend_backward(limit, q_s, k_s, v_s, o_s, d_os, lse_s, True)
    sibs = [net.swap_core(v) for v in (dq_s, dk_s, dv_s)]
    attn = gradient(0, ((x, x_sib), *zip((dq_s, dk_s, dv_s), sibs)))
    dq_s, dk_s, dv_s = step((dq_s, dk_s, dv_s), attn, up, down)
    d_hidden, dq_c, dk_c, dv_c, dq_s, dk_s, dv_s = step(
        (d_hidden, dq_c, dk_c, dv_c, dq_s, dk_s, dv_s), cross
    )
    state_back = dot_nt(dk_c, w_ck) + dot_nt(dv_c, w_cv)
    back = d_one + dot_nt(dq_s, w_sq) + dot_nt(dk_s, w_sk) + dot_nt(dv_s, w_sv)
    outputs, back = step((outputs, back), attn, up)
    step((), cross)
    input_grad = halved(back.astype(bf16))
    encoded_grad = halved(state_back.astype(bf16))
    sums = (
        jnp.sum(dq_s.astype(f32), axis=0),
        jnp.sum(dv_s.astype(f32), axis=0),
        jnp.sum(d_one, axis=0),
        dg_one,
        db_one,
        jnp.sum(dq_c.astype(f32), axis=0),
        jnp.sum(dv_c.astype(f32), axis=0),
        jnp.sum(d_two, axis=0),
        dg_two,
        db_two,
        jnp.sum(d_three, axis=0),
        dg_three,
        db_three,
        jnp.sum(d_hidden.astype(f32), axis=0),
    )
    vec_pair = jnp.concatenate([s.reshape(halves, -1) for s in sums], axis=1)
    vec_sum = pick(vec_pair, core) + net.swap_core(pick(vec_pair, 1 - core))
    step((), attn)
    vec_sum, input_grad, encoded_grad = step((vec_sum, input_grad, encoded_grad), attn, cross)
    natural = [f.finish() for f in (attn, cross, up, down)]

    parts, flag, vec_owned = last_pieces(net, jnp.concatenate(natural), block_slots, vec_sum)
    block_grad, left_new, right_new, weights_new = shampoo(
        flag, parts, weights, left_stat, right_stat, left_root, right_root
    )
    vec_stat_new = 0.5 * vec_stat + 0.5 * vec_owned * vec_owned
    vectors_new = vectors - 0.1 * vec_owned * lax.rsqrt(vec_stat_new)
    return (
        outputs,
        input_grad,
        encoded_grad,
        block_grad,
        left_new,
        right_new,
        weights_new,
        vec_owned,
        vec_stat_new,
        vectors_new,
    )


def solution(mesh):
    net = Net(mesh.shape["rep"], mesh.shape["shard"], mesh.shape["mp"])
    rows = P(("rep", "shard"), None, "mp")
    blocks = P("mp", "shard", None, None)
    vector = P("mp", "shard")
    in_specs = (rows, rows, rows, P(), P(), P()) + (blocks,) * 5 + (vector, vector)
    out_specs = (rows, rows, rows) + (blocks,) * 4 + (vector,) * 3
    return jax.shard_map(
        functools.partial(per_device, net),
        mesh=mesh,
        in_specs=in_specs,
        out_specs=out_specs,
        check_vma=False,
    )
```

```python
import functools

import jax
import jax.numpy as jnp
import numpy as np
from jax import lax
from jax.experimental import pallas as pl
from jax.experimental.pallas import tpu as pltpu
from jax.sharding import PartitionSpec as P

D = 1024
FF = 4096
HEAD_DIM = 64
BS = 256
LANES = 128

eps_norm = 1e-05
masked_score = -1e30
scale = HEAD_DIM**-0.5
bf16 = jnp.bfloat16
f32 = jnp.float32

NT = (((1,), (1,)), ((), ()))
TN = (((0,), (0,)), ((), ()))

VMEM_LIMIT = 60 * 1024 * 1024

ERFC_SLOPE = 0.3
ERFC_POLY = (
    0.1691880090604902,
    0.17071516163759975,
    0.14833963774537734,
    0.21492421686136995,
    -0.09464635292673967,
    0.5477136065073498,
    -0.5122723795383668,
    0.4855603950654946,
    -0.1295223139805042,
)


def dot_nn(a, b):
    return jnp.dot(a, b, preferred_element_type=f32)


def dot_nt(a, b):
    return lax.dot_general(a, b, NT, preferred_element_type=f32)


def dot_tn(a, b):
    return lax.dot_general(a, b, TN, preferred_element_type=f32)


def small():
    return pl.CostEstimate(flops=1 << 20, bytes_accessed=1 << 20, transcendentals=0)


def params(**kw):
    return pltpu.CompilerParams(vmem_limit_bytes=VMEM_LIMIT, **kw)


GROUPS = (
    (("sq", True), ("sk", True), ("sv", True)),
    (("so", False), ("cq", True), ("ck", True), ("cv", True), ("co", False)),
    (("fi", True),),
    (("fo", False),),
)
SHAPES = {name: (D, D) for name in ("sq", "sk", "sv", "so", "cq", "ck", "cv", "co")}
SHAPES["fi"], SHAPES["fo"] = (D, FF), (FF, D)


def chunk_of(i):
    return (i & 8) | ((i & 2) << 1) | ((i & 1) << 1) | ((i & 4) >> 2)


class Net:
    def __init__(self, n_rep, n_shard, n_mp):
        self.n_rep, self.n_shard, self.n_mp = n_rep, n_shard, n_mp
        self.n_data = n_rep * n_shard
        self.pieces = 16 if (n_rep, n_shard, n_mp) == (2, 8, 2) else 1
        self.rows = BS // self.pieces
        self.depth = self.pieces.bit_length() - 1
        x, z1, z2, y = 1, 2, 4, 8
        gathering = (
            ((z2, y, z1, x), (z2, z1, x, y)),
            ((z2, z1, y, x), (z2, z1, x, y)),
            ((z2, x, z1, y), (z2, y, z1, x)),
            ((z2, x, y, z1), (z2, y, z1, x)),
        )
        reducing = (((z2, y, z1, x), (z2, x, z1, y)),) + gathering[1:]
        self.orders = gathering + reducing

    def swap_core(self, value):
        return lax.ppermute(value, "mp", [(i, i ^ 1) for i in range(self.n_mp)])

    def swap_rep(self, value):
        return lax.ppermute(value, "rep", [(i, i ^ 1) for i in range(self.n_rep)])

    def swap_data(self, value, group, step):
        pairs = []
        for i in range(self.n_data):
            for m in range(self.n_mp):
                there = i ^ self.orders[group][m][step]
                pairs.append((i * self.n_mp + m, there * self.n_mp + m))
        return lax.ppermute(value, ("rep", "shard", "mp"), pairs)

    def table(self, group, core, data_index):
        many = self.pieces
        if many == 1:
            return jnp.stack([0, 0, 0, 0, core]).astype(jnp.int32)
        half = many // 4
        rel = []
        for order in self.orders[group]:
            rel.append([sum(b for s, b in enumerate(order) if q >> s & 1) for q in range(many)])
        rows = []
        for m in range(self.n_mp):
            place = [rel[1 - m].index(r) // 2 for r in rel[m][::2]]
            low = [p for p in place if p < half][0]
            high = [p - half for p in place if p >= half][0]
            lows, highs = [], []
            for p in place:
                low, high = (p, high) if p < half else (low, p - half)
                lows.append(low)
                highs.append(high)
            rows.append([chunk_of(r) for r in rel[m]] + lows + highs + [int(p >= half) for p in place])
        mine = jnp.asarray(np.array(rows, np.int32))[core]
        chunks = mine[:many] ^ chunk_of(data_index)
        return jnp.concatenate([chunks, mine[many:], core.reshape(1)]).astype(jnp.int32)


def together(*values):
    return lax.optimization_barrier(values)


class Flow:
    def __init__(self, rounds):
        self.rounds = rounds
        self.flying = next(rounds)

    def advance(self, values):
        try:
            self.flying = self.rounds.send(values)
        except StopIteration as stop:
            self.flying = None
            self.result = stop.value

    def finish(self):
        while self.flying is not None:
            self.advance(self.flying)
        return self.result


def step(main, *flows):
    flows = [f for f in flows if f.flying is not None]
    values = list(together(*main, *[v for f in flows for v in f.flying]))
    main, values = values[: len(main)], values[len(main) :]
    for f in flows:
        many = len(f.flying)
        f.advance(tuple(values[:many]))
        values = values[many:]
    return main


def blocks_of(name, n_mp):
    rows, cols = SHAPES[name]
    return rows * cols // n_mp // (BS * BS)


def group_blocks(group, n_mp):
    return sum(blocks_of(name, n_mp) for name, _ in GROUPS[group])


def place_body(s, *refs, dests, many, two):
    q = pl.program_id(0)
    steps = many // 2 if two else 1
    if two:
        own_lo, own_hi, sib_lo, sib_hi = refs[:4]
        outs = refs[4:]
    else:
        own_lo, sib_lo = refs[:2]
        outs = refs[2:]
    core = s[many + 3 * steps]
    rows = own_lo.shape[2]
    for t in range(own_lo.shape[0]):
        here = pl.ds(0, rows)
        if two:
            here = pl.ds(pl.multiple_of((s[2 * q + t] & 1) * rows, rows), rows)
        for b in range(own_lo.shape[1]):
            own, sib = own_lo[t, b], sib_lo[t, b]
            if two:
                own = jnp.where(q < steps // 2, own, own_hi[t, b])
                sib = jnp.where(s[many + 2 * steps + q] == 0, sib, sib_hi[t, b])
            for h in range(2):
                which, row, col = dests[h][b]
                outs[which][row, here, col : col + BS] = jnp.where(core == h, own, sib)


def place(net, group, table, own, sib):
    many, rows, n_mp = net.pieces, net.rows, net.n_mp
    two = many > 1
    per = 2 if two else 1
    steps = many // per
    half = max(steps // 2, 1)
    dests = ([], [])
    shapes, specs = [], []
    for which, (name, wide) in enumerate(GROUPS[group]):
        height, width = SHAPES[name]
        tall = height if wide else height // n_mp
        flat = width // n_mp if wide else width
        for h in range(n_mp):
            for r in range(tall // BS):
                for c in range(flat // BS):
                    if wide:
                        dests[h].append((which, r, h * flat + c * BS))
                    else:
                        dests[h].append((which, h * (tall // BS) + r, c * BS))
        shapes.append(jax.ShapeDtypeStruct((height // BS, BS, width), bf16))
        specs.append(
            pl.BlockSpec((height // BS, per * rows, width), lambda q, s: (0, s[per * q] // per, 0))
        )
    nb = own[0].shape[1]
    block = (per, nb, rows, BS)
    lo = pl.BlockSpec(block, lambda q, s: (jnp.minimum(q, half - 1), 0, 0, 0))
    hi = pl.BlockSpec(block, lambda q, s: (jnp.maximum(q - half, 0), 0, 0, 0))
    sib_lo = pl.BlockSpec(block, lambda q, s: (s[many + q], 0, 0, 0))
    sib_hi = pl.BlockSpec(block, lambda q, s: (s[many + steps + q], 0, 0, 0))
    out = pl.pallas_call(
        functools.partial(place_body, dests=dests, many=many, two=two),
        grid_spec=pltpu.PrefetchScalarGridSpec(
            num_scalar_prefetch=1,
            grid=(steps,),
            in_specs=[lo, hi, sib_lo, sib_hi] if two else [lo, sib_lo],
            out_specs=tuple(specs),
        ),
        out_shape=tuple(shapes),
        compiler_params=params(),
        cost_estimate=small(),
        name="place",
    )(table, *own, *sib)
    return [o.reshape(-1, o.shape[2]) for o in out]


def gather_rounds(net, group, piece):
    (piece,) = yield (piece,)
    cur = piece[None]
    if net.pieces == 1:
        (sib,) = yield (net.swap_core(cur),)
        return (cur,), (sib,)
    for k in range(net.depth - 1):
        (got,) = yield (net.swap_data(cur, group, k),)
        cur = jnp.concatenate([cur, got])
    got, sib_lo = yield (net.swap_data(cur, group, net.depth - 1), net.swap_core(cur))
    (sib_hi,) = yield (net.swap_core(got),)
    return (cur, got), (sib_lo, sib_hi)


def first_pieces(net, weights, vectors, inverse):
    low = weights[0].astype(bf16)
    vec = vectors.astype(bf16)
    if net.pieces == 1:
        every = lax.all_gather(low, "shard", axis=0, tiled=True)
        vec_every = lax.all_gather(vec, "shard", axis=1, tiled=True)
        return every.at[inverse].get(mode="promise_in_bounds"), vec_every
    nblk = low.shape[0]
    cut = low.reshape(nblk, 2, 2, 2, 2, net.rows, BS)
    cut = lax.dynamic_index_in_dim(cut, lax.axis_index("rep"), axis=1, keepdims=False)
    cut = cut.transpose(3, 1, 2, 0, 4, 5).reshape(net.n_shard, nblk, net.rows, BS)
    room = net.rows * BS
    vec_cut = jnp.pad(vec.reshape(-1), (0, room - vec.shape[1])).reshape(1, 1, net.rows, BS)
    cut = jnp.concatenate([cut, jnp.broadcast_to(vec_cut, (net.n_shard,) + vec_cut.shape[1:])], axis=1)
    every = lax.all_to_all(
        cut.reshape(-1, net.rows, BS), "shard", split_axis=0, concat_axis=0, tiled=True
    )
    pieces = every.at[inverse + inverse // nblk].get(mode="promise_in_bounds")
    vec_every = every.reshape(net.n_shard, nblk + 1, room)[:, nblk, : vec.shape[1]]
    return pieces, vec_every.reshape(1, -1)


def total_of(*terms):
    acc = terms[0].astype(f32)
    for t in terms[1:]:
        acc = acc + t.astype(f32)
    return acc.astype(bf16)


def reduce_rounds(net, group, parts):
    parts = yield parts
    if net.pieces == 1:
        return parts[0][0]
    lo, hi = parts
    (got,) = yield (net.swap_data(hi, group, net.depth - 1),)
    terms = [lo, got]
    for k in range(net.depth - 2, -1, -1):
        width = 1 << k
        send = total_of(*[t[width:] for t in terms])
        keep = total_of(*[t[:width] for t in terms])
        (got,) = yield (net.swap_data(send, group, k),)
        terms = [keep, got]
    return total_of(*terms)[0]


def last_pieces(net, natural, block_slots, vec_sum):
    if net.pieces == 1:
        dealt = natural.at[block_slots].get(mode="promise_in_bounds")
        owned = lax.psum_scatter(dealt, "shard", scatter_dimension=0, tiled=True)
        owned = total_of(owned, net.swap_rep(owned))
        cut = owned.reshape(-1, 2, 8, 16, BS).transpose(1, 2, 0, 3, 4)
        cut = cut[:, np.array([chunk_of(k) for k in range(8)])]
        vec = lax.psum_scatter(vec_sum, "shard", scatter_dimension=0, tiled=True)[None]
        parts = [(cut[0], cut[1], owned.shape[0])]
        return parts, jnp.zeros((1,), jnp.int32), vec + net.swap_rep(vec)
    n = net.n_shard
    slots = block_slots.reshape(n, -1)
    half = slots.shape[1] // 2
    room = net.rows * BS
    vec_cut = vec_sum.reshape(n, -1)
    width = vec_cut.shape[1]
    vec_cut = jnp.pad(vec_cut.astype(bf16), ((0, 0), (0, room - width)))
    vec_cut = vec_cut.reshape(n, 1, net.rows, BS)
    cuts = []
    for k in range(2):
        index = slots[:, k * half : (k + 1) * half].reshape(-1)
        cuts.append(natural.at[index].get(mode="promise_in_bounds").reshape(n, half, net.rows, BS))
    cuts[1] = jnp.concatenate([cuts[1], vec_cut], axis=1)

    def home(cut):
        back = lax.all_to_all(
            cut.reshape(-1, net.rows, BS), "shard", split_axis=0, concat_axis=0, tiled=True
        )
        return back.reshape(n, -1, net.rows, BS)

    mine, cuts[1] = together(home(cuts[0]), cuts[1])
    other = net.swap_rep(mine)
    other, last = together(other, home(cuts[1]))
    parts = [(mine, other, half), (last, net.swap_rep(last), half)]
    terms = [v[:, half].reshape(n, room)[:, :width].astype(f32) for v in parts[1][:2]]
    flag = lax.axis_index("rep").astype(jnp.int32).reshape(1)
    return parts, flag, jnp.sum(terms[0] + terms[1], axis=0, keepdims=True)


def attend_forward_body(lim, q_ref, k_ref, v_ref, o_ref, lse_ref, *, causal, rows):
    pair = pl.program_id(0)
    seq, keys = q_ref.shape[0], k_ref.shape[0]
    lane = lax.broadcasted_iota(jnp.int32, (1, LANES), 1)
    top = lim[0] - 1

    @pl.when(pair == 0)
    def _():
        lse_ref[...] = jnp.zeros_like(lse_ref)

    for blk in range(seq // rows):
        here = pl.ds(blk * rows, rows)
        width = (blk + 1) * rows if causal else keys
        q = q_ref[here, :] * bf16(scale)
        k = k_ref[pl.ds(0, width), :]
        v = v_ref[pl.ds(0, width), :]
        outs = []
        kept = lse_ref[here, :]
        if causal:
            row = lax.broadcasted_iota(jnp.int32, (rows, 1), 0) + blk * rows
            col = lax.broadcasted_iota(jnp.int32, (1, width), 1)
            allowed = col <= jnp.minimum(row, top)
        for h in range(2):
            mine = (lane // HEAD_DIM) == h
            s = dot_nt(jnp.where(mine, q, bf16(0)), k)
            if causal:
                s = jnp.where(allowed, s, masked_score)
            peak = jnp.max(s, axis=1, keepdims=True)
            e = jnp.exp(s - peak)
            mass = jnp.sum(e, axis=1, keepdims=True)
            outs.append(dot_nn(e.astype(bf16), v) * (1.0 / mass))
            kept = jnp.where(lane == 2 * pair + h, peak + jnp.log(mass), kept)
        o_ref[here, :] = jnp.where(lane < HEAD_DIM, outs[0], outs[1]).astype(bf16)
        lse_ref[here, :] = kept


def attend_forward(limit, q, k, v, causal):
    seq, width = q.shape
    keys = k.shape[0]
    pairs = width // LANES
    rows = min(128 if causal else 256, seq)
    o, lse = pl.pallas_call(
        functools.partial(attend_forward_body, causal=causal, rows=rows),
        grid=(pairs,),
        out_shape=(
            jax.ShapeDtypeStruct((seq, width), bf16),
            jax.ShapeDtypeStruct((seq, LANES), f32),
        ),
        in_specs=[
            pl.BlockSpec(memory_space=pltpu.SMEM),
            pl.BlockSpec((seq, LANES), lambda i: (0, i)),
            pl.BlockSpec((keys, LANES), lambda i: (0, i)),
            pl.BlockSpec((keys, LANES), lambda i: (0, i)),
        ],
        out_specs=(
            pl.BlockSpec((seq, LANES), lambda i: (0, i)),
            pl.BlockSpec((seq, LANES), lambda i: (0, 0)),
        ),
        compiler_params=params(),
        cost_estimate=small(),
        name="attend_forward",
    )(limit, q, k, v)
    return o, lse[:, : 2 * pairs].T.reshape(pairs, 2, seq)


def attend_backward_body(
    lim, q_ref, k_ref, v_ref, o_ref, do_ref, lse_ref, dq_ref, dk_ref, dv_ref, dk_acc, dv_acc, *, causal, rows
):
    seq, keys = q_ref.shape[0], k_ref.shape[0]
    lane = lax.broadcasted_iota(jnp.int32, (1, LANES), 1)
    top = lim[0] - 1
    dk_acc[...] = jnp.zeros_like(dk_acc)
    dv_acc[...] = jnp.zeros_like(dv_acc)
    head_row = lax.broadcasted_iota(jnp.int32, (8, LANES), 0)
    head_lane = lax.broadcasted_iota(jnp.int32, (8, LANES), 1) // HEAD_DIM
    pick = (head_row == head_lane).astype(bf16)
    for blk in range(seq // rows):
        here = pl.ds(blk * rows, rows)
        width = (blk + 1) * rows if causal else keys
        span = pl.ds(0, width)
        q = q_ref[here, :] * bf16(scale)
        do = do_ref[here, :]
        k = k_ref[span, :]
        v = v_ref[span, :]
        prod = do.astype(f32) * o_ref[here, :].astype(f32)
        hi = prod.astype(bf16)
        lo = (prod - hi.astype(f32)).astype(bf16)
        delta = dot_nt(pick, hi) + dot_nt(pick, lo)
        lse = lse_ref[0][:, blk * rows : (blk + 1) * rows]
        if causal:
            key = lax.broadcasted_iota(jnp.int32, (width, 1), 0)
            row = lax.broadcasted_iota(jnp.int32, (1, rows), 1) + blk * rows
            allowed = key <= jnp.minimum(row, top)
        dq = jnp.zeros((rows, LANES), f32)
        dk = jnp.zeros((width, LANES), f32)
        dv = jnp.zeros((width, LANES), f32)
        for h in range(2):
            mine = (lane // HEAD_DIM) == h
            qm = jnp.where(mine, q, bf16(0))
            dom = jnp.where(mine, do, bf16(0))
            km = jnp.where(mine, k, bf16(0))
            s = dot_nt(k, qm)
            if causal:
                s = jnp.where(allowed, s, masked_score)
            p = jnp.exp(s - lse[h : h + 1, :])
            dp = dot_nt(v, dom)
            ds = (p * (dp - delta[h : h + 1, :])).astype(bf16)
            dv = dv + dot_nn(p.astype(bf16), dom)
            dk = dk + dot_nn(ds, qm)
            dq = dq + dot_tn(ds, km)
        dq_ref[here, :] = (dq * scale).astype(bf16)
        dk_acc[span, :] += dk
        dv_acc[span, :] += dv
    dk_ref[...] = dk_acc[...].astype(bf16)
    dv_ref[...] = dv_acc[...].astype(bf16)


def attend_backward(limit, q, k, v, o, do, lse, causal):
    seq, width = q.shape
    keys = k.shape[0]
    pairs = width // LANES
    rows = min(128 if causal else 256, seq)
    q_spec = pl.BlockSpec((seq, LANES), lambda i: (0, i))
    k_spec = pl.BlockSpec((keys, LANES), lambda i: (0, i))
    return pl.pallas_call(
        functools.partial(attend_backward_body, causal=causal, rows=rows),
        grid=(pairs,),
        out_shape=(
            jax.ShapeDtypeStruct((seq, width), bf16),
            jax.ShapeDtypeStruct((keys, width), bf16),
            jax.ShapeDtypeStruct((keys, width), bf16),
        ),
        in_specs=[
            pl.BlockSpec(memory_space=pltpu.SMEM),
            q_spec,
            k_spec,
            k_spec,
            q_spec,
            q_spec,
            pl.BlockSpec((1, 2, seq), lambda i: (i, 0, 0)),
        ],
        out_specs=(q_spec, k_spec, k_spec),
        scratch_shapes=[pltpu.VMEM((keys, LANES), f32), pltpu.VMEM((keys, LANES), f32)],
        compiler_params=params(),
        cost_estimate=small(),
        name="attend_backward",
    )(limit, q, k, v, o, do, lse)


def gelu_body(h_ref, w_ref, b_ref, act_ref, slope_ref, u_ref, *, chunk):
    u_ref[...] = dot_nn(h_ref[...], w_ref[...]) + b_ref[...]

    def part(i):
        here = pl.ds(pl.multiple_of(i * chunk, chunk), chunk)
        u = u_ref[here, :]
        x = jnp.abs(u) * (0.5**0.5)
        t = 1.0 / (1.0 + ERFC_SLOPE * x)
        poly = jnp.full_like(t, ERFC_POLY[-1])
        for c in ERFC_POLY[-2::-1]:
            poly = poly * t + c
        bell = jnp.exp(-0.5 * (u * u))
        tail = 0.5 * (bell * (t * poly))
        cdf = jnp.where(u < 0, tail, 1.0 - tail)
        act_ref[here, :] = (u * cdf).astype(bf16)
        slope_ref[here, :] = (cdf + u * (bell * 0.3989422804014327)).astype(bf16)

    pl.loop(0, u_ref.shape[0] // chunk)(part)


def gelu_forward(h, w, b):
    seq, width = h.shape
    hidden = w.shape[1]
    tile = 512
    spec = pl.BlockSpec((seq, tile), lambda i: (0, i))
    return pl.pallas_call(
        functools.partial(gelu_body, chunk=32),
        grid=(hidden // tile,),
        out_shape=(jax.ShapeDtypeStruct((seq, hidden), bf16),) * 2,
        in_specs=[
            pl.BlockSpec((seq, width), lambda i: (0, 0)),
            pl.BlockSpec((width, tile), lambda i: (0, i)),
            pl.BlockSpec((1, tile), lambda i: (0, i)),
        ],
        out_specs=(spec, spec),
        scratch_shapes=[pltpu.VMEM((seq, tile), f32)],
        compiler_params=params(),
        cost_estimate=small(),
        name="gelu_forward",
    )(h, w, b)


def weight_grad_body(s, x_own, x_sib, *refs, count, outs, many, rows):
    y_own, y_sib = refs[:count], refs[count : 2 * count]
    targets = refs[-3 - outs : -3]
    t_own, t_sib, buf = refs[-3:]
    t_own[...] = x_own[...].T
    t_sib[...] = x_sib[...].T
    per = many // outs
    for k in range(count):
        acc = dot_nn(t_own[...], y_own[k][...]) + dot_nn(t_sib[...], y_sib[k][...])
        buf[k] = acc.astype(bf16)
    for q in range(many):
        here = pl.ds(pl.multiple_of(s[q] * rows, rows), rows)
        for k in range(count):
            for c in range(targets[0].shape[2]):
                targets[q // per][q % per, k, c] = buf[k, here, c * BS : (c + 1) * BS]


def weight_grad(net, group, table, xs, ys, held, first, wide):
    seq = xs[0].shape[0]
    many, rows, halves = net.pieces, net.rows, net.n_mp
    at_core = table.shape[0] - 1
    count = len(ys)
    width = ys[0][0].shape[1]
    if wide:
        steps = xs[0].shape[1] // BS
        y_width = width // halves
        x_spec = pl.BlockSpec((seq, BS), lambda i, s: (0, i))
        y_spec = pl.BlockSpec((seq, y_width), lambda i, s: (0, s[at_core]))
    else:
        steps = xs[0].shape[1] // halves // BS
        y_width = width
        x_spec = pl.BlockSpec((seq, BS), lambda i, s: (0, s[at_core] * steps + i))
        y_spec = pl.BlockSpec((seq, y_width), lambda i, s: (0, 0))
    nb = y_width // BS
    at = first // count
    outs = 2 if many > 1 else 1
    shape = (many // outs, len(GROUPS[group]), steps * nb, rows, BS)
    anyspec = pl.BlockSpec(memory_space=pl.ANY)
    held = held or ()
    before = 3 + 2 * count
    return pl.pallas_call(
        functools.partial(weight_grad_body, count=count, outs=outs, many=many, rows=rows),
        grid_spec=pltpu.PrefetchScalarGridSpec(
            num_scalar_prefetch=1,
            grid=(steps,),
            in_specs=[x_spec] * 2 + [y_spec] * (2 * count) + [anyspec] * len(held),
            out_specs=(
                pl.BlockSpec((many // outs, count, nb, rows, BS), lambda i, s: (0, at, i, 0, 0)),
            )
            * outs,
            scratch_shapes=[
                pltpu.VMEM((BS, seq), bf16),
                pltpu.VMEM((BS, seq), bf16),
                pltpu.VMEM((count, BS, y_width), bf16),
            ],
        ),
        out_shape=(jax.ShapeDtypeStruct(shape, bf16),) * outs,
        input_output_aliases={before + k: k for k in range(len(held))},
        compiler_params=params(),
        cost_estimate=small(),
        name="weight_grad",
    )(table, *xs, *[y[0] for y in ys], *[y[1] for y in ys], *held)


def split_low(a):
    hi = a.astype(bf16)
    return hi, (a - hi.astype(f32)).astype(bf16)


def shampoo_body(flag, mine_ref, other_ref, w_ref, ls_ref, rs_ref, lr_ref, rr_ref, *refs):
    og, ol, orr, ow, g_ref = refs[-5:]
    for k in range(mine_ref.shape[0]):
        for plane, src in ((flag[0], mine_ref), (1 - flag[0], other_ref)):
            row = pl.multiple_of(plane * 128 + chunk_of(k) * 16, 16)
            g_ref[pl.ds(row, 16), :] = src[k, 0]
    g = g_ref[...]
    og[0, 0] = g.astype(f32)
    ol[0, 0] = 0.5 * ls_ref[0, 0] + 0.5 * dot_nt(g, g)
    orr[0, 0] = 0.5 * rs_ref[0, 0] + 0.5 * dot_tn(g, g)
    r_hi, r_lo = split_low(rr_ref[0, 0])
    i_hi, i_lo = split_low(dot_nn(g, r_hi) + dot_nn(g, r_lo))
    l_hi, l_lo = split_low(lr_ref[0, 0])
    d = dot_nn(l_hi, i_hi) + (dot_nn(l_hi, i_lo) + dot_nn(l_lo, i_hi))
    mean = jnp.mean(jnp.mean(d * d, axis=1, keepdims=True), axis=0, keepdims=True)
    ow[0, 0] = w_ref[0, 0] - (D**-0.5) * d / jnp.sqrt(mean + 1e-06)


def shampoo(flag, parts, *states):
    total = states[0].shape[1]
    out, first = (), 0
    for mine, other, n in parts:
        at = first // n
        spec = pl.BlockSpec((1, 1, BS, BS), lambda i, at=at, n=n: (0, at * n + i, 0, 0))
        g_spec = pl.BlockSpec((mine.shape[0], 1, mine.shape[2], BS), lambda i: (0, i, 0, 0))
        anyspec = pl.BlockSpec(memory_space=pl.ANY)
        out = pl.pallas_call(
            shampoo_body,
            grid=(n,),
            out_shape=(jax.ShapeDtypeStruct((1, total, BS, BS), f32),) * 4,
            in_specs=[pl.BlockSpec(memory_space=pltpu.SMEM), g_spec, g_spec]
            + [spec] * 5
            + [anyspec] * len(out),
            out_specs=(spec,) * 4,
            scratch_shapes=[pltpu.VMEM((BS, BS), bf16)],
            input_output_aliases={8 + k: k for k in range(len(out))},
            compiler_params=params(),
            cost_estimate=small(),
            name="shampoo",
        )(flag, mine, other, *states, *out)
        first += n
    return out


def norm_forward(z, gain, shift):
    center = z - jnp.mean(z, axis=1, keepdims=True)
    inv = lax.rsqrt(jnp.mean(center * center, axis=1, keepdims=True) + eps_norm)
    normed = center * inv
    return normed * gain + shift, normed, inv


def norm_backward(grad, normed, inv, gain):
    scaled = grad * gain
    mean_plain = jnp.mean(scaled, axis=1, keepdims=True)
    mean_cross = jnp.mean(scaled * normed, axis=1, keepdims=True)
    back = inv * (scaled - mean_plain - normed * mean_cross)
    return back, jnp.sum(grad * normed, axis=0), jnp.sum(grad, axis=0)


def inverse_of(order):
    many = jnp.arange(order.shape[0], dtype=jnp.int32)
    return jnp.sum(jnp.where(order[:, None] == many[None, :], many[:, None], 0), axis=0)


def route_out(value):
    axes = ("rep", "shard")
    count = lax.axis_size(axes)
    cut = value.reshape(value.shape[0], count, value.shape[1] // count, value.shape[2])
    return lax.all_to_all(cut, axes, split_axis=1, concat_axis=0, tiled=True)


def route_home(pieces, ordering):
    moved = pieces.at[ordering].get(mode="promise_in_bounds")
    back = lax.all_to_all(moved, ("rep", "shard"), split_axis=0, concat_axis=1, tiled=True)
    return back.reshape(back.shape[0], -1, back.shape[3])


def per_device(
    net,
    inputs,
    encoded,
    cotangent,
    lengths,
    seq_slots,
    block_slots,
    weights,
    left_stat,
    right_stat,
    left_root,
    right_root,
    vectors,
    vec_stat,
):
    half_d = inputs.shape[2]
    halves = D // half_d
    core = lax.axis_index("mp")
    data_index = lax.axis_index(("rep", "shard"))
    seq_index = data_index * inputs.shape[0] + core
    limit = lax.dynamic_slice_in_dim(lengths, seq_index, 1)
    tables = [net.table(k, core, data_index) for k in range(2 * len(GROUPS))]
    is_first = core == 0

    def pick(pair, which):
        return lax.dynamic_index_in_dim(pair, which, axis=0, keepdims=False)

    def joined(low_half, high_half):
        return jnp.concatenate(
            [
                jnp.where(is_first, low_half, high_half),
                jnp.where(is_first, high_half, low_half),
            ],
            axis=1,
        )

    def whole(value):
        other = net.swap_core(value)
        own = joined(pick(value, core), pick(other, core))
        sib = joined(pick(value, 1 - core), pick(other, 1 - core))
        return own, sib

    def halved(full):
        mine = lax.dynamic_slice_in_dim(full, core * half_d, half_d, axis=1)
        away = lax.dynamic_slice_in_dim(full, (1 - core) * half_d, half_d, axis=1)
        got = net.swap_core(away)
        return jnp.stack([jnp.where(is_first, mine, got), jnp.where(is_first, got, mine)])

    x, x_sib = whole(inputs)
    e, e_sib = whole(encoded)

    pieces, vec_mine = first_pieces(net, weights, vectors, inverse_of(block_slots))
    flows, base = [], 0
    for k in range(len(GROUPS)):
        size = group_blocks(k, halves)
        flows.append(Flow(gather_rounds(net, k, pieces[base : base + size])))
        base += size
    attn, cross, up, down = flows

    def placed(k):
        return place(net, k, tables[k], *flows[k].finish())

    step((), attn)
    step((), attn, cross)
    step((), attn)
    step((), attn, cross)
    vec_mine, x, x_sib, e, e_sib = step((vec_mine, x, x_sib, e, e_sib), attn, cross, up)
    w_sq, w_sk, w_sv = step(placed(0), up)

    vec_other = net.swap_core(vec_mine)
    vec_both = jnp.concatenate(
        [jnp.where(is_first, vec_mine, vec_other), jnp.where(is_first, vec_other, vec_mine)]
    ).astype(f32)
    vecs = [vec_both[:, i * half_d : (i + 1) * half_d].reshape(1, D) for i in range(13)]
    vecs.append(vec_both[:, 13 * half_d :].reshape(1, FF))
    b_sq, b_sv, b_so, g_one, b_one, b_cq, b_cv, b_co, g_two, b_two, b_fo, g_three, b_three, b_fi = vecs

    q_s = (dot_nn(x, w_sq) + b_sq).astype(bf16)
    k_s = dot_nn(x, w_sk).astype(bf16)
    v_s = (dot_nn(x, w_sv) + b_sv).astype(bf16)
    q_s, k_s, v_s = step((q_s, k_s, v_s), cross, up, down)
    o_s, lse_s = attend_forward(limit, q_s, k_s, v_s, True)
    cotangent, o_s, lse_s = step((cotangent, o_s, lse_s), cross, up, down)
    cot_pieces = route_out(cotangent)
    w_so, w_cq, w_ck, w_cv, w_co = placed(1)
    z_one = x.astype(f32) + dot_nn(o_s, w_so) + b_so
    h_one, n_one, r_one = norm_forward(z_one, g_one, b_one)
    h_one_low = h_one.astype(bf16)
    q_c = (dot_nn(h_one_low, w_cq) + b_cq).astype(bf16)
    k_c = dot_nn(e, w_ck).astype(bf16)
    v_c = (dot_nn(e, w_cv) + b_cv).astype(bf16)
    cot_pieces, q_c, k_c, v_c = step((cot_pieces, q_c, k_c, v_c), down)
    cot_home = route_home(cot_pieces, seq_slots)
    o_c, lse_c = attend_forward(limit, q_c, k_c, v_c, False)
    z_two = h_one + dot_nn(o_c, w_co) + b_co
    h_two, n_two, r_two = norm_forward(z_two, g_two, b_two)
    h_two, h_two_low = step((h_two, h_two.astype(bf16)), up, down)
    (w_fi,) = placed(2)
    act, slope = gelu_forward(h_two_low, w_fi, b_fi)
    act_sib = net.swap_core(act)
    act, slope = step((act, slope), down)
    (w_fo,) = placed(3)
    z_three = h_two + dot_nn(act, w_fo) + b_fo
    h_three, n_three, r_three = norm_forward(z_three, g_three, b_three)
    live = (jnp.arange(x.shape[0]) < limit).astype(f32)[:, None]
    source = inverse_of(seq_slots)
    finished = halved((h_three * live).astype(bf16))

    def gradient(k, *calls):
        held, first = None, 0
        for xs, *ys in calls:
            held = weight_grad(net, k, tables[len(GROUPS) + k], xs, ys, held, first, GROUPS[k][first][1])
            first += len(ys)
        parts = tuple(h.reshape(h.shape[0], -1, net.rows, BS) for h in held)
        return Flow(reduce_rounds(net, len(GROUPS) + k, parts))

    cot, _ = whole(cot_home)
    grad_y = cot.astype(f32) * live
    d_three, dg_three, db_three = norm_backward(grad_y, n_three, r_three, g_three)
    a_three = d_three.astype(bf16)
    d_hidden = (dot_nt(a_three, w_fo) * slope.astype(f32)).astype(bf16)
    d_hidden_sib = net.swap_core(d_hidden)
    down = gradient(3, ((act, act_sib), (a_three, net.swap_core(a_three))))
    d_hidden, d_hidden_sib = step((d_hidden, d_hidden_sib), down)
    d_h_two = d_three + dot_nt(d_hidden, w_fi)
    d_two, dg_two, db_two = norm_backward(d_h_two, n_two, r_two, g_two)
    a_two = d_two.astype(bf16)
    d_oc = dot_nt(a_two, w_co).astype(bf16)
    finished, d_hidden, d_hidden_sib, d_oc = step((finished, d_hidden, d_hidden_sib, d_oc))
    out_pieces = route_out(finished)
    up = gradient(2, ((h_two_low, net.swap_core(h_two_low)), (d_hidden, d_hidden_sib)))
    (d_oc,) = step((d_oc,), up, down)
    dq_c, dk_c, dv_c = attend_backward(limit, q_c, k_c, v_c, o_c, d_oc, lse_c, False)
    dq_c_sib, dk_c_sib, dv_c_sib = [net.swap_core(v) for v in (dq_c, dk_c, dv_c)]
    dq_c, dk_c, dv_c = step((dq_c, dk_c, dv_c), down)
    d_h_one = d_two + dot_nt(dq_c, w_cq)
    d_one, dg_one, db_one = norm_backward(d_h_one, n_one, r_one, g_one)
    a_one = d_one.astype(bf16)
    a_one_sib = net.swap_core(a_one)
    d_os = dot_nt(a_one, w_so).astype(bf16)
    out_pieces, a_one, a_one_sib, d_os = step((out_pieces, a_one, a_one_sib, d_os), up, down)
    outputs = route_home(out_pieces, source)
    cross = gradient(
        1,
        ((o_s, net.swap_core(o_s)), (a_one, a_one_sib)),
        ((h_one_low, net.swap_core(h_one_low)), (dq_c, dq_c_sib)),
        ((e, e_sib), (dk_c, dk_c_sib), (dv_c, dv_c_sib)),
        ((o_c, net.swap_core(o_c)), (a_two, net.swap_core(a_two))),
    )
    (d_os,) = step((d_os,), cross, up, down)
    dq_s, dk_s, dv_s = attend_backward(limit, q_s, k_s, v_s, o_s, d_os, lse_s, True)
    sibs = [net.swap_core(v) for v in (dq_s, dk_s, dv_s)]
    dq_s, dk_s, dv_s = step((dq_s, dk_s, dv_s), cross, up)
    attn = gradient(0, ((x, x_sib), *zip((dq_s, dk_s, dv_s), sibs)))
    d_hidden, dq_c, dk_c, dv_c, dq_s, dk_s, dv_s = step(
        (d_hidden, dq_c, dk_c, dv_c, dq_s, dk_s, dv_s), attn, cross, up
    )
    state_back = dot_nt(dk_c, w_ck) + dot_nt(dv_c, w_cv)
    back = d_one + dot_nt(dq_s, w_sq) + dot_nt(dk_s, w_sk) + dot_nt(dv_s, w_sv)
    outputs, back = step((outputs, back), attn, cross)
    input_grad = halved(back.astype(bf16))
    encoded_grad = halved(state_back.astype(bf16))
    sums = (
        jnp.sum(dq_s.astype(f32), axis=0),
        jnp.sum(dv_s.astype(f32), axis=0),
        jnp.sum(d_one, axis=0),
        dg_one,
        db_one,
        jnp.sum(dq_c.astype(f32), axis=0),
        jnp.sum(dv_c.astype(f32), axis=0),
        jnp.sum(d_two, axis=0),
        dg_two,
        db_two,
        jnp.sum(d_three, axis=0),
        dg_three,
        db_three,
        jnp.sum(d_hidden.astype(f32), axis=0),
    )
    vec_pair = jnp.concatenate([s.reshape(halves, -1) for s in sums], axis=1)
    vec_sum = pick(vec_pair, core) + net.swap_core(pick(vec_pair, 1 - core))
    step((), attn)
    vec_sum, input_grad, encoded_grad = step((vec_sum, input_grad, encoded_grad), attn, cross)
    natural = [f.finish() for f in (attn, cross, up, down)]

    parts, flag, vec_owned = last_pieces(net, jnp.concatenate(natural), block_slots, vec_sum)
    block_grad, left_new, right_new, weights_new = shampoo(
        flag, parts, weights, left_stat, right_stat, left_root, right_root
    )
    vec_stat_new = 0.5 * vec_stat + 0.5 * vec_owned * vec_owned
    vectors_new = vectors - 0.1 * vec_owned * lax.rsqrt(vec_stat_new)
    return (
        outputs,
        input_grad,
        encoded_grad,
        block_grad,
        left_new,
        right_new,
        weights_new,
        vec_owned,
        vec_stat_new,
        vectors_new,
    )


def solution(mesh):
    net = Net(mesh.shape["rep"], mesh.shape["shard"], mesh.shape["mp"])
    rows = P(("rep", "shard"), None, "mp")
    blocks = P("mp", "shard", None, None)
    vector = P("mp", "shard")
    in_specs = (rows, rows, rows, P(), P(), P()) + (blocks,) * 5 + (vector, vector)
    out_specs = (rows, rows, rows) + (blocks,) * 4 + (vector,) * 3
    return jax.shard_map(
        functools.partial(per_device, net),
        mesh=mesh,
        in_specs=in_specs,
        out_specs=out_specs,
        check_vma=False,
    )
```

```python
import functools

import jax
import jax.numpy as jnp
import numpy as np
from jax import lax
from jax.experimental import pallas as pl
from jax.experimental.pallas import tpu as pltpu
from jax.sharding import PartitionSpec as P

D = 1024
FF = 4096
HEAD_DIM = 64
BS = 256
LANES = 128

eps_norm = 1e-05
masked_score = -1e30
scale = HEAD_DIM**-0.5
bf16 = jnp.bfloat16
f32 = jnp.float32

NT = (((1,), (1,)), ((), ()))
TN = (((0,), (0,)), ((), ()))

VMEM_LIMIT = 60 * 1024 * 1024

ERFC_SLOPE = 0.3
ERFC_POLY = (
    0.1691880090604902,
    0.17071516163759975,
    0.14833963774537734,
    0.21492421686136995,
    -0.09464635292673967,
    0.5477136065073498,
    -0.5122723795383668,
    0.4855603950654946,
    -0.1295223139805042,
)


def dot_nn(a, b):
    return jnp.dot(a, b, preferred_element_type=f32)


def dot_nt(a, b):
    return lax.dot_general(a, b, NT, preferred_element_type=f32)


def dot_tn(a, b):
    return lax.dot_general(a, b, TN, preferred_element_type=f32)


def small():
    return pl.CostEstimate(flops=1 << 20, bytes_accessed=1 << 20, transcendentals=0)


def params(**kw):
    return pltpu.CompilerParams(vmem_limit_bytes=VMEM_LIMIT, **kw)


GROUPS = (
    (("sq", True), ("sk", True), ("sv", True)),
    (("so", False), ("cq", True), ("ck", True), ("cv", True), ("co", False)),
    (("fi", True),),
    (("fo", False),),
)
SHAPES = {name: (D, D) for name in ("sq", "sk", "sv", "so", "cq", "ck", "cv", "co")}
SHAPES["fi"], SHAPES["fo"] = (D, FF), (FF, D)


def chunk_of(i):
    return (i & 8) | ((i & 2) << 1) | ((i & 1) << 1) | ((i & 4) >> 2)


class Net:
    def __init__(self, n_rep, n_shard, n_mp):
        self.n_rep, self.n_shard, self.n_mp = n_rep, n_shard, n_mp
        self.n_data = n_rep * n_shard
        self.pieces = 16 if (n_rep, n_shard, n_mp) == (2, 8, 2) else 1
        self.rows = BS // self.pieces
        self.depth = self.pieces.bit_length() - 1
        x, z1, z2, y = 1, 2, 4, 8
        gathering = (
            ((z2, y, z1, x), (z2, z1, x, y)),
            ((z2, z1, y, x), (z2, z1, x, y)),
            ((z2, x, z1, y), (z2, y, z1, x)),
            ((z2, x, y, z1), (z2, y, z1, x)),
        )
        reducing = (((z2, z1, y, x), (z2, z1, x, y)),) + gathering[1:]
        self.orders = gathering + reducing

    def swap_core(self, value):
        return lax.ppermute(value, "mp", [(i, i ^ 1) for i in range(self.n_mp)])

    def swap_rep(self, value):
        return lax.ppermute(value, "rep", [(i, i ^ 1) for i in range(self.n_rep)])

    def swap_data(self, value, group, step):
        pairs = []
        for i in range(self.n_data):
            for m in range(self.n_mp):
                there = i ^ self.orders[group][m][step]
                pairs.append((i * self.n_mp + m, there * self.n_mp + m))
        return lax.ppermute(value, ("rep", "shard", "mp"), pairs)

    def table(self, group, core, data_index):
        many = self.pieces
        if many == 1:
            return jnp.stack([0, 0, 0, 0, core]).astype(jnp.int32)
        half = many // 4
        rel = []
        for order in self.orders[group]:
            rel.append([sum(b for s, b in enumerate(order) if q >> s & 1) for q in range(many)])
        rows = []
        for m in range(self.n_mp):
            place = [rel[1 - m].index(r) // 2 for r in rel[m][::2]]
            low = [p for p in place if p < half][0]
            high = [p - half for p in place if p >= half][0]
            lows, highs = [], []
            for p in place:
                low, high = (p, high) if p < half else (low, p - half)
                lows.append(low)
                highs.append(high)
            rows.append([chunk_of(r) for r in rel[m]] + lows + highs + [int(p >= half) for p in place])
        mine = jnp.asarray(np.array(rows, np.int32))[core]
        chunks = mine[:many] ^ chunk_of(data_index)
        return jnp.concatenate([chunks, mine[many:], core.reshape(1)]).astype(jnp.int32)


def together(*values):
    return lax.optimization_barrier(values)


class Flow:
    def __init__(self, rounds):
        self.rounds = rounds
        self.flying = next(rounds)

    def advance(self, values):
        try:
            self.flying = self.rounds.send(values)
        except StopIteration as stop:
            self.flying = None
            self.result = stop.value

    def finish(self):
        while self.flying is not None:
            self.advance(self.flying)
        return self.result


def step(main, *flows):
    flows = [f for f in flows if f.flying is not None]
    values = list(together(*main, *[v for f in flows for v in f.flying]))
    main, values = values[: len(main)], values[len(main) :]
    for f in flows:
        many = len(f.flying)
        f.advance(tuple(values[:many]))
        values = values[many:]
    return main


def blocks_of(name, n_mp):
    rows, cols = SHAPES[name]
    return rows * cols // n_mp // (BS * BS)


def group_blocks(group, n_mp):
    return sum(blocks_of(name, n_mp) for name, _ in GROUPS[group])


def place_body(s, *refs, dests, many, two):
    q = pl.program_id(0)
    steps = many // 2 if two else 1
    if two:
        own_lo, own_hi, sib_lo, sib_hi = refs[:4]
        outs = refs[4:]
    else:
        own_lo, sib_lo = refs[:2]
        outs = refs[2:]
    core = s[many + 3 * steps]
    rows = own_lo.shape[2]
    for t in range(own_lo.shape[0]):
        here = pl.ds(0, rows)
        if two:
            here = pl.ds(pl.multiple_of((s[2 * q + t] & 1) * rows, rows), rows)
        for b in range(own_lo.shape[1]):
            own, sib = own_lo[t, b], sib_lo[t, b]
            if two:
                own = jnp.where(q < steps // 2, own, own_hi[t, b])
                sib = jnp.where(s[many + 2 * steps + q] == 0, sib, sib_hi[t, b])
            for h in range(2):
                which, row, col = dests[h][b]
                outs[which][row, here, col : col + BS] = jnp.where(core == h, own, sib)


def place(net, group, table, own, sib):
    many, rows, n_mp = net.pieces, net.rows, net.n_mp
    two = many > 1
    per = 2 if two else 1
    steps = many // per
    half = max(steps // 2, 1)
    dests = ([], [])
    shapes, specs = [], []
    for which, (name, wide) in enumerate(GROUPS[group]):
        height, width = SHAPES[name]
        tall = height if wide else height // n_mp
        flat = width // n_mp if wide else width
        for h in range(n_mp):
            for r in range(tall // BS):
                for c in range(flat // BS):
                    if wide:
                        dests[h].append((which, r, h * flat + c * BS))
                    else:
                        dests[h].append((which, h * (tall // BS) + r, c * BS))
        shapes.append(jax.ShapeDtypeStruct((height // BS, BS, width), bf16))
        specs.append(
            pl.BlockSpec((height // BS, per * rows, width), lambda q, s: (0, s[per * q] // per, 0))
        )
    nb = own[0].shape[1]
    block = (per, nb, rows, BS)
    lo = pl.BlockSpec(block, lambda q, s: (jnp.minimum(q, half - 1), 0, 0, 0))
    hi = pl.BlockSpec(block, lambda q, s: (jnp.maximum(q - half, 0), 0, 0, 0))
    sib_lo = pl.BlockSpec(block, lambda q, s: (s[many + q], 0, 0, 0))
    sib_hi = pl.BlockSpec(block, lambda q, s: (s[many + steps + q], 0, 0, 0))
    out = pl.pallas_call(
        functools.partial(place_body, dests=dests, many=many, two=two),
        grid_spec=pltpu.PrefetchScalarGridSpec(
            num_scalar_prefetch=1,
            grid=(steps,),
            in_specs=[lo, hi, sib_lo, sib_hi] if two else [lo, sib_lo],
            out_specs=tuple(specs),
        ),
        out_shape=tuple(shapes),
        compiler_params=params(),
        cost_estimate=small(),
        name="place",
    )(table, *own, *sib)
    return [o.reshape(-1, o.shape[2]) for o in out]


def gather_rounds(net, group, piece):
    (piece,) = yield (piece,)
    cur = piece[None]
    if net.pieces == 1:
        (sib,) = yield (net.swap_core(cur),)
        return (cur,), (sib,)
    for k in range(net.depth - 1):
        (got,) = yield (net.swap_data(cur, group, k),)
        cur = jnp.concatenate([cur, got])
    got, sib_lo = yield (net.swap_data(cur, group, net.depth - 1), net.swap_core(cur))
    (sib_hi,) = yield (net.swap_core(got),)
    return (cur, got), (sib_lo, sib_hi)


def first_pieces(net, weights, vectors, inverse):
    low = weights[0].astype(bf16)
    vec = vectors.astype(bf16)
    if net.pieces == 1:
        every = lax.all_gather(low, "shard", axis=0, tiled=True)
        vec_every = lax.all_gather(vec, "shard", axis=1, tiled=True)
        return every.at[inverse].get(mode="promise_in_bounds"), vec_every
    nblk = low.shape[0]
    cut = low.reshape(nblk, 2, 2, 2, 2, net.rows, BS)
    cut = lax.dynamic_index_in_dim(cut, lax.axis_index("rep"), axis=1, keepdims=False)
    cut = cut.transpose(3, 1, 2, 0, 4, 5).reshape(net.n_shard, nblk, net.rows, BS)
    room = net.rows * BS
    vec_cut = jnp.pad(vec.reshape(-1), (0, room - vec.shape[1])).reshape(1, 1, net.rows, BS)
    cut = jnp.concatenate([cut, jnp.broadcast_to(vec_cut, (net.n_shard,) + vec_cut.shape[1:])], axis=1)
    every = lax.all_to_all(
        cut.reshape(-1, net.rows, BS), "shard", split_axis=0, concat_axis=0, tiled=True
    )
    pieces = every.at[inverse + inverse // nblk].get(mode="promise_in_bounds")
    vec_every = every.reshape(net.n_shard, nblk + 1, room)[:, nblk, : vec.shape[1]]
    return pieces, vec_every.reshape(1, -1)


def total_of(*terms):
    acc = terms[0].astype(f32)
    for t in terms[1:]:
        acc = acc + t.astype(f32)
    return acc.astype(bf16)


def reduce_rounds(net, group, parts):
    parts = yield parts
    if net.pieces == 1:
        return parts[0][0]
    lo, hi = parts
    (got,) = yield (net.swap_data(hi, group, net.depth - 1),)
    terms = [lo, got]
    for k in range(net.depth - 2, -1, -1):
        width = 1 << k
        send = total_of(*[t[width:] for t in terms])
        keep = total_of(*[t[:width] for t in terms])
        (got,) = yield (net.swap_data(send, group, k),)
        terms = [keep, got]
    return total_of(*terms)[0]


def last_pieces(net, natural, block_slots, vec_sum):
    if net.pieces == 1:
        dealt = natural.at[block_slots].get(mode="promise_in_bounds")
        owned = lax.psum_scatter(dealt, "shard", scatter_dimension=0, tiled=True)
        owned = total_of(owned, net.swap_rep(owned))
        cut = owned.reshape(-1, 2, 8, 16, BS).transpose(1, 2, 0, 3, 4)
        cut = cut[:, np.array([chunk_of(k) for k in range(8)])]
        vec = lax.psum_scatter(vec_sum, "shard", scatter_dimension=0, tiled=True)[None]
        parts = [(cut[0], cut[1], owned.shape[0])]
        return parts, jnp.zeros((1,), jnp.int32), vec + net.swap_rep(vec)
    n = net.n_shard
    slots = block_slots.reshape(n, -1)
    half = slots.shape[1] // 2
    room = net.rows * BS
    vec_cut = vec_sum.reshape(n, -1)
    width = vec_cut.shape[1]
    vec_cut = jnp.pad(vec_cut.astype(bf16), ((0, 0), (0, room - width)))
    vec_cut = vec_cut.reshape(n, 1, net.rows, BS)
    cuts = []
    for k in range(2):
        index = slots[:, k * half : (k + 1) * half].reshape(-1)
        cuts.append(natural.at[index].get(mode="promise_in_bounds").reshape(n, half, net.rows, BS))
    cuts[1] = jnp.concatenate([cuts[1], vec_cut], axis=1)

    def home(cut):
        back = lax.all_to_all(
            cut.reshape(-1, net.rows, BS), "shard", split_axis=0, concat_axis=0, tiled=True
        )
        return back.reshape(n, -1, net.rows, BS)

    mine, cuts[1] = together(home(cuts[0]), cuts[1])
    other = net.swap_rep(mine)
    other, last = together(other, home(cuts[1]))
    parts = [(mine, other, half), (last, net.swap_rep(last), half)]
    terms = [v[:, half].reshape(n, room)[:, :width].astype(f32) for v in parts[1][:2]]
    flag = lax.axis_index("rep").astype(jnp.int32).reshape(1)
    return parts, flag, jnp.sum(terms[0] + terms[1], axis=0, keepdims=True)


def attend_forward_body(lim, q_ref, k_ref, v_ref, o_ref, lse_ref, *, causal, rows):
    pair = pl.program_id(0)
    seq, keys = q_ref.shape[0], k_ref.shape[0]
    lane = lax.broadcasted_iota(jnp.int32, (1, LANES), 1)
    top = lim[0] - 1

    @pl.when(pair == 0)
    def _():
        lse_ref[...] = jnp.zeros_like(lse_ref)

    for blk in range(seq // rows):
        here = pl.ds(blk * rows, rows)
        width = (blk + 1) * rows if causal else keys
        q = q_ref[here, :] * bf16(scale)
        k = k_ref[pl.ds(0, width), :]
        v = v_ref[pl.ds(0, width), :]
        outs = []
        kept = lse_ref[here, :]
        if causal:
            row = lax.broadcasted_iota(jnp.int32, (rows, 1), 0) + blk * rows
            col = lax.broadcasted_iota(jnp.int32, (1, width), 1)
            allowed = col <= jnp.minimum(row, top)
        for h in range(2):
            mine = (lane // HEAD_DIM) == h
            s = dot_nt(jnp.where(mine, q, bf16(0)), k)
            if causal:
                s = jnp.where(allowed, s, masked_score)
            peak = jnp.max(s, axis=1, keepdims=True)
            e = jnp.exp(s - peak)
            mass = jnp.sum(e, axis=1, keepdims=True)
            outs.append(dot_nn(e.astype(bf16), v) * (1.0 / mass))
            kept = jnp.where(lane == 2 * pair + h, peak + jnp.log(mass), kept)
        o_ref[here, :] = jnp.where(lane < HEAD_DIM, outs[0], outs[1]).astype(bf16)
        lse_ref[here, :] = kept


def attend_forward(limit, q, k, v, causal):
    seq, width = q.shape
    keys = k.shape[0]
    pairs = width // LANES
    rows = min(128 if causal else 256, seq)
    o, lse = pl.pallas_call(
        functools.partial(attend_forward_body, causal=causal, rows=rows),
        grid=(pairs,),
        out_shape=(
            jax.ShapeDtypeStruct((seq, width), bf16),
            jax.ShapeDtypeStruct((seq, LANES), f32),
        ),
        in_specs=[
            pl.BlockSpec(memory_space=pltpu.SMEM),
            pl.BlockSpec((seq, LANES), lambda i: (0, i)),
            pl.BlockSpec((keys, LANES), lambda i: (0, i)),
            pl.BlockSpec((keys, LANES), lambda i: (0, i)),
        ],
        out_specs=(
            pl.BlockSpec((seq, LANES), lambda i: (0, i)),
            pl.BlockSpec((seq, LANES), lambda i: (0, 0)),
        ),
        compiler_params=params(),
        cost_estimate=small(),
        name="attend_forward",
    )(limit, q, k, v)
    return o, lse[:, : 2 * pairs].T.reshape(pairs, 2, seq)


def attend_backward_body(
    lim, q_ref, k_ref, v_ref, o_ref, do_ref, lse_ref, dq_ref, dk_ref, dv_ref, dk_acc, dv_acc, *, causal, rows
):
    seq, keys = q_ref.shape[0], k_ref.shape[0]
    lane = lax.broadcasted_iota(jnp.int32, (1, LANES), 1)
    top = lim[0] - 1
    dk_acc[...] = jnp.zeros_like(dk_acc)
    dv_acc[...] = jnp.zeros_like(dv_acc)
    head_row = lax.broadcasted_iota(jnp.int32, (8, LANES), 0)
    head_lane = lax.broadcasted_iota(jnp.int32, (8, LANES), 1) // HEAD_DIM
    pick = (head_row == head_lane).astype(bf16)
    for blk in range(seq // rows):
        here = pl.ds(blk * rows, rows)
        width = (blk + 1) * rows if causal else keys
        span = pl.ds(0, width)
        q = q_ref[here, :] * bf16(scale)
        do = do_ref[here, :]
        k = k_ref[span, :]
        v = v_ref[span, :]
        prod = do.astype(f32) * o_ref[here, :].astype(f32)
        hi = prod.astype(bf16)
        lo = (prod - hi.astype(f32)).astype(bf16)
        delta = dot_nt(pick, hi) + dot_nt(pick, lo)
        lse = lse_ref[0][:, blk * rows : (blk + 1) * rows]
        if causal:
            key = lax.broadcasted_iota(jnp.int32, (width, 1), 0)
            row = lax.broadcasted_iota(jnp.int32, (1, rows), 1) + blk * rows
            allowed = key <= jnp.minimum(row, top)
        dq = jnp.zeros((rows, LANES), f32)
        dk = jnp.zeros((width, LANES), f32)
        dv = jnp.zeros((width, LANES), f32)
        for h in range(2):
            mine = (lane // HEAD_DIM) == h
            qm = jnp.where(mine, q, bf16(0))
            dom = jnp.where(mine, do, bf16(0))
            km = jnp.where(mine, k, bf16(0))
            s = dot_nt(k, qm)
            if causal:
                s = jnp.where(allowed, s, masked_score)
            p = jnp.exp(s - lse[h : h + 1, :])
            dp = dot_nt(v, dom)
            ds = (p * (dp - delta[h : h + 1, :])).astype(bf16)
            dv = dv + dot_nn(p.astype(bf16), dom)
            dk = dk + dot_nn(ds, qm)
            dq = dq + dot_tn(ds, km)
        dq_ref[here, :] = (dq * scale).astype(bf16)
        dk_acc[span, :] += dk
        dv_acc[span, :] += dv
    dk_ref[...] = dk_acc[...].astype(bf16)
    dv_ref[...] = dv_acc[...].astype(bf16)


def attend_backward(limit, q, k, v, o, do, lse, causal):
    seq, width = q.shape
    keys = k.shape[0]
    pairs = width // LANES
    rows = min(128 if causal else 256, seq)
    q_spec = pl.BlockSpec((seq, LANES), lambda i: (0, i))
    k_spec = pl.BlockSpec((keys, LANES), lambda i: (0, i))
    return pl.pallas_call(
        functools.partial(attend_backward_body, causal=causal, rows=rows),
        grid=(pairs,),
        out_shape=(
            jax.ShapeDtypeStruct((seq, width), bf16),
            jax.ShapeDtypeStruct((keys, width), bf16),
            jax.ShapeDtypeStruct((keys, width), bf16),
        ),
        in_specs=[
            pl.BlockSpec(memory_space=pltpu.SMEM),
            q_spec,
            k_spec,
            k_spec,
            q_spec,
            q_spec,
            pl.BlockSpec((1, 2, seq), lambda i: (i, 0, 0)),
        ],
        out_specs=(q_spec, k_spec, k_spec),
        scratch_shapes=[pltpu.VMEM((keys, LANES), f32), pltpu.VMEM((keys, LANES), f32)],
        compiler_params=params(),
        cost_estimate=small(),
        name="attend_backward",
    )(limit, q, k, v, o, do, lse)


def gelu_body(h_ref, w_ref, b_ref, act_ref, slope_ref, u_ref, *, chunk):
    u_ref[...] = dot_nn(h_ref[...], w_ref[...]) + b_ref[...]

    def part(i):
        here = pl.ds(pl.multiple_of(i * chunk, chunk), chunk)
        u = u_ref[here, :]
        x = jnp.abs(u) * (0.5**0.5)
        t = 1.0 / (1.0 + ERFC_SLOPE * x)
        poly = jnp.full_like(t, ERFC_POLY[-1])
        for c in ERFC_POLY[-2::-1]:
            poly = poly * t + c
        bell = jnp.exp(-0.5 * (u * u))
        tail = 0.5 * (bell * (t * poly))
        cdf = jnp.where(u < 0, tail, 1.0 - tail)
        act_ref[here, :] = (u * cdf).astype(bf16)
        slope_ref[here, :] = (cdf + u * (bell * 0.3989422804014327)).astype(bf16)

    pl.loop(0, u_ref.shape[0] // chunk)(part)


def gelu_forward(h, w, b):
    seq, width = h.shape
    hidden = w.shape[1]
    tile = 512
    spec = pl.BlockSpec((seq, tile), lambda i: (0, i))
    return pl.pallas_call(
        functools.partial(gelu_body, chunk=32),
        grid=(hidden // tile,),
        out_shape=(jax.ShapeDtypeStruct((seq, hidden), bf16),) * 2,
        in_specs=[
            pl.BlockSpec((seq, width), lambda i: (0, 0)),
            pl.BlockSpec((width, tile), lambda i: (0, i)),
            pl.BlockSpec((1, tile), lambda i: (0, i)),
        ],
        out_specs=(spec, spec),
        scratch_shapes=[pltpu.VMEM((seq, tile), f32)],
        compiler_params=params(),
        cost_estimate=small(),
        name="gelu_forward",
    )(h, w, b)


def weight_grad_body(s, x_own, x_sib, *refs, count, outs, many, rows):
    y_own, y_sib = refs[:count], refs[count : 2 * count]
    targets = refs[-3 - outs : -3]
    t_own, t_sib, buf = refs[-3:]
    t_own[...] = x_own[...].T
    t_sib[...] = x_sib[...].T
    per = many // outs
    for k in range(count):
        acc = dot_nn(t_own[...], y_own[k][...]) + dot_nn(t_sib[...], y_sib[k][...])
        buf[k] = acc.astype(bf16)
    for q in range(many):
        here = pl.ds(pl.multiple_of(s[q] * rows, rows), rows)
        for k in range(count):
            for c in range(targets[0].shape[2]):
                targets[q // per][q % per, k, c] = buf[k, here, c * BS : (c + 1) * BS]


def weight_grad(net, group, table, xs, ys, held, first, wide):
    seq = xs[0].shape[0]
    many, rows, halves = net.pieces, net.rows, net.n_mp
    at_core = table.shape[0] - 1
    count = len(ys)
    width = ys[0][0].shape[1]
    if wide:
        steps = xs[0].shape[1] // BS
        y_width = width // halves
        x_spec = pl.BlockSpec((seq, BS), lambda i, s: (0, i))
        y_spec = pl.BlockSpec((seq, y_width), lambda i, s: (0, s[at_core]))
    else:
        steps = xs[0].shape[1] // halves // BS
        y_width = width
        x_spec = pl.BlockSpec((seq, BS), lambda i, s: (0, s[at_core] * steps + i))
        y_spec = pl.BlockSpec((seq, y_width), lambda i, s: (0, 0))
    nb = y_width // BS
    at = first // count
    outs = 2 if many > 1 else 1
    shape = (many // outs, len(GROUPS[group]), steps * nb, rows, BS)
    anyspec = pl.BlockSpec(memory_space=pl.ANY)
    held = held or ()
    before = 3 + 2 * count
    return pl.pallas_call(
        functools.partial(weight_grad_body, count=count, outs=outs, many=many, rows=rows),
        grid_spec=pltpu.PrefetchScalarGridSpec(
            num_scalar_prefetch=1,
            grid=(steps,),
            in_specs=[x_spec] * 2 + [y_spec] * (2 * count) + [anyspec] * len(held),
            out_specs=(
                pl.BlockSpec((many // outs, count, nb, rows, BS), lambda i, s: (0, at, i, 0, 0)),
            )
            * outs,
            scratch_shapes=[
                pltpu.VMEM((BS, seq), bf16),
                pltpu.VMEM((BS, seq), bf16),
                pltpu.VMEM((count, BS, y_width), bf16),
            ],
        ),
        out_shape=(jax.ShapeDtypeStruct(shape, bf16),) * outs,
        input_output_aliases={before + k: k for k in range(len(held))},
        compiler_params=params(),
        cost_estimate=small(),
        name="weight_grad",
    )(table, *xs, *[y[0] for y in ys], *[y[1] for y in ys], *held)


def split_low(a):
    hi = a.astype(bf16)
    return hi, (a - hi.astype(f32)).astype(bf16)


def shampoo_body(flag, mine_ref, other_ref, w_ref, ls_ref, rs_ref, lr_ref, rr_ref, *refs):
    og, ol, orr, ow, g_ref = refs[-5:]
    for k in range(mine_ref.shape[0]):
        for plane, src in ((flag[0], mine_ref), (1 - flag[0], other_ref)):
            row = pl.multiple_of(plane * 128 + chunk_of(k) * 16, 16)
            g_ref[pl.ds(row, 16), :] = src[k, 0]
    g = g_ref[...]
    og[0, 0] = g.astype(f32)
    ol[0, 0] = 0.5 * ls_ref[0, 0] + 0.5 * dot_nt(g, g)
    orr[0, 0] = 0.5 * rs_ref[0, 0] + 0.5 * dot_tn(g, g)
    r_hi, r_lo = split_low(rr_ref[0, 0])
    i_hi, i_lo = split_low(dot_nn(g, r_hi) + dot_nn(g, r_lo))
    l_hi, l_lo = split_low(lr_ref[0, 0])
    d = dot_nn(l_hi, i_hi) + (dot_nn(l_hi, i_lo) + dot_nn(l_lo, i_hi))
    mean = jnp.mean(jnp.mean(d * d, axis=1, keepdims=True), axis=0, keepdims=True)
    ow[0, 0] = w_ref[0, 0] - (D**-0.5) * d / jnp.sqrt(mean + 1e-06)


def shampoo(flag, parts, *states):
    total = states[0].shape[1]
    out, first = (), 0
    for mine, other, n in parts:
        at = first // n
        spec = pl.BlockSpec((1, 1, BS, BS), lambda i, at=at, n=n: (0, at * n + i, 0, 0))
        g_spec = pl.BlockSpec((mine.shape[0], 1, mine.shape[2], BS), lambda i: (0, i, 0, 0))
        anyspec = pl.BlockSpec(memory_space=pl.ANY)
        out = pl.pallas_call(
            shampoo_body,
            grid=(n,),
            out_shape=(jax.ShapeDtypeStruct((1, total, BS, BS), f32),) * 4,
            in_specs=[pl.BlockSpec(memory_space=pltpu.SMEM), g_spec, g_spec]
            + [spec] * 5
            + [anyspec] * len(out),
            out_specs=(spec,) * 4,
            scratch_shapes=[pltpu.VMEM((BS, BS), bf16)],
            input_output_aliases={8 + k: k for k in range(len(out))},
            compiler_params=params(),
            cost_estimate=small(),
            name="shampoo",
        )(flag, mine, other, *states, *out)
        first += n
    return out


def norm_forward(z, gain, shift):
    center = z - jnp.mean(z, axis=1, keepdims=True)
    inv = lax.rsqrt(jnp.mean(center * center, axis=1, keepdims=True) + eps_norm)
    normed = center * inv
    return normed * gain + shift, normed, inv


def norm_backward(grad, normed, inv, gain):
    scaled = grad * gain
    mean_plain = jnp.mean(scaled, axis=1, keepdims=True)
    mean_cross = jnp.mean(scaled * normed, axis=1, keepdims=True)
    back = inv * (scaled - mean_plain - normed * mean_cross)
    return back, jnp.sum(grad * normed, axis=0), jnp.sum(grad, axis=0)


def inverse_of(order):
    many = jnp.arange(order.shape[0], dtype=jnp.int32)
    return jnp.sum(jnp.where(order[:, None] == many[None, :], many[:, None], 0), axis=0)


def route_out(value):
    axes = ("rep", "shard")
    count = lax.axis_size(axes)
    cut = value.reshape(value.shape[0], count, value.shape[1] // count, value.shape[2])
    return lax.all_to_all(cut, axes, split_axis=1, concat_axis=0, tiled=True)


def route_home(pieces, ordering):
    moved = pieces.at[ordering].get(mode="promise_in_bounds")
    back = lax.all_to_all(moved, ("rep", "shard"), split_axis=0, concat_axis=1, tiled=True)
    return back.reshape(back.shape[0], -1, back.shape[3])


def per_device(
    net,
    inputs,
    encoded,
    cotangent,
    lengths,
    seq_slots,
    block_slots,
    weights,
    left_stat,
    right_stat,
    left_root,
    right_root,
    vectors,
    vec_stat,
):
    half_d = inputs.shape[2]
    halves = D // half_d
    core = lax.axis_index("mp")
    data_index = lax.axis_index(("rep", "shard"))
    seq_index = data_index * inputs.shape[0] + core
    limit = lax.dynamic_slice_in_dim(lengths, seq_index, 1)
    tables = [net.table(k, core, data_index) for k in range(2 * len(GROUPS))]
    is_first = core == 0

    def pick(pair, which):
        return lax.dynamic_index_in_dim(pair, which, axis=0, keepdims=False)

    def joined(low_half, high_half):
        return jnp.concatenate(
            [
                jnp.where(is_first, low_half, high_half),
                jnp.where(is_first, high_half, low_half),
            ],
            axis=1,
        )

    def whole(value):
        other = net.swap_core(value)
        own = joined(pick(value, core), pick(other, core))
        sib = joined(pick(value, 1 - core), pick(other, 1 - core))
        return own, sib

    def halved(full):
        mine = lax.dynamic_slice_in_dim(full, core * half_d, half_d, axis=1)
        away = lax.dynamic_slice_in_dim(full, (1 - core) * half_d, half_d, axis=1)
        got = net.swap_core(away)
        return jnp.stack([jnp.where(is_first, mine, got), jnp.where(is_first, got, mine)])

    x, x_sib = whole(inputs)
    e, e_sib = whole(encoded)

    pieces, vec_mine = first_pieces(net, weights, vectors, inverse_of(block_slots))
    flows, base = [], 0
    for k in range(len(GROUPS)):
        size = group_blocks(k, halves)
        flows.append(Flow(gather_rounds(net, k, pieces[base : base + size])))
        base += size
    attn, cross, up, down = flows

    def placed(k):
        return place(net, k, tables[k], *flows[k].finish())

    step((), attn)
    step((), attn, cross)
    step((), attn)
    step((), attn, cross)
    vec_mine, x, x_sib, e, e_sib = step((vec_mine, x, x_sib, e, e_sib), attn, cross, up)
    w_sq, w_sk, w_sv = step(placed(0), up)

    vec_other = net.swap_core(vec_mine)
    vec_both = jnp.concatenate(
        [jnp.where(is_first, vec_mine, vec_other), jnp.where(is_first, vec_other, vec_mine)]
    ).astype(f32)
    vecs = [vec_both[:, i * half_d : (i + 1) * half_d].reshape(1, D) for i in range(13)]
    vecs.append(vec_both[:, 13 * half_d :].reshape(1, FF))
    b_sq, b_sv, b_so, g_one, b_one, b_cq, b_cv, b_co, g_two, b_two, b_fo, g_three, b_three, b_fi = vecs

    q_s = (dot_nn(x, w_sq) + b_sq).astype(bf16)
    k_s = dot_nn(x, w_sk).astype(bf16)
    v_s = (dot_nn(x, w_sv) + b_sv).astype(bf16)
    q_s, k_s, v_s = step((q_s, k_s, v_s), cross, up, down)
    o_s, lse_s = attend_forward(limit, q_s, k_s, v_s, True)
    cotangent, o_s, lse_s = step((cotangent, o_s, lse_s), cross, up, down)
    cot_pieces = route_out(cotangent)
    w_so, w_cq, w_ck, w_cv, w_co = placed(1)
    z_one = x.astype(f32) + dot_nn(o_s, w_so) + b_so
    h_one, n_one, r_one = norm_forward(z_one, g_one, b_one)
    h_one_low = h_one.astype(bf16)
    q_c = (dot_nn(h_one_low, w_cq) + b_cq).astype(bf16)
    k_c = dot_nn(e, w_ck).astype(bf16)
    v_c = (dot_nn(e, w_cv) + b_cv).astype(bf16)
    q_c, k_c, v_c = step((q_c, k_c, v_c), down)
    o_c, lse_c = attend_forward(limit, q_c, k_c, v_c, False)
    z_two = h_one + dot_nn(o_c, w_co) + b_co
    h_two, n_two, r_two = norm_forward(z_two, g_two, b_two)
    cot_pieces, h_two, h_two_low = step((cot_pieces, h_two, h_two.astype(bf16)), up, down)
    cot_home = route_home(cot_pieces, seq_slots)
    (w_fi,) = placed(2)
    act, slope = gelu_forward(h_two_low, w_fi, b_fi)
    act_sib = net.swap_core(act)
    act, slope = step((act, slope), down)
    (w_fo,) = placed(3)
    z_three = h_two + dot_nn(act, w_fo) + b_fo
    cot_home, z_three = step((cot_home, z_three))
    cot, _ = whole(cot_home)
    h_three, n_three, r_three = norm_forward(z_three, g_three, b_three)
    live = (jnp.arange(x.shape[0]) < limit).astype(f32)[:, None]
    source = inverse_of(seq_slots)
    finished = (h_three * live).astype(bf16)

    def gradient(k, *calls):
        held, first = None, 0
        for xs, *ys in calls:
            held = weight_grad(net, k, tables[len(GROUPS) + k], xs, ys, held, first, GROUPS[k][first][1])
            first += len(ys)
        parts = tuple(h.reshape(h.shape[0], -1, net.rows, BS) for h in held)
        return Flow(reduce_rounds(net, len(GROUPS) + k, parts))

    grad_y = cot.astype(f32) * live
    d_three, dg_three, db_three = norm_backward(grad_y, n_three, r_three, g_three)
    a_three = d_three.astype(bf16)
    d_hidden = (dot_nt(a_three, w_fo) * slope.astype(f32)).astype(bf16)
    d_hidden_sib = net.swap_core(d_hidden)
    down = gradient(3, ((act, act_sib), (a_three, net.swap_core(a_three))))
    finished, d_hidden, d_hidden_sib = step((finished, d_hidden, d_hidden_sib), down)
    finished = halved(finished)
    d_h_two = d_three + dot_nt(d_hidden, w_fi)
    d_two, dg_two, db_two = norm_backward(d_h_two, n_two, r_two, g_two)
    a_two = d_two.astype(bf16)
    d_oc = dot_nt(a_two, w_co).astype(bf16)
    finished, d_hidden, d_hidden_sib, d_oc = step((finished, d_hidden, d_hidden_sib, d_oc))
    out_pieces = route_out(finished)
    up = gradient(2, ((h_two_low, net.swap_core(h_two_low)), (d_hidden, d_hidden_sib)))
    (d_oc,) = step((d_oc,), up, down)
    dq_c, dk_c, dv_c = attend_backward(limit, q_c, k_c, v_c, o_c, d_oc, lse_c, False)
    dq_c_sib, dk_c_sib, dv_c_sib = [net.swap_core(v) for v in (dq_c, dk_c, dv_c)]
    dq_c, dk_c, dv_c = step((dq_c, dk_c, dv_c), down)
    d_h_one = d_two + dot_nt(dq_c, w_cq)
    d_one, dg_one, db_one = norm_backward(d_h_one, n_one, r_one, g_one)
    a_one = d_one.astype(bf16)
    a_one_sib = net.swap_core(a_one)
    d_os = dot_nt(a_one, w_so).astype(bf16)
    out_pieces, a_one, a_one_sib, d_os = step((out_pieces, a_one, a_one_sib, d_os))
    outputs = route_home(out_pieces, source)
    cross = gradient(
        1,
        ((o_s, net.swap_core(o_s)), (a_one, a_one_sib)),
        ((h_one_low, net.swap_core(h_one_low)), (dq_c, dq_c_sib)),
        ((e, e_sib), (dk_c, dk_c_sib), (dv_c, dv_c_sib)),
        ((o_c, net.swap_core(o_c)), (a_two, net.swap_core(a_two))),
    )
    outputs, d_os = step((outputs, d_os), cross, up, down)
    dq_s, dk_s, dv_s = attend_backward(limit, q_s, k_s, v_s, o_s, d_os, lse_s, True)
    sibs = [net.swap_core(v) for v in (dq_s, dk_s, dv_s)]
    dq_s, dk_s, dv_s = step((dq_s, dk_s, dv_s), cross, up)
    attn = gradient(0, ((x, x_sib), *zip((dq_s, dk_s, dv_s), sibs)))
    dk_c, dv_c, dq_s, dk_s, dv_s = step((dk_c, dv_c, dq_s, dk_s, dv_s), attn, cross, up, down)
    state_back = dot_nt(dk_c, w_ck) + dot_nt(dv_c, w_cv)
    back = d_one + dot_nt(dq_s, w_sq) + dot_nt(dk_s, w_sk) + dot_nt(dv_s, w_sv)
    back, d_hidden, dq_c, dv_c = step((back, d_hidden, dq_c, dv_c), attn, cross, up)
    input_grad = halved(back.astype(bf16))
    encoded_grad = halved(state_back.astype(bf16))
    dq_s, dv_s = step((dq_s, dv_s), attn)
    columns = [jnp.sum(v.astype(f32), axis=0) for v in (d_hidden, dq_c, dv_c, dq_s, dv_s)]
    *columns, input_grad, encoded_grad = step((*columns, input_grad, encoded_grad), attn, cross)
    sums = (
        columns[3],
        columns[4],
        jnp.sum(d_one, axis=0),
        dg_one,
        db_one,
        columns[1],
        columns[2],
        jnp.sum(d_two, axis=0),
        dg_two,
        db_two,
        jnp.sum(d_three, axis=0),
        dg_three,
        db_three,
        columns[0],
    )
    vec_pair = jnp.concatenate([s.reshape(halves, -1) for s in sums], axis=1)
    vec_sum = pick(vec_pair, core) + net.swap_core(pick(vec_pair, 1 - core))
    natural = [f.finish() for f in (attn, cross, up, down)]

    parts, flag, vec_owned = last_pieces(net, jnp.concatenate(natural), block_slots, vec_sum)
    block_grad, left_new, right_new, weights_new = shampoo(
        flag, parts, weights, left_stat, right_stat, left_root, right_root
    )
    vec_stat_new = 0.5 * vec_stat + 0.5 * vec_owned * vec_owned
    vectors_new = vectors - 0.1 * vec_owned * lax.rsqrt(vec_stat_new)
    return (
        outputs,
        input_grad,
        encoded_grad,
        block_grad,
        left_new,
        right_new,
        weights_new,
        vec_owned,
        vec_stat_new,
        vectors_new,
    )


def solution(mesh):
    net = Net(mesh.shape["rep"], mesh.shape["shard"], mesh.shape["mp"])
    rows = P(("rep", "shard"), None, "mp")
    blocks = P("mp", "shard", None, None)
    vector = P("mp", "shard")
    in_specs = (rows, rows, rows, P(), P(), P()) + (blocks,) * 5 + (vector, vector)
    out_specs = (rows, rows, rows) + (blocks,) * 4 + (vector,) * 3
    return jax.shard_map(
        functools.partial(per_device, net),
        mesh=mesh,
        in_specs=in_specs,
        out_specs=out_specs,
        check_vma=False,
    )
```

```python
import functools

import jax
import jax.numpy as jnp
import numpy as np
from jax import lax
from jax.experimental import pallas as pl
from jax.experimental.pallas import tpu as pltpu
from jax.sharding import PartitionSpec as P

D = 1024
FF = 4096
HEAD_DIM = 64
BS = 256
LANES = 128

eps_norm = 1e-05
masked_score = -1e30
scale = HEAD_DIM**-0.5
bf16 = jnp.bfloat16
f32 = jnp.float32

NT = (((1,), (1,)), ((), ()))
TN = (((0,), (0,)), ((), ()))

VMEM_LIMIT = 60 * 1024 * 1024

ERFC_SLOPE = 0.3
ERFC_POLY = (
    0.1691880090604902,
    0.17071516163759975,
    0.14833963774537734,
    0.21492421686136995,
    -0.09464635292673967,
    0.5477136065073498,
    -0.5122723795383668,
    0.4855603950654946,
    -0.1295223139805042,
)


def dot_nn(a, b):
    return jnp.dot(a, b, preferred_element_type=f32)


def dot_nt(a, b):
    return lax.dot_general(a, b, NT, preferred_element_type=f32)


def dot_tn(a, b):
    return lax.dot_general(a, b, TN, preferred_element_type=f32)


def small():
    return pl.CostEstimate(flops=1 << 20, bytes_accessed=1 << 20, transcendentals=0)


def params(**kw):
    return pltpu.CompilerParams(vmem_limit_bytes=VMEM_LIMIT, **kw)


GROUPS = (
    (("sq", True), ("sk", True), ("sv", True)),
    (("so", False), ("cq", True), ("ck", True), ("cv", True), ("co", False)),
    (("fi", True),),
    (("fo", False),),
)
SHAPES = {name: (D, D) for name in ("sq", "sk", "sv", "so", "cq", "ck", "cv", "co")}
SHAPES["fi"], SHAPES["fo"] = (D, FF), (FF, D)


def chunk_of(i):
    return (i & 8) | ((i & 2) << 1) | ((i & 1) << 1) | ((i & 4) >> 2)


class Net:
    def __init__(self, n_rep, n_shard, n_mp):
        self.n_rep, self.n_shard, self.n_mp = n_rep, n_shard, n_mp
        self.n_data = n_rep * n_shard
        self.pieces = 16 if (n_rep, n_shard, n_mp) == (2, 8, 2) else 1
        self.rows = BS // self.pieces
        self.depth = self.pieces.bit_length() - 1
        x, z1, z2, y = 1, 2, 4, 8
        gathering = (
            ((z2, y, z1, x), (z2, z1, x, y)),
            ((z2, z1, y, x), (z2, z1, x, y)),
            ((z2, x, z1, y), (z2, y, z1, x)),
            ((z2, x, y, z1), (z2, y, z1, x)),
        )
        reducing = (((z2, z1, y, x), (z2, z1, x, y)),) + gathering[1:]
        self.orders = gathering + reducing

    def swap_core(self, value):
        return lax.ppermute(value, "mp", [(i, i ^ 1) for i in range(self.n_mp)])

    def swap_rep(self, value):
        return lax.ppermute(value, "rep", [(i, i ^ 1) for i in range(self.n_rep)])

    def swap_data(self, value, group, step):
        pairs = []
        for i in range(self.n_data):
            for m in range(self.n_mp):
                there = i ^ self.orders[group][m][step]
                pairs.append((i * self.n_mp + m, there * self.n_mp + m))
        return lax.ppermute(value, ("rep", "shard", "mp"), pairs)

    def table(self, group, core, data_index):
        many = self.pieces
        if many == 1:
            return jnp.stack([0, 0, 0, 0, core]).astype(jnp.int32)
        half = many // 4
        rel = []
        for order in self.orders[group]:
            rel.append([sum(b for s, b in enumerate(order) if q >> s & 1) for q in range(many)])
        rows = []
        for m in range(self.n_mp):
            place = [rel[1 - m].index(r) // 2 for r in rel[m][::2]]
            low = [p for p in place if p < half][0]
            high = [p - half for p in place if p >= half][0]
            lows, highs = [], []
            for p in place:
                low, high = (p, high) if p < half else (low, p - half)
                lows.append(low)
                highs.append(high)
            rows.append([chunk_of(r) for r in rel[m]] + lows + highs + [int(p >= half) for p in place])
        mine = jnp.asarray(np.array(rows, np.int32))[core]
        chunks = mine[:many] ^ chunk_of(data_index)
        return jnp.concatenate([chunks, mine[many:], core.reshape(1)]).astype(jnp.int32)


def together(*values):
    return lax.optimization_barrier(values)


class Flow:
    def __init__(self, rounds):
        self.rounds = rounds
        self.flying = next(rounds)

    def advance(self, values):
        try:
            self.flying = self.rounds.send(values)
        except StopIteration as stop:
            self.flying = None
            self.result = stop.value

    def finish(self):
        while self.flying is not None:
            self.advance(self.flying)
        return self.result


def step(main, *flows):
    flows = [f for f in flows if f.flying is not None]
    values = list(together(*main, *[v for f in flows for v in f.flying]))
    main, values = values[: len(main)], values[len(main) :]
    for f in flows:
        many = len(f.flying)
        f.advance(tuple(values[:many]))
        values = values[many:]
    return main


def blocks_of(name, n_mp):
    rows, cols = SHAPES[name]
    return rows * cols // n_mp // (BS * BS)


def group_blocks(group, n_mp):
    return sum(blocks_of(name, n_mp) for name, _ in GROUPS[group])


def place_body(s, *refs, dests, many, two):
    q = pl.program_id(0)
    steps = many // 2 if two else 1
    if two:
        own_lo, own_hi, sib_lo, sib_hi = refs[:4]
        outs = refs[4:]
    else:
        own_lo, sib_lo = refs[:2]
        outs = refs[2:]
    core = s[many + 3 * steps]
    rows = own_lo.shape[2]
    for t in range(own_lo.shape[0]):
        here = pl.ds(0, rows)
        if two:
            here = pl.ds(pl.multiple_of((s[2 * q + t] & 1) * rows, rows), rows)
        for b in range(own_lo.shape[1]):
            own, sib = own_lo[t, b], sib_lo[t, b]
            if two:
                own = jnp.where(q < steps // 2, own, own_hi[t, b])
                sib = jnp.where(s[many + 2 * steps + q] == 0, sib, sib_hi[t, b])
            for h in range(2):
                which, row, col = dests[h][b]
                outs[which][row, here, col : col + BS] = jnp.where(core == h, own, sib)


def place(net, group, table, own, sib):
    many, rows, n_mp = net.pieces, net.rows, net.n_mp
    two = many > 1
    per = 2 if two else 1
    steps = many // per
    half = max(steps // 2, 1)
    dests = ([], [])
    shapes, specs = [], []
    for which, (name, wide) in enumerate(GROUPS[group]):
        height, width = SHAPES[name]
        tall = height if wide else height // n_mp
        flat = width // n_mp if wide else width
        for h in range(n_mp):
            for r in range(tall // BS):
                for c in range(flat // BS):
                    if wide:
                        dests[h].append((which, r, h * flat + c * BS))
                    else:
                        dests[h].append((which, h * (tall // BS) + r, c * BS))
        shapes.append(jax.ShapeDtypeStruct((height // BS, BS, width), bf16))
        specs.append(
            pl.BlockSpec((height // BS, per * rows, width), lambda q, s: (0, s[per * q] // per, 0))
        )
    nb = own[0].shape[1]
    block = (per, nb, rows, BS)
    lo = pl.BlockSpec(block, lambda q, s: (jnp.minimum(q, half - 1), 0, 0, 0))
    hi = pl.BlockSpec(block, lambda q, s: (jnp.maximum(q - half, 0), 0, 0, 0))
    sib_lo = pl.BlockSpec(block, lambda q, s: (s[many + q], 0, 0, 0))
    sib_hi = pl.BlockSpec(block, lambda q, s: (s[many + steps + q], 0, 0, 0))
    out = pl.pallas_call(
        functools.partial(place_body, dests=dests, many=many, two=two),
        grid_spec=pltpu.PrefetchScalarGridSpec(
            num_scalar_prefetch=1,
            grid=(steps,),
            in_specs=[lo, hi, sib_lo, sib_hi] if two else [lo, sib_lo],
            out_specs=tuple(specs),
        ),
        out_shape=tuple(shapes),
        compiler_params=params(),
        cost_estimate=small(),
        name="place",
    )(table, *own, *sib)
    return [o.reshape(-1, o.shape[2]) for o in out]


def gather_rounds(net, group, piece):
    (piece,) = yield (piece,)
    cur = piece[None]
    if net.pieces == 1:
        (sib,) = yield (net.swap_core(cur),)
        return (cur,), (sib,)
    for k in range(net.depth - 1):
        (got,) = yield (net.swap_data(cur, group, k),)
        cur = jnp.concatenate([cur, got])
    got, sib_lo = yield (net.swap_data(cur, group, net.depth - 1), net.swap_core(cur))
    (sib_hi,) = yield (net.swap_core(got),)
    return (cur, got), (sib_lo, sib_hi)


def first_pieces(net, weights, vectors, inverse):
    low = weights[0].astype(bf16)
    vec = vectors.astype(bf16)
    if net.pieces == 1:
        every = lax.all_gather(low, "shard", axis=0, tiled=True)
        vec_every = lax.all_gather(vec, "shard", axis=1, tiled=True)
        return every.at[inverse].get(mode="promise_in_bounds"), vec_every
    nblk = low.shape[0]
    cut = low.reshape(nblk, 2, 2, 2, 2, net.rows, BS)
    cut = lax.dynamic_index_in_dim(cut, lax.axis_index("rep"), axis=1, keepdims=False)
    cut = cut.transpose(3, 1, 2, 0, 4, 5).reshape(net.n_shard, nblk, net.rows, BS)
    room = net.rows * BS
    vec_cut = jnp.pad(vec.reshape(-1), (0, room - vec.shape[1])).reshape(1, 1, net.rows, BS)
    cut = jnp.concatenate([cut, jnp.broadcast_to(vec_cut, (net.n_shard,) + vec_cut.shape[1:])], axis=1)
    every = lax.all_to_all(
        cut.reshape(-1, net.rows, BS), "shard", split_axis=0, concat_axis=0, tiled=True
    )
    pieces = every.at[inverse + inverse // nblk].get(mode="promise_in_bounds")
    vec_every = every.reshape(net.n_shard, nblk + 1, room)[:, nblk, : vec.shape[1]]
    return pieces, vec_every.reshape(1, -1)


def total_of(*terms):
    acc = terms[0].astype(f32)
    for t in terms[1:]:
        acc = acc + t.astype(f32)
    return acc.astype(bf16)


def reduce_rounds(net, group, parts):
    parts = yield parts
    if net.pieces == 1:
        return parts[0][0]
    lo, hi = parts
    (got,) = yield (net.swap_data(hi, group, net.depth - 1),)
    terms = [lo, got]
    for k in range(net.depth - 2, -1, -1):
        width = 1 << k
        send = total_of(*[t[width:] for t in terms])
        keep = total_of(*[t[:width] for t in terms])
        (got,) = yield (net.swap_data(send, group, k),)
        terms = [keep, got]
    return total_of(*terms)[0]


def last_pieces(net, natural, block_slots, vec_sum):
    if net.pieces == 1:
        dealt = natural.at[block_slots].get(mode="promise_in_bounds")
        owned = lax.psum_scatter(dealt, "shard", scatter_dimension=0, tiled=True)
        owned = total_of(owned, net.swap_rep(owned))
        cut = owned.reshape(-1, 2, 8, 16, BS).transpose(1, 2, 0, 3, 4)
        cut = cut[:, np.array([chunk_of(k) for k in range(8)])]
        vec = lax.psum_scatter(vec_sum, "shard", scatter_dimension=0, tiled=True)[None]
        parts = [(cut[0], cut[1], owned.shape[0])]
        return parts, jnp.zeros((1,), jnp.int32), vec + net.swap_rep(vec)
    n = net.n_shard
    slots = block_slots.reshape(n, -1)
    half = slots.shape[1] // 2
    room = net.rows * BS
    vec_cut = vec_sum.reshape(n, -1)
    width = vec_cut.shape[1]
    vec_cut = jnp.pad(vec_cut.astype(bf16), ((0, 0), (0, room - width)))
    vec_cut = vec_cut.reshape(n, 1, net.rows, BS)
    cuts = []
    for k in range(2):
        index = slots[:, k * half : (k + 1) * half].reshape(-1)
        cuts.append(natural.at[index].get(mode="promise_in_bounds").reshape(n, half, net.rows, BS))
    cuts[1] = jnp.concatenate([cuts[1], vec_cut], axis=1)

    def home(cut):
        back = lax.all_to_all(
            cut.reshape(-1, net.rows, BS), "shard", split_axis=0, concat_axis=0, tiled=True
        )
        return back.reshape(n, -1, net.rows, BS)

    mine, cuts[1] = together(home(cuts[0]), cuts[1])
    other = net.swap_rep(mine)
    other, last = together(other, home(cuts[1]))
    parts = [(mine, other, half), (last, net.swap_rep(last), half)]
    terms = [v[:, half].reshape(n, room)[:, :width].astype(f32) for v in parts[1][:2]]
    flag = lax.axis_index("rep").astype(jnp.int32).reshape(1)
    return parts, flag, jnp.sum(terms[0] + terms[1], axis=0, keepdims=True)


def attend_forward_body(lim, q_ref, k_ref, v_ref, o_ref, lse_ref, *, causal, rows):
    pair = pl.program_id(0)
    seq, keys = q_ref.shape[0], k_ref.shape[0]
    lane = lax.broadcasted_iota(jnp.int32, (1, LANES), 1)
    top = lim[0] - 1

    @pl.when(pair == 0)
    def _():
        lse_ref[...] = jnp.zeros_like(lse_ref)

    for blk in range(seq // rows):
        here = pl.ds(blk * rows, rows)
        width = (blk + 1) * rows if causal else keys
        q = q_ref[here, :] * bf16(scale)
        k = k_ref[pl.ds(0, width), :]
        v = v_ref[pl.ds(0, width), :]
        outs = []
        kept = lse_ref[here, :]
        if causal:
            row = lax.broadcasted_iota(jnp.int32, (rows, 1), 0) + blk * rows
            col = lax.broadcasted_iota(jnp.int32, (1, width), 1)
            allowed = col <= jnp.minimum(row, top)
        for h in range(2):
            mine = (lane // HEAD_DIM) == h
            s = dot_nt(jnp.where(mine, q, bf16(0)), k)
            if causal:
                s = jnp.where(allowed, s, masked_score)
            peak = jnp.max(s, axis=1, keepdims=True)
            e = jnp.exp(s - peak)
            mass = jnp.sum(e, axis=1, keepdims=True)
            outs.append(dot_nn(e.astype(bf16), v) * (1.0 / mass))
            kept = jnp.where(lane == 2 * pair + h, peak + jnp.log(mass), kept)
        o_ref[here, :] = jnp.where(lane < HEAD_DIM, outs[0], outs[1]).astype(bf16)
        lse_ref[here, :] = kept


def attend_forward(limit, q, k, v, causal):
    seq, width = q.shape
    keys = k.shape[0]
    pairs = width // LANES
    rows = min(128 if causal else 256, seq)
    o, lse = pl.pallas_call(
        functools.partial(attend_forward_body, causal=causal, rows=rows),
        grid=(pairs,),
        out_shape=(
            jax.ShapeDtypeStruct((seq, width), bf16),
            jax.ShapeDtypeStruct((seq, LANES), f32),
        ),
        in_specs=[
            pl.BlockSpec(memory_space=pltpu.SMEM),
            pl.BlockSpec((seq, LANES), lambda i: (0, i)),
            pl.BlockSpec((keys, LANES), lambda i: (0, i)),
            pl.BlockSpec((keys, LANES), lambda i: (0, i)),
        ],
        out_specs=(
            pl.BlockSpec((seq, LANES), lambda i: (0, i)),
            pl.BlockSpec((seq, LANES), lambda i: (0, 0)),
        ),
        compiler_params=params(),
        cost_estimate=small(),
        name="attend_forward",
    )(limit, q, k, v)
    return o, lse[:, : 2 * pairs].T.reshape(pairs, 2, seq)


def attend_backward_body(
    lim, q_ref, k_ref, v_ref, o_ref, do_ref, lse_ref, dq_ref, dk_ref, dv_ref, dk_acc, dv_acc, *, causal, rows
):
    seq, keys = q_ref.shape[0], k_ref.shape[0]
    lane = lax.broadcasted_iota(jnp.int32, (1, LANES), 1)
    top = lim[0] - 1
    dk_acc[...] = jnp.zeros_like(dk_acc)
    dv_acc[...] = jnp.zeros_like(dv_acc)
    head_row = lax.broadcasted_iota(jnp.int32, (8, LANES), 0)
    head_lane = lax.broadcasted_iota(jnp.int32, (8, LANES), 1) // HEAD_DIM
    pick = (head_row == head_lane).astype(bf16)
    for blk in range(seq // rows):
        here = pl.ds(blk * rows, rows)
        width = (blk + 1) * rows if causal else keys
        span = pl.ds(0, width)
        q = q_ref[here, :] * bf16(scale)
        do = do_ref[here, :]
        k = k_ref[span, :]
        v = v_ref[span, :]
        prod = do.astype(f32) * o_ref[here, :].astype(f32)
        hi = prod.astype(bf16)
        lo = (prod - hi.astype(f32)).astype(bf16)
        delta = dot_nt(pick, hi) + dot_nt(pick, lo)
        lse = lse_ref[0][:, blk * rows : (blk + 1) * rows]
        if causal:
            key = lax.broadcasted_iota(jnp.int32, (width, 1), 0)
            row = lax.broadcasted_iota(jnp.int32, (1, rows), 1) + blk * rows
            allowed = key <= jnp.minimum(row, top)
        dq = jnp.zeros((rows, LANES), f32)
        dk = jnp.zeros((width, LANES), f32)
        dv = jnp.zeros((width, LANES), f32)
        for h in range(2):
            mine = (lane // HEAD_DIM) == h
            qm = jnp.where(mine, q, bf16(0))
            dom = jnp.where(mine, do, bf16(0))
            km = jnp.where(mine, k, bf16(0))
            s = dot_nt(k, qm)
            if causal:
                s = jnp.where(allowed, s, masked_score)
            p = jnp.exp(s - lse[h : h + 1, :])
            dp = dot_nt(v, dom)
            ds = (p * (dp - delta[h : h + 1, :])).astype(bf16)
            dv = dv + dot_nn(p.astype(bf16), dom)
            dk = dk + dot_nn(ds, qm)
            dq = dq + dot_tn(ds, km)
        dq_ref[here, :] = (dq * scale).astype(bf16)
        dk_acc[span, :] += dk
        dv_acc[span, :] += dv
    dk_ref[...] = dk_acc[...].astype(bf16)
    dv_ref[...] = dv_acc[...].astype(bf16)


def attend_backward(limit, q, k, v, o, do, lse, causal):
    seq, width = q.shape
    keys = k.shape[0]
    pairs = width // LANES
    rows = min(128 if causal else 256, seq)
    q_spec = pl.BlockSpec((seq, LANES), lambda i: (0, i))
    k_spec = pl.BlockSpec((keys, LANES), lambda i: (0, i))
    return pl.pallas_call(
        functools.partial(attend_backward_body, causal=causal, rows=rows),
        grid=(pairs,),
        out_shape=(
            jax.ShapeDtypeStruct((seq, width), bf16),
            jax.ShapeDtypeStruct((keys, width), bf16),
            jax.ShapeDtypeStruct((keys, width), bf16),
        ),
        in_specs=[
            pl.BlockSpec(memory_space=pltpu.SMEM),
            q_spec,
            k_spec,
            k_spec,
            q_spec,
            q_spec,
            pl.BlockSpec((1, 2, seq), lambda i: (i, 0, 0)),
        ],
        out_specs=(q_spec, k_spec, k_spec),
        scratch_shapes=[pltpu.VMEM((keys, LANES), f32), pltpu.VMEM((keys, LANES), f32)],
        compiler_params=params(),
        cost_estimate=small(),
        name="attend_backward",
    )(limit, q, k, v, o, do, lse)


def gelu_body(h_ref, w_ref, b_ref, act_ref, slope_ref, u_ref, *, chunk):
    u_ref[...] = dot_nn(h_ref[...], w_ref[...]) + b_ref[...]

    def part(i):
        here = pl.ds(pl.multiple_of(i * chunk, chunk), chunk)
        u = u_ref[here, :]
        x = jnp.abs(u) * (0.5**0.5)
        t = 1.0 / (1.0 + ERFC_SLOPE * x)
        poly = jnp.full_like(t, ERFC_POLY[-1])
        for c in ERFC_POLY[-2::-1]:
            poly = poly * t + c
        bell = jnp.exp(-0.5 * (u * u))
        tail = 0.5 * (bell * (t * poly))
        cdf = jnp.where(u < 0, tail, 1.0 - tail)
        act_ref[here, :] = (u * cdf).astype(bf16)
        slope_ref[here, :] = (cdf + u * (bell * 0.3989422804014327)).astype(bf16)

    pl.loop(0, u_ref.shape[0] // chunk)(part)


def gelu_forward(h, w, b):
    seq, width = h.shape
    hidden = w.shape[1]
    tile = 512
    spec = pl.BlockSpec((seq, tile), lambda i: (0, i))
    return pl.pallas_call(
        functools.partial(gelu_body, chunk=32),
        grid=(hidden // tile,),
        out_shape=(jax.ShapeDtypeStruct((seq, hidden), bf16),) * 2,
        in_specs=[
            pl.BlockSpec((seq, width), lambda i: (0, 0)),
            pl.BlockSpec((width, tile), lambda i: (0, i)),
            pl.BlockSpec((1, tile), lambda i: (0, i)),
        ],
        out_specs=(spec, spec),
        scratch_shapes=[pltpu.VMEM((seq, tile), f32)],
        compiler_params=params(),
        cost_estimate=small(),
        name="gelu_forward",
    )(h, w, b)


def weight_grad_body(s, x_own, x_sib, *refs, count, outs, many, rows):
    y_own, y_sib = refs[:count], refs[count : 2 * count]
    targets = refs[-3 - outs : -3]
    t_own, t_sib, buf = refs[-3:]
    t_own[...] = x_own[...].T
    t_sib[...] = x_sib[...].T
    per = many // outs
    for k in range(count):
        acc = dot_nn(t_own[...], y_own[k][...]) + dot_nn(t_sib[...], y_sib[k][...])
        buf[k] = acc.astype(bf16)
    for q in range(many):
        here = pl.ds(pl.multiple_of(s[q] * rows, rows), rows)
        for k in range(count):
            for c in range(targets[0].shape[2]):
                targets[q // per][q % per, k, c] = buf[k, here, c * BS : (c + 1) * BS]


def weight_grad(net, group, table, xs, ys, held, first, wide):
    seq = xs[0].shape[0]
    many, rows, halves = net.pieces, net.rows, net.n_mp
    at_core = table.shape[0] - 1
    count = len(ys)
    width = ys[0][0].shape[1]
    if wide:
        steps = xs[0].shape[1] // BS
        y_width = width // halves
        x_spec = pl.BlockSpec((seq, BS), lambda i, s: (0, i))
        y_spec = pl.BlockSpec((seq, y_width), lambda i, s: (0, s[at_core]))
    else:
        steps = xs[0].shape[1] // halves // BS
        y_width = width
        x_spec = pl.BlockSpec((seq, BS), lambda i, s: (0, s[at_core] * steps + i))
        y_spec = pl.BlockSpec((seq, y_width), lambda i, s: (0, 0))
    nb = y_width // BS
    at = first // count
    outs = 2 if many > 1 else 1
    shape = (many // outs, len(GROUPS[group]), steps * nb, rows, BS)
    anyspec = pl.BlockSpec(memory_space=pl.ANY)
    held = held or ()
    before = 3 + 2 * count
    return pl.pallas_call(
        functools.partial(weight_grad_body, count=count, outs=outs, many=many, rows=rows),
        grid_spec=pltpu.PrefetchScalarGridSpec(
            num_scalar_prefetch=1,
            grid=(steps,),
            in_specs=[x_spec] * 2 + [y_spec] * (2 * count) + [anyspec] * len(held),
            out_specs=(
                pl.BlockSpec((many // outs, count, nb, rows, BS), lambda i, s: (0, at, i, 0, 0)),
            )
            * outs,
            scratch_shapes=[
                pltpu.VMEM((BS, seq), bf16),
                pltpu.VMEM((BS, seq), bf16),
                pltpu.VMEM((count, BS, y_width), bf16),
            ],
        ),
        out_shape=(jax.ShapeDtypeStruct(shape, bf16),) * outs,
        input_output_aliases={before + k: k for k in range(len(held))},
        compiler_params=params(),
        cost_estimate=small(),
        name="weight_grad",
    )(table, *xs, *[y[0] for y in ys], *[y[1] for y in ys], *held)


def split_low(a):
    hi = a.astype(bf16)
    return hi, (a - hi.astype(f32)).astype(bf16)


def shampoo_body(flag, mine_ref, other_ref, w_ref, ls_ref, rs_ref, lr_ref, rr_ref, *refs):
    og, ol, orr, ow, g_ref = refs[-5:]
    for k in range(mine_ref.shape[0]):
        for plane, src in ((flag[0], mine_ref), (1 - flag[0], other_ref)):
            row = pl.multiple_of(plane * 128 + chunk_of(k) * 16, 16)
            g_ref[pl.ds(row, 16), :] = src[k, 0]
    g = g_ref[...]
    og[0, 0] = g.astype(f32)
    ol[0, 0] = 0.5 * ls_ref[0, 0] + 0.5 * dot_nt(g, g)
    orr[0, 0] = 0.5 * rs_ref[0, 0] + 0.5 * dot_tn(g, g)
    r_hi, r_lo = split_low(rr_ref[0, 0])
    i_hi, i_lo = split_low(dot_nn(g, r_hi) + dot_nn(g, r_lo))
    l_hi, l_lo = split_low(lr_ref[0, 0])
    d = dot_nn(l_hi, i_hi) + (dot_nn(l_hi, i_lo) + dot_nn(l_lo, i_hi))
    mean = jnp.mean(jnp.mean(d * d, axis=1, keepdims=True), axis=0, keepdims=True)
    ow[0, 0] = w_ref[0, 0] - (D**-0.5) * d / jnp.sqrt(mean + 1e-06)


def shampoo(flag, parts, *states):
    total = states[0].shape[1]
    out, first = (), 0
    for mine, other, n in parts:
        at = first // n
        spec = pl.BlockSpec((1, 1, BS, BS), lambda i, at=at, n=n: (0, at * n + i, 0, 0))
        g_spec = pl.BlockSpec((mine.shape[0], 1, mine.shape[2], BS), lambda i: (0, i, 0, 0))
        anyspec = pl.BlockSpec(memory_space=pl.ANY)
        out = pl.pallas_call(
            shampoo_body,
            grid=(n,),
            out_shape=(jax.ShapeDtypeStruct((1, total, BS, BS), f32),) * 4,
            in_specs=[pl.BlockSpec(memory_space=pltpu.SMEM), g_spec, g_spec]
            + [spec] * 5
            + [anyspec] * len(out),
            out_specs=(spec,) * 4,
            scratch_shapes=[pltpu.VMEM((BS, BS), bf16)],
            input_output_aliases={8 + k: k for k in range(len(out))},
            compiler_params=params(),
            cost_estimate=small(),
            name="shampoo",
        )(flag, mine, other, *states, *out)
        first += n
    return out


def norm_forward(z, gain, shift):
    center = z - jnp.mean(z, axis=1, keepdims=True)
    inv = lax.rsqrt(jnp.mean(center * center, axis=1, keepdims=True) + eps_norm)
    normed = center * inv
    return normed * gain + shift, normed, inv


def norm_backward(grad, normed, inv, gain):
    scaled = grad * gain
    mean_plain = jnp.mean(scaled, axis=1, keepdims=True)
    mean_cross = jnp.mean(scaled * normed, axis=1, keepdims=True)
    back = inv * (scaled - mean_plain - normed * mean_cross)
    return back, jnp.sum(grad * normed, axis=0), jnp.sum(grad, axis=0)


def inverse_of(order):
    many = jnp.arange(order.shape[0], dtype=jnp.int32)
    return jnp.sum(jnp.where(order[:, None] == many[None, :], many[:, None], 0), axis=0)


def route_out(value):
    axes = ("rep", "shard")
    count = lax.axis_size(axes)
    cut = value.reshape(value.shape[0], count, value.shape[1] // count, value.shape[2])
    return lax.all_to_all(cut, axes, split_axis=1, concat_axis=0, tiled=True)


def route_home(pieces, ordering):
    moved = pieces.at[ordering].get(mode="promise_in_bounds")
    back = lax.all_to_all(moved, ("rep", "shard"), split_axis=0, concat_axis=1, tiled=True)
    return back.reshape(back.shape[0], -1, back.shape[3])


def per_device(
    net,
    inputs,
    encoded,
    cotangent,
    lengths,
    seq_slots,
    block_slots,
    weights,
    left_stat,
    right_stat,
    left_root,
    right_root,
    vectors,
    vec_stat,
):
    half_d = inputs.shape[2]
    halves = D // half_d
    core = lax.axis_index("mp")
    data_index = lax.axis_index(("rep", "shard"))
    seq_index = data_index * inputs.shape[0] + core
    limit = lax.dynamic_slice_in_dim(lengths, seq_index, 1)
    tables = [net.table(k, core, data_index) for k in range(2 * len(GROUPS))]
    is_first = core == 0

    def pick(pair, which):
        return lax.dynamic_index_in_dim(pair, which, axis=0, keepdims=False)

    def joined(low_half, high_half):
        return jnp.concatenate(
            [
                jnp.where(is_first, low_half, high_half),
                jnp.where(is_first, high_half, low_half),
            ],
            axis=1,
        )

    def whole(value):
        other = net.swap_core(value)
        own = joined(pick(value, core), pick(other, core))
        sib = joined(pick(value, 1 - core), pick(other, 1 - core))
        return own, sib

    def halved(full):
        mine = lax.dynamic_slice_in_dim(full, core * half_d, half_d, axis=1)
        away = lax.dynamic_slice_in_dim(full, (1 - core) * half_d, half_d, axis=1)
        got = net.swap_core(away)
        return jnp.stack([jnp.where(is_first, mine, got), jnp.where(is_first, got, mine)])

    x, x_sib = whole(inputs)
    e, e_sib = whole(encoded)

    pieces, vec_mine = first_pieces(net, weights, vectors, inverse_of(block_slots))
    flows, base = [], 0
    for k in range(len(GROUPS)):
        size = group_blocks(k, halves)
        flows.append(Flow(gather_rounds(net, k, pieces[base : base + size])))
        base += size
    attn, cross, up, down = flows

    def placed(k):
        return place(net, k, tables[k], *flows[k].finish())

    step((), attn)
    step((), attn, cross)
    step((), attn)
    step((), attn, cross)
    vec_mine, x, x_sib, e, e_sib = step((vec_mine, x, x_sib, e, e_sib), attn, cross, up)
    w_sq, w_sk, w_sv = step(placed(0), up)

    vec_other = net.swap_core(vec_mine)
    vec_both = jnp.concatenate(
        [jnp.where(is_first, vec_mine, vec_other), jnp.where(is_first, vec_other, vec_mine)]
    ).astype(f32)
    vecs = [vec_both[:, i * half_d : (i + 1) * half_d].reshape(1, D) for i in range(13)]
    vecs.append(vec_both[:, 13 * half_d :].reshape(1, FF))
    b_sq, b_sv, b_so, g_one, b_one, b_cq, b_cv, b_co, g_two, b_two, b_fo, g_three, b_three, b_fi = vecs

    q_s = (dot_nn(x, w_sq) + b_sq).astype(bf16)
    k_s = dot_nn(x, w_sk).astype(bf16)
    v_s = (dot_nn(x, w_sv) + b_sv).astype(bf16)
    q_s, k_s, v_s = step((q_s, k_s, v_s), cross, up, down)
    o_s, lse_s = attend_forward(limit, q_s, k_s, v_s, True)
    cotangent, o_s, lse_s = step((cotangent, o_s, lse_s), cross, up, down)
    cot_pieces = route_out(cotangent)
    w_so, w_cq, w_ck, w_cv, w_co = placed(1)
    z_one = x.astype(f32) + dot_nn(o_s, w_so) + b_so
    h_one, n_one, r_one = norm_forward(z_one, g_one, b_one)
    h_one_low = h_one.astype(bf16)
    q_c = (dot_nn(h_one_low, w_cq) + b_cq).astype(bf16)
    k_c = dot_nn(e, w_ck).astype(bf16)
    v_c = (dot_nn(e, w_cv) + b_cv).astype(bf16)
    q_c, k_c, v_c = step((q_c, k_c, v_c), down)
    o_c, lse_c = attend_forward(limit, q_c, k_c, v_c, False)
    z_two = h_one + dot_nn(o_c, w_co) + b_co
    h_two, n_two, r_two = norm_forward(z_two, g_two, b_two)
    cot_pieces, h_two, h_two_low = step((cot_pieces, h_two, h_two.astype(bf16)), up, down)
    cot_home = route_home(cot_pieces, seq_slots)
    (w_fi,) = placed(2)
    act, slope = gelu_forward(h_two_low, w_fi, b_fi)
    act_sib = net.swap_core(act)
    act, slope = step((act, slope), down)
    (w_fo,) = placed(3)
    z_three = h_two + dot_nn(act, w_fo) + b_fo
    cot, _ = whole(cot_home)
    h_three, n_three, r_three = norm_forward(z_three, g_three, b_three)
    live = (jnp.arange(x.shape[0]) < limit).astype(f32)[:, None]
    source = inverse_of(seq_slots)
    finished = (h_three * live).astype(bf16)

    def gradient(k, *calls):
        held, first = None, 0
        for xs, *ys in calls:
            held = weight_grad(net, k, tables[len(GROUPS) + k], xs, ys, held, first, GROUPS[k][first][1])
            first += len(ys)
        parts = tuple(h.reshape(h.shape[0], -1, net.rows, BS) for h in held)
        return Flow(reduce_rounds(net, len(GROUPS) + k, parts))

    grad_y = cot.astype(f32) * live
    d_three, dg_three, db_three = norm_backward(grad_y, n_three, r_three, g_three)
    a_three = d_three.astype(bf16)
    d_hidden = (dot_nt(a_three, w_fo) * slope.astype(f32)).astype(bf16)
    a_three_sib, d_hidden = step((net.swap_core(a_three), d_hidden))
    d_hidden_sib = net.swap_core(d_hidden)
    down = gradient(3, ((act, act_sib), (a_three, a_three_sib)))
    finished, d_hidden, d_hidden_sib = step((finished, d_hidden, d_hidden_sib), down)
    finished = halved(finished)
    d_h_two = d_three + dot_nt(d_hidden, w_fi)
    d_two, dg_two, db_two = norm_backward(d_h_two, n_two, r_two, g_two)
    a_two = d_two.astype(bf16)
    d_oc = dot_nt(a_two, w_co).astype(bf16)
    finished, d_hidden, d_hidden_sib, d_oc = step((finished, d_hidden, d_hidden_sib, d_oc))
    out_pieces = route_out(finished)
    up = gradient(2, ((h_two_low, net.swap_core(h_two_low)), (d_hidden, d_hidden_sib)))
    (d_oc,) = step((d_oc,), up, down)
    dq_c, dk_c, dv_c = attend_backward(limit, q_c, k_c, v_c, o_c, d_oc, lse_c, False)
    dq_c_sib, dk_c_sib, dv_c_sib = [net.swap_core(v) for v in (dq_c, dk_c, dv_c)]
    dq_c, dk_c, dv_c = step((dq_c, dk_c, dv_c), down)
    d_h_one = d_two + dot_nt(dq_c, w_cq)
    d_one, dg_one, db_one = norm_backward(d_h_one, n_one, r_one, g_one)
    a_one = d_one.astype(bf16)
    a_one_sib = net.swap_core(a_one)
    d_os = dot_nt(a_one, w_so).astype(bf16)
    out_pieces, a_one, a_one_sib, d_os = step((out_pieces, a_one, a_one_sib, d_os))
    outputs = route_home(out_pieces, source)
    cross = gradient(
        1,
        ((o_s, net.swap_core(o_s)), (a_one, a_one_sib)),
        ((h_one_low, net.swap_core(h_one_low)), (dq_c, dq_c_sib)),
        ((e, e_sib), (dk_c, dk_c_sib), (dv_c, dv_c_sib)),
        ((o_c, net.swap_core(o_c)), (a_two, net.swap_core(a_two))),
    )
    outputs, d_os = step((outputs, d_os), cross, up, down)
    dq_s, dk_s, dv_s = attend_backward(limit, q_s, k_s, v_s, o_s, d_os, lse_s, True)
    sibs = [net.swap_core(v) for v in (dq_s, dk_s, dv_s)]
    dq_s, dk_s, dv_s = step((dq_s, dk_s, dv_s), cross)
    attn = gradient(0, ((x, x_sib), *zip((dq_s, dk_s, dv_s), sibs)))
    dk_c, dv_c, dq_s, dk_s, dv_s = step((dk_c, dv_c, dq_s, dk_s, dv_s), attn)
    dq_s, dk_s, dv_s = step((dq_s, dk_s, dv_s), cross, up)
    state_back = dot_nt(dk_c, w_ck) + dot_nt(dv_c, w_cv)
    back = d_one + dot_nt(dq_s, w_sq) + dot_nt(dk_s, w_sk) + dot_nt(dv_s, w_sv)
    back, d_hidden, dq_c, dv_c = step((back, d_hidden, dq_c, dv_c), attn, cross, up)
    input_grad = halved(back.astype(bf16))
    encoded_grad = halved(state_back.astype(bf16))
    dq_s, dv_s = step((dq_s, dv_s), attn)
    columns = [jnp.sum(v.astype(f32), axis=0) for v in (d_hidden, dq_c, dv_c, dq_s, dv_s)]
    *columns, input_grad, encoded_grad = step((*columns, input_grad, encoded_grad), attn, cross)
    sums = (
        columns[3],
        columns[4],
        jnp.sum(d_one, axis=0),
        dg_one,
        db_one,
        columns[1],
        columns[2],
        jnp.sum(d_two, axis=0),
        dg_two,
        db_two,
        jnp.sum(d_three, axis=0),
        dg_three,
        db_three,
        columns[0],
    )
    vec_pair = jnp.concatenate([s.reshape(halves, -1) for s in sums], axis=1)
    vec_sum = pick(vec_pair, core) + net.swap_core(pick(vec_pair, 1 - core))
    natural = [f.finish() for f in (attn, cross, up, down)]

    parts, flag, vec_owned = last_pieces(net, jnp.concatenate(natural), block_slots, vec_sum)
    block_grad, left_new, right_new, weights_new = shampoo(
        flag, parts, weights, left_stat, right_stat, left_root, right_root
    )
    vec_stat_new = 0.5 * vec_stat + 0.5 * vec_owned * vec_owned
    vectors_new = vectors - 0.1 * vec_owned * lax.rsqrt(vec_stat_new)
    return (
        outputs,
        input_grad,
        encoded_grad,
        block_grad,
        left_new,
        right_new,
        weights_new,
        vec_owned,
        vec_stat_new,
        vectors_new,
    )


def solution(mesh):
    net = Net(mesh.shape["rep"], mesh.shape["shard"], mesh.shape["mp"])
    rows = P(("rep", "shard"), None, "mp")
    blocks = P("mp", "shard", None, None)
    vector = P("mp", "shard")
    in_specs = (rows, rows, rows, P(), P(), P()) + (blocks,) * 5 + (vector, vector)
    out_specs = (rows, rows, rows) + (blocks,) * 4 + (vector,) * 3
    return jax.shard_map(
        functools.partial(per_device, net),
        mesh=mesh,
        in_specs=in_specs,
        out_specs=out_specs,
        check_vma=False,
    )
```

```python
import functools

import jax
import jax.numpy as jnp
import numpy as np
from jax import lax
from jax.experimental import pallas as pl
from jax.experimental.pallas import tpu as pltpu
from jax.sharding import PartitionSpec as P

D = 1024
FF = 4096
HEAD_DIM = 64
BS = 256
LANES = 128

eps_norm = 1e-05
masked_score = -1e30
scale = HEAD_DIM**-0.5
bf16 = jnp.bfloat16
f32 = jnp.float32

NT = (((1,), (1,)), ((), ()))
TN = (((0,), (0,)), ((), ()))

VMEM_LIMIT = 60 * 1024 * 1024

ERFC_SLOPE = 0.3
ERFC_POLY = (
    0.1691880090604902,
    0.17071516163759975,
    0.14833963774537734,
    0.21492421686136995,
    -0.09464635292673967,
    0.5477136065073498,
    -0.5122723795383668,
    0.4855603950654946,
    -0.1295223139805042,
)


def dot_nn(a, b):
    return jnp.dot(a, b, preferred_element_type=f32)


def dot_nt(a, b):
    return lax.dot_general(a, b, NT, preferred_element_type=f32)


def dot_tn(a, b):
    return lax.dot_general(a, b, TN, preferred_element_type=f32)


def small():
    return pl.CostEstimate(flops=1 << 20, bytes_accessed=1 << 20, transcendentals=0)


def params(**kw):
    return pltpu.CompilerParams(vmem_limit_bytes=VMEM_LIMIT, **kw)


GROUPS = (
    (("sq", True), ("sk", True), ("sv", True)),
    (("so", False), ("cq", True), ("ck", True), ("cv", True), ("co", False)),
    (("fi", True),),
    (("fo", False),),
)
SHAPES = {name: (D, D) for name in ("sq", "sk", "sv", "so", "cq", "ck", "cv", "co")}
SHAPES["fi"], SHAPES["fo"] = (D, FF), (FF, D)


def chunk_of(i):
    return (i & 8) | ((i & 2) << 1) | ((i & 1) << 1) | ((i & 4) >> 2)


class Net:
    def __init__(self, n_rep, n_shard, n_mp):
        self.n_rep, self.n_shard, self.n_mp = n_rep, n_shard, n_mp
        self.n_data = n_rep * n_shard
        self.pieces = 16 if (n_rep, n_shard, n_mp) == (2, 8, 2) else 1
        self.rows = BS // self.pieces
        self.depth = self.pieces.bit_length() - 1
        x, z1, z2, y = 1, 2, 4, 8
        gathering = (
            ((z2, y, z1, x), (z2, z1, x, y)),
            ((z2, z1, y, x), (z2, z1, x, y)),
            ((z2, x, z1, y), (z2, y, z1, x)),
            ((z2, x, y, z1), (z2, y, z1, x)),
        )
        reducing = (((z2, z1, y, x), (z2, z1, x, y)),) + gathering[1:]
        self.orders = gathering + reducing

    def swap_core(self, value):
        return lax.ppermute(value, "mp", [(i, i ^ 1) for i in range(self.n_mp)])

    def swap_rep(self, value):
        return lax.ppermute(value, "rep", [(i, i ^ 1) for i in range(self.n_rep)])

    def swap_data(self, value, group, step):
        pairs = []
        for i in range(self.n_data):
            for m in range(self.n_mp):
                there = i ^ self.orders[group][m][step]
                pairs.append((i * self.n_mp + m, there * self.n_mp + m))
        return lax.ppermute(value, ("rep", "shard", "mp"), pairs)

    def table(self, group, core, data_index):
        many = self.pieces
        if many == 1:
            return jnp.stack([0, 0, 0, 0, core]).astype(jnp.int32)
        half = many // 4
        rel = []
        for order in self.orders[group]:
            rel.append([sum(b for s, b in enumerate(order) if q >> s & 1) for q in range(many)])
        rows = []
        for m in range(self.n_mp):
            place = [rel[1 - m].index(r) // 2 for r in rel[m][::2]]
            low = [p for p in place if p < half][0]
            high = [p - half for p in place if p >= half][0]
            lows, highs = [], []
            for p in place:
                low, high = (p, high) if p < half else (low, p - half)
                lows.append(low)
                highs.append(high)
            rows.append([chunk_of(r) for r in rel[m]] + lows + highs + [int(p >= half) for p in place])
        mine = jnp.asarray(np.array(rows, np.int32))[core]
        chunks = mine[:many] ^ chunk_of(data_index)
        return jnp.concatenate([chunks, mine[many:], core.reshape(1)]).astype(jnp.int32)


def together(*values):
    return lax.optimization_barrier(values)


class Flow:
    def __init__(self, rounds):
        self.rounds = rounds
        self.flying = next(rounds)

    def advance(self, values):
        try:
            self.flying = self.rounds.send(values)
        except StopIteration as stop:
            self.flying = None
            self.result = stop.value

    def finish(self):
        while self.flying is not None:
            self.advance(self.flying)
        return self.result


def step(main, *flows):
    flows = [f for f in flows if f.flying is not None]
    values = list(together(*main, *[v for f in flows for v in f.flying]))
    main, values = values[: len(main)], values[len(main) :]
    for f in flows:
        many = len(f.flying)
        f.advance(tuple(values[:many]))
        values = values[many:]
    return main


def blocks_of(name, n_mp):
    rows, cols = SHAPES[name]
    return rows * cols // n_mp // (BS * BS)


def group_blocks(group, n_mp):
    return sum(blocks_of(name, n_mp) for name, _ in GROUPS[group])


def place_body(s, *refs, dests, many, two):
    q = pl.program_id(0)
    steps = many // 2 if two else 1
    if two:
        own_lo, own_hi, sib_lo, sib_hi = refs[:4]
        outs = refs[4:]
    else:
        own_lo, sib_lo = refs[:2]
        outs = refs[2:]
    core = s[many + 3 * steps]
    rows = own_lo.shape[2]
    for t in range(own_lo.shape[0]):
        here = pl.ds(0, rows)
        if two:
            here = pl.ds(pl.multiple_of((s[2 * q + t] & 1) * rows, rows), rows)
        for b in range(own_lo.shape[1]):
            own, sib = own_lo[t, b], sib_lo[t, b]
            if two:
                own = jnp.where(q < steps // 2, own, own_hi[t, b])
                sib = jnp.where(s[many + 2 * steps + q] == 0, sib, sib_hi[t, b])
            for h in range(2):
                which, row, col = dests[h][b]
                outs[which][row, here, col : col + BS] = jnp.where(core == h, own, sib)


def place(net, group, table, own, sib):
    many, rows, n_mp = net.pieces, net.rows, net.n_mp
    two = many > 1
    per = 2 if two else 1
    steps = many // per
    half = max(steps // 2, 1)
    dests = ([], [])
    shapes, specs = [], []
    for which, (name, wide) in enumerate(GROUPS[group]):
        height, width = SHAPES[name]
        tall = height if wide else height // n_mp
        flat = width // n_mp if wide else width
        for h in range(n_mp):
            for r in range(tall // BS):
                for c in range(flat // BS):
                    if wide:
                        dests[h].append((which, r, h * flat + c * BS))
                    else:
                        dests[h].append((which, h * (tall // BS) + r, c * BS))
        shapes.append(jax.ShapeDtypeStruct((height // BS, BS, width), bf16))
        specs.append(
            pl.BlockSpec((height // BS, per * rows, width), lambda q, s: (0, s[per * q] // per, 0))
        )
    nb = own[0].shape[1]
    block = (per, nb, rows, BS)
    lo = pl.BlockSpec(block, lambda q, s: (jnp.minimum(q, half - 1), 0, 0, 0))
    hi = pl.BlockSpec(block, lambda q, s: (jnp.maximum(q - half, 0), 0, 0, 0))
    sib_lo = pl.BlockSpec(block, lambda q, s: (s[many + q], 0, 0, 0))
    sib_hi = pl.BlockSpec(block, lambda q, s: (s[many + steps + q], 0, 0, 0))
    out = pl.pallas_call(
        functools.partial(place_body, dests=dests, many=many, two=two),
        grid_spec=pltpu.PrefetchScalarGridSpec(
            num_scalar_prefetch=1,
            grid=(steps,),
            in_specs=[lo, hi, sib_lo, sib_hi] if two else [lo, sib_lo],
            out_specs=tuple(specs),
        ),
        out_shape=tuple(shapes),
        compiler_params=params(),
        cost_estimate=small(),
        name="place",
    )(table, *own, *sib)
    return [o.reshape(-1, o.shape[2]) for o in out]


def gather_rounds(net, group, piece):
    (piece,) = yield (piece,)
    cur = piece[None]
    if net.pieces == 1:
        (sib,) = yield (net.swap_core(cur),)
        return (cur,), (sib,)
    for k in range(net.depth - 1):
        (got,) = yield (net.swap_data(cur, group, k),)
        cur = jnp.concatenate([cur, got])
    got, sib_lo = yield (net.swap_data(cur, group, net.depth - 1), net.swap_core(cur))
    (sib_hi,) = yield (net.swap_core(got),)
    return (cur, got), (sib_lo, sib_hi)


def first_pieces(net, weights, vectors, inverse):
    low = weights[0].astype(bf16)
    vec = vectors.astype(bf16)
    if net.pieces == 1:
        every = lax.all_gather(low, "shard", axis=0, tiled=True)
        vec_every = lax.all_gather(vec, "shard", axis=1, tiled=True)
        return every.at[inverse].get(mode="promise_in_bounds"), vec_every
    nblk = low.shape[0]
    cut = low.reshape(nblk, 2, 2, 2, 2, net.rows, BS)
    cut = lax.dynamic_index_in_dim(cut, lax.axis_index("rep"), axis=1, keepdims=False)
    cut = cut.transpose(3, 1, 2, 0, 4, 5).reshape(net.n_shard, nblk, net.rows, BS)
    room = net.rows * BS
    vec_cut = jnp.pad(vec.reshape(-1), (0, room - vec.shape[1])).reshape(1, 1, net.rows, BS)
    cut = jnp.concatenate([cut, jnp.broadcast_to(vec_cut, (net.n_shard,) + vec_cut.shape[1:])], axis=1)
    every = lax.all_to_all(
        cut.reshape(-1, net.rows, BS), "shard", split_axis=0, concat_axis=0, tiled=True
    )
    pieces = every.at[inverse + inverse // nblk].get(mode="promise_in_bounds")
    vec_every = every.reshape(net.n_shard, nblk + 1, room)[:, nblk, : vec.shape[1]]
    return pieces, vec_every.reshape(1, -1)


def total_of(*terms):
    acc = terms[0].astype(f32)
    for t in terms[1:]:
        acc = acc + t.astype(f32)
    return acc.astype(bf16)


def reduce_rounds(net, group, parts):
    parts = yield parts
    if net.pieces == 1:
        return parts[0][0]
    lo, hi = parts
    (got,) = yield (net.swap_data(hi, group, net.depth - 1),)
    terms = [lo, got]
    for k in range(net.depth - 2, -1, -1):
        width = 1 << k
        send = total_of(*[t[width:] for t in terms])
        keep = total_of(*[t[:width] for t in terms])
        (got,) = yield (net.swap_data(send, group, k),)
        terms = [keep, got]
    return total_of(*terms)[0]


def last_pieces(net, natural, block_slots, vec_sum):
    if net.pieces == 1:
        dealt = natural.at[block_slots].get(mode="promise_in_bounds")
        owned = lax.psum_scatter(dealt, "shard", scatter_dimension=0, tiled=True)
        owned = total_of(owned, net.swap_rep(owned))
        cut = owned.reshape(-1, 2, 8, 16, BS).transpose(1, 2, 0, 3, 4)
        cut = cut[:, np.array([chunk_of(k) for k in range(8)])]
        vec = lax.psum_scatter(vec_sum, "shard", scatter_dimension=0, tiled=True)[None]
        parts = [(cut[0], cut[1], owned.shape[0])]
        return parts, jnp.zeros((1,), jnp.int32), vec + net.swap_rep(vec)
    n = net.n_shard
    slots = block_slots.reshape(n, -1)
    half = slots.shape[1] // 2
    room = net.rows * BS
    vec_cut = vec_sum.reshape(n, -1)
    width = vec_cut.shape[1]
    vec_cut = jnp.pad(vec_cut.astype(bf16), ((0, 0), (0, room - width)))
    vec_cut = vec_cut.reshape(n, 1, net.rows, BS)
    cuts = []
    for k in range(2):
        index = slots[:, k * half : (k + 1) * half].reshape(-1)
        cuts.append(natural.at[index].get(mode="promise_in_bounds").reshape(n, half, net.rows, BS))
    cuts[1] = jnp.concatenate([cuts[1], vec_cut], axis=1)

    def home(cut):
        back = lax.all_to_all(
            cut.reshape(-1, net.rows, BS), "shard", split_axis=0, concat_axis=0, tiled=True
        )
        return back.reshape(n, -1, net.rows, BS)

    mine, cuts[1] = together(home(cuts[0]), cuts[1])
    other = net.swap_rep(mine)
    other, last = together(other, home(cuts[1]))
    parts = [(mine, other, half), (last, net.swap_rep(last), half)]
    terms = [v[:, half].reshape(n, room)[:, :width].astype(f32) for v in parts[1][:2]]
    flag = lax.axis_index("rep").astype(jnp.int32).reshape(1)
    return parts, flag, jnp.sum(terms[0] + terms[1], axis=0, keepdims=True)


def attend_forward_body(lim, q_ref, k_ref, v_ref, o_ref, lse_ref, *, causal, rows):
    pair = pl.program_id(0)
    seq, keys = q_ref.shape[0], k_ref.shape[0]
    lane = lax.broadcasted_iota(jnp.int32, (1, LANES), 1)
    top = lim[0] - 1

    @pl.when(pair == 0)
    def _():
        lse_ref[...] = jnp.zeros_like(lse_ref)

    for blk in range(seq // rows):
        here = pl.ds(blk * rows, rows)
        width = (blk + 1) * rows if causal else keys
        q = q_ref[here, :] * bf16(scale)
        k = k_ref[pl.ds(0, width), :]
        v = v_ref[pl.ds(0, width), :]
        outs = []
        kept = lse_ref[here, :]
        if causal:
            row = lax.broadcasted_iota(jnp.int32, (rows, 1), 0) + blk * rows
            col = lax.broadcasted_iota(jnp.int32, (1, width), 1)
            allowed = col <= jnp.minimum(row, top)
        for h in range(2):
            mine = (lane // HEAD_DIM) == h
            s = dot_nt(jnp.where(mine, q, bf16(0)), k)
            if causal:
                s = jnp.where(allowed, s, masked_score)
            peak = jnp.max(s, axis=1, keepdims=True)
            e = jnp.exp(s - peak)
            mass = jnp.sum(e, axis=1, keepdims=True)
            outs.append(dot_nn(e.astype(bf16), v) * (1.0 / mass))
            kept = jnp.where(lane == 2 * pair + h, peak + jnp.log(mass), kept)
        o_ref[here, :] = jnp.where(lane < HEAD_DIM, outs[0], outs[1]).astype(bf16)
        lse_ref[here, :] = kept


def attend_forward(limit, q, k, v, causal):
    seq, width = q.shape
    keys = k.shape[0]
    pairs = width // LANES
    rows = min(128 if causal else 256, seq)
    o, lse = pl.pallas_call(
        functools.partial(attend_forward_body, causal=causal, rows=rows),
        grid=(pairs,),
        out_shape=(
            jax.ShapeDtypeStruct((seq, width), bf16),
            jax.ShapeDtypeStruct((seq, LANES), f32),
        ),
        in_specs=[
            pl.BlockSpec(memory_space=pltpu.SMEM),
            pl.BlockSpec((seq, LANES), lambda i: (0, i)),
            pl.BlockSpec((keys, LANES), lambda i: (0, i)),
            pl.BlockSpec((keys, LANES), lambda i: (0, i)),
        ],
        out_specs=(
            pl.BlockSpec((seq, LANES), lambda i: (0, i)),
            pl.BlockSpec((seq, LANES), lambda i: (0, 0)),
        ),
        compiler_params=params(),
        cost_estimate=small(),
        name="attend_forward",
    )(limit, q, k, v)
    return o, lse[:, : 2 * pairs].T.reshape(pairs, 2, seq)


def attend_backward_body(
    lim, q_ref, k_ref, v_ref, o_ref, do_ref, lse_ref, dq_ref, dk_ref, dv_ref, dk_acc, dv_acc, *, causal, rows
):
    seq, keys = q_ref.shape[0], k_ref.shape[0]
    lane = lax.broadcasted_iota(jnp.int32, (1, LANES), 1)
    top = lim[0] - 1
    dk_acc[...] = jnp.zeros_like(dk_acc)
    dv_acc[...] = jnp.zeros_like(dv_acc)
    head_row = lax.broadcasted_iota(jnp.int32, (8, LANES), 0)
    head_lane = lax.broadcasted_iota(jnp.int32, (8, LANES), 1) // HEAD_DIM
    pick = (head_row == head_lane).astype(bf16)
    for blk in range(seq // rows):
        here = pl.ds(blk * rows, rows)
        width = (blk + 1) * rows if causal else keys
        span = pl.ds(0, width)
        q = q_ref[here, :] * bf16(scale)
        do = do_ref[here, :]
        k = k_ref[span, :]
        v = v_ref[span, :]
        prod = do.astype(f32) * o_ref[here, :].astype(f32)
        hi = prod.astype(bf16)
        lo = (prod - hi.astype(f32)).astype(bf16)
        delta = dot_nt(pick, hi) + dot_nt(pick, lo)
        lse = lse_ref[0][:, blk * rows : (blk + 1) * rows]
        if causal:
            key = lax.broadcasted_iota(jnp.int32, (width, 1), 0)
            row = lax.broadcasted_iota(jnp.int32, (1, rows), 1) + blk * rows
            allowed = key <= jnp.minimum(row, top)
        dq = jnp.zeros((rows, LANES), f32)
        dk = jnp.zeros((width, LANES), f32)
        dv = jnp.zeros((width, LANES), f32)
        for h in range(2):
            mine = (lane // HEAD_DIM) == h
            qm = jnp.where(mine, q, bf16(0))
            dom = jnp.where(mine, do, bf16(0))
            km = jnp.where(mine, k, bf16(0))
            s = dot_nt(k, qm)
            if causal:
                s = jnp.where(allowed, s, masked_score)
            p = jnp.exp(s - lse[h : h + 1, :])
            dp = dot_nt(v, dom)
            ds = (p * (dp - delta[h : h + 1, :])).astype(bf16)
            dv = dv + dot_nn(p.astype(bf16), dom)
            dk = dk + dot_nn(ds, qm)
            dq = dq + dot_tn(ds, km)
        dq_ref[here, :] = (dq * scale).astype(bf16)
        dk_acc[span, :] += dk
        dv_acc[span, :] += dv
    dk_ref[...] = dk_acc[...].astype(bf16)
    dv_ref[...] = dv_acc[...].astype(bf16)


def attend_backward(limit, q, k, v, o, do, lse, causal):
    seq, width = q.shape
    keys = k.shape[0]
    pairs = width // LANES
    rows = min(128 if causal else 256, seq)
    q_spec = pl.BlockSpec((seq, LANES), lambda i: (0, i))
    k_spec = pl.BlockSpec((keys, LANES), lambda i: (0, i))
    return pl.pallas_call(
        functools.partial(attend_backward_body, causal=causal, rows=rows),
        grid=(pairs,),
        out_shape=(
            jax.ShapeDtypeStruct((seq, width), bf16),
            jax.ShapeDtypeStruct((keys, width), bf16),
            jax.ShapeDtypeStruct((keys, width), bf16),
        ),
        in_specs=[
            pl.BlockSpec(memory_space=pltpu.SMEM),
            q_spec,
            k_spec,
            k_spec,
            q_spec,
            q_spec,
            pl.BlockSpec((1, 2, seq), lambda i: (i, 0, 0)),
        ],
        out_specs=(q_spec, k_spec, k_spec),
        scratch_shapes=[pltpu.VMEM((keys, LANES), f32), pltpu.VMEM((keys, LANES), f32)],
        compiler_params=params(),
        cost_estimate=small(),
        name="attend_backward",
    )(limit, q, k, v, o, do, lse)


def gelu_body(h_ref, w_ref, b_ref, act_ref, slope_ref, u_ref, *, chunk):
    u_ref[...] = dot_nn(h_ref[...], w_ref[...]) + b_ref[...]

    def part(i):
        here = pl.ds(pl.multiple_of(i * chunk, chunk), chunk)
        u = u_ref[here, :]
        x = jnp.abs(u) * (0.5**0.5)
        t = 1.0 / (1.0 + ERFC_SLOPE * x)
        poly = jnp.full_like(t, ERFC_POLY[-1])
        for c in ERFC_POLY[-2::-1]:
            poly = poly * t + c
        bell = jnp.exp(-0.5 * (u * u))
        tail = 0.5 * (bell * (t * poly))
        cdf = jnp.where(u < 0, tail, 1.0 - tail)
        act_ref[here, :] = (u * cdf).astype(bf16)
        slope_ref[here, :] = (cdf + u * (bell * 0.3989422804014327)).astype(bf16)

    pl.loop(0, u_ref.shape[0] // chunk)(part)


def gelu_forward(h, w, b):
    seq, width = h.shape
    hidden = w.shape[1]
    tile = 512
    spec = pl.BlockSpec((seq, tile), lambda i: (0, i))
    return pl.pallas_call(
        functools.partial(gelu_body, chunk=32),
        grid=(hidden // tile,),
        out_shape=(jax.ShapeDtypeStruct((seq, hidden), bf16),) * 2,
        in_specs=[
            pl.BlockSpec((seq, width), lambda i: (0, 0)),
            pl.BlockSpec((width, tile), lambda i: (0, i)),
            pl.BlockSpec((1, tile), lambda i: (0, i)),
        ],
        out_specs=(spec, spec),
        scratch_shapes=[pltpu.VMEM((seq, tile), f32)],
        compiler_params=params(),
        cost_estimate=small(),
        name="gelu_forward",
    )(h, w, b)


def weight_grad_body(s, x_own, x_sib, *refs, count, outs, many, rows, nb):
    y_own, y_sib = refs[:count], refs[count : 2 * count]
    targets = refs[-3 - outs : -3]
    t_own, t_sib, buf = refs[-3:]
    t_own[...] = x_own[...].T
    t_sib[...] = x_sib[...].T
    per = many // outs
    for k in range(count):
        acc = dot_nn(t_own[...], y_own[k][...]) + dot_nn(t_sib[...], y_sib[k][...])
        buf[k] = acc.astype(bf16)
    for q in range(many):
        for r in range(x_own.shape[1] // BS):
            here = pl.ds(pl.multiple_of(s[q] * rows + r * BS, rows), rows)
            for k in range(count):
                for c in range(nb):
                    targets[q // per][q % per, k, r * nb + c] = buf[k, here, c * BS : (c + 1) * BS]


def weight_grad(net, group, table, xs, ys, held, first, wide):
    seq = xs[0].shape[0]
    many, rows, halves = net.pieces, net.rows, net.n_mp
    at_core = table.shape[0] - 1
    count = len(ys)
    width = ys[0][0].shape[1]
    if wide:
        tall = xs[0].shape[1] // BS
        deep = 2 if tall >= 4 else 1
        steps = tall // deep
        y_width = width // halves
        x_spec = pl.BlockSpec((seq, deep * BS), lambda i, s: (0, i))
        y_spec = pl.BlockSpec((seq, y_width), lambda i, s: (0, s[at_core]))
    else:
        tall = xs[0].shape[1] // halves // BS
        deep = 2 if tall >= 4 else 1
        steps = tall // deep
        y_width = width
        x_spec = pl.BlockSpec((seq, deep * BS), lambda i, s: (0, s[at_core] * steps + i))
        y_spec = pl.BlockSpec((seq, y_width), lambda i, s: (0, 0))
    nb = y_width // BS
    at = first // count
    outs = 2 if many > 1 else 1
    shape = (many // outs, len(GROUPS[group]), tall * nb, rows, BS)
    anyspec = pl.BlockSpec(memory_space=pl.ANY)
    held = held or ()
    before = 3 + 2 * count
    return pl.pallas_call(
        functools.partial(
            weight_grad_body, count=count, outs=outs, many=many, rows=rows, nb=nb
        ),
        grid_spec=pltpu.PrefetchScalarGridSpec(
            num_scalar_prefetch=1,
            grid=(steps,),
            in_specs=[x_spec] * 2 + [y_spec] * (2 * count) + [anyspec] * len(held),
            out_specs=(
                pl.BlockSpec((many // outs, count, deep * nb, rows, BS), lambda i, s: (0, at, i, 0, 0)),
            )
            * outs,
            scratch_shapes=[
                pltpu.VMEM((deep * BS, seq), bf16),
                pltpu.VMEM((deep * BS, seq), bf16),
                pltpu.VMEM((count, deep * BS, y_width), bf16),
            ],
        ),
        out_shape=(jax.ShapeDtypeStruct(shape, bf16),) * outs,
        input_output_aliases={before + k: k for k in range(len(held))},
        compiler_params=params(),
        cost_estimate=small(),
        name="weight_grad",
    )(table, *xs, *[y[0] for y in ys], *[y[1] for y in ys], *held)


def split_low(a):
    hi = a.astype(bf16)
    return hi, (a - hi.astype(f32)).astype(bf16)


def shampoo_body(flag, mine_ref, other_ref, w_ref, ls_ref, rs_ref, lr_ref, rr_ref, *refs):
    og, ol, orr, ow, g_ref = refs[-5:]
    for k in range(mine_ref.shape[0]):
        for plane, src in ((flag[0], mine_ref), (1 - flag[0], other_ref)):
            row = pl.multiple_of(plane * 128 + chunk_of(k) * 16, 16)
            g_ref[pl.ds(row, 16), :] = src[k, 0]
    g = g_ref[...]
    og[0, 0] = g.astype(f32)
    ol[0, 0] = 0.5 * ls_ref[0, 0] + 0.5 * dot_nt(g, g)
    orr[0, 0] = 0.5 * rs_ref[0, 0] + 0.5 * dot_tn(g, g)
    r_hi, r_lo = split_low(rr_ref[0, 0])
    i_hi, i_lo = split_low(dot_nn(g, r_hi) + dot_nn(g, r_lo))
    l_hi, l_lo = split_low(lr_ref[0, 0])
    d = dot_nn(l_hi, i_hi) + (dot_nn(l_hi, i_lo) + dot_nn(l_lo, i_hi))
    mean = jnp.mean(jnp.mean(d * d, axis=1, keepdims=True), axis=0, keepdims=True)
    ow[0, 0] = w_ref[0, 0] - (D**-0.5) * d / jnp.sqrt(mean + 1e-06)


def shampoo(flag, parts, *states):
    total = states[0].shape[1]
    out, first = (), 0
    for mine, other, n in parts:
        at = first // n
        spec = pl.BlockSpec((1, 1, BS, BS), lambda i, at=at, n=n: (0, at * n + i, 0, 0))
        g_spec = pl.BlockSpec((mine.shape[0], 1, mine.shape[2], BS), lambda i: (0, i, 0, 0))
        anyspec = pl.BlockSpec(memory_space=pl.ANY)
        out = pl.pallas_call(
            shampoo_body,
            grid=(n,),
            out_shape=(jax.ShapeDtypeStruct((1, total, BS, BS), f32),) * 4,
            in_specs=[pl.BlockSpec(memory_space=pltpu.SMEM), g_spec, g_spec]
            + [spec] * 5
            + [anyspec] * len(out),
            out_specs=(spec,) * 4,
            scratch_shapes=[pltpu.VMEM((BS, BS), bf16)],
            input_output_aliases={8 + k: k for k in range(len(out))},
            compiler_params=params(),
            cost_estimate=small(),
            name="shampoo",
        )(flag, mine, other, *states, *out)
        first += n
    return out


def norm_forward(z, gain, shift):
    center = z - jnp.mean(z, axis=1, keepdims=True)
    inv = lax.rsqrt(jnp.mean(center * center, axis=1, keepdims=True) + eps_norm)
    normed = center * inv
    return normed * gain + shift, normed, inv


def norm_backward(grad, normed, inv, gain):
    scaled = grad * gain
    mean_plain = jnp.mean(scaled, axis=1, keepdims=True)
    mean_cross = jnp.mean(scaled * normed, axis=1, keepdims=True)
    back = inv * (scaled - mean_plain - normed * mean_cross)
    return back, jnp.sum(grad * normed, axis=0), jnp.sum(grad, axis=0)


def inverse_of(order):
    many = jnp.arange(order.shape[0], dtype=jnp.int32)
    return jnp.sum(jnp.where(order[:, None] == many[None, :], many[:, None], 0), axis=0)


def route_out(value):
    axes = ("rep", "shard")
    count = lax.axis_size(axes)
    cut = value.reshape(value.shape[0], count, value.shape[1] // count, value.shape[2])
    return lax.all_to_all(cut, axes, split_axis=1, concat_axis=0, tiled=True)


def route_home(pieces, ordering):
    moved = pieces.at[ordering].get(mode="promise_in_bounds")
    back = lax.all_to_all(moved, ("rep", "shard"), split_axis=0, concat_axis=1, tiled=True)
    return back.reshape(back.shape[0], -1, back.shape[3])


def per_device(
    net,
    inputs,
    encoded,
    cotangent,
    lengths,
    seq_slots,
    block_slots,
    weights,
    left_stat,
    right_stat,
    left_root,
    right_root,
    vectors,
    vec_stat,
):
    half_d = inputs.shape[2]
    halves = D // half_d
    core = lax.axis_index("mp")
    data_index = lax.axis_index(("rep", "shard"))
    seq_index = data_index * inputs.shape[0] + core
    limit = lax.dynamic_slice_in_dim(lengths, seq_index, 1)
    tables = [net.table(k, core, data_index) for k in range(2 * len(GROUPS))]
    is_first = core == 0

    def pick(pair, which):
        return lax.dynamic_index_in_dim(pair, which, axis=0, keepdims=False)

    def joined(low_half, high_half):
        return jnp.concatenate(
            [
                jnp.where(is_first, low_half, high_half),
                jnp.where(is_first, high_half, low_half),
            ],
            axis=1,
        )

    def whole(value):
        other = net.swap_core(value)
        own = joined(pick(value, core), pick(other, core))
        sib = joined(pick(value, 1 - core), pick(other, 1 - core))
        return own, sib

    def halved(full):
        mine = lax.dynamic_slice_in_dim(full, core * half_d, half_d, axis=1)
        away = lax.dynamic_slice_in_dim(full, (1 - core) * half_d, half_d, axis=1)
        got = net.swap_core(away)
        return jnp.stack([jnp.where(is_first, mine, got), jnp.where(is_first, got, mine)])

    x, x_sib = whole(inputs)
    e, e_sib = whole(encoded)

    pieces, vec_mine = first_pieces(net, weights, vectors, inverse_of(block_slots))
    flows, base = [], 0
    for k in range(len(GROUPS)):
        size = group_blocks(k, halves)
        flows.append(Flow(gather_rounds(net, k, pieces[base : base + size])))
        base += size
    attn, cross, up, down = flows

    def placed(k):
        return place(net, k, tables[k], *flows[k].finish())

    step((), attn)
    step((), attn, cross)
    step((), attn)
    step((), attn, cross)
    vec_mine, x, x_sib, e, e_sib = step((vec_mine, x, x_sib, e, e_sib), attn, cross, up)
    w_sq, w_sk, w_sv = step(placed(0), up)

    vec_other = net.swap_core(vec_mine)
    vec_both = jnp.concatenate(
        [jnp.where(is_first, vec_mine, vec_other), jnp.where(is_first, vec_other, vec_mine)]
    ).astype(f32)
    vecs = [vec_both[:, i * half_d : (i + 1) * half_d].reshape(1, D) for i in range(13)]
    vecs.append(vec_both[:, 13 * half_d :].reshape(1, FF))
    b_sq, b_sv, b_so, g_one, b_one, b_cq, b_cv, b_co, g_two, b_two, b_fo, g_three, b_three, b_fi = vecs

    q_s = (dot_nn(x, w_sq) + b_sq).astype(bf16)
    k_s = dot_nn(x, w_sk).astype(bf16)
    v_s = (dot_nn(x, w_sv) + b_sv).astype(bf16)
    q_s, k_s, v_s = step((q_s, k_s, v_s), cross, up, down)
    o_s, lse_s = attend_forward(limit, q_s, k_s, v_s, True)
    cotangent, o_s, lse_s = step((cotangent, o_s, lse_s), cross, up, down)
    cot_pieces = route_out(cotangent)
    w_so, w_cq, w_ck, w_cv, w_co = placed(1)
    z_one = x.astype(f32) + dot_nn(o_s, w_so) + b_so
    h_one, n_one, r_one = norm_forward(z_one, g_one, b_one)
    h_one_low = h_one.astype(bf16)
    q_c = (dot_nn(h_one_low, w_cq) + b_cq).astype(bf16)
    k_c = dot_nn(e, w_ck).astype(bf16)
    v_c = (dot_nn(e, w_cv) + b_cv).astype(bf16)
    q_c, k_c, v_c = step((q_c, k_c, v_c), down)
    o_c, lse_c = attend_forward(limit, q_c, k_c, v_c, False)
    z_two = h_one + dot_nn(o_c, w_co) + b_co
    h_two, n_two, r_two = norm_forward(z_two, g_two, b_two)
    cot_pieces, h_two, h_two_low = step((cot_pieces, h_two, h_two.astype(bf16)), up, down)
    cot_home = route_home(cot_pieces, seq_slots)
    (w_fi,) = placed(2)
    act, slope = gelu_forward(h_two_low, w_fi, b_fi)
    act_sib = net.swap_core(act)
    act, slope = step((act, slope), down)
    (w_fo,) = placed(3)
    z_three = h_two + dot_nn(act, w_fo) + b_fo
    cot, _ = whole(cot_home)
    h_three, n_three, r_three = norm_forward(z_three, g_three, b_three)
    live = (jnp.arange(x.shape[0]) < limit).astype(f32)[:, None]
    source = inverse_of(seq_slots)
    finished = (h_three * live).astype(bf16)

    def gradient(k, *calls):
        held, first = None, 0
        for xs, *ys in calls:
            held = weight_grad(net, k, tables[len(GROUPS) + k], xs, ys, held, first, GROUPS[k][first][1])
            first += len(ys)
        parts = tuple(h.reshape(h.shape[0], -1, net.rows, BS) for h in held)
        return Flow(reduce_rounds(net, len(GROUPS) + k, parts))

    grad_y = cot.astype(f32) * live
    d_three, dg_three, db_three = norm_backward(grad_y, n_three, r_three, g_three)
    a_three = d_three.astype(bf16)
    d_hidden = (dot_nt(a_three, w_fo) * slope.astype(f32)).astype(bf16)
    a_three_sib, d_hidden = step((net.swap_core(a_three), d_hidden))
    d_hidden_sib = net.swap_core(d_hidden)
    down = gradient(3, ((act, act_sib), (a_three, a_three_sib)))
    finished, d_hidden, d_hidden_sib = step((finished, d_hidden, d_hidden_sib), down)
    finished = halved(finished)
    d_h_two = d_three + dot_nt(d_hidden, w_fi)
    d_two, dg_two, db_two = norm_backward(d_h_two, n_two, r_two, g_two)
    a_two = d_two.astype(bf16)
    d_oc = dot_nt(a_two, w_co).astype(bf16)
    finished, d_hidden, d_hidden_sib, d_oc = step((finished, d_hidden, d_hidden_sib, d_oc))
    out_pieces = route_out(finished)
    up = gradient(2, ((h_two_low, net.swap_core(h_two_low)), (d_hidden, d_hidden_sib)))
    (d_oc,) = step((d_oc,), up, down)
    dq_c, dk_c, dv_c = attend_backward(limit, q_c, k_c, v_c, o_c, d_oc, lse_c, False)
    dq_c_sib, dk_c_sib, dv_c_sib = [net.swap_core(v) for v in (dq_c, dk_c, dv_c)]
    dq_c, dk_c, dv_c = step((dq_c, dk_c, dv_c), down)
    d_h_one = d_two + dot_nt(dq_c, w_cq)
    d_one, dg_one, db_one = norm_backward(d_h_one, n_one, r_one, g_one)
    a_one = d_one.astype(bf16)
    a_one_sib = net.swap_core(a_one)
    d_os = dot_nt(a_one, w_so).astype(bf16)
    out_pieces, a_one, a_one_sib, d_os = step((out_pieces, a_one, a_one_sib, d_os))
    outputs = route_home(out_pieces, source)
    cross = gradient(
        1,
        ((o_s, net.swap_core(o_s)), (a_one, a_one_sib)),
        ((h_one_low, net.swap_core(h_one_low)), (dq_c, dq_c_sib)),
        ((e, e_sib), (dk_c, dk_c_sib), (dv_c, dv_c_sib)),
        ((o_c, net.swap_core(o_c)), (a_two, net.swap_core(a_two))),
    )
    outputs, d_os = step((outputs, d_os), cross, up, down)
    dq_s, dk_s, dv_s = attend_backward(limit, q_s, k_s, v_s, o_s, d_os, lse_s, True)
    sibs = [net.swap_core(v) for v in (dq_s, dk_s, dv_s)]
    dq_s, dk_s, dv_s = step((dq_s, dk_s, dv_s), cross)
    attn = gradient(0, ((x, x_sib), *zip((dq_s, dk_s, dv_s), sibs)))
    dq_s, dk_s, dv_s = step((dq_s, dk_s, dv_s), attn)
    dk_c, dv_c, dq_s, dk_s, dv_s = step((dk_c, dv_c, dq_s, dk_s, dv_s), cross, up)
    state_back = dot_nt(dk_c, w_ck) + dot_nt(dv_c, w_cv)
    back = d_one + dot_nt(dq_s, w_sq) + dot_nt(dk_s, w_sk) + dot_nt(dv_s, w_sv)
    back, d_hidden, dq_c, dv_c = step((back, d_hidden, dq_c, dv_c), attn, cross, up)
    input_grad = halved(back.astype(bf16))
    encoded_grad = halved(state_back.astype(bf16))
    dq_s, dv_s = step((dq_s, dv_s), attn)
    columns = [jnp.sum(v.astype(f32), axis=0) for v in (d_hidden, dq_c, dv_c, dq_s, dv_s)]
    *columns, input_grad, encoded_grad = step((*columns, input_grad, encoded_grad), attn, cross, up)
    sums = (
        columns[3],
        columns[4],
        jnp.sum(d_one, axis=0),
        dg_one,
        db_one,
        columns[1],
        columns[2],
        jnp.sum(d_two, axis=0),
        dg_two,
        db_two,
        jnp.sum(d_three, axis=0),
        dg_three,
        db_three,
        columns[0],
    )
    vec_pair = jnp.concatenate([s.reshape(halves, -1) for s in sums], axis=1)
    vec_sum = pick(vec_pair, core) + net.swap_core(pick(vec_pair, 1 - core))
    natural = [f.finish() for f in (attn, cross, up, down)]

    parts, flag, vec_owned = last_pieces(net, jnp.concatenate(natural), block_slots, vec_sum)
    block_grad, left_new, right_new, weights_new = shampoo(
        flag, parts, weights, left_stat, right_stat, left_root, right_root
    )
    vec_stat_new = 0.5 * vec_stat + 0.5 * vec_owned * vec_owned
    vectors_new = vectors - 0.1 * vec_owned * lax.rsqrt(vec_stat_new)
    return (
        outputs,
        input_grad,
        encoded_grad,
        block_grad,
        left_new,
        right_new,
        weights_new,
        vec_owned,
        vec_stat_new,
        vectors_new,
    )


def solution(mesh):
    net = Net(mesh.shape["rep"], mesh.shape["shard"], mesh.shape["mp"])
    rows = P(("rep", "shard"), None, "mp")
    blocks = P("mp", "shard", None, None)
    vector = P("mp", "shard")
    in_specs = (rows, rows, rows, P(), P(), P()) + (blocks,) * 5 + (vector, vector)
    out_specs = (rows, rows, rows) + (blocks,) * 4 + (vector,) * 3
    return jax.shard_map(
        functools.partial(per_device, net),
        mesh=mesh,
        in_specs=in_specs,
        out_specs=out_specs,
        check_vma=False,
    )
```

```python
import functools

import jax
import jax.numpy as jnp
import numpy as np
from jax import lax
from jax.experimental import pallas as pl
from jax.experimental.pallas import tpu as pltpu
from jax.sharding import PartitionSpec as P

D = 1024
FF = 4096
HEAD_DIM = 64
BS = 256
LANES = 128

eps_norm = 1e-05
masked_score = -1e30
scale = HEAD_DIM**-0.5
bf16 = jnp.bfloat16
f32 = jnp.float32

NT = (((1,), (1,)), ((), ()))
TN = (((0,), (0,)), ((), ()))

VMEM_LIMIT = 60 * 1024 * 1024

ERFC_SLOPE = 0.3
ERFC_POLY = (
    0.1691880090604902,
    0.17071516163759975,
    0.14833963774537734,
    0.21492421686136995,
    -0.09464635292673967,
    0.5477136065073498,
    -0.5122723795383668,
    0.4855603950654946,
    -0.1295223139805042,
)


def dot_nn(a, b):
    return jnp.dot(a, b, preferred_element_type=f32)


def dot_nt(a, b):
    return lax.dot_general(a, b, NT, preferred_element_type=f32)


def dot_tn(a, b):
    return lax.dot_general(a, b, TN, preferred_element_type=f32)


def small():
    return pl.CostEstimate(flops=1 << 20, bytes_accessed=1 << 20, transcendentals=0)


def params(**kw):
    return pltpu.CompilerParams(vmem_limit_bytes=VMEM_LIMIT, **kw)


GROUPS = (
    (("sq", True), ("sk", True), ("sv", True)),
    (("so", False), ("cq", True), ("ck", True), ("cv", True), ("co", False)),
    (("fi", True),),
    (("fo", False),),
)
SHAPES = {name: (D, D) for name in ("sq", "sk", "sv", "so", "cq", "ck", "cv", "co")}
SHAPES["fi"], SHAPES["fo"] = (D, FF), (FF, D)


def chunk_of(i):
    return (i & 8) | ((i & 2) << 1) | ((i & 1) << 1) | ((i & 4) >> 2)


class Net:
    def __init__(self, n_rep, n_shard, n_mp):
        self.n_rep, self.n_shard, self.n_mp = n_rep, n_shard, n_mp
        self.n_data = n_rep * n_shard
        self.pieces = 16 if (n_rep, n_shard, n_mp) == (2, 8, 2) else 1
        self.rows = BS // self.pieces
        self.depth = self.pieces.bit_length() - 1
        x, z1, z2, y = 1, 2, 4, 8
        gathering = (
            ((z2, y, z1, x), (z2, z1, x, y)),
            ((z2, z1, y, x), (z2, z1, x, y)),
            ((z2, x, z1, y), (z2, y, z1, x)),
            ((z2, x, y, z1), (z2, y, z1, x)),
        )
        reducing = (((z2, z1, y, x), (z2, z1, x, y)),) + gathering[1:]
        self.orders = gathering + reducing

    def swap_core(self, value):
        return lax.ppermute(value, "mp", [(i, i ^ 1) for i in range(self.n_mp)])

    def swap_rep(self, value):
        return lax.ppermute(value, "rep", [(i, i ^ 1) for i in range(self.n_rep)])

    def swap_data(self, value, group, step):
        pairs = []
        for i in range(self.n_data):
            for m in range(self.n_mp):
                there = i ^ self.orders[group][m][step]
                pairs.append((i * self.n_mp + m, there * self.n_mp + m))
        return lax.ppermute(value, ("rep", "shard", "mp"), pairs)

    def table(self, group, core, data_index):
        many = self.pieces
        if many == 1:
            return jnp.stack([0, 0, 0, 0, core]).astype(jnp.int32)
        half = many // 4
        rel = []
        for order in self.orders[group]:
            rel.append([sum(b for s, b in enumerate(order) if q >> s & 1) for q in range(many)])
        rows = []
        for m in range(self.n_mp):
            place = [rel[1 - m].index(r) // 2 for r in rel[m][::2]]
            low = [p for p in place if p < half][0]
            high = [p - half for p in place if p >= half][0]
            lows, highs = [], []
            for p in place:
                low, high = (p, high) if p < half else (low, p - half)
                lows.append(low)
                highs.append(high)
            rows.append([chunk_of(r) for r in rel[m]] + lows + highs + [int(p >= half) for p in place])
        mine = jnp.asarray(np.array(rows, np.int32))[core]
        chunks = mine[:many] ^ chunk_of(data_index)
        return jnp.concatenate([chunks, mine[many:], core.reshape(1)]).astype(jnp.int32)


def together(*values):
    return lax.optimization_barrier(values)


class Flow:
    def __init__(self, rounds):
        self.rounds = rounds
        self.flying = next(rounds)

    def advance(self, values):
        try:
            self.flying = self.rounds.send(values)
        except StopIteration as stop:
            self.flying = None
            self.result = stop.value

    def finish(self):
        while self.flying is not None:
            self.advance(self.flying)
        return self.result


def step(main, *flows):
    flows = [f for f in flows if f.flying is not None]
    values = list(together(*main, *[v for f in flows for v in f.flying]))
    main, values = values[: len(main)], values[len(main) :]
    for f in flows:
        many = len(f.flying)
        f.advance(tuple(values[:many]))
        values = values[many:]
    return main


def blocks_of(name, n_mp):
    rows, cols = SHAPES[name]
    return rows * cols // n_mp // (BS * BS)


def group_blocks(group, n_mp):
    return sum(blocks_of(name, n_mp) for name, _ in GROUPS[group])


def place_body(s, *refs, dests, many, two):
    q = pl.program_id(0)
    steps = many // 2 if two else 1
    if two:
        own_lo, own_hi, sib_lo, sib_hi = refs[:4]
        outs = refs[4:]
    else:
        own_lo, sib_lo = refs[:2]
        outs = refs[2:]
    core = s[many + 3 * steps]
    rows = own_lo.shape[2]
    for t in range(own_lo.shape[0]):
        here = pl.ds(0, rows)
        if two:
            here = pl.ds(pl.multiple_of((s[2 * q + t] & 1) * rows, rows), rows)
        for b in range(own_lo.shape[1]):
            own, sib = own_lo[t, b], sib_lo[t, b]
            if two:
                own = jnp.where(q < steps // 2, own, own_hi[t, b])
                sib = jnp.where(s[many + 2 * steps + q] == 0, sib, sib_hi[t, b])
            for h in range(2):
                which, row, col = dests[h][b]
                outs[which][row, here, col : col + BS] = jnp.where(core == h, own, sib)


def place(net, group, table, own, sib):
    many, rows, n_mp = net.pieces, net.rows, net.n_mp
    two = many > 1
    per = 2 if two else 1
    steps = many // per
    half = max(steps // 2, 1)
    dests = ([], [])
    shapes, specs = [], []
    for which, (name, wide) in enumerate(GROUPS[group]):
        height, width = SHAPES[name]
        tall = height if wide else height // n_mp
        flat = width // n_mp if wide else width
        for h in range(n_mp):
            for r in range(tall // BS):
                for c in range(flat // BS):
                    if wide:
                        dests[h].append((which, r, h * flat + c * BS))
                    else:
                        dests[h].append((which, h * (tall // BS) + r, c * BS))
        shapes.append(jax.ShapeDtypeStruct((height // BS, BS, width), bf16))
        specs.append(
            pl.BlockSpec((height // BS, per * rows, width), lambda q, s: (0, s[per * q] // per, 0))
        )
    nb = own[0].shape[1]
    block = (per, nb, rows, BS)
    lo = pl.BlockSpec(block, lambda q, s: (jnp.minimum(q, half - 1), 0, 0, 0))
    hi = pl.BlockSpec(block, lambda q, s: (jnp.maximum(q - half, 0), 0, 0, 0))
    sib_lo = pl.BlockSpec(block, lambda q, s: (s[many + q], 0, 0, 0))
    sib_hi = pl.BlockSpec(block, lambda q, s: (s[many + steps + q], 0, 0, 0))
    out = pl.pallas_call(
        functools.partial(place_body, dests=dests, many=many, two=two),
        grid_spec=pltpu.PrefetchScalarGridSpec(
            num_scalar_prefetch=1,
            grid=(steps,),
            in_specs=[lo, hi, sib_lo, sib_hi] if two else [lo, sib_lo],
            out_specs=tuple(specs),
        ),
        out_shape=tuple(shapes),
        compiler_params=params(),
        cost_estimate=small(),
        name="place",
    )(table, *own, *sib)
    return [o.reshape(-1, o.shape[2]) for o in out]


def gather_rounds(net, group, piece):
    (piece,) = yield (piece,)
    cur = piece[None]
    if net.pieces == 1:
        (sib,) = yield (net.swap_core(cur),)
        return (cur,), (sib,)
    for k in range(net.depth - 1):
        (got,) = yield (net.swap_data(cur, group, k),)
        cur = jnp.concatenate([cur, got])
    got, sib_lo = yield (net.swap_data(cur, group, net.depth - 1), net.swap_core(cur))
    (sib_hi,) = yield (net.swap_core(got),)
    return (cur, got), (sib_lo, sib_hi)


def first_pieces(net, weights, vectors, inverse):
    low = weights[0].astype(bf16)
    vec = vectors.astype(bf16)
    if net.pieces == 1:
        every = lax.all_gather(low, "shard", axis=0, tiled=True)
        vec_every = lax.all_gather(vec, "shard", axis=1, tiled=True)
        return every.at[inverse].get(mode="promise_in_bounds"), vec_every
    nblk = low.shape[0]
    cut = low.reshape(nblk, 2, 2, 2, 2, net.rows, BS)
    cut = lax.dynamic_index_in_dim(cut, lax.axis_index("rep"), axis=1, keepdims=False)
    cut = cut.transpose(3, 1, 2, 0, 4, 5).reshape(net.n_shard, nblk, net.rows, BS)
    room = net.rows * BS
    vec_cut = jnp.pad(vec.reshape(-1), (0, room - vec.shape[1])).reshape(1, 1, net.rows, BS)
    cut = jnp.concatenate([cut, jnp.broadcast_to(vec_cut, (net.n_shard,) + vec_cut.shape[1:])], axis=1)
    every = lax.all_to_all(
        cut.reshape(-1, net.rows, BS), "shard", split_axis=0, concat_axis=0, tiled=True
    )
    pieces = every.at[inverse + inverse // nblk].get(mode="promise_in_bounds")
    vec_every = every.reshape(net.n_shard, nblk + 1, room)[:, nblk, : vec.shape[1]]
    return pieces, vec_every.reshape(1, -1)


def total_of(*terms):
    acc = terms[0].astype(f32)
    for t in terms[1:]:
        acc = acc + t.astype(f32)
    return acc.astype(bf16)


def reduce_rounds(net, group, parts):
    parts = yield parts
    if net.pieces == 1:
        return parts[0][0]
    lo, hi = parts
    (got,) = yield (net.swap_data(hi, group, net.depth - 1),)
    terms = [lo, got]
    for k in range(net.depth - 2, -1, -1):
        width = 1 << k
        send = total_of(*[t[width:] for t in terms])
        keep = total_of(*[t[:width] for t in terms])
        (got,) = yield (net.swap_data(send, group, k),)
        terms = [keep, got]
    return total_of(*terms)[0]


def last_pieces(net, natural, block_slots, vec_sum):
    if net.pieces == 1:
        dealt = natural.at[block_slots].get(mode="promise_in_bounds")
        owned = lax.psum_scatter(dealt, "shard", scatter_dimension=0, tiled=True)
        owned = total_of(owned, net.swap_rep(owned))
        cut = owned.reshape(-1, 2, 8, 16, BS).transpose(1, 2, 0, 3, 4)
        cut = cut[:, np.array([chunk_of(k) for k in range(8)])]
        vec = lax.psum_scatter(vec_sum, "shard", scatter_dimension=0, tiled=True)[None]
        parts = [(cut[0], cut[1], owned.shape[0])]
        return parts, jnp.zeros((1,), jnp.int32), vec + net.swap_rep(vec)
    n = net.n_shard
    slots = block_slots.reshape(n, -1)
    half = slots.shape[1] // 2
    room = net.rows * BS
    vec_cut = vec_sum.reshape(n, -1)
    width = vec_cut.shape[1]
    vec_cut = jnp.pad(vec_cut.astype(bf16), ((0, 0), (0, room - width)))
    vec_cut = vec_cut.reshape(n, 1, net.rows, BS)
    cuts = []
    for k in range(2):
        index = slots[:, k * half : (k + 1) * half].reshape(-1)
        cuts.append(natural.at[index].get(mode="promise_in_bounds").reshape(n, half, net.rows, BS))
    cuts[1] = jnp.concatenate([cuts[1], vec_cut], axis=1)

    def home(cut):
        back = lax.all_to_all(
            cut.reshape(-1, net.rows, BS), "shard", split_axis=0, concat_axis=0, tiled=True
        )
        return back.reshape(n, -1, net.rows, BS)

    mine, cuts[1] = together(home(cuts[0]), cuts[1])
    other = net.swap_rep(mine)
    other, last = together(other, home(cuts[1]))
    parts = [(mine, other, half), (last, net.swap_rep(last), half)]
    terms = [v[:, half].reshape(n, room)[:, :width].astype(f32) for v in parts[1][:2]]
    flag = lax.axis_index("rep").astype(jnp.int32).reshape(1)
    return parts, flag, jnp.sum(terms[0] + terms[1], axis=0, keepdims=True)


def attend_forward_body(lim, q_ref, k_ref, v_ref, o_ref, lse_ref, *, causal, rows):
    pair = pl.program_id(0)
    seq, keys = q_ref.shape[0], k_ref.shape[0]
    lane = lax.broadcasted_iota(jnp.int32, (1, LANES), 1)
    top = lim[0] - 1

    @pl.when(pair == 0)
    def _():
        lse_ref[...] = jnp.zeros_like(lse_ref)

    for blk in range(seq // rows):
        here = pl.ds(blk * rows, rows)
        width = (blk + 1) * rows if causal else keys
        q = q_ref[here, :] * bf16(scale)
        k = k_ref[pl.ds(0, width), :]
        v = v_ref[pl.ds(0, width), :]
        outs = []
        kept = lse_ref[here, :]
        if causal:
            row = lax.broadcasted_iota(jnp.int32, (rows, 1), 0) + blk * rows
            col = lax.broadcasted_iota(jnp.int32, (1, width), 1)
            allowed = col <= jnp.minimum(row, top)
        for h in range(2):
            mine = (lane // HEAD_DIM) == h
            s = dot_nt(jnp.where(mine, q, bf16(0)), k)
            if causal:
                s = jnp.where(allowed, s, masked_score)
            peak = jnp.max(s, axis=1, keepdims=True)
            e = jnp.exp(s - peak)
            mass = jnp.sum(e, axis=1, keepdims=True)
            outs.append(dot_nn(e.astype(bf16), v) * (1.0 / mass))
            kept = jnp.where(lane == 2 * pair + h, peak + jnp.log(mass), kept)
        o_ref[here, :] = jnp.where(lane < HEAD_DIM, outs[0], outs[1]).astype(bf16)
        lse_ref[here, :] = kept


def attend_forward(limit, q, k, v, causal):
    seq, width = q.shape
    keys = k.shape[0]
    pairs = width // LANES
    rows = min(128 if causal else 256, seq)
    o, lse = pl.pallas_call(
        functools.partial(attend_forward_body, causal=causal, rows=rows),
        grid=(pairs,),
        out_shape=(
            jax.ShapeDtypeStruct((seq, width), bf16),
            jax.ShapeDtypeStruct((seq, LANES), f32),
        ),
        in_specs=[
            pl.BlockSpec(memory_space=pltpu.SMEM),
            pl.BlockSpec((seq, LANES), lambda i: (0, i)),
            pl.BlockSpec((keys, LANES), lambda i: (0, i)),
            pl.BlockSpec((keys, LANES), lambda i: (0, i)),
        ],
        out_specs=(
            pl.BlockSpec((seq, LANES), lambda i: (0, i)),
            pl.BlockSpec((seq, LANES), lambda i: (0, 0)),
        ),
        compiler_params=params(),
        cost_estimate=small(),
        name="attend_forward",
    )(limit, q, k, v)
    return o, lse[:, : 2 * pairs].T.reshape(pairs, 2, seq)


def attend_backward_body(
    lim, q_ref, k_ref, v_ref, o_ref, do_ref, lse_ref, dq_ref, dk_ref, dv_ref, dk_acc, dv_acc, *, causal, rows
):
    seq, keys = q_ref.shape[0], k_ref.shape[0]
    lane = lax.broadcasted_iota(jnp.int32, (1, LANES), 1)
    top = lim[0] - 1
    dk_acc[...] = jnp.zeros_like(dk_acc)
    dv_acc[...] = jnp.zeros_like(dv_acc)
    head_row = lax.broadcasted_iota(jnp.int32, (8, LANES), 0)
    head_lane = lax.broadcasted_iota(jnp.int32, (8, LANES), 1) // HEAD_DIM
    pick = (head_row == head_lane).astype(bf16)
    for blk in range(seq // rows):
        here = pl.ds(blk * rows, rows)
        width = (blk + 1) * rows if causal else keys
        span = pl.ds(0, width)
        q = q_ref[here, :] * bf16(scale)
        do = do_ref[here, :]
        k = k_ref[span, :]
        v = v_ref[span, :]
        prod = do.astype(f32) * o_ref[here, :].astype(f32)
        hi = prod.astype(bf16)
        lo = (prod - hi.astype(f32)).astype(bf16)
        delta = dot_nt(pick, hi) + dot_nt(pick, lo)
        lse = lse_ref[0][:, blk * rows : (blk + 1) * rows]
        if causal:
            key = lax.broadcasted_iota(jnp.int32, (width, 1), 0)
            row = lax.broadcasted_iota(jnp.int32, (1, rows), 1) + blk * rows
            allowed = key <= jnp.minimum(row, top)
        dq = jnp.zeros((rows, LANES), f32)
        dk = jnp.zeros((width, LANES), f32)
        dv = jnp.zeros((width, LANES), f32)
        for h in range(2):
            mine = (lane // HEAD_DIM) == h
            qm = jnp.where(mine, q, bf16(0))
            dom = jnp.where(mine, do, bf16(0))
            km = jnp.where(mine, k, bf16(0))
            s = dot_nt(k, qm)
            if causal:
                s = jnp.where(allowed, s, masked_score)
            p = jnp.exp(s - lse[h : h + 1, :])
            dp = dot_nt(v, dom)
            ds = (p * (dp - delta[h : h + 1, :])).astype(bf16)
            dv = dv + dot_nn(p.astype(bf16), dom)
            dk = dk + dot_nn(ds, qm)
            dq = dq + dot_tn(ds, km)
        dq_ref[here, :] = (dq * scale).astype(bf16)
        dk_acc[span, :] += dk
        dv_acc[span, :] += dv
    dk_ref[...] = dk_acc[...].astype(bf16)
    dv_ref[...] = dv_acc[...].astype(bf16)


def attend_backward(limit, q, k, v, o, do, lse, causal):
    seq, width = q.shape
    keys = k.shape[0]
    pairs = width // LANES
    rows = min(128 if causal else 256, seq)
    q_spec = pl.BlockSpec((seq, LANES), lambda i: (0, i))
    k_spec = pl.BlockSpec((keys, LANES), lambda i: (0, i))
    return pl.pallas_call(
        functools.partial(attend_backward_body, causal=causal, rows=rows),
        grid=(pairs,),
        out_shape=(
            jax.ShapeDtypeStruct((seq, width), bf16),
            jax.ShapeDtypeStruct((keys, width), bf16),
            jax.ShapeDtypeStruct((keys, width), bf16),
        ),
        in_specs=[
            pl.BlockSpec(memory_space=pltpu.SMEM),
            q_spec,
            k_spec,
            k_spec,
            q_spec,
            q_spec,
            pl.BlockSpec((1, 2, seq), lambda i: (i, 0, 0)),
        ],
        out_specs=(q_spec, k_spec, k_spec),
        scratch_shapes=[pltpu.VMEM((keys, LANES), f32), pltpu.VMEM((keys, LANES), f32)],
        compiler_params=params(),
        cost_estimate=small(),
        name="attend_backward",
    )(limit, q, k, v, o, do, lse)


def gelu_body(h_ref, w_ref, b_ref, act_ref, slope_ref, u_ref, *, chunk):
    u_ref[...] = dot_nn(h_ref[...], w_ref[...]) + b_ref[...]

    def part(i):
        here = pl.ds(pl.multiple_of(i * chunk, chunk), chunk)
        u = u_ref[here, :]
        x = jnp.abs(u) * (0.5**0.5)
        t = 1.0 / (1.0 + ERFC_SLOPE * x)
        poly = jnp.full_like(t, ERFC_POLY[-1])
        for c in ERFC_POLY[-2::-1]:
            poly = poly * t + c
        bell = jnp.exp(-0.5 * (u * u))
        tail = 0.5 * (bell * (t * poly))
        cdf = jnp.where(u < 0, tail, 1.0 - tail)
        act_ref[here, :] = (u * cdf).astype(bf16)
        slope_ref[here, :] = (cdf + u * (bell * 0.3989422804014327)).astype(bf16)

    pl.loop(0, u_ref.shape[0] // chunk)(part)


def gelu_forward(h, w, b):
    seq, width = h.shape
    hidden = w.shape[1]
    tile = 512
    spec = pl.BlockSpec((seq, tile), lambda i: (0, i))
    return pl.pallas_call(
        functools.partial(gelu_body, chunk=32),
        grid=(hidden // tile,),
        out_shape=(jax.ShapeDtypeStruct((seq, hidden), bf16),) * 2,
        in_specs=[
            pl.BlockSpec((seq, width), lambda i: (0, 0)),
            pl.BlockSpec((width, tile), lambda i: (0, i)),
            pl.BlockSpec((1, tile), lambda i: (0, i)),
        ],
        out_specs=(spec, spec),
        scratch_shapes=[pltpu.VMEM((seq, tile), f32)],
        compiler_params=params(),
        cost_estimate=small(),
        name="gelu_forward",
    )(h, w, b)


def weight_grad_body(s, x_own, x_sib, *refs, count, outs, many, rows, nb):
    y_own, y_sib = refs[:count], refs[count : 2 * count]
    targets = refs[-3 - outs : -3]
    t_own, t_sib, buf = refs[-3:]
    t_own[...] = x_own[...].T
    t_sib[...] = x_sib[...].T
    per = many // outs
    for k in range(count):
        acc = dot_nn(t_own[...], y_own[k][...]) + dot_nn(t_sib[...], y_sib[k][...])
        buf[k] = acc.astype(bf16)
    for q in range(many):
        for r in range(x_own.shape[1] // BS):
            here = pl.ds(pl.multiple_of(s[q] * rows + r * BS, rows), rows)
            for k in range(count):
                for c in range(nb):
                    targets[q // per][q % per, k, r * nb + c] = buf[k, here, c * BS : (c + 1) * BS]


def weight_grad(net, group, table, xs, ys, held, first, wide):
    seq = xs[0].shape[0]
    many, rows, halves = net.pieces, net.rows, net.n_mp
    at_core = table.shape[0] - 1
    count = len(ys)
    width = ys[0][0].shape[1]
    if wide:
        tall = xs[0].shape[1] // BS
        deep = 2 if tall >= 4 else 1
        steps = tall // deep
        y_width = width // halves
        x_spec = pl.BlockSpec((seq, deep * BS), lambda i, s: (0, i))
        y_spec = pl.BlockSpec((seq, y_width), lambda i, s: (0, s[at_core]))
    else:
        tall = xs[0].shape[1] // halves // BS
        deep = 2 if tall >= 4 else 1
        steps = tall // deep
        y_width = width
        x_spec = pl.BlockSpec((seq, deep * BS), lambda i, s: (0, s[at_core] * steps + i))
        y_spec = pl.BlockSpec((seq, y_width), lambda i, s: (0, 0))
    nb = y_width // BS
    at = first // count
    outs = 2 if many > 1 else 1
    shape = (many // outs, len(GROUPS[group]), tall * nb, rows, BS)
    anyspec = pl.BlockSpec(memory_space=pl.ANY)
    held = held or ()
    before = 3 + 2 * count
    return pl.pallas_call(
        functools.partial(
            weight_grad_body, count=count, outs=outs, many=many, rows=rows, nb=nb
        ),
        grid_spec=pltpu.PrefetchScalarGridSpec(
            num_scalar_prefetch=1,
            grid=(steps,),
            in_specs=[x_spec] * 2 + [y_spec] * (2 * count) + [anyspec] * len(held),
            out_specs=(
                pl.BlockSpec((many // outs, count, deep * nb, rows, BS), lambda i, s: (0, at, i, 0, 0)),
            )
            * outs,
            scratch_shapes=[
                pltpu.VMEM((deep * BS, seq), bf16),
                pltpu.VMEM((deep * BS, seq), bf16),
                pltpu.VMEM((count, deep * BS, y_width), bf16),
            ],
        ),
        out_shape=(jax.ShapeDtypeStruct(shape, bf16),) * outs,
        input_output_aliases={before + k: k for k in range(len(held))},
        compiler_params=params(),
        cost_estimate=small(),
        name="weight_grad",
    )(table, *xs, *[y[0] for y in ys], *[y[1] for y in ys], *held)


def split_low(a):
    hi = a.astype(bf16)
    return hi, (a - hi.astype(f32)).astype(bf16)


def shampoo_body(flag, mine_ref, other_ref, w_ref, ls_ref, rs_ref, lr_ref, rr_ref, *refs):
    og, ol, orr, ow, g_ref = refs[-5:]
    for k in range(mine_ref.shape[0]):
        for plane, src in ((flag[0], mine_ref), (1 - flag[0], other_ref)):
            row = pl.multiple_of(plane * 128 + chunk_of(k) * 16, 16)
            g_ref[pl.ds(row, 16), :] = src[k, 0]
    g = g_ref[...]
    og[0, 0] = g.astype(f32)
    ol[0, 0] = 0.5 * ls_ref[0, 0] + 0.5 * dot_nt(g, g)
    orr[0, 0] = 0.5 * rs_ref[0, 0] + 0.5 * dot_tn(g, g)
    r_hi, r_lo = split_low(rr_ref[0, 0])
    i_hi, i_lo = split_low(dot_nn(g, r_hi) + dot_nn(g, r_lo))
    l_hi, l_lo = split_low(lr_ref[0, 0])
    d = dot_nn(l_hi, i_hi) + (dot_nn(l_hi, i_lo) + dot_nn(l_lo, i_hi))
    mean = jnp.mean(jnp.mean(d * d, axis=1, keepdims=True), axis=0, keepdims=True)
    ow[0, 0] = w_ref[0, 0] - (D**-0.5) * d / jnp.sqrt(mean + 1e-06)


def shampoo(flag, parts, *states):
    total = states[0].shape[1]
    out, first = (), 0
    for mine, other, n in parts:
        at = first // n
        spec = pl.BlockSpec((1, 1, BS, BS), lambda i, at=at, n=n: (0, at * n + i, 0, 0))
        g_spec = pl.BlockSpec((mine.shape[0], 1, mine.shape[2], BS), lambda i: (0, i, 0, 0))
        anyspec = pl.BlockSpec(memory_space=pl.ANY)
        out = pl.pallas_call(
            shampoo_body,
            grid=(n,),
            out_shape=(jax.ShapeDtypeStruct((1, total, BS, BS), f32),) * 4,
            in_specs=[pl.BlockSpec(memory_space=pltpu.SMEM), g_spec, g_spec]
            + [spec] * 5
            + [anyspec] * len(out),
            out_specs=(spec,) * 4,
            scratch_shapes=[pltpu.VMEM((BS, BS), bf16)],
            input_output_aliases={8 + k: k for k in range(len(out))},
            compiler_params=params(),
            cost_estimate=small(),
            name="shampoo",
        )(flag, mine, other, *states, *out)
        first += n
    return out


def norm_forward(z, gain, shift):
    center = z - jnp.mean(z, axis=1, keepdims=True)
    inv = lax.rsqrt(jnp.mean(center * center, axis=1, keepdims=True) + eps_norm)
    normed = center * inv
    return normed * gain + shift, normed, inv


def norm_backward(grad, normed, inv, gain):
    scaled = grad * gain
    mean_plain = jnp.mean(scaled, axis=1, keepdims=True)
    mean_cross = jnp.mean(scaled * normed, axis=1, keepdims=True)
    back = inv * (scaled - mean_plain - normed * mean_cross)
    return back, jnp.sum(grad * normed, axis=0), jnp.sum(grad, axis=0)


def inverse_of(order):
    many = jnp.arange(order.shape[0], dtype=jnp.int32)
    return jnp.sum(jnp.where(order[:, None] == many[None, :], many[:, None], 0), axis=0)


def route_out(value):
    axes = ("rep", "shard")
    count = lax.axis_size(axes)
    cut = value.reshape(value.shape[0], count, value.shape[1] // count, value.shape[2])
    return lax.all_to_all(cut, axes, split_axis=1, concat_axis=0, tiled=True)


def route_home(pieces, ordering):
    moved = pieces.at[ordering].get(mode="promise_in_bounds")
    back = lax.all_to_all(moved, ("rep", "shard"), split_axis=0, concat_axis=1, tiled=True)
    return back.reshape(back.shape[0], -1, back.shape[3])


def per_device(
    net,
    inputs,
    encoded,
    cotangent,
    lengths,
    seq_slots,
    block_slots,
    weights,
    left_stat,
    right_stat,
    left_root,
    right_root,
    vectors,
    vec_stat,
):
    half_d = inputs.shape[2]
    halves = D // half_d
    core = lax.axis_index("mp")
    data_index = lax.axis_index(("rep", "shard"))
    seq_index = data_index * inputs.shape[0] + core
    limit = lax.dynamic_slice_in_dim(lengths, seq_index, 1)
    tables = [net.table(k, core, data_index) for k in range(2 * len(GROUPS))]
    is_first = core == 0

    def pick(pair, which):
        return lax.dynamic_index_in_dim(pair, which, axis=0, keepdims=False)

    def joined(low_half, high_half):
        return jnp.concatenate(
            [
                jnp.where(is_first, low_half, high_half),
                jnp.where(is_first, high_half, low_half),
            ],
            axis=1,
        )

    def whole(value):
        other = net.swap_core(value)
        own = joined(pick(value, core), pick(other, core))
        sib = joined(pick(value, 1 - core), pick(other, 1 - core))
        return own, sib

    def halved(full):
        mine = lax.dynamic_slice_in_dim(full, core * half_d, half_d, axis=1)
        away = lax.dynamic_slice_in_dim(full, (1 - core) * half_d, half_d, axis=1)
        got = net.swap_core(away)
        return jnp.stack([jnp.where(is_first, mine, got), jnp.where(is_first, got, mine)])

    x, x_sib = whole(inputs)
    e, e_sib = whole(encoded)

    pieces, vec_mine = first_pieces(net, weights, vectors, inverse_of(block_slots))
    flows, base = [], 0
    for k in range(len(GROUPS)):
        size = group_blocks(k, halves)
        flows.append(Flow(gather_rounds(net, k, pieces[base : base + size])))
        base += size
    attn, cross, up, down = flows

    def placed(k):
        return place(net, k, tables[k], *flows[k].finish())

    step((), attn)
    step((), attn, cross)
    step((), attn)
    step((), attn, cross)
    vec_mine, x, x_sib, e, e_sib = step((vec_mine, x, x_sib, e, e_sib), attn, cross, up)
    w_sq, w_sk, w_sv = step(placed(0), up)

    vec_other = net.swap_core(vec_mine)
    vec_both = jnp.concatenate(
        [jnp.where(is_first, vec_mine, vec_other), jnp.where(is_first, vec_other, vec_mine)]
    ).astype(f32)
    vecs = [vec_both[:, i * half_d : (i + 1) * half_d].reshape(1, D) for i in range(13)]
    vecs.append(vec_both[:, 13 * half_d :].reshape(1, FF))
    b_sq, b_sv, b_so, g_one, b_one, b_cq, b_cv, b_co, g_two, b_two, b_fo, g_three, b_three, b_fi = vecs

    q_s = (dot_nn(x, w_sq) + b_sq).astype(bf16)
    k_s = dot_nn(x, w_sk).astype(bf16)
    v_s = (dot_nn(x, w_sv) + b_sv).astype(bf16)
    q_s, k_s, v_s = step((q_s, k_s, v_s), cross, up, down)
    o_s, lse_s = attend_forward(limit, q_s, k_s, v_s, True)
    cotangent, o_s, lse_s = step((cotangent, o_s, lse_s), cross, up, down)
    cot_pieces = route_out(cotangent)
    w_so, w_cq, w_ck, w_cv, w_co = placed(1)
    z_one = x.astype(f32) + dot_nn(o_s, w_so) + b_so
    h_one, n_one, r_one = norm_forward(z_one, g_one, b_one)
    h_one_low = h_one.astype(bf16)
    q_c = (dot_nn(h_one_low, w_cq) + b_cq).astype(bf16)
    k_c = dot_nn(e, w_ck).astype(bf16)
    v_c = (dot_nn(e, w_cv) + b_cv).astype(bf16)
    q_c, k_c, v_c = step((q_c, k_c, v_c), down)
    o_c, lse_c = attend_forward(limit, q_c, k_c, v_c, False)
    z_two = h_one + dot_nn(o_c, w_co) + b_co
    h_two, n_two, r_two = norm_forward(z_two, g_two, b_two)
    cot_pieces, h_two, h_two_low = step((cot_pieces, h_two, h_two.astype(bf16)), up, down)
    cot_home = route_home(cot_pieces, seq_slots)
    (w_fi,) = placed(2)
    act, slope = gelu_forward(h_two_low, w_fi, b_fi)
    act_sib = net.swap_core(act)
    act, slope = step((act, slope), down)
    (w_fo,) = placed(3)
    z_three = h_two + dot_nn(act, w_fo) + b_fo
    cot, _ = whole(cot_home)
    h_three, n_three, r_three = norm_forward(z_three, g_three, b_three)
    live = (jnp.arange(x.shape[0]) < limit).astype(f32)[:, None]
    source = inverse_of(seq_slots)
    finished = (h_three * live).astype(bf16)

    def gradient(k, *calls):
        held, first = None, 0
        for xs, *ys in calls:
            held = weight_grad(net, k, tables[len(GROUPS) + k], xs, ys, held, first, GROUPS[k][first][1])
            first += len(ys)
        parts = tuple(h.reshape(h.shape[0], -1, net.rows, BS) for h in held)
        return Flow(reduce_rounds(net, len(GROUPS) + k, parts))

    grad_y = cot.astype(f32) * live
    d_three, dg_three, db_three = norm_backward(grad_y, n_three, r_three, g_three)
    a_three = d_three.astype(bf16)
    d_hidden = (dot_nt(a_three, w_fo) * slope.astype(f32)).astype(bf16)
    a_three_sib, d_hidden = step((net.swap_core(a_three), d_hidden))
    d_hidden_sib = net.swap_core(d_hidden)
    down = gradient(3, ((act, act_sib), (a_three, a_three_sib)))
    finished, d_hidden, d_hidden_sib = step((finished, d_hidden, d_hidden_sib), down)
    finished = halved(finished)
    d_h_two = d_three + dot_nt(d_hidden, w_fi)
    d_two, dg_two, db_two = norm_backward(d_h_two, n_two, r_two, g_two)
    a_two = d_two.astype(bf16)
    d_oc = dot_nt(a_two, w_co).astype(bf16)
    finished, d_hidden, d_hidden_sib, d_oc = step((finished, d_hidden, d_hidden_sib, d_oc))
    out_pieces = route_out(finished)
    up = gradient(2, ((h_two_low, net.swap_core(h_two_low)), (d_hidden, d_hidden_sib)))
    (d_oc,) = step((d_oc,), up, down)
    dq_c, dk_c, dv_c = attend_backward(limit, q_c, k_c, v_c, o_c, d_oc, lse_c, False)
    dq_c_sib, dk_c_sib, dv_c_sib = [net.swap_core(v) for v in (dq_c, dk_c, dv_c)]
    dq_c, dk_c, dv_c = step((dq_c, dk_c, dv_c), down)
    d_h_one = d_two + dot_nt(dq_c, w_cq)
    d_one, dg_one, db_one = norm_backward(d_h_one, n_one, r_one, g_one)
    a_one = d_one.astype(bf16)
    a_one_sib = net.swap_core(a_one)
    d_os = dot_nt(a_one, w_so).astype(bf16)
    out_pieces, a_one, a_one_sib, d_os = step((out_pieces, a_one, a_one_sib, d_os))
    outputs = route_home(out_pieces, source)
    cross = gradient(
        1,
        ((o_s, net.swap_core(o_s)), (a_one, a_one_sib)),
        ((h_one_low, net.swap_core(h_one_low)), (dq_c, dq_c_sib)),
        ((e, e_sib), (dk_c, dk_c_sib), (dv_c, dv_c_sib)),
        ((o_c, net.swap_core(o_c)), (a_two, net.swap_core(a_two))),
    )
    outputs, d_os = step((outputs, d_os), cross, up, down)
    dq_s, dk_s, dv_s = attend_backward(limit, q_s, k_s, v_s, o_s, d_os, lse_s, True)
    sibs = [net.swap_core(v) for v in (dq_s, dk_s, dv_s)]
    dq_s, dk_s, dv_s = step((dq_s, dk_s, dv_s), cross, up)
    attn = gradient(0, ((x, x_sib), *zip((dq_s, dk_s, dv_s), sibs)))
    dq_s, dk_s, dv_s = step((dq_s, dk_s, dv_s), attn)
    dk_c, dv_c, dq_s, dk_s, dv_s = step((dk_c, dv_c, dq_s, dk_s, dv_s), cross, up)
    state_back = dot_nt(dk_c, w_ck) + dot_nt(dv_c, w_cv)
    back = d_one + dot_nt(dq_s, w_sq) + dot_nt(dk_s, w_sk) + dot_nt(dv_s, w_sv)
    back, d_hidden, dq_c, dv_c = step((back, d_hidden, dq_c, dv_c), attn, cross, up)
    input_grad = halved(back.astype(bf16))
    encoded_grad = halved(state_back.astype(bf16))
    dq_s, dv_s = step((dq_s, dv_s), attn)
    columns = [jnp.sum(v.astype(f32), axis=0) for v in (d_hidden, dq_c, dv_c, dq_s, dv_s)]
    *columns, input_grad, encoded_grad = step((*columns, input_grad, encoded_grad), attn, cross, up)
    sums = (
        columns[3],
        columns[4],
        jnp.sum(d_one, axis=0),
        dg_one,
        db_one,
        columns[1],
        columns[2],
        jnp.sum(d_two, axis=0),
        dg_two,
        db_two,
        jnp.sum(d_three, axis=0),
        dg_three,
        db_three,
        columns[0],
    )
    vec_pair = jnp.concatenate([s.reshape(halves, -1) for s in sums], axis=1)
    vec_sum = pick(vec_pair, core) + net.swap_core(pick(vec_pair, 1 - core))
    natural = [f.finish() for f in (attn, cross, up, down)]

    parts, flag, vec_owned = last_pieces(net, jnp.concatenate(natural), block_slots, vec_sum)
    block_grad, left_new, right_new, weights_new = shampoo(
        flag, parts, weights, left_stat, right_stat, left_root, right_root
    )
    vec_stat_new = 0.5 * vec_stat + 0.5 * vec_owned * vec_owned
    vectors_new = vectors - 0.1 * vec_owned * lax.rsqrt(vec_stat_new)
    return (
        outputs,
        input_grad,
        encoded_grad,
        block_grad,
        left_new,
        right_new,
        weights_new,
        vec_owned,
        vec_stat_new,
        vectors_new,
    )


def solution(mesh):
    net = Net(mesh.shape["rep"], mesh.shape["shard"], mesh.shape["mp"])
    rows = P(("rep", "shard"), None, "mp")
    blocks = P("mp", "shard", None, None)
    vector = P("mp", "shard")
    in_specs = (rows, rows, rows, P(), P(), P()) + (blocks,) * 5 + (vector, vector)
    out_specs = (rows, rows, rows) + (blocks,) * 4 + (vector,) * 3
    return jax.shard_map(
        functools.partial(per_device, net),
        mesh=mesh,
        in_specs=in_specs,
        out_specs=out_specs,
        check_vma=False,
    )
```

```python
import functools

import jax
import jax.numpy as jnp
import numpy as np
from jax import lax
from jax.experimental import pallas as pl
from jax.experimental.pallas import tpu as pltpu
from jax.sharding import PartitionSpec as P

D = 1024
FF = 4096
HEAD_DIM = 64
BS = 256
LANES = 128

eps_norm = 1e-05
masked_score = -1e30
scale = HEAD_DIM**-0.5
bf16 = jnp.bfloat16
f32 = jnp.float32

NT = (((1,), (1,)), ((), ()))
TN = (((0,), (0,)), ((), ()))

VMEM_LIMIT = 60 * 1024 * 1024

ERFC_SLOPE = 0.3
ERFC_POLY = (
    0.1691880090604902,
    0.17071516163759975,
    0.14833963774537734,
    0.21492421686136995,
    -0.09464635292673967,
    0.5477136065073498,
    -0.5122723795383668,
    0.4855603950654946,
    -0.1295223139805042,
)


def dot_nn(a, b):
    return jnp.dot(a, b, preferred_element_type=f32)


def dot_nt(a, b):
    return lax.dot_general(a, b, NT, preferred_element_type=f32)


def dot_tn(a, b):
    return lax.dot_general(a, b, TN, preferred_element_type=f32)


def small():
    return pl.CostEstimate(flops=1 << 20, bytes_accessed=1 << 20, transcendentals=0)


def params(**kw):
    return pltpu.CompilerParams(vmem_limit_bytes=VMEM_LIMIT, **kw)


GROUPS = (
    (("sq", True), ("sk", True), ("sv", True)),
    (("so", False), ("cq", True), ("ck", True), ("cv", True), ("co", False)),
    (("fi", True),),
    (("fo", False),),
)
SHAPES = {name: (D, D) for name in ("sq", "sk", "sv", "so", "cq", "ck", "cv", "co")}
SHAPES["fi"], SHAPES["fo"] = (D, FF), (FF, D)


def chunk_of(i):
    return (i & 8) | ((i & 2) << 1) | ((i & 1) << 1) | ((i & 4) >> 2)


class Net:
    def __init__(self, n_rep, n_shard, n_mp):
        self.n_rep, self.n_shard, self.n_mp = n_rep, n_shard, n_mp
        self.n_data = n_rep * n_shard
        self.pieces = 16 if (n_rep, n_shard, n_mp) == (2, 8, 2) else 1
        self.rows = BS // self.pieces
        self.depth = self.pieces.bit_length() - 1
        x, z1, z2, y = 1, 2, 4, 8
        gathering = (
            ((z2, y, z1, x), (z2, z1, x, y)),
            ((z2, z1, y, x), (z2, z1, x, y)),
            ((z2, x, z1, y), (z2, y, z1, x)),
            ((z2, x, y, z1), (z2, y, z1, x)),
        )
        reducing = (((z2, z1, y, x), (z2, z1, x, y)),) + gathering[1:]
        self.orders = gathering + reducing

    def swap_core(self, value):
        return lax.ppermute(value, "mp", [(i, i ^ 1) for i in range(self.n_mp)])

    def swap_rep(self, value):
        return lax.ppermute(value, "rep", [(i, i ^ 1) for i in range(self.n_rep)])

    def swap_data(self, value, group, step):
        pairs = []
        for i in range(self.n_data):
            for m in range(self.n_mp):
                there = i ^ self.orders[group][m][step]
                pairs.append((i * self.n_mp + m, there * self.n_mp + m))
        return lax.ppermute(value, ("rep", "shard", "mp"), pairs)

    def table(self, group, core, data_index):
        many = self.pieces
        if many == 1:
            return jnp.stack([0, 0, 0, 0, core]).astype(jnp.int32)
        half = many // 4
        rel = []
        for order in self.orders[group]:
            rel.append([sum(b for s, b in enumerate(order) if q >> s & 1) for q in range(many)])
        rows = []
        for m in range(self.n_mp):
            place = [rel[1 - m].index(r) // 2 for r in rel[m][::2]]
            low = [p for p in place if p < half][0]
            high = [p - half for p in place if p >= half][0]
            lows, highs = [], []
            for p in place:
                low, high = (p, high) if p < half else (low, p - half)
                lows.append(low)
                highs.append(high)
            rows.append([chunk_of(r) for r in rel[m]] + lows + highs + [int(p >= half) for p in place])
        mine = jnp.asarray(np.array(rows, np.int32))[core]
        chunks = mine[:many] ^ chunk_of(data_index)
        return jnp.concatenate([chunks, mine[many:], core.reshape(1)]).astype(jnp.int32)


def together(*values):
    return lax.optimization_barrier(values)


class Flow:
    def __init__(self, rounds):
        self.rounds = rounds
        self.flying = next(rounds)

    def advance(self, values):
        try:
            self.flying = self.rounds.send(values)
        except StopIteration as stop:
            self.flying = None
            self.result = stop.value

    def finish(self):
        while self.flying is not None:
            self.advance(self.flying)
        return self.result


def step(main, *flows):
    flows = [f for f in flows if f.flying is not None]
    values = list(together(*main, *[v for f in flows for v in f.flying]))
    main, values = values[: len(main)], values[len(main) :]
    for f in flows:
        many = len(f.flying)
        f.advance(tuple(values[:many]))
        values = values[many:]
    return main


def blocks_of(name, n_mp):
    rows, cols = SHAPES[name]
    return rows * cols // n_mp // (BS * BS)


def group_blocks(group, n_mp):
    return sum(blocks_of(name, n_mp) for name, _ in GROUPS[group])


def place_body(s, *refs, dests, many, two):
    q = pl.program_id(0)
    steps = many // 2 if two else 1
    if two:
        own_lo, own_hi, sib_lo, sib_hi = refs[:4]
        outs = refs[4:]
    else:
        own_lo, sib_lo = refs[:2]
        outs = refs[2:]
    core = s[many + 3 * steps]
    rows = own_lo.shape[2]
    for t in range(own_lo.shape[0]):
        here = pl.ds(0, rows)
        if two:
            here = pl.ds(pl.multiple_of((s[2 * q + t] & 1) * rows, rows), rows)
        for b in range(own_lo.shape[1]):
            own, sib = own_lo[t, b], sib_lo[t, b]
            if two:
                own = jnp.where(q < steps // 2, own, own_hi[t, b])
                sib = jnp.where(s[many + 2 * steps + q] == 0, sib, sib_hi[t, b])
            for h in range(2):
                which, row, col = dests[h][b]
                outs[which][row, here, col : col + BS] = jnp.where(core == h, own, sib)


def place(net, group, table, own, sib):
    many, rows, n_mp = net.pieces, net.rows, net.n_mp
    two = many > 1
    per = 2 if two else 1
    steps = many // per
    half = max(steps // 2, 1)
    dests = ([], [])
    shapes, specs = [], []
    for which, (name, wide) in enumerate(GROUPS[group]):
        height, width = SHAPES[name]
        tall = height if wide else height // n_mp
        flat = width // n_mp if wide else width
        for h in range(n_mp):
            for r in range(tall // BS):
                for c in range(flat // BS):
                    if wide:
                        dests[h].append((which, r, h * flat + c * BS))
                    else:
                        dests[h].append((which, h * (tall // BS) + r, c * BS))
        shapes.append(jax.ShapeDtypeStruct((height // BS, BS, width), bf16))
        specs.append(
            pl.BlockSpec((height // BS, per * rows, width), lambda q, s: (0, s[per * q] // per, 0))
        )
    nb = own[0].shape[1]
    block = (per, nb, rows, BS)
    lo = pl.BlockSpec(block, lambda q, s: (jnp.minimum(q, half - 1), 0, 0, 0))
    hi = pl.BlockSpec(block, lambda q, s: (jnp.maximum(q - half, 0), 0, 0, 0))
    sib_lo = pl.BlockSpec(block, lambda q, s: (s[many + q], 0, 0, 0))
    sib_hi = pl.BlockSpec(block, lambda q, s: (s[many + steps + q], 0, 0, 0))
    out = pl.pallas_call(
        functools.partial(place_body, dests=dests, many=many, two=two),
        grid_spec=pltpu.PrefetchScalarGridSpec(
            num_scalar_prefetch=1,
            grid=(steps,),
            in_specs=[lo, hi, sib_lo, sib_hi] if two else [lo, sib_lo],
            out_specs=tuple(specs),
        ),
        out_shape=tuple(shapes),
        compiler_params=params(),
        cost_estimate=small(),
        name="place",
    )(table, *own, *sib)
    return [o.reshape(-1, o.shape[2]) for o in out]


def gather_rounds(net, group, piece):
    (piece,) = yield (piece,)
    cur = piece[None]
    if net.pieces == 1:
        (sib,) = yield (net.swap_core(cur),)
        return (cur,), (sib,)
    for k in range(net.depth - 1):
        (got,) = yield (net.swap_data(cur, group, k),)
        cur = jnp.concatenate([cur, got])
    got, sib_lo = yield (net.swap_data(cur, group, net.depth - 1), net.swap_core(cur))
    (sib_hi,) = yield (net.swap_core(got),)
    return (cur, got), (sib_lo, sib_hi)


def first_pieces(net, weights, vectors, inverse):
    low = weights[0].astype(bf16)
    vec = vectors.astype(bf16)
    if net.pieces == 1:
        every = lax.all_gather(low, "shard", axis=0, tiled=True)
        vec_every = lax.all_gather(vec, "shard", axis=1, tiled=True)
        return every.at[inverse].get(mode="promise_in_bounds"), vec_every
    nblk = low.shape[0]
    cut = low.reshape(nblk, 2, 2, 2, 2, net.rows, BS)
    cut = lax.dynamic_index_in_dim(cut, lax.axis_index("rep"), axis=1, keepdims=False)
    cut = cut.transpose(3, 1, 2, 0, 4, 5).reshape(net.n_shard, nblk, net.rows, BS)
    room = net.rows * BS
    vec_cut = jnp.pad(vec.reshape(-1), (0, room - vec.shape[1])).reshape(1, 1, net.rows, BS)
    cut = jnp.concatenate([cut, jnp.broadcast_to(vec_cut, (net.n_shard,) + vec_cut.shape[1:])], axis=1)
    every = lax.all_to_all(
        cut.reshape(-1, net.rows, BS), "shard", split_axis=0, concat_axis=0, tiled=True
    )
    pieces = every.at[inverse + inverse // nblk].get(mode="promise_in_bounds")
    vec_every = every.reshape(net.n_shard, nblk + 1, room)[:, nblk, : vec.shape[1]]
    return pieces, vec_every.reshape(1, -1)


def total_of(*terms):
    acc = terms[0].astype(f32)
    for t in terms[1:]:
        acc = acc + t.astype(f32)
    return acc.astype(bf16)


def reduce_rounds(net, group, parts):
    parts = yield parts
    if net.pieces == 1:
        return parts[0][0]
    lo, hi = parts
    (got,) = yield (net.swap_data(hi, group, net.depth - 1),)
    terms = [lo, got]
    for k in range(net.depth - 2, -1, -1):
        width = 1 << k
        send = total_of(*[t[width:] for t in terms])
        keep = total_of(*[t[:width] for t in terms])
        (got,) = yield (net.swap_data(send, group, k),)
        terms = [keep, got]
    return total_of(*terms)[0]


def last_pieces(net, natural, block_slots, vec_sum):
    if net.pieces == 1:
        dealt = natural.at[block_slots].get(mode="promise_in_bounds")
        owned = lax.psum_scatter(dealt, "shard", scatter_dimension=0, tiled=True)
        owned = total_of(owned, net.swap_rep(owned))
        cut = owned.reshape(-1, 2, 8, 16, BS).transpose(1, 2, 0, 3, 4)
        cut = cut[:, np.array([chunk_of(k) for k in range(8)])]
        vec = lax.psum_scatter(vec_sum, "shard", scatter_dimension=0, tiled=True)[None]
        parts = [(cut[0], cut[1], owned.shape[0])]
        return parts, jnp.zeros((1,), jnp.int32), vec + net.swap_rep(vec)
    n = net.n_shard
    slots = block_slots.reshape(n, -1)
    half = slots.shape[1] // 2
    room = net.rows * BS
    vec_cut = vec_sum.reshape(n, -1)
    width = vec_cut.shape[1]
    vec_cut = jnp.pad(vec_cut.astype(bf16), ((0, 0), (0, room - width)))
    vec_cut = vec_cut.reshape(n, 1, net.rows, BS)
    cuts = []
    for k in range(2):
        index = slots[:, k * half : (k + 1) * half].reshape(-1)
        cuts.append(natural.at[index].get(mode="promise_in_bounds").reshape(n, half, net.rows, BS))
    cuts[1] = jnp.concatenate([cuts[1], vec_cut], axis=1)

    def home(cut):
        back = lax.all_to_all(
            cut.reshape(-1, net.rows, BS), "shard", split_axis=0, concat_axis=0, tiled=True
        )
        return back.reshape(n, -1, net.rows, BS)

    mine, cuts[1] = together(home(cuts[0]), cuts[1])
    other = net.swap_rep(mine)
    other, last = together(other, home(cuts[1]))
    parts = [(mine, other, half), (last, net.swap_rep(last), half)]
    terms = [v[:, half].reshape(n, room)[:, :width].astype(f32) for v in parts[1][:2]]
    flag = lax.axis_index("rep").astype(jnp.int32).reshape(1)
    return parts, flag, jnp.sum(terms[0] + terms[1], axis=0, keepdims=True)


def attend_forward_body(lim, q_ref, k_ref, v_ref, o_ref, lse_ref, *, causal, rows):
    pair = pl.program_id(0)
    seq, keys = q_ref.shape[0], k_ref.shape[0]
    lane = lax.broadcasted_iota(jnp.int32, (1, LANES), 1)
    top = lim[0] - 1

    @pl.when(pair == 0)
    def _():
        lse_ref[...] = jnp.zeros_like(lse_ref)

    for blk in range(seq // rows):
        here = pl.ds(blk * rows, rows)
        width = (blk + 1) * rows if causal else keys
        q = q_ref[here, :] * bf16(scale)
        k = k_ref[pl.ds(0, width), :]
        v = v_ref[pl.ds(0, width), :]
        outs = []
        kept = lse_ref[here, :]
        if causal:
            row = lax.broadcasted_iota(jnp.int32, (rows, 1), 0) + blk * rows
            col = lax.broadcasted_iota(jnp.int32, (1, width), 1)
            allowed = col <= jnp.minimum(row, top)
        for h in range(2):
            mine = (lane // HEAD_DIM) == h
            s = dot_nt(jnp.where(mine, q, bf16(0)), k)
            if causal:
                s = jnp.where(allowed, s, masked_score)
            peak = jnp.max(s, axis=1, keepdims=True)
            e = jnp.exp(s - peak)
            mass = jnp.sum(e, axis=1, keepdims=True)
            outs.append(dot_nn(e.astype(bf16), v) * (1.0 / mass))
            kept = jnp.where(lane == 2 * pair + h, peak + jnp.log(mass), kept)
        o_ref[here, :] = jnp.where(lane < HEAD_DIM, outs[0], outs[1]).astype(bf16)
        lse_ref[here, :] = kept


def attend_forward(limit, q, k, v, causal):
    seq, width = q.shape
    keys = k.shape[0]
    pairs = width // LANES
    rows = min(128 if causal else 256, seq)
    o, lse = pl.pallas_call(
        functools.partial(attend_forward_body, causal=causal, rows=rows),
        grid=(pairs,),
        out_shape=(
            jax.ShapeDtypeStruct((seq, width), bf16),
            jax.ShapeDtypeStruct((seq, LANES), f32),
        ),
        in_specs=[
            pl.BlockSpec(memory_space=pltpu.SMEM),
            pl.BlockSpec((seq, LANES), lambda i: (0, i)),
            pl.BlockSpec((keys, LANES), lambda i: (0, i)),
            pl.BlockSpec((keys, LANES), lambda i: (0, i)),
        ],
        out_specs=(
            pl.BlockSpec((seq, LANES), lambda i: (0, i)),
            pl.BlockSpec((seq, LANES), lambda i: (0, 0)),
        ),
        compiler_params=params(),
        cost_estimate=small(),
        name="attend_forward",
    )(limit, q, k, v)
    return o, lse[:, : 2 * pairs].T.reshape(pairs, 2, seq)


def attend_backward_body(
    lim, q_ref, k_ref, v_ref, o_ref, do_ref, lse_ref, dq_ref, dk_ref, dv_ref, dk_acc, dv_acc, *, causal, rows
):
    seq, keys = q_ref.shape[0], k_ref.shape[0]
    lane = lax.broadcasted_iota(jnp.int32, (1, LANES), 1)
    top = lim[0] - 1
    dk_acc[...] = jnp.zeros_like(dk_acc)
    dv_acc[...] = jnp.zeros_like(dv_acc)
    head_row = lax.broadcasted_iota(jnp.int32, (8, LANES), 0)
    head_lane = lax.broadcasted_iota(jnp.int32, (8, LANES), 1) // HEAD_DIM
    pick = (head_row == head_lane).astype(bf16)
    for blk in range(seq // rows):
        here = pl.ds(blk * rows, rows)
        width = (blk + 1) * rows if causal else keys
        span = pl.ds(0, width)
        q = q_ref[here, :] * bf16(scale)
        do = do_ref[here, :]
        k = k_ref[span, :]
        v = v_ref[span, :]
        prod = do.astype(f32) * o_ref[here, :].astype(f32)
        hi = prod.astype(bf16)
        lo = (prod - hi.astype(f32)).astype(bf16)
        delta = dot_nt(pick, hi) + dot_nt(pick, lo)
        lse = lse_ref[0][:, blk * rows : (blk + 1) * rows]
        if causal:
            key = lax.broadcasted_iota(jnp.int32, (width, 1), 0)
            row = lax.broadcasted_iota(jnp.int32, (1, rows), 1) + blk * rows
            allowed = key <= jnp.minimum(row, top)
        dq = jnp.zeros((rows, LANES), f32)
        dk = jnp.zeros((width, LANES), f32)
        dv = jnp.zeros((width, LANES), f32)
        for h in range(2):
            mine = (lane // HEAD_DIM) == h
            qm = jnp.where(mine, q, bf16(0))
            dom = jnp.where(mine, do, bf16(0))
            km = jnp.where(mine, k, bf16(0))
            s = dot_nt(k, qm)
            if causal:
                s = jnp.where(allowed, s, masked_score)
            p = jnp.exp(s - lse[h : h + 1, :])
            dp = dot_nt(v, dom)
            ds = (p * (dp - delta[h : h + 1, :])).astype(bf16)
            dv = dv + dot_nn(p.astype(bf16), dom)
            dk = dk + dot_nn(ds, qm)
            dq = dq + dot_tn(ds, km)
        dq_ref[here, :] = (dq * scale).astype(bf16)
        dk_acc[span, :] += dk
        dv_acc[span, :] += dv
    dk_ref[...] = dk_acc[...].astype(bf16)
    dv_ref[...] = dv_acc[...].astype(bf16)


def attend_backward(limit, q, k, v, o, do, lse, causal):
    seq, width = q.shape
    keys = k.shape[0]
    pairs = width // LANES
    rows = min(128 if causal else 256, seq)
    q_spec = pl.BlockSpec((seq, LANES), lambda i: (0, i))
    k_spec = pl.BlockSpec((keys, LANES), lambda i: (0, i))
    return pl.pallas_call(
        functools.partial(attend_backward_body, causal=causal, rows=rows),
        grid=(pairs,),
        out_shape=(
            jax.ShapeDtypeStruct((seq, width), bf16),
            jax.ShapeDtypeStruct((keys, width), bf16),
            jax.ShapeDtypeStruct((keys, width), bf16),
        ),
        in_specs=[
            pl.BlockSpec(memory_space=pltpu.SMEM),
            q_spec,
            k_spec,
            k_spec,
            q_spec,
            q_spec,
            pl.BlockSpec((1, 2, seq), lambda i: (i, 0, 0)),
        ],
        out_specs=(q_spec, k_spec, k_spec),
        scratch_shapes=[pltpu.VMEM((keys, LANES), f32), pltpu.VMEM((keys, LANES), f32)],
        compiler_params=params(),
        cost_estimate=small(),
        name="attend_backward",
    )(limit, q, k, v, o, do, lse)


def gelu_body(h_ref, w_ref, b_ref, act_ref, slope_ref, u_ref, *, chunk):
    u_ref[...] = dot_nn(h_ref[...], w_ref[...]) + b_ref[...]

    def part(i):
        here = pl.ds(pl.multiple_of(i * chunk, chunk), chunk)
        u = u_ref[here, :]
        x = jnp.abs(u) * (0.5**0.5)
        t = 1.0 / (1.0 + ERFC_SLOPE * x)
        poly = jnp.full_like(t, ERFC_POLY[-1])
        for c in ERFC_POLY[-2::-1]:
            poly = poly * t + c
        bell = jnp.exp(-0.5 * (u * u))
        tail = 0.5 * (bell * (t * poly))
        cdf = jnp.where(u < 0, tail, 1.0 - tail)
        act_ref[here, :] = (u * cdf).astype(bf16)
        slope_ref[here, :] = (cdf + u * (bell * 0.3989422804014327)).astype(bf16)

    pl.loop(0, u_ref.shape[0] // chunk)(part)


def gelu_forward(h, w, b):
    seq, width = h.shape
    hidden = w.shape[1]
    tile = 512
    spec = pl.BlockSpec((seq, tile), lambda i: (0, i))
    return pl.pallas_call(
        functools.partial(gelu_body, chunk=32),
        grid=(hidden // tile,),
        out_shape=(jax.ShapeDtypeStruct((seq, hidden), bf16),) * 2,
        in_specs=[
            pl.BlockSpec((seq, width), lambda i: (0, 0)),
            pl.BlockSpec((width, tile), lambda i: (0, i)),
            pl.BlockSpec((1, tile), lambda i: (0, i)),
        ],
        out_specs=(spec, spec),
        scratch_shapes=[pltpu.VMEM((seq, tile), f32)],
        compiler_params=params(),
        cost_estimate=small(),
        name="gelu_forward",
    )(h, w, b)


def weight_grad_body(s, x_own, x_sib, *refs, count, outs, many, rows, nb):
    y_own, y_sib = refs[:count], refs[count : 2 * count]
    targets = refs[-3 - outs : -3]
    t_own, t_sib, buf = refs[-3:]
    t_own[...] = x_own[...].T
    t_sib[...] = x_sib[...].T
    per = many // outs
    for k in range(count):
        acc = dot_nn(t_own[...], y_own[k][...]) + dot_nn(t_sib[...], y_sib[k][...])
        buf[k] = acc.astype(bf16)
    for q in range(many):
        for r in range(x_own.shape[1] // BS):
            here = pl.ds(pl.multiple_of(s[q] * rows + r * BS, rows), rows)
            for k in range(count):
                for c in range(nb):
                    targets[q // per][q % per, k, r * nb + c] = buf[k, here, c * BS : (c + 1) * BS]


def weight_grad(net, group, table, xs, ys, held, first, wide):
    seq = xs[0].shape[0]
    many, rows, halves = net.pieces, net.rows, net.n_mp
    at_core = table.shape[0] - 1
    count = len(ys)
    width = ys[0][0].shape[1]
    if wide:
        tall = xs[0].shape[1] // BS
        deep = 2 if tall >= 4 else 1
        steps = tall // deep
        y_width = width // halves
        x_spec = pl.BlockSpec((seq, deep * BS), lambda i, s: (0, i))
        y_spec = pl.BlockSpec((seq, y_width), lambda i, s: (0, s[at_core]))
    else:
        tall = xs[0].shape[1] // halves // BS
        deep = 2 if tall >= 4 else 1
        steps = tall // deep
        y_width = width
        x_spec = pl.BlockSpec((seq, deep * BS), lambda i, s: (0, s[at_core] * steps + i))
        y_spec = pl.BlockSpec((seq, y_width), lambda i, s: (0, 0))
    nb = y_width // BS
    at = first // count
    outs = 2 if many > 1 else 1
    shape = (many // outs, len(GROUPS[group]), tall * nb, rows, BS)
    anyspec = pl.BlockSpec(memory_space=pl.ANY)
    held = held or ()
    before = 3 + 2 * count
    return pl.pallas_call(
        functools.partial(
            weight_grad_body, count=count, outs=outs, many=many, rows=rows, nb=nb
        ),
        grid_spec=pltpu.PrefetchScalarGridSpec(
            num_scalar_prefetch=1,
            grid=(steps,),
            in_specs=[x_spec] * 2 + [y_spec] * (2 * count) + [anyspec] * len(held),
            out_specs=(
                pl.BlockSpec((many // outs, count, deep * nb, rows, BS), lambda i, s: (0, at, i, 0, 0)),
            )
            * outs,
            scratch_shapes=[
                pltpu.VMEM((deep * BS, seq), bf16),
                pltpu.VMEM((deep * BS, seq), bf16),
                pltpu.VMEM((count, deep * BS, y_width), bf16),
            ],
        ),
        out_shape=(jax.ShapeDtypeStruct(shape, bf16),) * outs,
        input_output_aliases={before + k: k for k in range(len(held))},
        compiler_params=params(),
        cost_estimate=small(),
        name="weight_grad",
    )(table, *xs, *[y[0] for y in ys], *[y[1] for y in ys], *held)


def split_low(a):
    hi = a.astype(bf16)
    return hi, (a - hi.astype(f32)).astype(bf16)


def shampoo_body(flag, mine_ref, other_ref, w_ref, ls_ref, rs_ref, lr_ref, rr_ref, *refs):
    og, ol, orr, ow, g_ref = refs[-5:]
    for k in range(mine_ref.shape[0]):
        for plane, src in ((flag[0], mine_ref), (1 - flag[0], other_ref)):
            row = pl.multiple_of(plane * 128 + chunk_of(k) * 16, 16)
            g_ref[pl.ds(row, 16), :] = src[k, 0]
    g = g_ref[...]
    og[0, 0] = g.astype(f32)
    ol[0, 0] = 0.5 * ls_ref[0, 0] + 0.5 * dot_nt(g, g)
    orr[0, 0] = 0.5 * rs_ref[0, 0] + 0.5 * dot_tn(g, g)
    r_hi, r_lo = split_low(rr_ref[0, 0])
    i_hi, i_lo = split_low(dot_nn(g, r_hi) + dot_nn(g, r_lo))
    l_hi, l_lo = split_low(lr_ref[0, 0])
    d = dot_nn(l_hi, i_hi) + (dot_nn(l_hi, i_lo) + dot_nn(l_lo, i_hi))
    mean = jnp.mean(jnp.mean(d * d, axis=1, keepdims=True), axis=0, keepdims=True)
    ow[0, 0] = w_ref[0, 0] - (D**-0.5) * d / jnp.sqrt(mean + 1e-06)


def shampoo(flag, parts, *states):
    total = states[0].shape[1]
    out, first = (), 0
    for mine, other, n in parts:
        at = first // n
        spec = pl.BlockSpec((1, 1, BS, BS), lambda i, at=at, n=n: (0, at * n + i, 0, 0))
        g_spec = pl.BlockSpec((mine.shape[0], 1, mine.shape[2], BS), lambda i: (0, i, 0, 0))
        anyspec = pl.BlockSpec(memory_space=pl.ANY)
        out = pl.pallas_call(
            shampoo_body,
            grid=(n,),
            out_shape=(jax.ShapeDtypeStruct((1, total, BS, BS), f32),) * 4,
            in_specs=[pl.BlockSpec(memory_space=pltpu.SMEM), g_spec, g_spec]
            + [spec] * 5
            + [anyspec] * len(out),
            out_specs=(spec,) * 4,
            scratch_shapes=[pltpu.VMEM((BS, BS), bf16)],
            input_output_aliases={8 + k: k for k in range(len(out))},
            compiler_params=params(),
            cost_estimate=small(),
            name="shampoo",
        )(flag, mine, other, *states, *out)
        first += n
    return out


def norm_forward(z, gain, shift):
    center = z - jnp.mean(z, axis=1, keepdims=True)
    inv = lax.rsqrt(jnp.mean(center * center, axis=1, keepdims=True) + eps_norm)
    normed = center * inv
    return normed * gain + shift, normed, inv


def norm_backward(grad, normed, inv, gain):
    scaled = grad * gain
    mean_plain = jnp.mean(scaled, axis=1, keepdims=True)
    mean_cross = jnp.mean(scaled * normed, axis=1, keepdims=True)
    back = inv * (scaled - mean_plain - normed * mean_cross)
    return back, jnp.sum(grad * normed, axis=0), jnp.sum(grad, axis=0)


def inverse_of(order):
    many = jnp.arange(order.shape[0], dtype=jnp.int32)
    return jnp.sum(jnp.where(order[:, None] == many[None, :], many[:, None], 0), axis=0)


def route_out(value):
    axes = ("rep", "shard")
    count = lax.axis_size(axes)
    cut = value.reshape(value.shape[0], count, value.shape[1] // count, value.shape[2])
    return lax.all_to_all(cut, axes, split_axis=1, concat_axis=0, tiled=True)


def route_home(pieces, ordering):
    moved = pieces.at[ordering].get(mode="promise_in_bounds")
    back = lax.all_to_all(moved, ("rep", "shard"), split_axis=0, concat_axis=1, tiled=True)
    return back.reshape(back.shape[0], -1, back.shape[3])


def per_device(
    net,
    inputs,
    encoded,
    cotangent,
    lengths,
    seq_slots,
    block_slots,
    weights,
    left_stat,
    right_stat,
    left_root,
    right_root,
    vectors,
    vec_stat,
):
    half_d = inputs.shape[2]
    halves = D // half_d
    core = lax.axis_index("mp")
    data_index = lax.axis_index(("rep", "shard"))
    seq_index = data_index * inputs.shape[0] + core
    limit = lax.dynamic_slice_in_dim(lengths, seq_index, 1)
    tables = [net.table(k, core, data_index) for k in range(2 * len(GROUPS))]
    is_first = core == 0

    def pick(pair, which):
        return lax.dynamic_index_in_dim(pair, which, axis=0, keepdims=False)

    def joined(low_half, high_half):
        return jnp.concatenate(
            [
                jnp.where(is_first, low_half, high_half),
                jnp.where(is_first, high_half, low_half),
            ],
            axis=1,
        )

    def whole(value):
        other = net.swap_core(value)
        own = joined(pick(value, core), pick(other, core))
        sib = joined(pick(value, 1 - core), pick(other, 1 - core))
        return own, sib

    def halved(full):
        mine = lax.dynamic_slice_in_dim(full, core * half_d, half_d, axis=1)
        away = lax.dynamic_slice_in_dim(full, (1 - core) * half_d, half_d, axis=1)
        got = net.swap_core(away)
        return jnp.stack([jnp.where(is_first, mine, got), jnp.where(is_first, got, mine)])

    x, x_sib = whole(inputs)
    e, e_sib = whole(encoded)

    pieces, vec_mine = first_pieces(net, weights, vectors, inverse_of(block_slots))
    flows, base = [], 0
    for k in range(len(GROUPS)):
        size = group_blocks(k, halves)
        flows.append(Flow(gather_rounds(net, k, pieces[base : base + size])))
        base += size
    attn, cross, up, down = flows

    def placed(k):
        return place(net, k, tables[k], *flows[k].finish())

    step((), attn)
    step((), attn, cross)
    step((), attn)
    step((), attn, cross)
    vec_mine, x, x_sib, e, e_sib = step((vec_mine, x, x_sib, e, e_sib), attn, cross, up)
    w_sq, w_sk, w_sv = step(placed(0), up)

    vec_other = net.swap_core(vec_mine)
    vec_both = jnp.concatenate(
        [jnp.where(is_first, vec_mine, vec_other), jnp.where(is_first, vec_other, vec_mine)]
    ).astype(f32)
    vecs = [vec_both[:, i * half_d : (i + 1) * half_d].reshape(1, D) for i in range(13)]
    vecs.append(vec_both[:, 13 * half_d :].reshape(1, FF))
    b_sq, b_sv, b_so, g_one, b_one, b_cq, b_cv, b_co, g_two, b_two, b_fo, g_three, b_three, b_fi = vecs

    q_s = (dot_nn(x, w_sq) + b_sq).astype(bf16)
    k_s = dot_nn(x, w_sk).astype(bf16)
    v_s = (dot_nn(x, w_sv) + b_sv).astype(bf16)
    q_s, k_s, v_s = step((q_s, k_s, v_s), cross, up, down)
    o_s, lse_s = attend_forward(limit, q_s, k_s, v_s, True)
    cotangent, o_s, lse_s = step((cotangent, o_s, lse_s), cross, up, down)
    cot_pieces = route_out(cotangent)
    w_so, w_cq, w_ck, w_cv, w_co = placed(1)
    z_one = x.astype(f32) + dot_nn(o_s, w_so) + b_so
    h_one, n_one, r_one = norm_forward(z_one, g_one, b_one)
    h_one_low = h_one.astype(bf16)
    q_c = (dot_nn(h_one_low, w_cq) + b_cq).astype(bf16)
    k_c = dot_nn(e, w_ck).astype(bf16)
    v_c = (dot_nn(e, w_cv) + b_cv).astype(bf16)
    q_c, k_c, v_c = step((q_c, k_c, v_c), down)
    o_c, lse_c = attend_forward(limit, q_c, k_c, v_c, False)
    z_two = h_one + dot_nn(o_c, w_co) + b_co
    h_two, n_two, r_two = norm_forward(z_two, g_two, b_two)
    cot_pieces, h_two, h_two_low = step((cot_pieces, h_two, h_two.astype(bf16)), up, down)
    cot_home = route_home(cot_pieces, seq_slots)
    (w_fi,) = placed(2)
    act, slope = gelu_forward(h_two_low, w_fi, b_fi)
    act_sib = net.swap_core(act)
    act, slope = step((act, slope), down)
    (w_fo,) = placed(3)
    z_three = h_two + dot_nn(act, w_fo) + b_fo
    cot, _ = whole(cot_home)
    h_three, n_three, r_three = norm_forward(z_three, g_three, b_three)
    live = (jnp.arange(x.shape[0]) < limit).astype(f32)[:, None]
    source = inverse_of(seq_slots)
    finished = (h_three * live).astype(bf16)

    def gradient(k, *calls):
        held, first = None, 0
        for xs, *ys in calls:
            held = weight_grad(net, k, tables[len(GROUPS) + k], xs, ys, held, first, GROUPS[k][first][1])
            first += len(ys)
        parts = tuple(h.reshape(h.shape[0], -1, net.rows, BS) for h in held)
        return Flow(reduce_rounds(net, len(GROUPS) + k, parts))

    grad_y = cot.astype(f32) * live
    d_three, dg_three, db_three = norm_backward(grad_y, n_three, r_three, g_three)
    a_three = d_three.astype(bf16)
    d_hidden = (dot_nt(a_three, w_fo) * slope.astype(f32)).astype(bf16)
    a_three_sib, d_hidden = step((net.swap_core(a_three), d_hidden))
    d_hidden_sib = net.swap_core(d_hidden)
    down = gradient(3, ((act, act_sib), (a_three, a_three_sib)))
    finished, d_hidden, d_hidden_sib = step((finished, d_hidden, d_hidden_sib), down)
    finished = halved(finished)
    d_h_two = d_three + dot_nt(d_hidden, w_fi)
    d_two, dg_two, db_two = norm_backward(d_h_two, n_two, r_two, g_two)
    a_two = d_two.astype(bf16)
    d_oc = dot_nt(a_two, w_co).astype(bf16)
    finished, d_hidden, d_hidden_sib, d_oc = step((finished, d_hidden, d_hidden_sib, d_oc))
    out_pieces = route_out(finished)
    up = gradient(2, ((h_two_low, net.swap_core(h_two_low)), (d_hidden, d_hidden_sib)))
    (d_oc,) = step((d_oc,), up, down)
    dq_c, dk_c, dv_c = attend_backward(limit, q_c, k_c, v_c, o_c, d_oc, lse_c, False)
    dq_c_sib, dk_c_sib, dv_c_sib = [net.swap_core(v) for v in (dq_c, dk_c, dv_c)]
    dq_c, dk_c, dv_c = step((dq_c, dk_c, dv_c), down)
    d_h_one = d_two + dot_nt(dq_c, w_cq)
    d_one, dg_one, db_one = norm_backward(d_h_one, n_one, r_one, g_one)
    a_one = d_one.astype(bf16)
    a_one_sib = net.swap_core(a_one)
    d_os = dot_nt(a_one, w_so).astype(bf16)
    out_pieces, a_one, a_one_sib, d_os = step((out_pieces, a_one, a_one_sib, d_os))
    outputs = route_home(out_pieces, source)
    cross = gradient(
        1,
        ((o_s, net.swap_core(o_s)), (a_one, a_one_sib)),
        ((h_one_low, net.swap_core(h_one_low)), (dq_c, dq_c_sib)),
        ((e, e_sib), (dk_c, dk_c_sib), (dv_c, dv_c_sib)),
        ((o_c, net.swap_core(o_c)), (a_two, net.swap_core(a_two))),
    )
    outputs, d_os = step((outputs, d_os), cross, up, down)
    dq_s, dk_s, dv_s = attend_backward(limit, q_s, k_s, v_s, o_s, d_os, lse_s, True)
    sibs = [net.swap_core(v) for v in (dq_s, dk_s, dv_s)]
    dq_s, dk_s, dv_s = step((dq_s, dk_s, dv_s), cross, up)
    attn = gradient(0, ((x, x_sib), *zip((dq_s, dk_s, dv_s), sibs)))
    dq_s, dk_s, dv_s = step((dq_s, dk_s, dv_s), attn)
    dk_c, dv_c, dq_s, dk_s, dv_s = step((dk_c, dv_c, dq_s, dk_s, dv_s), cross, up, down)
    state_back = dot_nt(dk_c, w_ck) + dot_nt(dv_c, w_cv)
    back = d_one + dot_nt(dq_s, w_sq) + dot_nt(dk_s, w_sk) + dot_nt(dv_s, w_sv)
    back, d_hidden, dq_c, dv_c = step((back, d_hidden, dq_c, dv_c), attn, cross, up)
    input_grad = halved(back.astype(bf16))
    encoded_grad = halved(state_back.astype(bf16))
    dq_s, dv_s = step((dq_s, dv_s), attn)
    columns = [jnp.sum(v.astype(f32), axis=0) for v in (d_hidden, dq_c, dv_c, dq_s, dv_s)]
    *columns, input_grad, encoded_grad = step((*columns, input_grad, encoded_grad), attn, cross, up)
    sums = (
        columns[3],
        columns[4],
        jnp.sum(d_one, axis=0),
        dg_one,
        db_one,
        columns[1],
        columns[2],
        jnp.sum(d_two, axis=0),
        dg_two,
        db_two,
        jnp.sum(d_three, axis=0),
        dg_three,
        db_three,
        columns[0],
    )
    vec_pair = jnp.concatenate([s.reshape(halves, -1) for s in sums], axis=1)
    vec_sum = pick(vec_pair, core) + net.swap_core(pick(vec_pair, 1 - core))
    natural = [f.finish() for f in (attn, cross, up, down)]

    parts, flag, vec_owned = last_pieces(net, jnp.concatenate(natural), block_slots, vec_sum)
    block_grad, left_new, right_new, weights_new = shampoo(
        flag, parts, weights, left_stat, right_stat, left_root, right_root
    )
    vec_stat_new = 0.5 * vec_stat + 0.5 * vec_owned * vec_owned
    vectors_new = vectors - 0.1 * vec_owned * lax.rsqrt(vec_stat_new)
    return (
        outputs,
        input_grad,
        encoded_grad,
        block_grad,
        left_new,
        right_new,
        weights_new,
        vec_owned,
        vec_stat_new,
        vectors_new,
    )


def solution(mesh):
    net = Net(mesh.shape["rep"], mesh.shape["shard"], mesh.shape["mp"])
    rows = P(("rep", "shard"), None, "mp")
    blocks = P("mp", "shard", None, None)
    vector = P("mp", "shard")
    in_specs = (rows, rows, rows, P(), P(), P()) + (blocks,) * 5 + (vector, vector)
    out_specs = (rows, rows, rows) + (blocks,) * 4 + (vector,) * 3
    return jax.shard_map(
        functools.partial(per_device, net),
        mesh=mesh,
        in_specs=in_specs,
        out_specs=out_specs,
        check_vma=False,
    )
```

```python
import functools

import jax
import jax.numpy as jnp
import numpy as np
from jax import lax
from jax.experimental import pallas as pl
from jax.experimental.pallas import tpu as pltpu
from jax.sharding import PartitionSpec as P

D = 1024
FF = 4096
HEAD_DIM = 64
BS = 256
LANES = 128

eps_norm = 1e-05
masked_score = -1e30
scale = HEAD_DIM**-0.5
bf16 = jnp.bfloat16
f32 = jnp.float32

NT = (((1,), (1,)), ((), ()))
TN = (((0,), (0,)), ((), ()))

VMEM_LIMIT = 60 * 1024 * 1024

ERFC_SLOPE = 0.3
ERFC_POLY = (
    0.1691880090604902,
    0.17071516163759975,
    0.14833963774537734,
    0.21492421686136995,
    -0.09464635292673967,
    0.5477136065073498,
    -0.5122723795383668,
    0.4855603950654946,
    -0.1295223139805042,
)


def dot_nn(a, b):
    return jnp.dot(a, b, preferred_element_type=f32)


def dot_nt(a, b):
    return lax.dot_general(a, b, NT, preferred_element_type=f32)


def dot_tn(a, b):
    return lax.dot_general(a, b, TN, preferred_element_type=f32)


def small():
    return pl.CostEstimate(flops=1 << 20, bytes_accessed=1 << 20, transcendentals=0)


def params(**kw):
    return pltpu.CompilerParams(vmem_limit_bytes=VMEM_LIMIT, **kw)


GROUPS = (
    (("sq", True), ("sk", True), ("sv", True)),
    (("so", False), ("cq", True), ("ck", True), ("cv", True), ("co", False)),
    (("fi", True),),
    (("fo", False),),
)
SHAPES = {name: (D, D) for name in ("sq", "sk", "sv", "so", "cq", "ck", "cv", "co")}
SHAPES["fi"], SHAPES["fo"] = (D, FF), (FF, D)


def chunk_of(i):
    return (i & 8) | ((i & 2) << 1) | ((i & 1) << 1) | ((i & 4) >> 2)


class Net:
    def __init__(self, n_rep, n_shard, n_mp):
        self.n_rep, self.n_shard, self.n_mp = n_rep, n_shard, n_mp
        self.n_data = n_rep * n_shard
        self.pieces = 16 if (n_rep, n_shard, n_mp) == (2, 8, 2) else 1
        self.rows = BS // self.pieces
        self.depth = self.pieces.bit_length() - 1
        x, z1, z2, y = 1, 2, 4, 8
        gathering = (
            ((z2, y, z1, x), (z2, z1, x, y)),
            ((z2, z1, y, x), (z2, z1, x, y)),
            ((z2, x, z1, y), (z2, y, z1, x)),
            ((z2, x, y, z1), (z2, y, z1, x)),
        )
        reducing = (((z2, z1, y, x), (z2, z1, x, y)),) + gathering[1:]
        self.orders = gathering + reducing

    def swap_core(self, value):
        return lax.ppermute(value, "mp", [(i, i ^ 1) for i in range(self.n_mp)])

    def swap_rep(self, value):
        return lax.ppermute(value, "rep", [(i, i ^ 1) for i in range(self.n_rep)])

    def swap_data(self, value, group, step):
        pairs = []
        for i in range(self.n_data):
            for m in range(self.n_mp):
                there = i ^ self.orders[group][m][step]
                pairs.append((i * self.n_mp + m, there * self.n_mp + m))
        return lax.ppermute(value, ("rep", "shard", "mp"), pairs)

    def table(self, group, core, data_index):
        many = self.pieces
        if many == 1:
            return jnp.stack([0, 0, 0, 0, core]).astype(jnp.int32)
        half = many // 4
        rel = []
        for order in self.orders[group]:
            rel.append([sum(b for s, b in enumerate(order) if q >> s & 1) for q in range(many)])
        rows = []
        for m in range(self.n_mp):
            place = [rel[1 - m].index(r) // 2 for r in rel[m][::2]]
            low = [p for p in place if p < half][0]
            high = [p - half for p in place if p >= half][0]
            lows, highs = [], []
            for p in place:
                low, high = (p, high) if p < half else (low, p - half)
                lows.append(low)
                highs.append(high)
            rows.append([chunk_of(r) for r in rel[m]] + lows + highs + [int(p >= half) for p in place])
        mine = jnp.asarray(np.array(rows, np.int32))[core]
        chunks = mine[:many] ^ chunk_of(data_index)
        return jnp.concatenate([chunks, mine[many:], core.reshape(1)]).astype(jnp.int32)


def together(*values):
    return lax.optimization_barrier(values)


class Flow:
    def __init__(self, rounds):
        self.rounds = rounds
        self.flying = next(rounds)

    def advance(self, values):
        try:
            self.flying = self.rounds.send(values)
        except StopIteration as stop:
            self.flying = None
            self.result = stop.value

    def finish(self):
        while self.flying is not None:
            self.advance(self.flying)
        return self.result


def step(main, *flows):
    flows = [f for f in flows if f.flying is not None]
    values = list(together(*main, *[v for f in flows for v in f.flying]))
    main, values = values[: len(main)], values[len(main) :]
    for f in flows:
        many = len(f.flying)
        f.advance(tuple(values[:many]))
        values = values[many:]
    return main


def blocks_of(name, n_mp):
    rows, cols = SHAPES[name]
    return rows * cols // n_mp // (BS * BS)


def group_blocks(group, n_mp):
    return sum(blocks_of(name, n_mp) for name, _ in GROUPS[group])


def place_body(s, *refs, dests, many, two):
    q = pl.program_id(0)
    steps = many // 2 if two else 1
    if two:
        own_lo, own_hi, sib_lo, sib_hi = refs[:4]
        outs = refs[4:]
    else:
        own_lo, sib_lo = refs[:2]
        outs = refs[2:]
    core = s[many + 3 * steps]
    rows = own_lo.shape[2]
    for t in range(own_lo.shape[0]):
        here = pl.ds(0, rows)
        if two:
            here = pl.ds(pl.multiple_of((s[2 * q + t] & 1) * rows, rows), rows)
        for b in range(own_lo.shape[1]):
            own, sib = own_lo[t, b], sib_lo[t, b]
            if two:
                own = jnp.where(q < steps // 2, own, own_hi[t, b])
                sib = jnp.where(s[many + 2 * steps + q] == 0, sib, sib_hi[t, b])
            for h in range(2):
                which, row, col = dests[h][b]
                outs[which][row, here, col : col + BS] = jnp.where(core == h, own, sib)


def place(net, group, table, own, sib):
    many, rows, n_mp = net.pieces, net.rows, net.n_mp
    two = many > 1
    per = 2 if two else 1
    steps = many // per
    half = max(steps // 2, 1)
    dests = ([], [])
    shapes, specs = [], []
    for which, (name, wide) in enumerate(GROUPS[group]):
        height, width = SHAPES[name]
        tall = height if wide else height // n_mp
        flat = width // n_mp if wide else width
        for h in range(n_mp):
            for r in range(tall // BS):
                for c in range(flat // BS):
                    if wide:
                        dests[h].append((which, r, h * flat + c * BS))
                    else:
                        dests[h].append((which, h * (tall // BS) + r, c * BS))
        shapes.append(jax.ShapeDtypeStruct((height // BS, BS, width), bf16))
        specs.append(
            pl.BlockSpec((height // BS, per * rows, width), lambda q, s: (0, s[per * q] // per, 0))
        )
    nb = own[0].shape[1]
    block = (per, nb, rows, BS)
    lo = pl.BlockSpec(block, lambda q, s: (jnp.minimum(q, half - 1), 0, 0, 0))
    hi = pl.BlockSpec(block, lambda q, s: (jnp.maximum(q - half, 0), 0, 0, 0))
    sib_lo = pl.BlockSpec(block, lambda q, s: (s[many + q], 0, 0, 0))
    sib_hi = pl.BlockSpec(block, lambda q, s: (s[many + steps + q], 0, 0, 0))
    out = pl.pallas_call(
        functools.partial(place_body, dests=dests, many=many, two=two),
        grid_spec=pltpu.PrefetchScalarGridSpec(
            num_scalar_prefetch=1,
            grid=(steps,),
            in_specs=[lo, hi, sib_lo, sib_hi] if two else [lo, sib_lo],
            out_specs=tuple(specs),
        ),
        out_shape=tuple(shapes),
        compiler_params=params(),
        cost_estimate=small(),
        name="place",
    )(table, *own, *sib)
    return [o.reshape(-1, o.shape[2]) for o in out]


def gather_rounds(net, group, piece):
    (piece,) = yield (piece,)
    cur = piece[None]
    if net.pieces == 1:
        (sib,) = yield (net.swap_core(cur),)
        return (cur,), (sib,)
    for k in range(net.depth - 1):
        (got,) = yield (net.swap_data(cur, group, k),)
        cur = jnp.concatenate([cur, got])
    got, sib_lo = yield (net.swap_data(cur, group, net.depth - 1), net.swap_core(cur))
    (sib_hi,) = yield (net.swap_core(got),)
    return (cur, got), (sib_lo, sib_hi)


def first_pieces(net, weights, vectors, inverse):
    low = weights[0].astype(bf16)
    vec = vectors.astype(bf16)
    if net.pieces == 1:
        every = lax.all_gather(low, "shard", axis=0, tiled=True)
        vec_every = lax.all_gather(vec, "shard", axis=1, tiled=True)
        return every.at[inverse].get(mode="promise_in_bounds"), vec_every
    nblk = low.shape[0]
    cut = low.reshape(nblk, 2, 2, 2, 2, net.rows, BS)
    cut = lax.dynamic_index_in_dim(cut, lax.axis_index("rep"), axis=1, keepdims=False)
    cut = cut.transpose(3, 1, 2, 0, 4, 5).reshape(net.n_shard, nblk, net.rows, BS)
    room = net.rows * BS
    vec_cut = jnp.pad(vec.reshape(-1), (0, room - vec.shape[1])).reshape(1, 1, net.rows, BS)
    cut = jnp.concatenate([cut, jnp.broadcast_to(vec_cut, (net.n_shard,) + vec_cut.shape[1:])], axis=1)
    every = lax.all_to_all(
        cut.reshape(-1, net.rows, BS), "shard", split_axis=0, concat_axis=0, tiled=True
    )
    pieces = every.at[inverse + inverse // nblk].get(mode="promise_in_bounds")
    vec_every = every.reshape(net.n_shard, nblk + 1, room)[:, nblk, : vec.shape[1]]
    return pieces, vec_every.reshape(1, -1)


def total_of(*terms):
    acc = terms[0].astype(f32)
    for t in terms[1:]:
        acc = acc + t.astype(f32)
    return acc.astype(bf16)


def reduce_rounds(net, group, parts):
    parts = yield parts
    if net.pieces == 1:
        return parts[0][0]
    lo, hi = parts
    (got,) = yield (net.swap_data(hi, group, net.depth - 1),)
    terms = [lo, got]
    for k in range(net.depth - 2, -1, -1):
        width = 1 << k
        send = total_of(*[t[width:] for t in terms])
        keep = total_of(*[t[:width] for t in terms])
        (got,) = yield (net.swap_data(send, group, k),)
        terms = [keep, got]
    return total_of(*terms)[0]


def last_pieces(net, natural, block_slots, vec_sum):
    if net.pieces == 1:
        dealt = natural.at[block_slots].get(mode="promise_in_bounds")
        owned = lax.psum_scatter(dealt, "shard", scatter_dimension=0, tiled=True)
        owned = total_of(owned, net.swap_rep(owned))
        cut = owned.reshape(-1, 2, 8, 16, BS).transpose(1, 2, 0, 3, 4)
        cut = cut[:, np.array([chunk_of(k) for k in range(8)])]
        vec = lax.psum_scatter(vec_sum, "shard", scatter_dimension=0, tiled=True)[None]
        parts = [(cut[0], cut[1], owned.shape[0])]
        return parts, jnp.zeros((1,), jnp.int32), vec + net.swap_rep(vec)
    n = net.n_shard
    slots = block_slots.reshape(n, -1)
    half = slots.shape[1] // 2
    room = net.rows * BS
    vec_cut = vec_sum.reshape(n, -1)
    width = vec_cut.shape[1]
    vec_cut = jnp.pad(vec_cut.astype(bf16), ((0, 0), (0, room - width)))
    vec_cut = vec_cut.reshape(n, 1, net.rows, BS)
    cuts = []
    for k in range(2):
        index = slots[:, k * half : (k + 1) * half].reshape(-1)
        cuts.append(natural.at[index].get(mode="promise_in_bounds").reshape(n, half, net.rows, BS))
    cuts[1] = jnp.concatenate([cuts[1], vec_cut], axis=1)

    def home(cut):
        back = lax.all_to_all(
            cut.reshape(-1, net.rows, BS), "shard", split_axis=0, concat_axis=0, tiled=True
        )
        return back.reshape(n, -1, net.rows, BS)

    mine, cuts[1] = together(home(cuts[0]), cuts[1])
    other = net.swap_rep(mine)
    other, last = together(other, home(cuts[1]))
    parts = [(mine, other, half), (last, net.swap_rep(last), half)]
    terms = [v[:, half].reshape(n, room)[:, :width].astype(f32) for v in parts[1][:2]]
    flag = lax.axis_index("rep").astype(jnp.int32).reshape(1)
    return parts, flag, jnp.sum(terms[0] + terms[1], axis=0, keepdims=True)


def attend_forward_body(lim, q_ref, k_ref, v_ref, o_ref, lse_ref, *, causal, rows):
    pair = pl.program_id(0)
    seq, keys = q_ref.shape[0], k_ref.shape[0]
    lane = lax.broadcasted_iota(jnp.int32, (1, LANES), 1)
    top = lim[0] - 1

    @pl.when(pair == 0)
    def _():
        lse_ref[...] = jnp.zeros_like(lse_ref)

    for blk in range(seq // rows):
        here = pl.ds(blk * rows, rows)
        width = (blk + 1) * rows if causal else keys
        q = q_ref[here, :] * bf16(scale)
        k = k_ref[pl.ds(0, width), :]
        v = v_ref[pl.ds(0, width), :]
        outs = []
        kept = lse_ref[here, :]
        if causal:
            row = lax.broadcasted_iota(jnp.int32, (rows, 1), 0) + blk * rows
            col = lax.broadcasted_iota(jnp.int32, (1, width), 1)
            allowed = col <= jnp.minimum(row, top)
        for h in range(2):
            mine = (lane // HEAD_DIM) == h
            s = dot_nt(jnp.where(mine, q, bf16(0)), k)
            if causal:
                s = jnp.where(allowed, s, masked_score)
            peak = jnp.max(s, axis=1, keepdims=True)
            e = jnp.exp(s - peak)
            mass = jnp.sum(e, axis=1, keepdims=True)
            outs.append(dot_nn(e.astype(bf16), v) * (1.0 / mass))
            kept = jnp.where(lane == 2 * pair + h, peak + jnp.log(mass), kept)
        o_ref[here, :] = jnp.where(lane < HEAD_DIM, outs[0], outs[1]).astype(bf16)
        lse_ref[here, :] = kept


def attend_forward(limit, q, k, v, causal):
    seq, width = q.shape
    keys = k.shape[0]
    pairs = width // LANES
    rows = min(128 if causal else 256, seq)
    o, lse = pl.pallas_call(
        functools.partial(attend_forward_body, causal=causal, rows=rows),
        grid=(pairs,),
        out_shape=(
            jax.ShapeDtypeStruct((seq, width), bf16),
            jax.ShapeDtypeStruct((seq, LANES), f32),
        ),
        in_specs=[
            pl.BlockSpec(memory_space=pltpu.SMEM),
            pl.BlockSpec((seq, LANES), lambda i: (0, i)),
            pl.BlockSpec((keys, LANES), lambda i: (0, i)),
            pl.BlockSpec((keys, LANES), lambda i: (0, i)),
        ],
        out_specs=(
            pl.BlockSpec((seq, LANES), lambda i: (0, i)),
            pl.BlockSpec((seq, LANES), lambda i: (0, 0)),
        ),
        compiler_params=params(),
        cost_estimate=small(),
        name="attend_forward",
    )(limit, q, k, v)
    return o, lse[:, : 2 * pairs].T.reshape(pairs, 2, seq)


def attend_backward_body(
    lim, q_ref, k_ref, v_ref, o_ref, do_ref, lse_ref, dq_ref, dk_ref, dv_ref, dk_acc, dv_acc, *, causal, rows
):
    seq, keys = q_ref.shape[0], k_ref.shape[0]
    lane = lax.broadcasted_iota(jnp.int32, (1, LANES), 1)
    top = lim[0] - 1
    dk_acc[...] = jnp.zeros_like(dk_acc)
    dv_acc[...] = jnp.zeros_like(dv_acc)
    head_row = lax.broadcasted_iota(jnp.int32, (8, LANES), 0)
    head_lane = lax.broadcasted_iota(jnp.int32, (8, LANES), 1) // HEAD_DIM
    pick = (head_row == head_lane).astype(bf16)
    for blk in range(seq // rows):
        here = pl.ds(blk * rows, rows)
        width = (blk + 1) * rows if causal else keys
        span = pl.ds(0, width)
        q = q_ref[here, :] * bf16(scale)
        do = do_ref[here, :]
        k = k_ref[span, :]
        v = v_ref[span, :]
        prod = do.astype(f32) * o_ref[here, :].astype(f32)
        hi = prod.astype(bf16)
        lo = (prod - hi.astype(f32)).astype(bf16)
        delta = dot_nt(pick, hi) + dot_nt(pick, lo)
        lse = lse_ref[0][:, blk * rows : (blk + 1) * rows]
        if causal:
            key = lax.broadcasted_iota(jnp.int32, (width, 1), 0)
            row = lax.broadcasted_iota(jnp.int32, (1, rows), 1) + blk * rows
            allowed = key <= jnp.minimum(row, top)
        dq = jnp.zeros((rows, LANES), f32)
        dk = jnp.zeros((width, LANES), f32)
        dv = jnp.zeros((width, LANES), f32)
        for h in range(2):
            mine = (lane // HEAD_DIM) == h
            qm = jnp.where(mine, q, bf16(0))
            dom = jnp.where(mine, do, bf16(0))
            km = jnp.where(mine, k, bf16(0))
            s = dot_nt(k, qm)
            if causal:
                s = jnp.where(allowed, s, masked_score)
            p = jnp.exp(s - lse[h : h + 1, :])
            dp = dot_nt(v, dom)
            ds = (p * (dp - delta[h : h + 1, :])).astype(bf16)
            dv = dv + dot_nn(p.astype(bf16), dom)
            dk = dk + dot_nn(ds, qm)
            dq = dq + dot_tn(ds, km)
        dq_ref[here, :] = (dq * scale).astype(bf16)
        dk_acc[span, :] += dk
        dv_acc[span, :] += dv
    dk_ref[...] = dk_acc[...].astype(bf16)
    dv_ref[...] = dv_acc[...].astype(bf16)


def attend_backward(limit, q, k, v, o, do, lse, causal):
    seq, width = q.shape
    keys = k.shape[0]
    pairs = width // LANES
    rows = min(128 if causal else 256, seq)
    q_spec = pl.BlockSpec((seq, LANES), lambda i: (0, i))
    k_spec = pl.BlockSpec((keys, LANES), lambda i: (0, i))
    return pl.pallas_call(
        functools.partial(attend_backward_body, causal=causal, rows=rows),
        grid=(pairs,),
        out_shape=(
            jax.ShapeDtypeStruct((seq, width), bf16),
            jax.ShapeDtypeStruct((keys, width), bf16),
            jax.ShapeDtypeStruct((keys, width), bf16),
        ),
        in_specs=[
            pl.BlockSpec(memory_space=pltpu.SMEM),
            q_spec,
            k_spec,
            k_spec,
            q_spec,
            q_spec,
            pl.BlockSpec((1, 2, seq), lambda i: (i, 0, 0)),
        ],
        out_specs=(q_spec, k_spec, k_spec),
        scratch_shapes=[pltpu.VMEM((keys, LANES), f32), pltpu.VMEM((keys, LANES), f32)],
        compiler_params=params(),
        cost_estimate=small(),
        name="attend_backward",
    )(limit, q, k, v, o, do, lse)


def gelu_body(h_ref, w_ref, b_ref, act_ref, slope_ref, u_ref, *, chunk):
    u_ref[...] = dot_nn(h_ref[...], w_ref[...]) + b_ref[...]

    def part(i):
        here = pl.ds(pl.multiple_of(i * chunk, chunk), chunk)
        u = u_ref[here, :]
        x = jnp.abs(u) * (0.5**0.5)
        t = 1.0 / (1.0 + ERFC_SLOPE * x)
        poly = jnp.full_like(t, ERFC_POLY[-1])
        for c in ERFC_POLY[-2::-1]:
            poly = poly * t + c
        bell = jnp.exp(-0.5 * (u * u))
        tail = 0.5 * (bell * (t * poly))
        cdf = jnp.where(u < 0, tail, 1.0 - tail)
        act_ref[here, :] = (u * cdf).astype(bf16)
        slope_ref[here, :] = (cdf + u * (bell * 0.3989422804014327)).astype(bf16)

    pl.loop(0, u_ref.shape[0] // chunk)(part)


def gelu_forward(h, w, b):
    seq, width = h.shape
    hidden = w.shape[1]
    tile = 512
    spec = pl.BlockSpec((seq, tile), lambda i: (0, i))
    return pl.pallas_call(
        functools.partial(gelu_body, chunk=32),
        grid=(hidden // tile,),
        out_shape=(jax.ShapeDtypeStruct((seq, hidden), bf16),) * 2,
        in_specs=[
            pl.BlockSpec((seq, width), lambda i: (0, 0)),
            pl.BlockSpec((width, tile), lambda i: (0, i)),
            pl.BlockSpec((1, tile), lambda i: (0, i)),
        ],
        out_specs=(spec, spec),
        scratch_shapes=[pltpu.VMEM((seq, tile), f32)],
        compiler_params=params(),
        cost_estimate=small(),
        name="gelu_forward",
    )(h, w, b)


def weight_grad_body(s, x_own, x_sib, *refs, count, outs, many, rows, nb):
    y_own, y_sib = refs[:count], refs[count : 2 * count]
    targets = refs[-3 - outs : -3]
    t_own, t_sib, buf = refs[-3:]
    t_own[...] = x_own[...].T
    t_sib[...] = x_sib[...].T
    per = many // outs
    for k in range(count):
        acc = dot_nn(t_own[...], y_own[k][...]) + dot_nn(t_sib[...], y_sib[k][...])
        buf[k] = acc.astype(bf16)
    for q in range(many):
        for r in range(x_own.shape[1] // BS):
            here = pl.ds(pl.multiple_of(s[q] * rows + r * BS, rows), rows)
            for k in range(count):
                for c in range(nb):
                    targets[q // per][q % per, k, r * nb + c] = buf[k, here, c * BS : (c + 1) * BS]


def weight_grad(net, group, table, xs, ys, held, first, wide):
    seq = xs[0].shape[0]
    many, rows, halves = net.pieces, net.rows, net.n_mp
    at_core = table.shape[0] - 1
    count = len(ys)
    width = ys[0][0].shape[1]
    if wide:
        tall = xs[0].shape[1] // BS
        deep = 2 if tall >= 4 else 1
        steps = tall // deep
        y_width = width // halves
        x_spec = pl.BlockSpec((seq, deep * BS), lambda i, s: (0, i))
        y_spec = pl.BlockSpec((seq, y_width), lambda i, s: (0, s[at_core]))
    else:
        tall = xs[0].shape[1] // halves // BS
        deep = 2 if tall >= 4 else 1
        steps = tall // deep
        y_width = width
        x_spec = pl.BlockSpec((seq, deep * BS), lambda i, s: (0, s[at_core] * steps + i))
        y_spec = pl.BlockSpec((seq, y_width), lambda i, s: (0, 0))
    nb = y_width // BS
    at = first // count
    outs = 2 if many > 1 else 1
    shape = (many // outs, len(GROUPS[group]), tall * nb, rows, BS)
    anyspec = pl.BlockSpec(memory_space=pl.ANY)
    held = held or ()
    before = 3 + 2 * count
    return pl.pallas_call(
        functools.partial(
            weight_grad_body, count=count, outs=outs, many=many, rows=rows, nb=nb
        ),
        grid_spec=pltpu.PrefetchScalarGridSpec(
            num_scalar_prefetch=1,
            grid=(steps,),
            in_specs=[x_spec] * 2 + [y_spec] * (2 * count) + [anyspec] * len(held),
            out_specs=(
                pl.BlockSpec((many // outs, count, deep * nb, rows, BS), lambda i, s: (0, at, i, 0, 0)),
            )
            * outs,
            scratch_shapes=[
                pltpu.VMEM((deep * BS, seq), bf16),
                pltpu.VMEM((deep * BS, seq), bf16),
                pltpu.VMEM((count, deep * BS, y_width), bf16),
            ],
        ),
        out_shape=(jax.ShapeDtypeStruct(shape, bf16),) * outs,
        input_output_aliases={before + k: k for k in range(len(held))},
        compiler_params=params(),
        cost_estimate=small(),
        name="weight_grad",
    )(table, *xs, *[y[0] for y in ys], *[y[1] for y in ys], *held)


def split_low(a):
    hi = a.astype(bf16)
    return hi, (a - hi.astype(f32)).astype(bf16)


def shampoo_body(flag, mine_ref, other_ref, w_ref, ls_ref, rs_ref, lr_ref, rr_ref, *refs):
    og, ol, orr, ow, g_ref = refs[-5:]
    for j in range(mine_ref.shape[1]):
        for k in range(mine_ref.shape[0]):
            for plane, src in ((flag[0], mine_ref), (1 - flag[0], other_ref)):
                row = pl.multiple_of(plane * 128 + chunk_of(k) * 16, 16)
                g_ref[j, pl.ds(row, 16), :] = src[k, j]
    for j in range(mine_ref.shape[1]):
        g = g_ref[j]
        og[0, j] = g.astype(f32)
        ol[0, j] = 0.5 * ls_ref[0, j] + 0.5 * dot_nt(g, g)
        orr[0, j] = 0.5 * rs_ref[0, j] + 0.5 * dot_tn(g, g)
        r_hi, r_lo = split_low(rr_ref[0, j])
        i_hi, i_lo = split_low(dot_nn(g, r_hi) + dot_nn(g, r_lo))
        l_hi, l_lo = split_low(lr_ref[0, j])
        d = dot_nn(l_hi, i_hi) + (dot_nn(l_hi, i_lo) + dot_nn(l_lo, i_hi))
        mean = jnp.mean(jnp.mean(d * d, axis=1, keepdims=True), axis=0, keepdims=True)
        ow[0, j] = w_ref[0, j] - (D**-0.5) * d / jnp.sqrt(mean + 1e-06)


def shampoo(flag, parts, *states):
    total = states[0].shape[1]
    out, first = (), 0
    for mine, other, n in parts:
        per = 2 if n % 2 == 0 else 1
        at = first // per
        spec = pl.BlockSpec((1, per, BS, BS), lambda i, at=at: (0, at + i, 0, 0))
        g_spec = pl.BlockSpec((mine.shape[0], per, mine.shape[2], BS), lambda i: (0, i, 0, 0))
        anyspec = pl.BlockSpec(memory_space=pl.ANY)
        out = pl.pallas_call(
            shampoo_body,
            grid=(n // per,),
            out_shape=(jax.ShapeDtypeStruct((1, total, BS, BS), f32),) * 4,
            in_specs=[pl.BlockSpec(memory_space=pltpu.SMEM), g_spec, g_spec]
            + [spec] * 5
            + [anyspec] * len(out),
            out_specs=(spec,) * 4,
            scratch_shapes=[pltpu.VMEM((per, BS, BS), bf16)],
            input_output_aliases={8 + k: k for k in range(len(out))},
            compiler_params=params(),
            cost_estimate=small(),
            name="shampoo",
        )(flag, mine, other, *states, *out)
        first += n
    return out


def norm_forward(z, gain, shift):
    center = z - jnp.mean(z, axis=1, keepdims=True)
    inv = lax.rsqrt(jnp.mean(center * center, axis=1, keepdims=True) + eps_norm)
    normed = center * inv
    return normed * gain + shift, normed, inv


def norm_backward(grad, normed, inv, gain):
    scaled = grad * gain
    mean_plain = jnp.mean(scaled, axis=1, keepdims=True)
    mean_cross = jnp.mean(scaled * normed, axis=1, keepdims=True)
    back = inv * (scaled - mean_plain - normed * mean_cross)
    return back, jnp.sum(grad * normed, axis=0), jnp.sum(grad, axis=0)


def inverse_of(order):
    many = jnp.arange(order.shape[0], dtype=jnp.int32)
    return jnp.sum(jnp.where(order[:, None] == many[None, :], many[:, None], 0), axis=0)


def route_out(value):
    axes = ("rep", "shard")
    count = lax.axis_size(axes)
    cut = value.reshape(value.shape[0], count, value.shape[1] // count, value.shape[2])
    return lax.all_to_all(cut, axes, split_axis=1, concat_axis=0, tiled=True)


def route_home(pieces, ordering):
    moved = pieces.at[ordering].get(mode="promise_in_bounds")
    back = lax.all_to_all(moved, ("rep", "shard"), split_axis=0, concat_axis=1, tiled=True)
    return back.reshape(back.shape[0], -1, back.shape[3])


def per_device(
    net,
    inputs,
    encoded,
    cotangent,
    lengths,
    seq_slots,
    block_slots,
    weights,
    left_stat,
    right_stat,
    left_root,
    right_root,
    vectors,
    vec_stat,
):
    half_d = inputs.shape[2]
    halves = D // half_d
    core = lax.axis_index("mp")
    data_index = lax.axis_index(("rep", "shard"))
    seq_index = data_index * inputs.shape[0] + core
    limit = lax.dynamic_slice_in_dim(lengths, seq_index, 1)
    tables = [net.table(k, core, data_index) for k in range(2 * len(GROUPS))]
    is_first = core == 0

    def pick(pair, which):
        return lax.dynamic_index_in_dim(pair, which, axis=0, keepdims=False)

    def joined(low_half, high_half):
        return jnp.concatenate(
            [
                jnp.where(is_first, low_half, high_half),
                jnp.where(is_first, high_half, low_half),
            ],
            axis=1,
        )

    def whole(value):
        other = net.swap_core(value)
        own = joined(pick(value, core), pick(other, core))
        sib = joined(pick(value, 1 - core), pick(other, 1 - core))
        return own, sib

    def halved(full):
        mine = lax.dynamic_slice_in_dim(full, core * half_d, half_d, axis=1)
        away = lax.dynamic_slice_in_dim(full, (1 - core) * half_d, half_d, axis=1)
        got = net.swap_core(away)
        return jnp.stack([jnp.where(is_first, mine, got), jnp.where(is_first, got, mine)])

    x, x_sib = whole(inputs)
    e, e_sib = whole(encoded)

    pieces, vec_mine = first_pieces(net, weights, vectors, inverse_of(block_slots))
    flows, base = [], 0
    for k in range(len(GROUPS)):
        size = group_blocks(k, halves)
        flows.append(Flow(gather_rounds(net, k, pieces[base : base + size])))
        base += size
    attn, cross, up, down = flows

    def placed(k):
        return place(net, k, tables[k], *flows[k].finish())

    step((), attn)
    step((), attn, cross)
    step((), attn)
    step((), attn, cross)
    vec_mine, x, x_sib, e, e_sib = step((vec_mine, x, x_sib, e, e_sib), attn, cross, up)
    w_sq, w_sk, w_sv = step(placed(0), up)

    vec_other = net.swap_core(vec_mine)
    vec_both = jnp.concatenate(
        [jnp.where(is_first, vec_mine, vec_other), jnp.where(is_first, vec_other, vec_mine)]
    ).astype(f32)
    vecs = [vec_both[:, i * half_d : (i + 1) * half_d].reshape(1, D) for i in range(13)]
    vecs.append(vec_both[:, 13 * half_d :].reshape(1, FF))
    b_sq, b_sv, b_so, g_one, b_one, b_cq, b_cv, b_co, g_two, b_two, b_fo, g_three, b_three, b_fi = vecs

    q_s = (dot_nn(x, w_sq) + b_sq).astype(bf16)
    k_s = dot_nn(x, w_sk).astype(bf16)
    v_s = (dot_nn(x, w_sv) + b_sv).astype(bf16)
    q_s, k_s, v_s = step((q_s, k_s, v_s), cross, up, down)
    o_s, lse_s = attend_forward(limit, q_s, k_s, v_s, True)
    cotangent, o_s, lse_s = step((cotangent, o_s, lse_s), cross, up, down)
    cot_pieces = route_out(cotangent)
    w_so, w_cq, w_ck, w_cv, w_co = placed(1)
    z_one = x.astype(f32) + dot_nn(o_s, w_so) + b_so
    h_one, n_one, r_one = norm_forward(z_one, g_one, b_one)
    h_one_low = h_one.astype(bf16)
    q_c = (dot_nn(h_one_low, w_cq) + b_cq).astype(bf16)
    k_c = dot_nn(e, w_ck).astype(bf16)
    v_c = (dot_nn(e, w_cv) + b_cv).astype(bf16)
    q_c, k_c, v_c = step((q_c, k_c, v_c), down)
    o_c, lse_c = attend_forward(limit, q_c, k_c, v_c, False)
    z_two = h_one + dot_nn(o_c, w_co) + b_co
    h_two, n_two, r_two = norm_forward(z_two, g_two, b_two)
    cot_pieces, h_two, h_two_low = step((cot_pieces, h_two, h_two.astype(bf16)), up, down)
    cot_home = route_home(cot_pieces, seq_slots)
    (w_fi,) = placed(2)
    act, slope = gelu_forward(h_two_low, w_fi, b_fi)
    act_sib = net.swap_core(act)
    act, slope = step((act, slope), down)
    (w_fo,) = placed(3)
    z_three = h_two + dot_nn(act, w_fo) + b_fo
    cot, _ = whole(cot_home)
    h_three, n_three, r_three = norm_forward(z_three, g_three, b_three)
    live = (jnp.arange(x.shape[0]) < limit).astype(f32)[:, None]
    source = inverse_of(seq_slots)
    finished = (h_three * live).astype(bf16)

    def gradient(k, *calls):
        held, first = None, 0
        for xs, *ys in calls:
            held = weight_grad(net, k, tables[len(GROUPS) + k], xs, ys, held, first, GROUPS[k][first][1])
            first += len(ys)
        parts = tuple(h.reshape(h.shape[0], -1, net.rows, BS) for h in held)
        return Flow(reduce_rounds(net, len(GROUPS) + k, parts))

    grad_y = cot.astype(f32) * live
    d_three, dg_three, db_three = norm_backward(grad_y, n_three, r_three, g_three)
    a_three = d_three.astype(bf16)
    d_hidden = (dot_nt(a_three, w_fo) * slope.astype(f32)).astype(bf16)
    a_three_sib, d_hidden = step((net.swap_core(a_three), d_hidden))
    d_hidden_sib = net.swap_core(d_hidden)
    down = gradient(3, ((act, act_sib), (a_three, a_three_sib)))
    finished, d_hidden, d_hidden_sib = step((finished, d_hidden, d_hidden_sib), down)
    finished = halved(finished)
    d_h_two = d_three + dot_nt(d_hidden, w_fi)
    d_two, dg_two, db_two = norm_backward(d_h_two, n_two, r_two, g_two)
    a_two = d_two.astype(bf16)
    d_oc = dot_nt(a_two, w_co).astype(bf16)
    finished, d_hidden, d_hidden_sib, d_oc = step((finished, d_hidden, d_hidden_sib, d_oc))
    out_pieces = route_out(finished)
    up = gradient(2, ((h_two_low, net.swap_core(h_two_low)), (d_hidden, d_hidden_sib)))
    (d_oc,) = step((d_oc,), up, down)
    dq_c, dk_c, dv_c = attend_backward(limit, q_c, k_c, v_c, o_c, d_oc, lse_c, False)
    dq_c_sib, dk_c_sib, dv_c_sib = [net.swap_core(v) for v in (dq_c, dk_c, dv_c)]
    dq_c, dk_c, dv_c = step((dq_c, dk_c, dv_c), down)
    d_h_one = d_two + dot_nt(dq_c, w_cq)
    d_one, dg_one, db_one = norm_backward(d_h_one, n_one, r_one, g_one)
    a_one = d_one.astype(bf16)
    a_one_sib = net.swap_core(a_one)
    d_os = dot_nt(a_one, w_so).astype(bf16)
    out_pieces, a_one, a_one_sib, d_os = step((out_pieces, a_one, a_one_sib, d_os))
    outputs = route_home(out_pieces, source)
    cross = gradient(
        1,
        ((o_s, net.swap_core(o_s)), (a_one, a_one_sib)),
        ((h_one_low, net.swap_core(h_one_low)), (dq_c, dq_c_sib)),
        ((e, e_sib), (dk_c, dk_c_sib), (dv_c, dv_c_sib)),
        ((o_c, net.swap_core(o_c)), (a_two, net.swap_core(a_two))),
    )
    outputs, d_os = step((outputs, d_os), cross, up, down)
    dq_s, dk_s, dv_s = attend_backward(limit, q_s, k_s, v_s, o_s, d_os, lse_s, True)
    sibs = [net.swap_core(v) for v in (dq_s, dk_s, dv_s)]
    dq_s, dk_s, dv_s = step((dq_s, dk_s, dv_s), cross, up)
    attn = gradient(0, ((x, x_sib), *zip((dq_s, dk_s, dv_s), sibs)))
    dq_s, dk_s, dv_s = step((dq_s, dk_s, dv_s), attn)
    dk_c, dv_c, dq_s, dk_s, dv_s = step((dk_c, dv_c, dq_s, dk_s, dv_s), cross, up, down)
    state_back = dot_nt(dk_c, w_ck) + dot_nt(dv_c, w_cv)
    back = d_one + dot_nt(dq_s, w_sq) + dot_nt(dk_s, w_sk) + dot_nt(dv_s, w_sv)
    back, d_hidden, dq_c, dv_c = step((back, d_hidden, dq_c, dv_c), attn, cross, up)
    input_grad = halved(back.astype(bf16))
    encoded_grad = halved(state_back.astype(bf16))
    dq_s, dv_s = step((dq_s, dv_s), attn)
    columns = [jnp.sum(v.astype(f32), axis=0) for v in (d_hidden, dq_c, dv_c, dq_s, dv_s)]
    *columns, input_grad, encoded_grad = step((*columns, input_grad, encoded_grad), attn, cross, up)
    sums = (
        columns[3],
        columns[4],
        jnp.sum(d_one, axis=0),
        dg_one,
        db_one,
        columns[1],
        columns[2],
        jnp.sum(d_two, axis=0),
        dg_two,
        db_two,
        jnp.sum(d_three, axis=0),
        dg_three,
        db_three,
        columns[0],
    )
    vec_pair = jnp.concatenate([s.reshape(halves, -1) for s in sums], axis=1)
    vec_sum = pick(vec_pair, core) + net.swap_core(pick(vec_pair, 1 - core))
    natural = [f.finish() for f in (attn, cross, up, down)]

    parts, flag, vec_owned = last_pieces(net, jnp.concatenate(natural), block_slots, vec_sum)
    block_grad, left_new, right_new, weights_new = shampoo(
        flag, parts, weights, left_stat, right_stat, left_root, right_root
    )
    vec_stat_new = 0.5 * vec_stat + 0.5 * vec_owned * vec_owned
    vectors_new = vectors - 0.1 * vec_owned * lax.rsqrt(vec_stat_new)
    return (
        outputs,
        input_grad,
        encoded_grad,
        block_grad,
        left_new,
        right_new,
        weights_new,
        vec_owned,
        vec_stat_new,
        vectors_new,
    )


def solution(mesh):
    net = Net(mesh.shape["rep"], mesh.shape["shard"], mesh.shape["mp"])
    rows = P(("rep", "shard"), None, "mp")
    blocks = P("mp", "shard", None, None)
    vector = P("mp", "shard")
    in_specs = (rows, rows, rows, P(), P(), P()) + (blocks,) * 5 + (vector, vector)
    out_specs = (rows, rows, rows) + (blocks,) * 4 + (vector,) * 3
    return jax.shard_map(
        functools.partial(per_device, net),
        mesh=mesh,
        in_specs=in_specs,
        out_specs=out_specs,
        check_vma=False,
    )
```
